32 devices in a mesh: ctx: 8 (over y, x, core), fsdp: 4 (over z).
Axes of the slice: x: 2, y: 2, z: 4, core: 2. Of those that a mesh axis runs over, the one named last changes fastest.
Arguments:
- tokens: bfloat16 [4, 1024, 2048], P('fsdp', 'ctx'), may hold values from -6 to 6
- per_layer: bfloat16 [4, 1024, 256], P('fsdp', 'ctx'), may hold values from -6 to 6
- out_grad: bfloat16 [4, 1024, 2048], P('fsdp', 'ctx'), may hold values from -6 to 6
- segment_ids: int32 [4, 1024], P('fsdp'), may hold values from 0 to 8, as said below
- query_weight: bfloat16 [2048, 2048], P('fsdp'), may hold values from -0.125 to 0.125
- key_weight: bfloat16 [2048, 512], P('fsdp'), may hold values from -0.125 to 0.125
- value_weight: bfloat16 [2048, 512], P('fsdp'), may hold values from -0.125 to 0.125
- out_weight: bfloat16 [2048, 2048], P('fsdp'), may hold values from -0.125 to 0.125
- left_weight: bfloat16 [2048, 64], P('fsdp'), may hold values from -0.125 to 0.125
- right_weight: bfloat16 [64, 2048], P(None, 'fsdp'), may hold values from -0.75 to 0.75
- gate_weight: bfloat16 [2048, 8192], P(None, 'fsdp'), may hold values from -0.125 to 0.125
- up_weight: bfloat16 [2048, 8192], P(None, 'fsdp'), may hold values from -0.125 to 0.125
- down_weight: bfloat16 [8192, 2048], P('fsdp'), may hold values from -0.0625 to 0.0625
- side_gate: bfloat16 [2048, 256], P('fsdp'), may hold values from -0.125 to 0.125
- side_out: bfloat16 [256, 2048], P('fsdp'), may hold values from -0.375 to 0.375
- input_gain: float32 [2048], replicated, may hold values from 0.25 to 1.75
- laurel_gain: float32 [2048], replicated, may hold values from 0.25 to 1.75
- attn_gain: float32 [2048], replicated, may hold values from 0.25 to 1.75
- pre_gain: float32 [2048], replicated, may hold values from 0.25 to 1.75
- post_gain: float32 [2048], replicated, may hold values from 0.25 to 1.75
- side_gain: float32 [2048], replicated, may hold values from 0.25 to 1.75
- query_gain: float32 [256], replicated, may hold values from 0.25 to 0.5
- key_gain: float32 [256], replicated, may hold values from 0.25 to 0.5
Outputs:
- block_out: bfloat16 [4, 1024, 2048], P('fsdp', 'ctx')
- tokens_grad: bfloat16 [4, 1024, 2048], P('fsdp', 'ctx')
- per_layer_grad: bfloat16 [4, 1024, 256], P('fsdp', 'ctx')
- query_weight_grad: float32 [2048, 2048], P('ctx', 'fsdp')
- key_weight_grad: float32 [2048, 512], P('ctx', 'fsdp')
- value_weight_grad: float32 [2048, 512], P('ctx', 'fsdp')
- out_weight_grad: float32 [2048, 2048], P('ctx', 'fsdp')
- left_weight_grad: float32 [2048, 64], P(('ctx', 'fsdp'))
- right_weight_grad: float32 [64, 2048], P(None, ('ctx', 'fsdp'))
- gate_weight_grad: float32 [2048, 8192], P('ctx', 'fsdp')
- up_weight_grad: float32 [2048, 8192], P('ctx', 'fsdp')
- down_weight_grad: float32 [8192, 2048], P('fsdp', 'ctx')
- side_gate_grad: float32 [2048, 256], P('ctx', 'fsdp')
- side_out_grad: float32 [256, 2048], P('ctx', 'fsdp')
- input_gain_grad: float32 [2048], P(('ctx', 'fsdp'))
- laurel_gain_grad: float32 [2048], P(('ctx', 'fsdp'))
- attn_gain_grad: float32 [2048], P(('ctx', 'fsdp'))
- pre_gain_grad: float32 [2048], P(('ctx', 'fsdp'))
- post_gain_grad: float32 [2048], P(('ctx', 'fsdp'))
- side_gain_grad: float32 [2048], P(('ctx', 'fsdp'))
- query_gain_grad: float32 [256], P(('ctx', 'fsdp'))
- key_gain_grad: float32 [256], P(('ctx', 'fsdp'))
The draws below stay inside these ranges and needn't reach their ends.
Inputs may be any that keep to these rules, and one draw needn't show every extreme that they name: `segment_ids`: within a sequence the ids never fall; one document of each sequence begins within the first 128 tokens and ends within the last 128; every other document lies wholly within the first 128 or the last 128 tokens.
All inputs are finite; a program needn't handle non-finite values.
Results may differ from the reference program's by a relative error of at most 0.034.
Values may be sent and summed in bfloat16 or wider, within the bound.
A program may use at most 448 MiB of HBM per device.

```python
import math
import jax
import jax.numpy as jnp
from jax import lax

D = 2048
HEADS = 8
KV_HEADS = 2
HD = 256
FF = 8192
RANK = 64
PL = 256
TOK_DEV = 128
SEQS = 4
LEN = 1024


def draw_segment_ids(key, part):
    subkeys = jax.random.split(key, 4)
    positions = jnp.arange(LEN, dtype=jnp.int32)
    opening = jax.random.randint(subkeys[0], (SEQS, 1), 2, TOK_DEV, dtype=jnp.int32)
    finish = LEN - jax.random.randint(subkeys[1], (SEQS, 1), 2, TOK_DEV, dtype=jnp.int32)
    early_cuts = jax.random.randint(subkeys[2], (SEQS, 3), 1, opening, dtype=jnp.int32)
    late_cuts = jax.random.randint(subkeys[3], (SEQS, 3), finish + 1, LEN, dtype=jnp.int32)
    result = (positions[None, :] >= opening).astype(jnp.int32) + (positions[None, :] >= finish).astype(jnp.int32)
    result = result + jnp.sum((positions[None, :, None] >= early_cuts[:, None, :]).astype(jnp.int32), axis=-1)
    result = result + jnp.sum((positions[None, :, None] >= late_cuts[:, None, :]).astype(jnp.int32), axis=-1)
    return result.astype(jnp.int32)


def with_spikes(values, key, source, target, parts, factor):
    owner, partner = [(jnp.arange(values.shape[dim]) // (values.shape[dim] // parts)).reshape([-1 if axis == dim else 1 for axis in range(values.ndim)]) for dim in (source, target)]
    chosen = jax.random.permutation(key, parts)[partner]
    strong = (owner == chosen) | (owner == (partner + parts // 2) % parts)
    return jnp.where(strong, factor * values, values)


def block_levels(stream_key, dims, cuts, smallest, largest):
    level = 1.0
    for axis_at, blocks in cuts:
        draws = jax.random.uniform(jax.random.fold_in(jax.random.fold_in(stream_key, 6), axis_at), (blocks,), jnp.float32, smallest / len(cuts), largest / len(cuts))
        level = level * jnp.repeat(jnp.exp(draws), dims[axis_at] // blocks).reshape((-1,) + (1,) * (len(dims) - 1 - axis_at))
    return level


def gaussian(stream_key, shape, spread, bound, cuts=(), kind=jnp.bfloat16):
    loudness = block_levels(stream_key, shape, cuts, -0.22, 0.18) if cuts else 1.0
    array = jax.random.normal(stream_key, shape, jnp.float32) * spread * loudness
    return jnp.minimum(jnp.maximum(array, -bound), bound).astype(kind)


def bell_draw_with(own_key, dims, deviation, limit, cuts, heavy, kind=jnp.bfloat16):
    entries = deviation * jax.random.normal(own_key, dims, jnp.float32)
    if cuts:
        entries = entries * block_levels(own_key, dims, cuts, -0.22, 0.18)
    return jnp.clip(with_spikes(entries, jax.random.fold_in(own_key, 3), *heavy), -limit, limit).astype(kind)


def setup_inputs(seed: int = 0) -> dict:
    streams_of = jax.random.split(jax.random.key(seed), 24)
    tokens = gaussian(streams_of[0], (SEQS, LEN, D), 1.0, 6.0, ((0, 4), (1, 8)))
    per_layer = gaussian(streams_of[1], (SEQS, LEN, PL), 1.0, 6.0, ((0, 4), (1, 8)))
    out_grad = bell_draw_with(streams_of[2], (SEQS, LEN, D), 1.0, 6.0, ((0, 4), (1, 8)), (1, 2, 8, 2.0))
    segment_ids = draw_segment_ids(jax.random.fold_in(streams_of[23], 71), 0)
    query_weight = gaussian(streams_of[4], (D, HEADS * HD), D ** -0.5, 0.125, ((0, 4),))
    key_weight = gaussian(streams_of[5], (D, KV_HEADS * HD), D ** -0.5, 0.125, ((0, 4),))
    value_weight = gaussian(streams_of[6], (D, KV_HEADS * HD), D ** -0.5, 0.125, ((0, 4),))
    out_weight = gaussian(streams_of[7], (HEADS * HD, D), (HEADS * HD) ** -0.5, 0.125, ((0, 4),))
    left_weight = gaussian(streams_of[8], (D, RANK), D ** -0.5, 0.125, ((0, 4),))
    right_weight = gaussian(streams_of[9], (RANK, D), RANK ** -0.5, 0.75, ((1, 4),))
    gate_weight = gaussian(streams_of[10], (D, FF), D ** -0.5, 0.125, ((1, 4),))
    up_weight = gaussian(streams_of[11], (D, FF), D ** -0.5, 0.125, ((1, 4),))
    down_weight = gaussian(streams_of[12], (FF, D), FF ** -0.5, 0.0625, ((0, 4),))
    side_gate = gaussian(streams_of[13], (D, PL), D ** -0.5, 0.125, ((0, 4),))
    side_out = gaussian(streams_of[14], (PL, D), PL ** -0.5, 0.375, ((0, 4),))
    input_gain = jnp.clip(1.0 + 0.15 * jax.random.normal(streams_of[15], (D,), jnp.float32), 0.25, 1.75)
    laurel_gain = jnp.clip(1.0 + 0.15 * jax.random.normal(streams_of[16], (D,), jnp.float32), 0.25, 1.75)
    attn_gain = jnp.clip(1.0 + 0.15 * jax.random.normal(streams_of[17], (D,), jnp.float32), 0.25, 1.75)
    pre_gain = jnp.clip(1.0 + 0.15 * jax.random.normal(streams_of[18], (D,), jnp.float32), 0.25, 1.75)
    post_gain = jnp.clip(1.0 + 0.15 * jax.random.normal(streams_of[19], (D,), jnp.float32), 0.25, 1.75)
    side_gain = jnp.clip(1.0 + 0.15 * jax.random.normal(streams_of[20], (D,), jnp.float32), 0.25, 1.75)
    query_gain = jnp.clip(jnp.exp(jax.random.uniform(streams_of[21], (HD,), jnp.float32, math.log(0.25), math.log(0.5))), 0.25, 0.5)
    key_gain = jnp.clip(jnp.exp(jax.random.uniform(streams_of[22], (HD,), jnp.float32, math.log(0.25), math.log(0.5))), 0.25, 0.5)
    return {"tokens": tokens, "per_layer": per_layer, "out_grad": out_grad, "segment_ids": segment_ids, "query_weight": query_weight, "key_weight": key_weight, "value_weight": value_weight, "out_weight": out_weight, "left_weight": left_weight, "right_weight": right_weight, "gate_weight": gate_weight, "up_weight": up_weight, "down_weight": down_weight, "side_gate": side_gate, "side_out": side_out, "input_gain": input_gain, "laurel_gain": laurel_gain, "attn_gain": attn_gain, "pre_gain": pre_gain, "post_gain": post_gain, "side_gain": side_gain, "query_gain": query_gain, "key_gain": key_gain}


epsilon = 1e-06
rope_theta = 1000000.0
masked_score = -1e+30
inverse_root = 1.0 / math.sqrt(2.0)
highest = lax.Precision.HIGHEST

@jax.custom_vjp
def low(v):
    return lax.optimization_barrier(v.astype(jnp.bfloat16)).astype(jnp.float32)

@jax.custom_vjp
def low_back(v):
    return v

def low_keep(v):
    return (low(v), None)

def low_pass(kept, grad):
    return (grad,)

def back_keep(v):
    return (v, None)

def back_low(kept, grad):
    return (low(grad),)
low.defvjp(low_keep, low_pass)
low_back.defvjp(back_keep, back_low)

def product(a, b):
    return jnp.dot(a, b, precision=highest, preferred_element_type=jnp.float32)

def rms_norm(v, factor):
    return v * lax.rsqrt(lax.optimization_barrier(jnp.mean(v * v, axis=-1, keepdims=True)) + epsilon) * factor

def rotate(v, positions):
    halfway = v.shape[-1] // 2
    frequency = jnp.exp(jnp.arange(halfway).astype(jnp.float32) * (-2.0 * math.log(rope_theta) / v.shape[-1]))
    angles = positions.astype(jnp.float32)[:, None] * frequency[None, :]
    cosine = jnp.cos(angles)[:, None, :]
    sine_part = jnp.sin(angles)[:, None, :]
    leading = v[..., :halfway]
    trailing = v[..., halfway:]
    return jnp.concatenate([leading * cosine - trailing * sine_part, trailing * cosine + leading * sine_part], axis=-1)

def attend(query_low, key_low, value_low, segments):
    groups = HEADS // KV_HEADS
    blocks = LEN // TOK_DEV
    positions = jnp.arange(LEN).astype(jnp.int32)
    query_blocks = query_low.reshape(KV_HEADS, groups, blocks, TOK_DEV, HD).transpose(2, 0, 1, 3, 4)
    starts = (jnp.arange(blocks) * TOK_DEV).astype(jnp.int32)

    def one_block(item):
        query_block, first_row = item
        scores = low_back(jnp.einsum('kgqd,kjd->kgqj', query_block, key_low, precision=highest))
        query_pos = first_row + jnp.arange(TOK_DEV).astype(jnp.int32)
        query_ids = lax.dynamic_slice_in_dim(segments, first_row, TOK_DEV)
        allowed = (query_ids[:, None] == segments[None, :]) & (positions[None, :] <= query_pos[:, None])
        scores = jnp.where(allowed, scores, masked_score)
        row_max = lax.optimization_barrier(jnp.max(scores, axis=-1, keepdims=True))
        log_total = jnp.log(lax.optimization_barrier(jnp.sum(jnp.exp(scores - row_max), axis=-1, keepdims=True))) + row_max
        weights = jnp.exp(scores - log_total)
        return jnp.einsum('kgqj,kjd->kgqd', low(weights), value_low, precision=highest)
    outputs = lax.map(jax.checkpoint(one_block), (query_blocks, starts))
    return outputs.transpose(1, 2, 0, 3, 4).reshape(KV_HEADS, groups, LEN, HD)

def layer(params, x, per_layer, segments):
    query_weight, key_weight, value_weight, out_weight, left_weight, right_weight, gate_weight, up_weight, down_weight, side_gate, side_out, input_gain, laurel_gain, attn_gain, pre_gain, post_gain, side_gain, query_gain, key_gain = params
    length = x.shape[0]
    groups = HEADS // KV_HEADS
    positions = jnp.arange(length).astype(jnp.int32)
    normed = rms_norm(x, input_gain)
    normed_low = low(normed)
    query_raw = low_back(product(normed_low, query_weight))
    key_raw = low_back(product(normed_low, key_weight))
    value_raw = low_back(product(normed_low, value_weight))
    left_low = low(low_back(product(normed_low, left_weight)))
    right_out = low_back(product(left_low, right_weight))
    query_heads = rotate(rms_norm(query_raw.reshape(length, HEADS, HD), query_gain), positions)
    key_heads = rotate(rms_norm(key_raw.reshape(length, KV_HEADS, HD), key_gain), positions)
    value_heads = rms_norm(value_raw.reshape(length, KV_HEADS, HD), 1.0)
    query_low = low(query_heads).reshape(length, KV_HEADS, groups, HD).transpose(1, 2, 0, 3)
    key_low = low(key_heads).transpose(1, 0, 2)
    value_low = low(value_heads).transpose(1, 0, 2)
    attended = attend(query_low, key_low, value_low, segments)
    attended = attended.transpose(2, 0, 1, 3).reshape(length, HEADS * HD)
    attended_low = low(low_back(attended))
    attn_raw = low_back(product(attended_low, out_weight))
    mixed = (x + rms_norm(attn_raw, attn_gain) + normed + rms_norm(right_out, laurel_gain)) * inverse_root
    ffn_low = low(rms_norm(mixed, pre_gain))
    gate_raw = low_back(product(ffn_low, gate_weight))
    up_raw = low_back(product(ffn_low, up_weight))
    hidden_low = low(jax.nn.gelu(gate_raw, approximate=True) * up_raw)
    ffn_out = low_back(product(hidden_low, down_weight))
    middle = mixed + rms_norm(ffn_out, post_gain)
    middle_low = low(middle)
    layer_gate = low_back(product(middle_low, side_gate))
    layer_low = low(jax.nn.gelu(layer_gate, approximate=True) * per_layer)
    layer_out = low_back(product(layer_low, side_out))
    return middle + rms_norm(layer_out, side_gain)

def reference(tokens, per_layer, out_grad, segment_ids, query_weight, key_weight, value_weight, out_weight, left_weight, right_weight, gate_weight, up_weight, down_weight, side_gate, side_out, input_gain, laurel_gain, attn_gain, pre_gain, post_gain, side_gain, query_gain, key_gain):
    params = (query_weight.astype(jnp.float32), key_weight.astype(jnp.float32), value_weight.astype(jnp.float32), out_weight.astype(jnp.float32), left_weight.astype(jnp.float32), right_weight.astype(jnp.float32), gate_weight.astype(jnp.float32), up_weight.astype(jnp.float32), down_weight.astype(jnp.float32), side_gate.astype(jnp.float32), side_out.astype(jnp.float32), input_gain.astype(jnp.float32), laurel_gain.astype(jnp.float32), attn_gain.astype(jnp.float32), pre_gain.astype(jnp.float32), post_gain.astype(jnp.float32), side_gain.astype(jnp.float32), query_gain.astype(jnp.float32), key_gain.astype(jnp.float32))
    zeros = jax.tree.map(jnp.zeros_like, params)

    def one_sequence(carry, item):
        x, extra, segments, cotangent = item

        def forward(p, a, b):
            return layer(p, a, b, segments)
        result, pullback = jax.vjp(forward, params, x, extra)
        grads, x_grad, extra_grad = pullback(cotangent)
        carry = jax.tree.map(jnp.add, carry, grads)
        return (carry, (result.astype(jnp.bfloat16), x_grad.astype(jnp.bfloat16), extra_grad.astype(jnp.bfloat16)))
    totals, (block_out, tokens_grad, per_layer_grad) = lax.scan(one_sequence, zeros, (tokens.astype(jnp.float32), per_layer.astype(jnp.float32), segment_ids, out_grad.astype(jnp.float32)))
    return (block_out, tokens_grad, per_layer_grad, totals[0], totals[1], totals[2], totals[3], totals[4], totals[5], totals[6], totals[7], totals[8], totals[9], totals[10], totals[11], totals[12], totals[13], totals[14], totals[15], totals[16], totals[17], totals[18])
```

```python
import math

import jax
import jax.numpy as jnp
from jax import lax
from jax.sharding import PartitionSpec as P

HEADS = 8
KV_HEADS = 2
HD = 256


epsilon = 1e-06
rope_theta = 1000000.0
masked_score = -1e30
inverse_root = 1.0 / math.sqrt(2.0)


def rms_norm(v, factor):
    return v * lax.rsqrt(jnp.mean(v * v, axis=-1, keepdims=True) + epsilon) * factor


def rotate(v, positions):
    halfway = v.shape[-1] // 2
    frequency = jnp.exp(
        jnp.arange(halfway).astype(jnp.float32) * (-2.0 * math.log(rope_theta) / v.shape[-1])
    )
    angles = positions.astype(jnp.float32)[:, None] * frequency[None, :]
    cosine = jnp.cos(angles)[:, None, :]
    sine_part = jnp.sin(angles)[:, None, :]
    leading = v[..., :halfway]
    trailing = v[..., halfway:]
    return jnp.concatenate(
        [leading * cosine - trailing * sine_part, trailing * cosine + leading * sine_part], axis=-1
    )


def forward_product(a, b):
    return jnp.dot(a, b, preferred_element_type=jnp.float32)


def across(a, b):
    return lax.dot_general(a, b, (((1,), (1,)), ((), ())), preferred_element_type=jnp.float32)


def over_rows(a, b):
    return lax.dot_general(a, b, (((0,), (0,)), ((), ())), preferred_element_type=jnp.float32)


def hidden_piece(gate_in, up_in):
    return jax.nn.gelu(gate_in, approximate=True) * up_in


def middle_piece(mixed_in, ffn_in_rows, factor):
    return mixed_in + rms_norm(ffn_in_rows, factor)


def gather(x, axis):
    return lax.all_gather(x, axis, axis=0, tiled=True)


def scatter_sum(x, axis):
    return lax.psum_scatter(x, axis, scatter_dimension=0, tiled=True)


def blocks_of(grad, rows, columns):
    tall = grad.reshape(rows, grad.shape[0] // rows, columns, grad.shape[1] // columns)
    return tall.transpose(0, 2, 1, 3).reshape(rows * columns, -1)


def body(
    tokens,
    per_layer,
    out_grad,
    segment_ids,
    query_weight,
    key_weight,
    value_weight,
    out_weight,
    left_weight,
    right_weight,
    gate_weight,
    up_weight,
    down_weight,
    side_gate,
    side_out,
    input_gain,
    laurel_gain,
    attn_gain,
    pre_gain,
    post_gain,
    side_gain,
    query_gain,
    key_gain,
):
    low = jnp.bfloat16
    inputs = tokens[0].astype(jnp.float32)
    extra_rows = per_layer[0].astype(jnp.float32)
    cotangent = out_grad[0].astype(jnp.float32)
    sequence_ids = segment_ids[0]
    rows_here, width = inputs.shape
    ctx_count = lax.axis_size("ctx")
    fsdp_count = lax.axis_size("fsdp")
    count = ctx_count * fsdp_count
    ctx_place = lax.axis_index("ctx")
    groups = HEADS // KV_HEADS
    rank = left_weight.shape[1]
    side = side_gate.shape[1]
    length = sequence_ids.shape[0]
    query_width = HEADS * HD
    kv_width = KV_HEADS * HD
    query_pos = ctx_place * rows_here + jnp.arange(rows_here, dtype=jnp.int32)

    piece = width // count

    def own_rows(weight):
        step = weight.shape[0] // ctx_count
        return lax.dynamic_slice_in_dim(weight, ctx_place * step, step)

    first_set = jnp.concatenate(
        [own_rows(w) for w in (query_weight, key_weight, value_weight, left_weight)], axis=1
    )
    second_set = jnp.concatenate(
        [
            own_rows(out_weight),
            own_rows(side_gate),
            own_rows(side_out).reshape(piece, -1),
            own_rows(right_weight).reshape(piece, -1),
        ],
        axis=1,
    )
    full_first = gather(first_set, ("fsdp", "ctx"))
    full_second = gather(second_set, ("fsdp", "ctx"))
    qkv_width = query_width + 2 * kv_width
    full_qkv = full_first[:, :qkv_width]
    full_left = full_first[:, qkv_width:]
    full_out = full_second[:, :width]
    full_side_gate = full_second[:, width : width + side]
    full_side_out = full_second[:, width + side : width + 2 * side].reshape(side, width)
    full_right = full_second[:, width + 2 * side :]
    full_right = full_right.reshape(fsdp_count, rank, width // fsdp_count)
    full_right = full_right.transpose(1, 0, 2).reshape(rank, width)

    normed, input_pull = jax.vjp(rms_norm, inputs, input_gain)
    normed_low = normed.astype(low)
    normed_all = gather(normed_low, "fsdp")
    qkv_raw = forward_product(normed_low, full_qkv)
    left_low = forward_product(normed_low, full_left).astype(low)
    right_out = forward_product(left_low, full_right)

    def heads_piece(qkv_in, gain_one, gain_two):
        query_in = qkv_in[:, :query_width].reshape(rows_here, HEADS, HD)
        key_in = qkv_in[:, query_width : query_width + kv_width].reshape(rows_here, KV_HEADS, HD)
        value_in = qkv_in[:, query_width + kv_width :].reshape(rows_here, KV_HEADS, HD)
        query_heads = rotate(rms_norm(query_in, gain_one), query_pos)
        key_heads = rotate(rms_norm(key_in, gain_two), query_pos)
        value_heads = rms_norm(value_in, 1.0)
        return (query_heads, key_heads, value_heads)

    (query_heads, key_heads, value_heads), heads_pull = jax.vjp(
        heads_piece, qkv_raw, query_gain, key_gain
    )
    query_low = query_heads.astype(low).reshape(rows_here, KV_HEADS, groups, HD)
    query_low = query_low.transpose(1, 2, 0, 3).reshape(KV_HEADS, groups * rows_here, HD)
    kv_low = jnp.concatenate(
        [key_heads.astype(low).reshape(rows_here, -1), value_heads.astype(low).reshape(rows_here, -1)],
        axis=1,
    )
    kv_all = gather(kv_low, "ctx")
    key_all = kv_all[:, :kv_width].reshape(length, KV_HEADS, HD).transpose(1, 0, 2)
    value_all = kv_all[:, kv_width:].reshape(length, KV_HEADS, HD).transpose(1, 0, 2)

    query_ids = lax.dynamic_slice_in_dim(sequence_ids, ctx_place * rows_here, rows_here)
    key_pos = jnp.arange(length, dtype=jnp.int32)
    allowed = (query_ids[:, None] == sequence_ids[None, :]) & (
        key_pos[None, :] <= query_pos[:, None]
    )
    allowed = jnp.tile(allowed, (groups, 1))[None]
    scores = jnp.einsum("kqd,kjd->kqj", query_low, key_all, preferred_element_type=jnp.float32)
    scores = jnp.where(allowed, scores, masked_score)
    row_max = jnp.max(scores, axis=-1, keepdims=True)
    weights = jnp.where(allowed, jnp.exp(scores - row_max), 0.0)
    weights = weights / jnp.sum(weights, axis=-1, keepdims=True)
    weights_low = weights.astype(low)
    attended_rows = jnp.einsum(
        "kqj,kjd->kqd", weights_low, value_all, preferred_element_type=jnp.float32
    )
    attended = attended_rows.reshape(KV_HEADS, groups, rows_here, HD).transpose(2, 0, 1, 3)
    attended_low = attended.reshape(rows_here, query_width).astype(low)
    attended_all = gather(attended_low, "fsdp")
    attn_raw = forward_product(attended_low, full_out)

    def mix_piece(x, normed_in, attn_in, right_in, gain_one, gain_two, gain_three):
        mixed = (
            x + rms_norm(attn_in, gain_one) + normed_in + rms_norm(right_in, gain_two)
        ) * inverse_root
        return (mixed, rms_norm(mixed, gain_three))

    (mixed, ffn_in), mix_pull = jax.vjp(
        mix_piece, inputs, normed, attn_raw, right_out, attn_gain, laurel_gain, pre_gain
    )

    ffn_all = gather(ffn_in.astype(low), "fsdp")
    gate_raw = forward_product(ffn_all, gate_weight)
    up_raw = forward_product(ffn_all, up_weight)
    hidden, hidden_pull = jax.vjp(hidden_piece, gate_raw, up_raw)
    hidden_low = hidden.astype(low)
    ffn_out = scatter_sum(forward_product(hidden_low, down_weight).astype(low), "fsdp")
    ffn_out = ffn_out.astype(jnp.float32)
    middle, middle_pull = jax.vjp(middle_piece, mixed, ffn_out, post_gain)
    middle_low = middle.astype(low)
    layer_gate = forward_product(middle_low, full_side_gate)
    layer_act, extra_pull = jax.vjp(hidden_piece, layer_gate, extra_rows)
    layer_low = layer_act.astype(low)
    layer_out = forward_product(layer_low, full_side_out)
    result, out_pull = jax.vjp(middle_piece, middle, layer_out, side_gain)

    middle_grad_one, layer_out_grad, side_gain_grad = out_pull(cotangent)
    layer_grad_low = layer_out_grad.astype(low)
    side_out_grad = over_rows(layer_low, layer_grad_low)
    layer_gate_grad, extra_grad = extra_pull(across(layer_grad_low, full_side_out))
    gate_grad_low = layer_gate_grad.astype(low)
    side_gate_grad = over_rows(middle_low, gate_grad_low)
    mixed_grad_one, ffn_out_grad, post_gain_grad = middle_pull(
        middle_grad_one + across(gate_grad_low, full_side_gate)
    )
    ffn_grad_all = gather(ffn_out_grad.astype(low), "fsdp")
    down_weight_grad = over_rows(ffn_grad_all, hidden_low)
    gate_raw_grad, up_raw_grad = hidden_pull(across(ffn_grad_all, down_weight))
    gate_back_low = gate_raw_grad.astype(low)
    up_back_low = up_raw_grad.astype(low)
    ffn_in_grad = scatter_sum(
        (across(gate_back_low, gate_weight) + across(up_back_low, up_weight)).astype(low), "fsdp"
    )
    gate_weight_grad = over_rows(ffn_all, gate_back_low)
    up_weight_grad = over_rows(ffn_all, up_back_low)
    (
        inputs_grad_one,
        normed_grad_one,
        attn_raw_grad,
        right_out_grad,
        attn_gain_grad,
        laurel_gain_grad,
        pre_gain_grad,
    ) = mix_pull((mixed_grad_one, ffn_in_grad.astype(jnp.float32)))
    attn_grad_low = attn_raw_grad.astype(low)
    attended_grad_low = across(attn_grad_low, full_out).astype(low)
    right_grad_low = right_out_grad.astype(low)
    right_weight_grad = over_rows(right_grad_low, left_low)
    left_grad_low = across(right_grad_low, full_right).astype(low)
    left_weight_grad = over_rows(normed_low, left_grad_low)
    grad_rows = attended_grad_low.reshape(rows_here, KV_HEADS, groups, HD).transpose(1, 2, 0, 3)
    grad_rows = grad_rows.reshape(KV_HEADS, groups * rows_here, HD)
    correction = jnp.sum(
        grad_rows.astype(jnp.float32) * attended_rows, axis=-1, keepdims=True
    )
    weight_grad = jnp.einsum(
        "kqd,kjd->kqj", grad_rows, value_all, preferred_element_type=jnp.float32
    )
    score_grad = (weights * (weight_grad - correction)).astype(low)
    query_grad = jnp.einsum(
        "kqj,kjd->kqd", score_grad, key_all, preferred_element_type=jnp.float32
    )
    key_grad = jnp.einsum(
        "kqj,kqd->kjd", score_grad, query_low, preferred_element_type=jnp.float32
    )
    value_grad = jnp.einsum(
        "kqj,kqd->kjd", weights_low, grad_rows, preferred_element_type=jnp.float32
    )
    kv_grad = jnp.concatenate([key_grad.astype(low), value_grad.astype(low)], axis=0)
    kv_grad = kv_grad.transpose(1, 0, 2).reshape(length, 2 * kv_width)
    kv_grad = scatter_sum(kv_grad, "ctx").astype(jnp.float32)
    kv_grad = kv_grad.reshape(rows_here, 2, KV_HEADS, HD)
    query_heads_grad = query_grad.reshape(KV_HEADS, groups, rows_here, HD).transpose(2, 0, 1, 3)
    query_heads_grad = query_heads_grad.reshape(rows_here, HEADS, HD)
    qkv_grad, query_gain_grad, key_gain_grad = heads_pull(
        (query_heads_grad, kv_grad[:, 0], kv_grad[:, 1])
    )
    qkv_back_low = qkv_grad.astype(low)
    normed_grad_two = across(qkv_back_low, full_qkv) + across(left_grad_low, full_left)
    inputs_grad_two, input_gain_grad = input_pull(normed_grad_one + normed_grad_two)
    block_out = result.astype(low)[None]
    tokens_grad = (inputs_grad_one + inputs_grad_two).astype(low)[None]
    per_layer_grad = extra_grad.astype(low)[None]

    def columns_to_owner(x):
        parts = x.reshape(rows_here, fsdp_count, -1).transpose(1, 0, 2)
        return lax.all_to_all(parts, "fsdp", 0, 0, tiled=True).reshape(fsdp_count * rows_here, -1)

    out_columns = columns_to_owner(attn_grad_low)
    out_weight_grad = scatter_sum(over_rows(attended_all, out_columns).astype(low), "ctx")
    qkv_parts = jnp.concatenate(
        [
            part.reshape(rows_here, fsdp_count, -1)
            for part in (
                qkv_back_low[:, :query_width],
                qkv_back_low[:, query_width : query_width + kv_width],
                qkv_back_low[:, query_width + kv_width :],
            )
        ],
        axis=2,
    )
    qkv_columns = columns_to_owner(qkv_parts.reshape(rows_here, -1))
    qkv_weight_grad = scatter_sum(over_rows(normed_all, qkv_columns).astype(low), "ctx")
    query_part = query_width // fsdp_count
    kv_part = kv_width // fsdp_count
    query_weight_grad = qkv_weight_grad[:, :query_part]
    key_weight_grad = qkv_weight_grad[:, query_part : query_part + kv_part]
    value_weight_grad = qkv_weight_grad[:, query_part + kv_part :]
    down_weight_grad = scatter_sum(down_weight_grad.astype(low), "ctx").T
    gate_weight_grad = scatter_sum(gate_weight_grad.astype(low), "ctx")
    up_weight_grad = scatter_sum(up_weight_grad.astype(low), "ctx")

    small = [
        left_weight_grad.reshape(count, -1),
        right_weight_grad.reshape(count, -1),
        blocks_of(side_gate_grad, ctx_count, fsdp_count),
        blocks_of(side_out_grad, ctx_count, fsdp_count),
        input_gain_grad.reshape(count, -1),
        laurel_gain_grad.reshape(count, -1),
        attn_gain_grad.reshape(count, -1),
        pre_gain_grad.reshape(count, -1),
        post_gain_grad.reshape(count, -1),
        side_gain_grad.reshape(count, -1),
        query_gain_grad.reshape(count, -1),
        key_gain_grad.reshape(count, -1),
    ]
    sizes = [part.shape[1] for part in small]
    packed = jnp.concatenate([part.astype(low) for part in small], axis=1)
    packed = jnp.pad(packed, ((0, 0), (0, -packed.shape[1] % 128)))
    packed = scatter_sum(packed.reshape(-1, 128), ("ctx", "fsdp")).reshape(-1)
    shares = []
    start = 0
    for size in sizes:
        shares.append(packed[start : start + size].astype(jnp.float32))
        start += size
    left_weight_grad = shares[0].reshape(-1, rank)
    right_weight_grad = shares[1].reshape(-1, rank).T
    side_gate_grad = shares[2].reshape(width // ctx_count, -1)
    side_out_grad = shares[3].reshape(side // ctx_count, -1)
    wide = jnp.float32
    return (
        block_out,
        tokens_grad,
        per_layer_grad,
        query_weight_grad.astype(wide),
        key_weight_grad.astype(wide),
        value_weight_grad.astype(wide),
        out_weight_grad.astype(wide),
        left_weight_grad,
        right_weight_grad,
        gate_weight_grad.astype(wide),
        up_weight_grad.astype(wide),
        down_weight_grad.astype(wide),
        side_gate_grad,
        side_out_grad,
        *shares[4:],
    )


def solution(mesh):
    placed = (
        P("fsdp", "ctx", None),
        P("fsdp", "ctx", None),
        P("fsdp", "ctx", None),
        P("fsdp", None),
        P("fsdp", None),
        P("fsdp", None),
        P("fsdp", None),
        P("fsdp", None),
        P("fsdp", None),
        P(None, "fsdp"),
        P(None, "fsdp"),
        P(None, "fsdp"),
        P("fsdp", None),
        P("fsdp", None),
        P("fsdp", None),
        P(),
        P(),
        P(),
        P(),
        P(),
        P(),
        P(),
        P(),
    )
    return jax.shard_map(
        body,
        mesh=mesh,
        in_specs=placed,
        out_specs=(
            P("fsdp", "ctx", None),
            P("fsdp", "ctx", None),
            P("fsdp", "ctx", None),
            P("ctx", "fsdp"),
            P("ctx", "fsdp"),
            P("ctx", "fsdp"),
            P("ctx", "fsdp"),
            P(("ctx", "fsdp"), None),
            P(None, ("ctx", "fsdp")),
            P("ctx", "fsdp"),
            P("ctx", "fsdp"),
            P("fsdp", "ctx"),
            P("ctx", "fsdp"),
            P("ctx", "fsdp"),
            P(("ctx", "fsdp")),
            P(("ctx", "fsdp")),
            P(("ctx", "fsdp")),
            P(("ctx", "fsdp")),
            P(("ctx", "fsdp")),
            P(("ctx", "fsdp")),
            P(("ctx", "fsdp")),
            P(("ctx", "fsdp")),
        ),
        check_vma=False,
    )
```

```python
import functools
import math

import jax
import jax.numpy as jnp
from jax import lax
from jax.experimental import pallas as pl
from jax.experimental.pallas import tpu as pltpu
from jax.sharding import PartitionSpec as P

HEADS = 8
KV_HEADS = 2
HD = 256
MESH = pl.DeviceIdType.MESH


epsilon = 1e-06
rope_theta = 1000000.0
masked_score = -1e30
inverse_root = 1.0 / math.sqrt(2.0)


def rms_norm(v, factor):
    return v * lax.rsqrt(jnp.mean(v * v, axis=-1, keepdims=True) + epsilon) * factor


def rotate(v, positions):
    halfway = v.shape[-1] // 2
    frequency = jnp.exp(
        jnp.arange(halfway).astype(jnp.float32) * (-2.0 * math.log(rope_theta) / v.shape[-1])
    )
    angles = positions.astype(jnp.float32)[:, None] * frequency[None, :]
    cosine = jnp.cos(angles)[:, None, :]
    sine_part = jnp.sin(angles)[:, None, :]
    leading = v[..., :halfway]
    trailing = v[..., halfway:]
    return jnp.concatenate(
        [leading * cosine - trailing * sine_part, trailing * cosine + leading * sine_part], axis=-1
    )


def forward_product(a, b):
    return jnp.dot(a, b, preferred_element_type=jnp.float32)


def across(a, b):
    return lax.dot_general(a, b, (((1,), (1,)), ((), ())), preferred_element_type=jnp.float32)


def over_rows(a, b):
    return lax.dot_general(a, b, (((0,), (0,)), ((), ())), preferred_element_type=jnp.float32)


def hidden_piece(gate_in, up_in):
    return jax.nn.gelu(gate_in, approximate=True) * up_in


def middle_piece(mixed_in, ffn_in_rows, factor):
    return mixed_in + rms_norm(ffn_in_rows, factor)


def gather(x, axis):
    return lax.all_gather(x, axis, axis=0, tiled=True)


def scatter_sum(x, axis):
    return lax.psum_scatter(x, axis, scatter_dimension=0, tiled=True)


def partner_barrier(partners):
    barrier = pltpu.get_barrier_semaphore()
    for partner in partners:
        pl.semaphore_signal(barrier, inc=1, device_id=partner, device_id_type=MESH)
    pl.semaphore_wait(barrier, len(partners))


def add_rows(target, source, first, rows):
    tile = 16

    def one(step, carry):
        at = pl.ds(pl.multiple_of(first + step * tile, tile), tile)
        from_at = pl.ds(pl.multiple_of(step * tile, tile), tile)
        total = target[at].astype(jnp.float32) + source[from_at].astype(jnp.float32)
        target[at] = total.astype(target.dtype)
        return carry

    lax.fori_loop(0, rows // tile, one, 0)


def owner_sum_kernel(ctx_count, fsdp_count, shapes, *refs):
    many = len(shapes)
    ins, outs = refs[:many], refs[many : 2 * many]
    rest = refs[2 * many :]
    held, first_in = rest[:many], rest[many : 2 * many]
    later_in = rest[2 * many : 3 * many]
    across_in, own_sem, send_zero, recv_zero, send_sem, recv_sem, send_z, recv_z = rest[3 * many :]
    bits = ctx_count.bit_length() - 1
    pairs = ctx_count // 2
    place = lax.axis_index("ctx")
    along = lax.axis_index("fsdp")
    mine = [lax.rem(place // (1 << t), 2) for t in range(bits)]
    partners = [(place + (1 - 2 * mine[t]) * (1 << t), along) for t in range(bits)]
    across = [(place, lax.rem(along + d, fsdp_count)) for d in range(1, fsdp_count)]
    partner_barrier(partners + across)

    own_copies = []
    zero_copies = []
    for i, (rows, _) in enumerate(shapes):
        for b in range(pairs):
            keep = pl.ds(pl.multiple_of((2 * b + mine[0]) * rows, 16), rows)
            give = pl.ds(pl.multiple_of((2 * b + 1 - mine[0]) * rows, 16), rows)
            copy = pltpu.make_async_remote_copy(
                src_ref=ins[i].at[give],
                dst_ref=first_in[i].at[b],
                send_sem=send_zero.at[i, b],
                recv_sem=recv_zero.at[i, b],
                device_id=partners[0],
                device_id_type=MESH,
            )
            copy.start()
            zero_copies.append(copy)
            own = pltpu.make_async_copy(ins[i].at[keep], held[i].at[b], own_sem.at[i, b])
            own.start()
            own_copies.append(own)

    orders = [list(range(1, bits)), list(range(bits - 1, 0, -1))]

    def block_sets(half, stage):
        order = orders[half]
        bit = order[stage]
        free = order[stage + 1 :]
        fixed = sum(mine[t] * (1 << (t - 1)) for t in order[:stage])
        sent, kept = [], []
        for combo in range(1 << len(free)):
            value = sum(((combo >> n) & 1) << (t - 1) for n, t in enumerate(free))
            sent.append(fixed + (1 - mine[bit]) * (1 << (bit - 1)) + value)
            kept.append(fixed + mine[bit] * (1 << (bit - 1)) + value)
        return bit, sent, kept

    def start_stage(i, stage):
        rows = shapes[i][0] // 2
        copies = []
        for half in range(2):
            bit, sent, _ = block_sets(half, stage)
            for n, block in enumerate(sent):
                copy = pltpu.make_async_remote_copy(
                    src_ref=held[i].at[block, pl.ds(half * rows, rows)],
                    dst_ref=later_in[i].at[half, slot_of(stage) + n],
                    send_sem=send_sem.at[i, half, slot_of(stage) + n],
                    recv_sem=recv_sem.at[i, half, slot_of(stage) + n],
                    device_id=partners[bit],
                    device_id_type=MESH,
                )
                copy.start()
                copies.append(copy)
        return copies

    def slot_of(stage):
        return sum(1 << (bits - 2 - s) for s in range(stage))

    def add_stage(i, stage):
        rows = shapes[i][0] // 2
        for half in range(2):
            _, _, kept = block_sets(half, stage)
            for n, block in enumerate(kept):
                add_rows(held[i].at[block], later_in[i].at[half, slot_of(stage) + n], half * rows, rows)

    flying = {}
    for i in range(many):
        for b in range(pairs):
            zero_copies[i * pairs + b].wait()
            own_copies[i * pairs + b].wait()
            add_rows(held[i].at[b], first_in[i].at[b], 0, shapes[i][0])
        flying[i] = start_stage(i, 0)
    for stage in range(1, bits - 1):
        for i in range(many):
            for copy in flying[i]:
                copy.wait()
            add_stage(i, stage - 1)
            flying[i] = start_stage(i, stage)
    block = place // 2
    for i in range(many):
        for copy in flying[i]:
            copy.wait()
        add_stage(i, bits - 2)
        if i < many - 1:
            outs[i][...] = held[i][block]
    last = many - 1
    share = shapes[last][0] // fsdp_count
    copies = []
    for d, peer in enumerate(across):
        part = pl.ds(pl.multiple_of(peer[1] * share, 16), share)
        copy = pltpu.make_async_remote_copy(
            src_ref=held[last].at[block, part],
            dst_ref=across_in.at[d],
            send_sem=send_z.at[d],
            recv_sem=recv_z.at[d],
            device_id=peer,
            device_id_type=MESH,
        )
        copy.start()
        copies.append(copy)
    for copy in copies:
        copy.wait()
    part = pl.ds(pl.multiple_of(along * share, 16), share)
    total = held[last][block, part].astype(jnp.float32)
    for d in range(fsdp_count - 1):
        total = total + across_in[d].astype(jnp.float32)
    outs[last][...] = total.astype(outs[last].dtype)


def owner_sums(arrays):
    ctx_count = lax.axis_size("ctx")
    fsdp_count = lax.axis_size("fsdp")
    bits = ctx_count.bit_length() - 1
    pairs = ctx_count // 2
    many = len(arrays)
    shapes = [(a.shape[0] // ctx_count, a.shape[1]) for a in arrays]
    low = jnp.bfloat16
    slots = pairs - 1
    last_share = (shapes[-1][0] // fsdp_count, shapes[-1][1])
    out_shapes = shapes[:-1] + [last_share]
    scratch = [pltpu.VMEM((pairs,) + s, low) for s in shapes]
    scratch += [pltpu.VMEM((pairs,) + s, low) for s in shapes]
    scratch += [pltpu.VMEM((2, slots, s[0] // 2, s[1]), low) for s in shapes]
    scratch += [
        pltpu.VMEM((fsdp_count - 1,) + last_share, low),
        pltpu.SemaphoreType.DMA((many, pairs)),
        pltpu.SemaphoreType.DMA((many, pairs)),
        pltpu.SemaphoreType.DMA((many, pairs)),
        pltpu.SemaphoreType.DMA((many, 2, slots)),
        pltpu.SemaphoreType.DMA((many, 2, slots)),
        pltpu.SemaphoreType.DMA((fsdp_count - 1,)),
        pltpu.SemaphoreType.DMA((fsdp_count - 1,)),
    ]
    total = sum(a.size for a in arrays)
    return pl.pallas_call(
        functools.partial(owner_sum_kernel, ctx_count, fsdp_count, shapes),
        out_shape=[jax.ShapeDtypeStruct(s, low) for s in out_shapes],
        in_specs=[pl.BlockSpec(memory_space=pl.ANY)] * many,
        out_specs=[pl.BlockSpec(memory_space=pltpu.VMEM)] * many,
        scratch_shapes=scratch,
        compiler_params=pltpu.CompilerParams(
            collective_id=0, has_side_effects=True, vmem_limit_bytes=58 << 20
        ),
        cost_estimate=pl.CostEstimate(flops=total, bytes_accessed=4 * total, transcendentals=0),
        name="owner_sums",
    )(*arrays)


def blocks_of(grad, rows, columns):
    tall = grad.reshape(rows, grad.shape[0] // rows, columns, grad.shape[1] // columns)
    return tall.transpose(0, 2, 1, 3).reshape(rows * columns, -1)


def body(
    tokens,
    per_layer,
    out_grad,
    segment_ids,
    query_weight,
    key_weight,
    value_weight,
    out_weight,
    left_weight,
    right_weight,
    gate_weight,
    up_weight,
    down_weight,
    side_gate,
    side_out,
    input_gain,
    laurel_gain,
    attn_gain,
    pre_gain,
    post_gain,
    side_gain,
    query_gain,
    key_gain,
):
    low = jnp.bfloat16
    inputs = tokens[0].astype(jnp.float32)
    extra_rows = per_layer[0].astype(jnp.float32)
    cotangent = out_grad[0].astype(jnp.float32)
    sequence_ids = segment_ids[0]
    rows_here, width = inputs.shape
    ctx_count = lax.axis_size("ctx")
    fsdp_count = lax.axis_size("fsdp")
    count = ctx_count * fsdp_count
    ctx_place = lax.axis_index("ctx")
    groups = HEADS // KV_HEADS
    rank = left_weight.shape[1]
    side = side_gate.shape[1]
    length = sequence_ids.shape[0]
    query_width = HEADS * HD
    kv_width = KV_HEADS * HD
    query_pos = ctx_place * rows_here + jnp.arange(rows_here, dtype=jnp.int32)

    piece = width // count

    def own_rows(weight):
        step = weight.shape[0] // ctx_count
        return lax.dynamic_slice_in_dim(weight, ctx_place * step, step)

    first_set = jnp.concatenate(
        [own_rows(w) for w in (query_weight, key_weight, value_weight, left_weight)], axis=1
    )
    second_set = jnp.concatenate(
        [
            own_rows(out_weight),
            own_rows(side_gate),
            own_rows(side_out).reshape(piece, -1),
            own_rows(right_weight).reshape(piece, -1),
        ],
        axis=1,
    )
    full_first = gather(first_set, ("fsdp", "ctx"))
    full_second = gather(second_set, ("fsdp", "ctx"))
    qkv_width = query_width + 2 * kv_width
    full_qkv = full_first[:, :qkv_width]
    full_left = full_first[:, qkv_width:]
    full_out = full_second[:, :width]
    full_side_gate = full_second[:, width : width + side]
    full_side_out = full_second[:, width + side : width + 2 * side].reshape(side, width)
    full_right = full_second[:, width + 2 * side :]
    full_right = full_right.reshape(fsdp_count, rank, width // fsdp_count)
    full_right = full_right.transpose(1, 0, 2).reshape(rank, width)

    normed, input_pull = jax.vjp(rms_norm, inputs, input_gain)
    normed_low = normed.astype(low)
    normed_all = gather(normed_low, "fsdp")
    qkv_raw = forward_product(normed_low, full_qkv)
    left_low = forward_product(normed_low, full_left).astype(low)
    right_out = forward_product(left_low, full_right)

    def heads_piece(qkv_in, gain_one, gain_two):
        query_in = qkv_in[:, :query_width].reshape(rows_here, HEADS, HD)
        key_in = qkv_in[:, query_width : query_width + kv_width].reshape(rows_here, KV_HEADS, HD)
        value_in = qkv_in[:, query_width + kv_width :].reshape(rows_here, KV_HEADS, HD)
        query_heads = rotate(rms_norm(query_in, gain_one), query_pos)
        key_heads = rotate(rms_norm(key_in, gain_two), query_pos)
        value_heads = rms_norm(value_in, 1.0)
        return (query_heads, key_heads, value_heads)

    (query_heads, key_heads, value_heads), heads_pull = jax.vjp(
        heads_piece, qkv_raw, query_gain, key_gain
    )
    query_low = query_heads.astype(low).reshape(rows_here, KV_HEADS, groups, HD)
    query_low = query_low.transpose(1, 2, 0, 3).reshape(KV_HEADS, groups * rows_here, HD)
    kv_low = jnp.concatenate(
        [key_heads.astype(low).reshape(rows_here, -1), value_heads.astype(low).reshape(rows_here, -1)],
        axis=1,
    )
    kv_all = gather(kv_low, "ctx")
    key_all = kv_all[:, :kv_width].reshape(length, KV_HEADS, HD).transpose(1, 0, 2)
    value_all = kv_all[:, kv_width:].reshape(length, KV_HEADS, HD).transpose(1, 0, 2)

    query_ids = lax.dynamic_slice_in_dim(sequence_ids, ctx_place * rows_here, rows_here)
    key_pos = jnp.arange(length, dtype=jnp.int32)
    allowed = (query_ids[:, None] == sequence_ids[None, :]) & (
        key_pos[None, :] <= query_pos[:, None]
    )
    allowed = jnp.tile(allowed, (groups, 1))[None]
    scores = jnp.einsum("kqd,kjd->kqj", query_low, key_all, preferred_element_type=jnp.float32)
    scores = jnp.where(allowed, scores, masked_score)
    row_max = jnp.max(scores, axis=-1, keepdims=True)
    weights = jnp.where(allowed, jnp.exp(scores - row_max), 0.0)
    weights = weights / jnp.sum(weights, axis=-1, keepdims=True)
    weights_low = weights.astype(low)
    attended_rows = jnp.einsum(
        "kqj,kjd->kqd", weights_low, value_all, preferred_element_type=jnp.float32
    )
    attended = attended_rows.reshape(KV_HEADS, groups, rows_here, HD).transpose(2, 0, 1, 3)
    attended_low = attended.reshape(rows_here, query_width).astype(low)
    attended_all = gather(attended_low, "fsdp")
    attn_raw = forward_product(attended_low, full_out)

    def mix_piece(x, normed_in, attn_in, right_in, gain_one, gain_two, gain_three):
        mixed = (
            x + rms_norm(attn_in, gain_one) + normed_in + rms_norm(right_in, gain_two)
        ) * inverse_root
        return (mixed, rms_norm(mixed, gain_three))

    (mixed, ffn_in), mix_pull = jax.vjp(
        mix_piece, inputs, normed, attn_raw, right_out, attn_gain, laurel_gain, pre_gain
    )

    ffn_all = gather(ffn_in.astype(low), "fsdp")
    gate_raw = forward_product(ffn_all, gate_weight)
    up_raw = forward_product(ffn_all, up_weight)
    hidden, hidden_pull = jax.vjp(hidden_piece, gate_raw, up_raw)
    hidden_low = hidden.astype(low)
    ffn_out = scatter_sum(forward_product(hidden_low, down_weight).astype(low), "fsdp")
    ffn_out = ffn_out.astype(jnp.float32)
    middle, middle_pull = jax.vjp(middle_piece, mixed, ffn_out, post_gain)
    middle_low = middle.astype(low)
    layer_gate = forward_product(middle_low, full_side_gate)
    layer_act, extra_pull = jax.vjp(hidden_piece, layer_gate, extra_rows)
    layer_low = layer_act.astype(low)
    layer_out = forward_product(layer_low, full_side_out)
    result, out_pull = jax.vjp(middle_piece, middle, layer_out, side_gain)

    middle_grad_one, layer_out_grad, side_gain_grad = out_pull(cotangent)
    layer_grad_low = layer_out_grad.astype(low)
    side_out_grad = over_rows(layer_low, layer_grad_low)
    layer_gate_grad, extra_grad = extra_pull(across(layer_grad_low, full_side_out))
    gate_grad_low = layer_gate_grad.astype(low)
    side_gate_grad = over_rows(middle_low, gate_grad_low)
    mixed_grad_one, ffn_out_grad, post_gain_grad = middle_pull(
        middle_grad_one + across(gate_grad_low, full_side_gate)
    )
    ffn_grad_all = gather(ffn_out_grad.astype(low), "fsdp")
    down_weight_grad = over_rows(ffn_grad_all, hidden_low)
    gate_raw_grad, up_raw_grad = hidden_pull(across(ffn_grad_all, down_weight))
    gate_back_low = gate_raw_grad.astype(low)
    up_back_low = up_raw_grad.astype(low)
    ffn_in_grad = scatter_sum(
        (across(gate_back_low, gate_weight) + across(up_back_low, up_weight)).astype(low), "fsdp"
    )
    gate_weight_grad = over_rows(ffn_all, gate_back_low)
    up_weight_grad = over_rows(ffn_all, up_back_low)
    (
        inputs_grad_one,
        normed_grad_one,
        attn_raw_grad,
        right_out_grad,
        attn_gain_grad,
        laurel_gain_grad,
        pre_gain_grad,
    ) = mix_pull((mixed_grad_one, ffn_in_grad.astype(jnp.float32)))
    attn_grad_low = attn_raw_grad.astype(low)
    attended_grad_low = across(attn_grad_low, full_out).astype(low)
    right_grad_low = right_out_grad.astype(low)
    right_weight_grad = over_rows(right_grad_low, left_low)
    left_grad_low = across(right_grad_low, full_right).astype(low)
    left_weight_grad = over_rows(normed_low, left_grad_low)
    grad_rows = attended_grad_low.reshape(rows_here, KV_HEADS, groups, HD).transpose(1, 2, 0, 3)
    grad_rows = grad_rows.reshape(KV_HEADS, groups * rows_here, HD)
    correction = jnp.sum(
        grad_rows.astype(jnp.float32) * attended_rows, axis=-1, keepdims=True
    )
    weight_grad = jnp.einsum(
        "kqd,kjd->kqj", grad_rows, value_all, preferred_element_type=jnp.float32
    )
    score_grad = (weights * (weight_grad - correction)).astype(low)
    query_grad = jnp.einsum(
        "kqj,kjd->kqd", score_grad, key_all, preferred_element_type=jnp.float32
    )
    key_grad = jnp.einsum(
        "kqj,kqd->kjd", score_grad, query_low, preferred_element_type=jnp.float32
    )
    value_grad = jnp.einsum(
        "kqj,kqd->kjd", weights_low, grad_rows, preferred_element_type=jnp.float32
    )
    kv_grad = jnp.concatenate([key_grad.astype(low), value_grad.astype(low)], axis=0)
    kv_grad = kv_grad.transpose(1, 0, 2).reshape(length, 2 * kv_width)
    kv_grad = scatter_sum(kv_grad, "ctx").astype(jnp.float32)
    kv_grad = kv_grad.reshape(rows_here, 2, KV_HEADS, HD)
    query_heads_grad = query_grad.reshape(KV_HEADS, groups, rows_here, HD).transpose(2, 0, 1, 3)
    query_heads_grad = query_heads_grad.reshape(rows_here, HEADS, HD)
    qkv_grad, query_gain_grad, key_gain_grad = heads_pull(
        (query_heads_grad, kv_grad[:, 0], kv_grad[:, 1])
    )
    qkv_back_low = qkv_grad.astype(low)
    normed_grad_two = across(qkv_back_low, full_qkv) + across(left_grad_low, full_left)
    inputs_grad_two, input_gain_grad = input_pull(normed_grad_one + normed_grad_two)
    block_out = result.astype(low)[None]
    tokens_grad = (inputs_grad_one + inputs_grad_two).astype(low)[None]
    per_layer_grad = extra_grad.astype(low)[None]

    def columns_to_owner(x):
        parts = x.reshape(rows_here, fsdp_count, -1).transpose(1, 0, 2)
        return lax.all_to_all(parts, "fsdp", 0, 0, tiled=True).reshape(fsdp_count * rows_here, -1)

    out_columns = columns_to_owner(attn_grad_low)
    out_weight_grad = over_rows(attended_all, out_columns)
    qkv_parts = jnp.concatenate(
        [
            part.reshape(rows_here, fsdp_count, -1)
            for part in (
                qkv_back_low[:, :query_width],
                qkv_back_low[:, query_width : query_width + kv_width],
                qkv_back_low[:, query_width + kv_width :],
            )
        ],
        axis=2,
    )
    qkv_columns = columns_to_owner(qkv_parts.reshape(rows_here, -1))
    qkv_weight_grad = over_rows(normed_all, qkv_columns)

    small = [
        left_weight_grad.reshape(count, -1),
        right_weight_grad.reshape(count, -1),
        blocks_of(side_gate_grad, ctx_count, fsdp_count),
        blocks_of(side_out_grad, ctx_count, fsdp_count),
        input_gain_grad.reshape(count, -1),
        laurel_gain_grad.reshape(count, -1),
        attn_gain_grad.reshape(count, -1),
        pre_gain_grad.reshape(count, -1),
        post_gain_grad.reshape(count, -1),
        side_gain_grad.reshape(count, -1),
        query_gain_grad.reshape(count, -1),
        key_gain_grad.reshape(count, -1),
    ]
    sizes = [part.shape[1] for part in small]
    packed = jnp.concatenate([part.astype(low) for part in small], axis=1)
    packed = jnp.pad(packed, ((0, 0), (0, -packed.shape[1] % (16 * 128))))
    sums = owner_sums(
        [
            grad.astype(low)
            for grad in (
                down_weight_grad,
                gate_weight_grad,
                up_weight_grad,
                out_weight_grad,
                qkv_weight_grad,
                packed.reshape(count * 16, -1),
            )
        ]
    )
    down_weight_grad, gate_weight_grad, up_weight_grad, out_weight_grad, qkv_weight_grad = sums[:5]
    down_weight_grad = down_weight_grad.T
    packed = sums[5].reshape(-1)
    query_part = query_width // fsdp_count
    kv_part = kv_width // fsdp_count
    query_weight_grad = qkv_weight_grad[:, :query_part]
    key_weight_grad = qkv_weight_grad[:, query_part : query_part + kv_part]
    value_weight_grad = qkv_weight_grad[:, query_part + kv_part :]
    shares = []
    start = 0
    for size in sizes:
        shares.append(packed[start : start + size].astype(jnp.float32))
        start += size
    left_weight_grad = shares[0].reshape(-1, rank)
    right_weight_grad = shares[1].reshape(-1, rank).T
    side_gate_grad = shares[2].reshape(width // ctx_count, -1)
    side_out_grad = shares[3].reshape(side // ctx_count, -1)
    wide = jnp.float32
    return (
        block_out,
        tokens_grad,
        per_layer_grad,
        query_weight_grad.astype(wide),
        key_weight_grad.astype(wide),
        value_weight_grad.astype(wide),
        out_weight_grad.astype(wide),
        left_weight_grad,
        right_weight_grad,
        gate_weight_grad.astype(wide),
        up_weight_grad.astype(wide),
        down_weight_grad.astype(wide),
        side_gate_grad,
        side_out_grad,
        *shares[4:],
    )


def solution(mesh):
    placed = (
        P("fsdp", "ctx", None),
        P("fsdp", "ctx", None),
        P("fsdp", "ctx", None),
        P("fsdp", None),
        P("fsdp", None),
        P("fsdp", None),
        P("fsdp", None),
        P("fsdp", None),
        P("fsdp", None),
        P(None, "fsdp"),
        P(None, "fsdp"),
        P(None, "fsdp"),
        P("fsdp", None),
        P("fsdp", None),
        P("fsdp", None),
        P(),
        P(),
        P(),
        P(),
        P(),
        P(),
        P(),
        P(),
    )
    return jax.shard_map(
        body,
        mesh=mesh,
        in_specs=placed,
        out_specs=(
            P("fsdp", "ctx", None),
            P("fsdp", "ctx", None),
            P("fsdp", "ctx", None),
            P("ctx", "fsdp"),
            P("ctx", "fsdp"),
            P("ctx", "fsdp"),
            P("ctx", "fsdp"),
            P(("ctx", "fsdp"), None),
            P(None, ("ctx", "fsdp")),
            P("ctx", "fsdp"),
            P("ctx", "fsdp"),
            P("fsdp", "ctx"),
            P("ctx", "fsdp"),
            P("ctx", "fsdp"),
            P(("ctx", "fsdp")),
            P(("ctx", "fsdp")),
            P(("ctx", "fsdp")),
            P(("ctx", "fsdp")),
            P(("ctx", "fsdp")),
            P(("ctx", "fsdp")),
            P(("ctx", "fsdp")),
            P(("ctx", "fsdp")),
        ),
        check_vma=False,
    )
```

```python
import functools
import math

import jax
import jax.numpy as jnp
from jax import lax
from jax.experimental import pallas as pl
from jax.experimental.pallas import tpu as pltpu
from jax.sharding import PartitionSpec as P

HEADS = 8
KV_HEADS = 2
HD = 256
MESH = pl.DeviceIdType.MESH


epsilon = 1e-06
rope_theta = 1000000.0
masked_score = -1e30
inverse_root = 1.0 / math.sqrt(2.0)


def rms_norm(v, factor):
    return v * lax.rsqrt(jnp.mean(v * v, axis=-1, keepdims=True) + epsilon) * factor


def rotate(v, positions):
    halfway = v.shape[-1] // 2
    frequency = jnp.exp(
        jnp.arange(halfway).astype(jnp.float32) * (-2.0 * math.log(rope_theta) / v.shape[-1])
    )
    angles = positions.astype(jnp.float32)[:, None] * frequency[None, :]
    cosine = jnp.cos(angles)[:, None, :]
    sine_part = jnp.sin(angles)[:, None, :]
    leading = v[..., :halfway]
    trailing = v[..., halfway:]
    return jnp.concatenate(
        [leading * cosine - trailing * sine_part, trailing * cosine + leading * sine_part], axis=-1
    )


def forward_product(a, b):
    return jnp.dot(a, b, preferred_element_type=jnp.float32)


def across(a, b):
    return lax.dot_general(a, b, (((1,), (1,)), ((), ())), preferred_element_type=jnp.float32)


def over_rows(a, b):
    return lax.dot_general(a, b, (((0,), (0,)), ((), ())), preferred_element_type=jnp.float32)


def hidden_piece(gate_in, up_in):
    return jax.nn.gelu(gate_in, approximate=True) * up_in


def middle_piece(mixed_in, ffn_in_rows, factor):
    return mixed_in + rms_norm(ffn_in_rows, factor)


def gather(x, axis):
    return lax.all_gather(x, axis, axis=0, tiled=True)


def scatter_sum(x, axis):
    return lax.psum_scatter(x, axis, scatter_dimension=0, tiled=True)


def partner_barrier(partners):
    barrier = pltpu.get_barrier_semaphore()
    for partner in partners:
        pl.semaphore_signal(barrier, inc=1, device_id=partner, device_id_type=MESH)
    pl.semaphore_wait(barrier, len(partners))


def add_rows(target, source, first, rows):
    tile = 16

    def one(step, carry):
        at = pl.ds(pl.multiple_of(first + step * tile, tile), tile)
        from_at = pl.ds(pl.multiple_of(step * tile, tile), tile)
        total = target[at].astype(jnp.float32) + source[from_at].astype(jnp.float32)
        target[at] = total.astype(target.dtype)
        return carry

    lax.fori_loop(0, rows // tile, one, 0)


def owner_sum_kernel(ctx_count, fsdp_count, shapes, shared, *refs):
    many = len(shapes)
    ins, outs = refs[:many], refs[many : 2 * many]
    rest = refs[2 * many :]
    held, first_in = rest[:many], rest[many : 2 * many]
    later_in = rest[2 * many : 3 * many]
    across_in, own_sem, send_zero, recv_zero, send_sem, recv_sem, send_z, recv_z = rest[3 * many :]
    pairs = ctx_count // 2
    bits, place, along, mine, partners, orders = ctx_position(ctx_count)
    across = [(place, lax.rem(along + d, fsdp_count)) for d in range(1, fsdp_count) if shared]
    partner_barrier(partners + across)

    own_copies = []
    zero_copies = []
    for i, (rows, _) in enumerate(shapes):
        for b in range(pairs):
            keep = pl.ds(pl.multiple_of((2 * b + mine[0]) * rows, 16), rows)
            give = pl.ds(pl.multiple_of((2 * b + 1 - mine[0]) * rows, 16), rows)
            copy = pltpu.make_async_remote_copy(
                src_ref=ins[i].at[give],
                dst_ref=first_in[i].at[b],
                send_sem=send_zero.at[i, b],
                recv_sem=recv_zero.at[i, b],
                device_id=partners[0],
                device_id_type=MESH,
            )
            copy.start()
            zero_copies.append(copy)
            own = pltpu.make_async_copy(ins[i].at[keep], held[i].at[b], own_sem.at[i, b])
            own.start()
            own_copies.append(own)

    def block_sets(half, stage):
        order = orders[half]
        bit = order[stage]
        free = order[stage + 1 :]
        fixed = sum(mine[t] * (1 << (t - 1)) for t in order[:stage])
        sent, kept = [], []
        for combo in range(1 << len(free)):
            value = sum(((combo >> n) & 1) << (t - 1) for n, t in enumerate(free))
            sent.append(fixed + (1 - mine[bit]) * (1 << (bit - 1)) + value)
            kept.append(fixed + mine[bit] * (1 << (bit - 1)) + value)
        return bit, sent, kept

    def start_stage(i, stage):
        rows = shapes[i][0] // 2
        copies = []
        for half in range(2):
            bit, sent, _ = block_sets(half, stage)
            for n, block in enumerate(sent):
                copy = pltpu.make_async_remote_copy(
                    src_ref=held[i].at[block, pl.ds(half * rows, rows)],
                    dst_ref=later_in[i].at[half, slot_of(stage) + n],
                    send_sem=send_sem.at[i, half, slot_of(stage) + n],
                    recv_sem=recv_sem.at[i, half, slot_of(stage) + n],
                    device_id=partners[bit],
                    device_id_type=MESH,
                )
                copy.start()
                copies.append(copy)
        return copies

    def slot_of(stage):
        return sum(1 << (bits - 2 - s) for s in range(stage))

    def add_stage(i, stage):
        rows = shapes[i][0] // 2
        for half in range(2):
            _, _, kept = block_sets(half, stage)
            for n, block in enumerate(kept):
                add_rows(held[i].at[block], later_in[i].at[half, slot_of(stage) + n], half * rows, rows)

    flying = {}
    for i in range(many):
        for b in range(pairs):
            zero_copies[i * pairs + b].wait()
            own_copies[i * pairs + b].wait()
            add_rows(held[i].at[b], first_in[i].at[b], 0, shapes[i][0])
        flying[i] = start_stage(i, 0)
    for stage in range(1, bits - 1):
        for i in range(many):
            for copy in flying[i]:
                copy.wait()
            add_stage(i, stage - 1)
            flying[i] = start_stage(i, stage)
    block = place // 2
    for i in range(many):
        for copy in flying[i]:
            copy.wait()
        add_stage(i, bits - 2)
        if i < many - 1 or not shared:
            outs[i][...] = held[i][block]
    if not shared:
        return
    last = many - 1
    share = shapes[last][0] // fsdp_count
    copies = []
    for d, peer in enumerate(across):
        part = pl.ds(pl.multiple_of(peer[1] * share, 16), share)
        copy = pltpu.make_async_remote_copy(
            src_ref=held[last].at[block, part],
            dst_ref=across_in.at[d],
            send_sem=send_z.at[d],
            recv_sem=recv_z.at[d],
            device_id=peer,
            device_id_type=MESH,
        )
        copy.start()
        copies.append(copy)
    for copy in copies:
        copy.wait()
    part = pl.ds(pl.multiple_of(along * share, 16), share)
    total = held[last][block, part].astype(jnp.float32)
    for d in range(fsdp_count - 1):
        total = total + across_in[d].astype(jnp.float32)
    outs[last][...] = total.astype(outs[last].dtype)


def owner_sums(arrays, shared, collective_id):
    ctx_count = lax.axis_size("ctx")
    fsdp_count = lax.axis_size("fsdp")
    bits = ctx_count.bit_length() - 1
    pairs = ctx_count // 2
    many = len(arrays)
    shapes = [(a.shape[0] // ctx_count, a.shape[1]) for a in arrays]
    low = jnp.bfloat16
    slots = pairs - 1
    last_share = (shapes[-1][0] // (fsdp_count if shared else 1), shapes[-1][1])
    out_shapes = shapes[:-1] + [last_share]
    scratch = [pltpu.VMEM((pairs,) + s, low) for s in shapes]
    scratch += [pltpu.VMEM((pairs,) + s, low) for s in shapes]
    scratch += [pltpu.VMEM((2, slots, s[0] // 2, s[1]), low) for s in shapes]
    scratch += [
        pltpu.VMEM((fsdp_count - 1,) + last_share, low),
        pltpu.SemaphoreType.DMA((many, pairs)),
        pltpu.SemaphoreType.DMA((many, pairs)),
        pltpu.SemaphoreType.DMA((many, pairs)),
        pltpu.SemaphoreType.DMA((many, 2, slots)),
        pltpu.SemaphoreType.DMA((many, 2, slots)),
        pltpu.SemaphoreType.DMA((fsdp_count - 1,)),
        pltpu.SemaphoreType.DMA((fsdp_count - 1,)),
    ]
    total = sum(a.size for a in arrays)
    return pl.pallas_call(
        functools.partial(owner_sum_kernel, ctx_count, fsdp_count, shapes, shared),
        out_shape=[jax.ShapeDtypeStruct(s, low) for s in out_shapes],
        in_specs=[pl.BlockSpec(memory_space=pl.ANY)] * many,
        out_specs=[pl.BlockSpec(memory_space=pltpu.VMEM)] * many,
        scratch_shapes=scratch,
        compiler_params=pltpu.CompilerParams(
            collective_id=collective_id, has_side_effects=True, vmem_limit_bytes=58 << 20
        ),
        cost_estimate=pl.CostEstimate(flops=total, bytes_accessed=4 * total, transcendentals=0),
        name="owner_sums",
    )(*arrays)


def held_index(mine, done, bits):
    return tuple(slice(None) if t in done else mine[t] for t in reversed(range(bits)))


def ctx_position(ctx_count):
    bits = ctx_count.bit_length() - 1
    place = lax.axis_index("ctx")
    along = lax.axis_index("fsdp")
    mine = [lax.rem(place // (1 << t), 2) for t in range(bits)]
    partners = [(place + (1 - 2 * mine[t]) * (1 << t), along) for t in range(bits)]
    orders = [list(range(1, bits)), list(range(bits - 1, 0, -1))]
    return bits, place, along, mine, partners, orders


def spread_copy(out, lead, half, stage, position, send_sem, recv_sem):
    bits, _, _, mine, partners, orders = position
    order = orders[half]
    rows = out.shape[-2] // 2
    at = lead + held_index(mine, order[:stage], bits) + (pl.ds(half * rows, rows),)
    return pltpu.make_async_remote_copy(
        src_ref=out.at[at],
        dst_ref=out.at[at],
        send_sem=send_sem.at[half, stage],
        recv_sem=recv_sem.at[half, stage],
        device_id=partners[order[stage]],
        device_id_type=MESH,
    )


def sibling_copy(out, lead, position, send_sem, recv_sem):
    bits, _, _, mine, partners, orders = position
    at = lead + held_index(mine, orders[0], bits)
    return pltpu.make_async_remote_copy(
        src_ref=out.at[at],
        dst_ref=out.at[at],
        send_sem=send_sem,
        recv_sem=recv_sem,
        device_id=partners[0],
        device_id_type=MESH,
    )


def weight_gather_kernel(ctx_count, fsdp_count, members, *refs):
    sets = len(members)
    locals_count = sum(members)
    pieces, own = refs[:sets], refs[sets : sets + locals_count]
    outs = refs[sets + locals_count : 2 * sets + locals_count]
    rest = refs[2 * sets + locals_count :]
    passing = rest[:locals_count]
    own_sem, line_send, line_recv, send_sem, recv_sem, core_send, core_recv = rest[locals_count:]
    position = ctx_position(ctx_count)
    bits, place, along, mine, partners, _ = position
    steps = fsdp_count - 1
    here = held_index(mine, (), bits)
    loads = []
    for n in range(locals_count):
        loads.append(pltpu.make_async_copy(own[n], passing[n], own_sem.at[0, n]))
        loads[-1].start()
    partner_barrier(
        partners
        + [(place, lax.rem(along + 1, fsdp_count)), (place, lax.rem(along + steps, fsdp_count))]
    )

    def line_copy(i, way, step, origin):
        toward = along + 1 if way == 0 else along - 1
        return pltpu.make_async_remote_copy(
            src_ref=pieces[i] if step == 1 else outs[i].at[(origin,) + here],
            dst_ref=outs[i].at[(origin,) + here],
            send_sem=line_send.at[i, way, step - 1],
            recv_sem=line_recv.at[i, way, step - 1],
            device_id=(place, toward),
            device_id_type=MESH,
        )

    def comes(way, step):
        return along >= step if way == 0 else along + step < fsdp_count

    def goes(way, step):
        if way == 0:
            return (along + 1 < fsdp_count) & (along >= step - 1)
        return (along >= 1) & (along + step - 1 < fsdp_count)

    def origin_of(way, step):
        return along - step if way == 0 else along + step

    def each(flag, action):
        pl.when(flag)(action)

    def forward(i, step):
        for way in range(2):
            each(goes(way, step), lambda: line_copy(i, way, step, origin_of(way, step - 1)).start())

    for i in range(sets):
        forward(i, 1)
    copies = []
    n = 0
    for i in range(sets):
        column = 0
        for _ in range(members[i]):
            wide = own[n].shape[-1]
            target = outs[i].at[
                (along,) + (slice(None),) * (bits + 1) + (pl.ds(column, wide),)
            ]
            loads[n].wait()
            copies.append(pltpu.make_async_copy(passing[n], target, own_sem.at[1, n]))
            copies[-1].start()
            column += wide
            n += 1

    def stage_copies(i, way, step, stage):
        lead = (origin_of(way, step),)
        at = (i, way, step - 1)
        return [
            spread_copy(outs[i], lead, half, stage, position, send_sem.at[at], recv_sem.at[at])
            for half in range(2)
        ]

    def core_copy(i, way, step):
        at = (i, way, step - 1)
        return sibling_copy(
            outs[i], (origin_of(way, step),), position, core_send.at[at], core_recv.at[at]
        )

    def arrive(i, step):
        for way in range(2):

            def landed():
                line_copy(i, way, step, origin_of(way, step)).wait_recv()

            each(comes(way, step), landed)
        if step < steps:
            forward(i, step + 1)
        for way in range(2):

            def begin():
                for copy in stage_copies(i, way, step, 0):
                    copy.start()

            each(comes(way, step), begin)

    def advance(i, step, stage):
        for way in range(2):

            def proceed():
                for copy in stage_copies(i, way, step, stage):
                    copy.wait_recv()
                if stage < bits - 2:
                    for copy in stage_copies(i, way, step, stage + 1):
                        copy.start()
                else:
                    core_copy(i, way, step).start()

            each(comes(way, step), proceed)

    order = [(i, step) for i in range(sets) for step in range(1, steps + 1)]
    for tick in range(len(order) + bits - 1):
        if tick < len(order):
            arrive(*order[tick])
        for stage in range(bits - 1):
            at = tick - 1 - stage
            if 0 <= at < len(order):
                advance(*order[at], stage)
    for copy in copies:
        copy.wait()
    for i, step in order:
        for way in range(2):

            def leave():
                line_copy(i, way, step, origin_of(way, step - 1)).wait_send()

            def finish():
                for stage in range(bits - 1):
                    for copy in stage_copies(i, way, step, stage):
                        copy.wait_send()
                core_copy(i, way, step).wait()

            each(goes(way, step), leave)
            each(comes(way, step), finish)


def weight_gather(pieces, own):
    ctx_count = lax.axis_size("ctx")
    fsdp_count = lax.axis_size("fsdp")
    bits = ctx_count.bit_length() - 1
    steps = fsdp_count - 1
    sets = len(pieces)
    cut = (2,) * bits
    flat = [w.reshape(cut + (w.shape[0] // ctx_count, w.shape[1])) for group in own for w in group]
    out_shapes = [(fsdp_count,) + cut + p.shape for p in pieces]
    total = sum(p.size for p in pieces) * ctx_count * fsdp_count
    outs = pl.pallas_call(
        functools.partial(weight_gather_kernel, ctx_count, fsdp_count, [len(g) for g in own]),
        out_shape=[jax.ShapeDtypeStruct(s, jnp.bfloat16) for s in out_shapes],
        in_specs=[pl.BlockSpec(memory_space=pl.ANY)] * (sets + len(flat)),
        out_specs=[pl.BlockSpec(memory_space=pl.ANY)] * sets,
        scratch_shapes=[pltpu.VMEM(w.shape, w.dtype) for w in flat]
        + [
            pltpu.SemaphoreType.DMA((2, len(flat))),
            pltpu.SemaphoreType.DMA((sets, 2, steps)),
            pltpu.SemaphoreType.DMA((sets, 2, steps)),
            pltpu.SemaphoreType.DMA((sets, 2, steps, 2, bits - 1)),
            pltpu.SemaphoreType.DMA((sets, 2, steps, 2, bits - 1)),
            pltpu.SemaphoreType.DMA((sets, 2, steps)),
            pltpu.SemaphoreType.DMA((sets, 2, steps)),
        ],
        compiler_params=pltpu.CompilerParams(
            collective_id=1, has_side_effects=True, vmem_limit_bytes=16 << 20
        ),
        cost_estimate=pl.CostEstimate(flops=0, bytes_accessed=4 * total, transcendentals=0),
        name="weight_gather",
    )(*pieces, *flat)
    return [o.reshape(-1, o.shape[-1]) for o in outs]


def sequence_gather_kernel(ctx_count, own, out, own_sem, send_sem, recv_sem, core_send, core_recv):
    position = ctx_position(ctx_count)
    bits, _, _, mine, partners, _ = position
    copy = pltpu.make_async_copy(own, out.at[held_index(mine, (), bits)], own_sem)
    copy.start()
    partner_barrier(partners)
    copy.wait()
    for stage in range(bits - 1):
        copies = [spread_copy(out, (), h, stage, position, send_sem, recv_sem) for h in range(2)]
        for copy in copies:
            copy.start()
        for copy in copies:
            copy.wait()
    last = sibling_copy(out, (), position, core_send, core_recv)
    last.start()
    last.wait()


def sequence_gather(own):
    ctx_count = lax.axis_size("ctx")
    bits = ctx_count.bit_length() - 1
    out_shape = (2,) * bits + own.shape
    out = pl.pallas_call(
        functools.partial(sequence_gather_kernel, ctx_count),
        out_shape=jax.ShapeDtypeStruct(out_shape, own.dtype),
        in_specs=[pl.BlockSpec(memory_space=pltpu.VMEM)],
        out_specs=pl.BlockSpec(memory_space=pltpu.VMEM),
        scratch_shapes=[
            pltpu.SemaphoreType.DMA,
            pltpu.SemaphoreType.DMA((2, bits - 1)),
            pltpu.SemaphoreType.DMA((2, bits - 1)),
            pltpu.SemaphoreType.DMA,
            pltpu.SemaphoreType.DMA,
        ],
        compiler_params=pltpu.CompilerParams(
            collective_id=2, has_side_effects=True, vmem_limit_bytes=32 << 20
        ),
        cost_estimate=pl.CostEstimate(
            flops=0, bytes_accessed=4 * own.size * ctx_count, transcendentals=0
        ),
        name="sequence_gather",
    )(own)
    return out.reshape(-1, own.shape[-1])


def blocks_of(grad, rows, columns):
    tall = grad.reshape(rows, grad.shape[0] // rows, columns, grad.shape[1] // columns)
    return tall.transpose(0, 2, 1, 3).reshape(rows * columns, -1)


def body(
    tokens,
    per_layer,
    out_grad,
    segment_ids,
    query_weight,
    key_weight,
    value_weight,
    out_weight,
    left_weight,
    right_weight,
    gate_weight,
    up_weight,
    down_weight,
    side_gate,
    side_out,
    input_gain,
    laurel_gain,
    attn_gain,
    pre_gain,
    post_gain,
    side_gain,
    query_gain,
    key_gain,
):
    low = jnp.bfloat16
    inputs = tokens[0].astype(jnp.float32)
    extra_rows = per_layer[0].astype(jnp.float32)
    cotangent = out_grad[0].astype(jnp.float32)
    sequence_ids = segment_ids[0]
    rows_here, width = inputs.shape
    ctx_count = lax.axis_size("ctx")
    fsdp_count = lax.axis_size("fsdp")
    count = ctx_count * fsdp_count
    ctx_place = lax.axis_index("ctx")
    groups = HEADS // KV_HEADS
    rank = left_weight.shape[1]
    side = side_gate.shape[1]
    length = sequence_ids.shape[0]
    query_width = HEADS * HD
    kv_width = KV_HEADS * HD
    query_pos = ctx_place * rows_here + jnp.arange(rows_here, dtype=jnp.int32)


    def own_rows(weight):
        step = weight.shape[0] // ctx_count
        return lax.dynamic_slice_in_dim(weight, ctx_place * step, step)

    def widened(parts, columns):
        return jnp.pad(jnp.concatenate(parts, axis=1), ((0, 0), (0, columns)))

    shard = width // fsdp_count
    spare = -rank % 128
    first_own = [query_weight, key_weight, value_weight, widened([left_weight], spare)]
    second_own = [
        out_weight,
        side_gate,
        widened([side_out.reshape(shard, -1), right_weight.reshape(shard, -1)], spare),
    ]
    first_piece = jnp.concatenate([own_rows(w) for w in first_own], axis=1)
    second_piece = jnp.concatenate([own_rows(w) for w in second_own], axis=1)
    full_first, full_second = weight_gather(
        [first_piece, second_piece], [first_own, second_own]
    )
    qkv_width = query_width + 2 * kv_width
    full_qkv = full_first[:, :qkv_width]
    full_left = full_first[:, qkv_width : qkv_width + rank]
    full_out = full_second[:, :width]
    full_side_gate = full_second[:, width : width + side]
    full_side_out = full_second[:, width + side : width + 2 * side].reshape(side, width)
    full_right = full_second[:, width + 2 * side : width + 2 * side + rank]
    full_right = full_right.reshape(fsdp_count, rank, width // fsdp_count)
    full_right = full_right.transpose(1, 0, 2).reshape(rank, width)

    normed, input_pull = jax.vjp(rms_norm, inputs, input_gain)
    normed_low = normed.astype(low)
    normed_all = gather(normed_low, "fsdp")
    qkv_raw = forward_product(normed_low, full_qkv)
    left_low = forward_product(normed_low, full_left).astype(low)
    right_out = forward_product(left_low, full_right)

    def heads_piece(qkv_in, gain_one, gain_two):
        query_in = qkv_in[:, :query_width].reshape(rows_here, HEADS, HD)
        key_in = qkv_in[:, query_width : query_width + kv_width].reshape(rows_here, KV_HEADS, HD)
        value_in = qkv_in[:, query_width + kv_width :].reshape(rows_here, KV_HEADS, HD)
        query_heads = rotate(rms_norm(query_in, gain_one), query_pos)
        key_heads = rotate(rms_norm(key_in, gain_two), query_pos)
        value_heads = rms_norm(value_in, 1.0)
        return (query_heads, key_heads, value_heads)

    (query_heads, key_heads, value_heads), heads_pull = jax.vjp(
        heads_piece, qkv_raw, query_gain, key_gain
    )
    query_low = query_heads.astype(low).reshape(rows_here, KV_HEADS, groups, HD)
    query_low = query_low.transpose(1, 2, 0, 3).reshape(KV_HEADS, groups * rows_here, HD)
    kv_low = jnp.concatenate(
        [key_heads.astype(low).reshape(rows_here, -1), value_heads.astype(low).reshape(rows_here, -1)],
        axis=1,
    )
    kv_all = sequence_gather(kv_low)
    key_all = kv_all[:, :kv_width].reshape(length, KV_HEADS, HD).transpose(1, 0, 2)
    value_all = kv_all[:, kv_width:].reshape(length, KV_HEADS, HD).transpose(1, 0, 2)

    query_ids = lax.dynamic_slice_in_dim(sequence_ids, ctx_place * rows_here, rows_here)
    key_pos = jnp.arange(length, dtype=jnp.int32)
    allowed = (query_ids[:, None] == sequence_ids[None, :]) & (
        key_pos[None, :] <= query_pos[:, None]
    )
    allowed = jnp.tile(allowed, (groups, 1))[None]
    scores = jnp.einsum("kqd,kjd->kqj", query_low, key_all, preferred_element_type=jnp.float32)
    scores = jnp.where(allowed, scores, masked_score)
    row_max = jnp.max(scores, axis=-1, keepdims=True)
    weights = jnp.where(allowed, jnp.exp(scores - row_max), 0.0)
    weights = weights / jnp.sum(weights, axis=-1, keepdims=True)
    weights_low = weights.astype(low)
    attended_rows = jnp.einsum(
        "kqj,kjd->kqd", weights_low, value_all, preferred_element_type=jnp.float32
    )
    attended = attended_rows.reshape(KV_HEADS, groups, rows_here, HD).transpose(2, 0, 1, 3)
    attended_low = attended.reshape(rows_here, query_width).astype(low)
    attended_all = gather(attended_low, "fsdp")
    attn_raw = forward_product(attended_low, full_out)

    def mix_piece(x, normed_in, attn_in, right_in, gain_one, gain_two, gain_three):
        mixed = (
            x + rms_norm(attn_in, gain_one) + normed_in + rms_norm(right_in, gain_two)
        ) * inverse_root
        return (mixed, rms_norm(mixed, gain_three))

    (mixed, ffn_in), mix_pull = jax.vjp(
        mix_piece, inputs, normed, attn_raw, right_out, attn_gain, laurel_gain, pre_gain
    )

    ffn_all = gather(ffn_in.astype(low), "fsdp")
    gate_raw = forward_product(ffn_all, gate_weight)
    up_raw = forward_product(ffn_all, up_weight)
    hidden, hidden_pull = jax.vjp(hidden_piece, gate_raw, up_raw)
    hidden_low = hidden.astype(low)
    ffn_out = scatter_sum(forward_product(hidden_low, down_weight).astype(low), "fsdp")
    ffn_out = ffn_out.astype(jnp.float32)
    middle, middle_pull = jax.vjp(middle_piece, mixed, ffn_out, post_gain)
    middle_low = middle.astype(low)
    layer_gate = forward_product(middle_low, full_side_gate)
    layer_act, extra_pull = jax.vjp(hidden_piece, layer_gate, extra_rows)
    layer_low = layer_act.astype(low)
    layer_out = forward_product(layer_low, full_side_out)
    result, out_pull = jax.vjp(middle_piece, middle, layer_out, side_gain)

    middle_grad_one, layer_out_grad, side_gain_grad = out_pull(cotangent)
    layer_grad_low = layer_out_grad.astype(low)
    side_out_grad = over_rows(layer_low, layer_grad_low)
    layer_gate_grad, extra_grad = extra_pull(across(layer_grad_low, full_side_out))
    gate_grad_low = layer_gate_grad.astype(low)
    side_gate_grad = over_rows(middle_low, gate_grad_low)
    mixed_grad_one, ffn_out_grad, post_gain_grad = middle_pull(
        middle_grad_one + across(gate_grad_low, full_side_gate)
    )
    ffn_grad_all = gather(ffn_out_grad.astype(low), "fsdp")
    down_weight_grad = over_rows(ffn_grad_all, hidden_low)
    gate_raw_grad, up_raw_grad = hidden_pull(across(ffn_grad_all, down_weight))
    gate_back_low = gate_raw_grad.astype(low)
    up_back_low = up_raw_grad.astype(low)
    ffn_in_grad = scatter_sum(
        (across(gate_back_low, gate_weight) + across(up_back_low, up_weight)).astype(low), "fsdp"
    )
    gate_weight_grad = over_rows(ffn_all, gate_back_low)
    up_weight_grad = over_rows(ffn_all, up_back_low)
    (
        inputs_grad_one,
        normed_grad_one,
        attn_raw_grad,
        right_out_grad,
        attn_gain_grad,
        laurel_gain_grad,
        pre_gain_grad,
    ) = mix_pull((mixed_grad_one, ffn_in_grad.astype(jnp.float32)))
    attn_grad_low = attn_raw_grad.astype(low)
    attended_grad_low = across(attn_grad_low, full_out).astype(low)
    right_grad_low = right_out_grad.astype(low)
    right_weight_grad = over_rows(right_grad_low, left_low)
    left_grad_low = across(right_grad_low, full_right).astype(low)
    left_weight_grad = over_rows(normed_low, left_grad_low)
    grad_rows = attended_grad_low.reshape(rows_here, KV_HEADS, groups, HD).transpose(1, 2, 0, 3)
    grad_rows = grad_rows.reshape(KV_HEADS, groups * rows_here, HD)
    correction = jnp.sum(
        grad_rows.astype(jnp.float32) * attended_rows, axis=-1, keepdims=True
    )
    weight_grad = jnp.einsum(
        "kqd,kjd->kqj", grad_rows, value_all, preferred_element_type=jnp.float32
    )
    score_grad = (weights * (weight_grad - correction)).astype(low)
    query_grad = jnp.einsum(
        "kqj,kjd->kqd", score_grad, key_all, preferred_element_type=jnp.float32
    )
    key_grad = jnp.einsum(
        "kqj,kqd->kjd", score_grad, query_low, preferred_element_type=jnp.float32
    )
    value_grad = jnp.einsum(
        "kqj,kqd->kjd", weights_low, grad_rows, preferred_element_type=jnp.float32
    )
    kv_grad = jnp.concatenate([key_grad.astype(low), value_grad.astype(low)], axis=0)
    kv_grad = kv_grad.transpose(1, 0, 2).reshape(length, 2 * kv_width)
    kv_grad = owner_sums([kv_grad], False, 3)[0].astype(jnp.float32)
    kv_grad = kv_grad.reshape(rows_here, 2, KV_HEADS, HD)
    query_heads_grad = query_grad.reshape(KV_HEADS, groups, rows_here, HD).transpose(2, 0, 1, 3)
    query_heads_grad = query_heads_grad.reshape(rows_here, HEADS, HD)
    qkv_grad, query_gain_grad, key_gain_grad = heads_pull(
        (query_heads_grad, kv_grad[:, 0], kv_grad[:, 1])
    )
    qkv_back_low = qkv_grad.astype(low)
    normed_grad_two = across(qkv_back_low, full_qkv) + across(left_grad_low, full_left)
    inputs_grad_two, input_gain_grad = input_pull(normed_grad_one + normed_grad_two)
    block_out = result.astype(low)[None]
    tokens_grad = (inputs_grad_one + inputs_grad_two).astype(low)[None]
    per_layer_grad = extra_grad.astype(low)[None]

    def columns_to_owner(x):
        parts = x.reshape(rows_here, fsdp_count, -1).transpose(1, 0, 2)
        return lax.all_to_all(parts, "fsdp", 0, 0, tiled=True).reshape(fsdp_count * rows_here, -1)

    out_columns = columns_to_owner(attn_grad_low)
    out_weight_grad = over_rows(attended_all, out_columns)
    qkv_parts = jnp.concatenate(
        [
            part.reshape(rows_here, fsdp_count, -1)
            for part in (
                qkv_back_low[:, :query_width],
                qkv_back_low[:, query_width : query_width + kv_width],
                qkv_back_low[:, query_width + kv_width :],
            )
        ],
        axis=2,
    )
    qkv_columns = columns_to_owner(qkv_parts.reshape(rows_here, -1))
    qkv_weight_grad = over_rows(normed_all, qkv_columns)

    small = [
        left_weight_grad.reshape(count, -1),
        right_weight_grad.reshape(count, -1),
        blocks_of(side_gate_grad, ctx_count, fsdp_count),
        blocks_of(side_out_grad, ctx_count, fsdp_count),
        input_gain_grad.reshape(count, -1),
        laurel_gain_grad.reshape(count, -1),
        attn_gain_grad.reshape(count, -1),
        pre_gain_grad.reshape(count, -1),
        post_gain_grad.reshape(count, -1),
        side_gain_grad.reshape(count, -1),
        query_gain_grad.reshape(count, -1),
        key_gain_grad.reshape(count, -1),
    ]
    sizes = [part.shape[1] for part in small]
    packed = jnp.concatenate([part.astype(low) for part in small], axis=1)
    packed = jnp.pad(packed, ((0, 0), (0, -packed.shape[1] % (16 * 128))))
    sums = owner_sums(
        [
            grad.astype(low)
            for grad in (
                down_weight_grad,
                gate_weight_grad,
                up_weight_grad,
                out_weight_grad,
                qkv_weight_grad,
                packed.reshape(count * 16, -1),
            )
        ],
        True,
        0,
    )
    down_weight_grad, gate_weight_grad, up_weight_grad, out_weight_grad, qkv_weight_grad = sums[:5]
    down_weight_grad = down_weight_grad.T
    packed = sums[5].reshape(-1)
    query_part = query_width // fsdp_count
    kv_part = kv_width // fsdp_count
    query_weight_grad = qkv_weight_grad[:, :query_part]
    key_weight_grad = qkv_weight_grad[:, query_part : query_part + kv_part]
    value_weight_grad = qkv_weight_grad[:, query_part + kv_part :]
    shares = []
    start = 0
    for size in sizes:
        shares.append(packed[start : start + size].astype(jnp.float32))
        start += size
    left_weight_grad = shares[0].reshape(-1, rank)
    right_weight_grad = shares[1].reshape(-1, rank).T
    side_gate_grad = shares[2].reshape(width // ctx_count, -1)
    side_out_grad = shares[3].reshape(side // ctx_count, -1)
    wide = jnp.float32
    return (
        block_out,
        tokens_grad,
        per_layer_grad,
        query_weight_grad.astype(wide),
        key_weight_grad.astype(wide),
        value_weight_grad.astype(wide),
        out_weight_grad.astype(wide),
        left_weight_grad,
        right_weight_grad,
        gate_weight_grad.astype(wide),
        up_weight_grad.astype(wide),
        down_weight_grad.astype(wide),
        side_gate_grad,
        side_out_grad,
        *shares[4:],
    )


def solution(mesh):
    placed = (
        P("fsdp", "ctx", None),
        P("fsdp", "ctx", None),
        P("fsdp", "ctx", None),
        P("fsdp", None),
        P("fsdp", None),
        P("fsdp", None),
        P("fsdp", None),
        P("fsdp", None),
        P("fsdp", None),
        P(None, "fsdp"),
        P(None, "fsdp"),
        P(None, "fsdp"),
        P("fsdp", None),
        P("fsdp", None),
        P("fsdp", None),
        P(),
        P(),
        P(),
        P(),
        P(),
        P(),
        P(),
        P(),
    )
    return jax.shard_map(
        body,
        mesh=mesh,
        in_specs=placed,
        out_specs=(
            P("fsdp", "ctx", None),
            P("fsdp", "ctx", None),
            P("fsdp", "ctx", None),
            P("ctx", "fsdp"),
            P("ctx", "fsdp"),
            P("ctx", "fsdp"),
            P("ctx", "fsdp"),
            P(("ctx", "fsdp"), None),
            P(None, ("ctx", "fsdp")),
            P("ctx", "fsdp"),
            P("ctx", "fsdp"),
            P("fsdp", "ctx"),
            P("ctx", "fsdp"),
            P("ctx", "fsdp"),
            P(("ctx", "fsdp")),
            P(("ctx", "fsdp")),
            P(("ctx", "fsdp")),
            P(("ctx", "fsdp")),
            P(("ctx", "fsdp")),
            P(("ctx", "fsdp")),
            P(("ctx", "fsdp")),
            P(("ctx", "fsdp")),
        ),
        check_vma=False,
    )
```

```python
import functools
import math

import jax
import jax.numpy as jnp
from jax import lax
from jax.experimental import pallas as pl
from jax.experimental.pallas import tpu as pltpu
from jax.sharding import PartitionSpec as P

HEADS = 8
KV_HEADS = 2
HD = 256
MESH = pl.DeviceIdType.MESH


epsilon = 1e-06
rope_theta = 1000000.0
masked_score = -1e30
inverse_root = 1.0 / math.sqrt(2.0)


def rms_norm(v, factor):
    return v * lax.rsqrt(jnp.mean(v * v, axis=-1, keepdims=True) + epsilon) * factor


def forward_product(a, b):
    return jnp.dot(a, b, preferred_element_type=jnp.float32)


def across(a, b):
    return lax.dot_general(a, b, (((1,), (1,)), ((), ())), preferred_element_type=jnp.float32)


def over_rows(a, b):
    return lax.dot_general(a, b, (((0,), (0,)), ((), ())), preferred_element_type=jnp.float32)


def hidden_piece(gate_in, up_in):
    return jax.nn.gelu(gate_in, approximate=True) * up_in


def middle_piece(mixed_in, ffn_in_rows, factor):
    return mixed_in + rms_norm(ffn_in_rows, factor)


def gather(x, axis):
    return lax.all_gather(x, axis, axis=0, tiled=True)


def scatter_sum(x, axis):
    return lax.psum_scatter(x, axis, scatter_dimension=0, tiled=True)


def partner_barrier(partners):
    barrier = pltpu.get_barrier_semaphore()
    for partner in partners:
        pl.semaphore_signal(barrier, inc=1, device_id=partner, device_id_type=MESH)
    pl.semaphore_wait(barrier, len(partners))


def add_rows(target, source, first, rows):
    tile = 16

    def one(step, carry):
        at = pl.ds(pl.multiple_of(first + step * tile, tile), tile)
        from_at = pl.ds(pl.multiple_of(step * tile, tile), tile)
        total = target[at].astype(jnp.float32) + source[from_at].astype(jnp.float32)
        target[at] = total.astype(target.dtype)
        return carry

    lax.fori_loop(0, rows // tile, one, 0)


def held_index(mine, done, bits):
    return tuple(slice(None) if t in done else mine[t] for t in reversed(range(bits)))


def ctx_position(ctx_count):
    bits = ctx_count.bit_length() - 1
    place = lax.axis_index("ctx")
    along = lax.axis_index("fsdp")
    mine = [lax.rem(place // (1 << t), 2) for t in range(bits)]
    partners = [(place + (1 - 2 * mine[t]) * (1 << t), along) for t in range(bits)]
    orders = [list(range(1, bits)), list(range(bits - 1, 0, -1))]
    return bits, place, along, mine, partners, orders


def spread_copy(out, lead, half, stage, position, send_sem, recv_sem):
    bits, _, _, mine, partners, orders = position
    order = orders[half]
    rows = out.shape[-2] // 2
    at = lead + held_index(mine, order[:stage], bits) + (pl.ds(half * rows, rows),)
    return pltpu.make_async_remote_copy(
        src_ref=out.at[at],
        dst_ref=out.at[at],
        send_sem=send_sem.at[half, stage],
        recv_sem=recv_sem.at[half, stage],
        device_id=partners[order[stage]],
        device_id_type=MESH,
    )


def sibling_copy(out, lead, position, send_sem, recv_sem):
    bits, _, _, mine, partners, orders = position
    at = lead + held_index(mine, orders[0], bits)
    return pltpu.make_async_remote_copy(
        src_ref=out.at[at],
        dst_ref=out.at[at],
        send_sem=send_sem,
        recv_sem=recv_sem,
        device_id=partners[0],
        device_id_type=MESH,
    )


def weight_gather_kernel(ctx_count, fsdp_count, members, lines, *refs):
    sets = len(members)
    own_count = sum(members)
    own, line_own = refs[:own_count], refs[own_count : own_count + lines]
    rest = refs[own_count + lines :]
    outs, line_outs = rest[:sets], rest[sets : sets + lines]
    rest = rest[sets + lines :]
    passing, pieces = rest[: own_count + lines], rest[own_count + lines : own_count + lines + sets]
    own_sem, line_send, line_recv, send_sem, recv_sem, core_send, core_recv = rest[
        own_count + lines + sets :
    ]
    position = ctx_position(ctx_count)
    bits, place, along, mine, partners, _ = position
    steps = fsdp_count - 1
    here = held_index(mine, (), bits)
    columns = []
    for i in range(sets):
        start = 0
        for _ in range(members[i]):
            wide = own[len(columns)].shape[-1]
            columns.append((i, pl.ds(start, wide)))
            start += wide
    piece_loads = [
        pltpu.make_async_copy(own[n].at[here], pieces[i].at[:, at], own_sem.at[0, n])
        for n, (i, at) in enumerate(columns)
    ]
    for load in piece_loads:
        load.start()
    loads = [
        pltpu.make_async_copy(source, passing[n], own_sem.at[1, n])
        for n, source in enumerate(own + line_own)
    ]
    for load in loads:
        load.start()
    partner_barrier(
        partners
        + [(place, lax.rem(along + 1, fsdp_count)), (place, lax.rem(along + steps, fsdp_count))]
    )

    def line_copy(i, way, step, origin):
        toward = along + 1 if way == 0 else along - 1
        if i < sets:
            first, target = pieces[i], outs[i].at[(origin,) + here]
        else:
            first, target = line_own[i - sets], line_outs[i - sets].at[origin]
        return pltpu.make_async_remote_copy(
            src_ref=first if step == 1 else target,
            dst_ref=target,
            send_sem=line_send.at[i, way, step - 1],
            recv_sem=line_recv.at[i, way, step - 1],
            device_id=(place, toward),
            device_id_type=MESH,
        )

    def comes(way, step):
        return along >= step if way == 0 else along + step < fsdp_count

    def goes(way, step):
        if way == 0:
            return (along + 1 < fsdp_count) & (along >= step - 1)
        return (along >= 1) & (along + step - 1 < fsdp_count)

    def origin_of(way, step):
        return along - step if way == 0 else along + step

    def each(flag, action):
        pl.when(flag)(action)

    def forward(i, step):
        for way in range(2):
            each(goes(way, step), lambda: line_copy(i, way, step, origin_of(way, step - 1)).start())

    for load in piece_loads:
        load.wait()
    for i in range(sets):
        forward(i, 1)
    stores = []
    for n, load in enumerate(loads):
        load.wait()
        if n < own_count:
            i, at = columns[n]
            target = outs[i].at[(along,) + (slice(None),) * (bits + 1) + (at,)]
        else:
            target = line_outs[n - own_count].at[along]
        stores.append(pltpu.make_async_copy(passing[n], target, own_sem.at[2, n]))
        stores[-1].start()

    def stage_copies(i, way, step, stage):
        lead = (origin_of(way, step),)
        at = (i, way, step - 1)
        return [
            spread_copy(outs[i], lead, half, stage, position, send_sem.at[at], recv_sem.at[at])
            for half in range(2)
        ]

    def core_copy(i, way, step):
        at = (i, way, step - 1)
        return sibling_copy(
            outs[i], (origin_of(way, step),), position, core_send.at[at], core_recv.at[at]
        )

    def arrive(i, step):
        for way in range(2):

            def landed():
                line_copy(i, way, step, origin_of(way, step)).wait_recv()

            each(comes(way, step), landed)
        if step < steps:
            forward(i, step + 1)
        if i >= sets:
            return
        for way in range(2):

            def begin():
                for copy in stage_copies(i, way, step, 0):
                    copy.start()

            each(comes(way, step), begin)

    def advance(i, step, stage):
        if i >= sets:
            return
        for way in range(2):

            def proceed():
                for copy in stage_copies(i, way, step, stage):
                    copy.wait_recv()
                if stage < bits - 2:
                    for copy in stage_copies(i, way, step, stage + 1):
                        copy.start()
                else:
                    core_copy(i, way, step).start()

            each(comes(way, step), proceed)

    order = [(i, step) for i in range(sets + lines) for step in range(1, steps + 1)]
    for tick in range(len(order) + bits - 1):
        if tick < len(order):
            if order[tick] == (sets - 1, 1):
                for i in range(sets, sets + lines):
                    forward(i, 1)
            arrive(*order[tick])
        for stage in range(bits - 1):
            at = tick - 1 - stage
            if 0 <= at < len(order):
                advance(*order[at], stage)
    for copy in stores:
        copy.wait()
    for i, step in order:
        for way in range(2):

            def leave():
                line_copy(i, way, step, origin_of(way, step - 1)).wait_send()

            def finish():
                for stage in range(bits - 1):
                    for copy in stage_copies(i, way, step, stage):
                        copy.wait_send()
                core_copy(i, way, step).wait()

            each(goes(way, step), leave)
            if i < sets:
                each(comes(way, step), finish)


def weight_gather(own, lines):
    ctx_count = lax.axis_size("ctx")
    fsdp_count = lax.axis_size("fsdp")
    bits = ctx_count.bit_length() - 1
    steps = fsdp_count - 1
    sets = len(own)
    cut = (2,) * bits
    low = jnp.bfloat16
    flat = [w.reshape(cut + (w.shape[0] // ctx_count, w.shape[1])) for group in own for w in group]
    pieces = [(g[0].shape[0] // ctx_count, sum(w.shape[1] for w in g)) for g in own]
    out_shapes = [(fsdp_count,) + cut + p for p in pieces]
    out_shapes += [(fsdp_count,) + w.shape for w in lines]
    total = sum(rows * columns for rows, columns in pieces) * ctx_count * fsdp_count
    outs = pl.pallas_call(
        functools.partial(
            weight_gather_kernel, ctx_count, fsdp_count, [len(g) for g in own], len(lines)
        ),
        out_shape=[jax.ShapeDtypeStruct(s, low) for s in out_shapes],
        in_specs=[pl.BlockSpec(memory_space=pltpu.HBM)] * (len(flat) + len(lines)),
        out_specs=[pl.BlockSpec(memory_space=pltpu.HBM)] * len(out_shapes),
        scratch_shapes=[pltpu.VMEM(w.shape, low) for w in flat + list(lines)]
        + [pltpu.VMEM(p, low) for p in pieces]
        + [
            pltpu.SemaphoreType.DMA((3, len(flat) + len(lines))),
            pltpu.SemaphoreType.DMA((sets + len(lines), 2, steps)),
            pltpu.SemaphoreType.DMA((sets + len(lines), 2, steps)),
            pltpu.SemaphoreType.DMA((sets, 2, steps, 2, bits - 1)),
            pltpu.SemaphoreType.DMA((sets, 2, steps, 2, bits - 1)),
            pltpu.SemaphoreType.DMA((sets, 2, steps)),
            pltpu.SemaphoreType.DMA((sets, 2, steps)),
        ],
        compiler_params=pltpu.CompilerParams(
            collective_id=1, has_side_effects=True, vmem_limit_bytes=60 << 20
        ),
        cost_estimate=pl.CostEstimate(flops=0, bytes_accessed=4 * total, transcendentals=0),
        name="weight_gather",
    )(*flat, *lines)
    return [o.reshape(-1, o.shape[-1]) for o in outs[:sets]] + list(outs[sets:])


class Halving:
    def __init__(self, position, rows, give, held, first_in, later_in, sems):
        self.bits, self.place, self.along, self.mine, self.partners, self.orders = position
        self.rows, self.give, self.held = rows, give, held
        self.first_in, self.later_in = first_in, later_in
        self.send_zero, self.recv_zero, self.send_sem, self.recv_sem = sems
        self.pairs = 1 << (self.bits - 1)

    def first_copy(self, b):
        return pltpu.make_async_remote_copy(
            src_ref=self.give(b),
            dst_ref=self.first_in.at[b],
            send_sem=self.send_zero.at[b],
            recv_sem=self.recv_zero.at[b],
            device_id=self.partners[0],
            device_id_type=MESH,
        )

    def start_first(self):
        for b in range(self.pairs):
            self.first_copy(b).start()

    def end_first(self, b):
        self.first_copy(b).wait()
        add_rows(self.held(b), self.first_in.at[b], 0, self.rows)

    def slot_of(self, stage):
        return sum(1 << (self.bits - 2 - s) for s in range(stage))

    def block_sets(self, half, stage):
        order = self.orders[half]
        bit = order[stage]
        free = order[stage + 1 :]
        fixed = sum(self.mine[t] * (1 << (t - 1)) for t in order[:stage])
        sent, kept = [], []
        for combo in range(1 << len(free)):
            value = sum(((combo >> n) & 1) << (t - 1) for n, t in enumerate(free))
            sent.append(fixed + (1 - self.mine[bit]) * (1 << (bit - 1)) + value)
            kept.append(fixed + self.mine[bit] * (1 << (bit - 1)) + value)
        return bit, sent, kept

    def stage_copies(self, stage):
        rows = self.rows // 2
        copies = []
        for half in range(2):
            bit, sent, _ = self.block_sets(half, stage)
            for n, block in enumerate(sent):
                at = (half, self.slot_of(stage) + n)
                copies.append(
                    pltpu.make_async_remote_copy(
                        src_ref=self.held(block).at[pl.ds(half * rows, rows)],
                        dst_ref=self.later_in.at[at],
                        send_sem=self.send_sem.at[at],
                        recv_sem=self.recv_sem.at[at],
                        device_id=self.partners[bit],
                        device_id_type=MESH,
                    )
                )
        return copies

    def start(self, stage):
        for copy in self.stage_copies(stage):
            copy.start()

    def end(self, stage):
        for copy in self.stage_copies(stage):
            copy.wait()
        rows = self.rows // 2
        for half in range(2):
            _, _, kept = self.block_sets(half, stage)
            for n, block in enumerate(kept):
                at = (half, self.slot_of(stage) + n)
                add_rows(self.held(block), self.later_in.at[at], half * rows, rows)

    def mine_now(self):
        return self.held(self.place // 2)


def halving_scratch(ctx_count, rows, columns):
    pairs = ctx_count // 2
    return [
        pltpu.VMEM((pairs, rows, columns), jnp.bfloat16),
        pltpu.VMEM((2, pairs - 1, rows // 2, columns), jnp.bfloat16),
        pltpu.SemaphoreType.DMA((pairs,)),
        pltpu.SemaphoreType.DMA((pairs,)),
        pltpu.SemaphoreType.DMA((2, pairs - 1)),
        pltpu.SemaphoreType.DMA((2, pairs - 1)),
    ]


def unit_rows(v):
    scale = lax.rsqrt(jnp.mean(v * v, axis=-1, keepdims=True) + epsilon)
    return v * scale, scale


def turned(v, cosine, sine_part):
    halfway = v.shape[-1] // 2
    leading, trailing = v[:, :halfway], v[:, halfway:]
    return jnp.concatenate(
        [leading * cosine - trailing * sine_part, trailing * cosine + leading * sine_part], axis=-1
    )


def unit_rows_pull(v, grad, gain):
    unit, scale = unit_rows(v)
    gain_grad = jnp.sum(grad * unit, axis=0, keepdims=True)
    scaled = grad * gain
    return scale * (scaled - unit * jnp.mean(unit * scaled, axis=-1, keepdims=True)), gain_grad


def head_at(h):
    return pl.ds(pl.multiple_of(h * HD, HD), HD)


def attention_forward_kernel(
    ctx_count,
    raw,
    cosine_ref,
    sine_ref,
    query_gain,
    key_gain,
    row_ids,
    key_ids,
    kv,
    query_low,
    attended_low,
    log_totals,
    bias,
    send_sem,
    recv_sem,
    core_send,
    core_recv,
):
    position = ctx_position(ctx_count)
    bits, place, _, mine, partners, _ = position
    rows = raw.shape[0]
    groups = HEADS // KV_HEADS
    length = ctx_count * rows
    here = held_index(mine, (), bits)
    cosine, sine_part = cosine_ref[...], sine_ref[...]
    for k in range(KV_HEADS):
        unit, _ = unit_rows(raw[:, pl.ds((HEADS + k) * HD, HD)])
        key = turned(unit * key_gain[...], cosine, sine_part)
        kv[here + (slice(None), pl.ds(k * HD, HD))] = key.astype(kv.dtype)
        value, _ = unit_rows(raw[:, pl.ds((HEADS + KV_HEADS + k) * HD, HD)])
        kv[here + (slice(None), pl.ds((KV_HEADS + k) * HD, HD))] = value.astype(kv.dtype)
    partner_barrier(partners)

    def copies_of(stage):
        return [spread_copy(kv, (), h, stage, position, send_sem, recv_sem) for h in range(2)]

    for copy in copies_of(0):
        copy.start()
    allowed = (row_ids[...] == key_ids[...]) & (
        lax.broadcasted_iota(jnp.int32, (rows, length), 1)
        <= lax.broadcasted_iota(jnp.int32, (rows, length), 0) + place * rows
    )
    bias[...] = jnp.where(allowed, 0.0, masked_score)

    def one_query(h, carry):
        unit, _ = unit_rows(raw[:, head_at(h)])
        query = turned(unit * query_gain[...], cosine, sine_part)
        query_low[:, head_at(h)] = query.astype(query_low.dtype)
        return carry

    lax.fori_loop(0, HEADS, one_query, 0)
    for stage in range(1, bits - 1):
        for copy in copies_of(stage - 1):
            copy.wait()
        for copy in copies_of(stage):
            copy.start()
    for copy in copies_of(bits - 2):
        copy.wait()
    last = sibling_copy(kv, (), position, core_send, core_recv)
    last.start()
    last.wait()
    everywhere = (slice(None),) * (bits + 1)
    for k in range(KV_HEADS):
        key = kv[everywhere + (pl.ds(k * HD, HD),)].reshape(length, HD)
        value = kv[everywhere + (pl.ds((KV_HEADS + k) * HD, HD),)].reshape(length, HD)

        def one_head(g, carry, k=k, key=key, value=value):
            h = k * groups + g
            scores = across(query_low[:, head_at(h)], key) + bias[...]
            row_max = jnp.max(scores, axis=-1, keepdims=True)
            weights = jnp.exp(scores - row_max)
            row_total = jnp.sum(weights, axis=-1, keepdims=True)
            weights = (weights * (1.0 / row_total)).astype(value.dtype)
            attended_low[:, head_at(h)] = forward_product(weights, value).astype(attended_low.dtype)
            log_total = jnp.broadcast_to(row_max + jnp.log(row_total), (rows, rows))
            log_totals[h] = log_total.T[:8]
            return carry

        lax.fori_loop(0, groups, one_head, 0)


def attention_forward(raw, cosine, sine_part, query_gain, key_gain, row_ids, key_ids):
    ctx_count = lax.axis_size("ctx")
    bits = ctx_count.bit_length() - 1
    rows = raw.shape[0]
    length = ctx_count * rows
    low = jnp.bfloat16
    vmem = pl.BlockSpec(memory_space=pltpu.VMEM)
    return pl.pallas_call(
        functools.partial(attention_forward_kernel, ctx_count),
        out_shape=[
            jax.ShapeDtypeStruct((2,) * bits + (rows, 2 * KV_HEADS * HD), low),
            jax.ShapeDtypeStruct((rows, HEADS * HD), low),
            jax.ShapeDtypeStruct((rows, HEADS * HD), low),
            jax.ShapeDtypeStruct((HEADS, 8, rows), jnp.float32),
        ],
        in_specs=[vmem] * 7,
        out_specs=[vmem] * 4,
        scratch_shapes=[
            pltpu.VMEM((rows, length), jnp.float32),
            pltpu.SemaphoreType.DMA((2, bits - 1)),
            pltpu.SemaphoreType.DMA((2, bits - 1)),
            pltpu.SemaphoreType.DMA,
            pltpu.SemaphoreType.DMA,
        ],
        compiler_params=pltpu.CompilerParams(
            collective_id=2, has_side_effects=True, vmem_limit_bytes=40 << 20
        ),
        cost_estimate=pl.CostEstimate(
            flops=4 * HEADS * HD * rows * length,
            bytes_accessed=8 << 20,
            transcendentals=HEADS * rows * length,
        ),
        name="attention_forward",
    )(raw, cosine, sine_part, query_gain[None], key_gain[None], row_ids[:, None], key_ids[None])


def attention_backward_kernel(ctx_count, extra, *refs):
    (
        grads,
        query_low,
        kv,
        log_totals,
        raw,
        cosine_ref,
        sine_ref,
        query_gain,
        key_gain,
        row_ids,
        key_ids,
    ) = refs[:11]
    many = len(extra)
    extra_in = refs[11 : 11 + many]
    back, gain_grads = refs[11 + many : 13 + many]
    extra_out = refs[13 + many : 13 + 2 * many]
    rest = refs[13 + 2 * many :]
    bias, score_grads, weights_low, query_grads, kv_grads = rest[:5]
    kv_parts = rest[5:11]
    extra_parts = [rest[11 + 8 * i : 19 + 8 * i] for i in range(many)]
    position = ctx_position(ctx_count)
    bits, place, _, mine, partners, _ = position
    pairs = ctx_count // 2
    rows = raw.shape[0]
    groups = HEADS // KV_HEADS
    length = ctx_count * rows
    low = jnp.bfloat16

    kv_sum = Halving(
        position,
        rows,
        lambda b: kv_grads.at[2 * b + 1 - mine[0]],
        lambda b: kv_grads.at[2 * b + mine[0]],
        kv_parts[0],
        kv_parts[1],
        kv_parts[2:6],
    )
    sums, own_copies = [], []
    for i, (block, _) in enumerate(extra):
        held, first_in, later_in, own_sem = extra_parts[i][:4]

        def give(b, i=i, block=block):
            at = pl.multiple_of((2 * b + 1 - mine[0]) * block, 16)
            return extra_in[i].at[pl.ds(at, block)]

        sums.append(
            Halving(
                position,
                block,
                give,
                lambda b, held=held: held.at[b],
                first_in,
                later_in,
                extra_parts[i][4:8],
            )
        )
        copies = []
        for b in range(pairs):
            at = pl.multiple_of((2 * b + mine[0]) * block, 16)
            copies.append(
                pltpu.make_async_copy(
                    extra_in[i].at[pl.ds(at, block)], held.at[b], own_sem.at[b]
                )
            )
            copies[-1].start()
        own_copies.append(copies)

    partner_barrier(partners)
    for one in sums:
        one.start_first()

    def open_extra(i):
        for b in range(pairs):
            own_copies[i][b].wait()
            sums[i].end_first(b)
        sums[i].start(0)

    allowed = (key_ids[...] == row_ids[...]) & (
        lax.broadcasted_iota(jnp.int32, (length, rows), 0)
        <= lax.broadcasted_iota(jnp.int32, (length, rows), 1) + place * rows
    )
    bias[...] = jnp.where(allowed, 0.0, masked_score)
    everywhere = (slice(None),) * (bits + 1)
    for k in range(KV_HEADS):
        if k < many:
            open_extra(k)
        key = kv[everywhere + (pl.ds(k * HD, HD),)].reshape(length, HD)
        value = kv[everywhere + (pl.ds((KV_HEADS + k) * HD, HD),)].reshape(length, HD)

        def one_head(g, carry, k=k, key=key, value=value):
            h = k * groups + g
            columns = pl.ds(pl.multiple_of(g * rows, rows), rows)
            scores = across(key, query_low[:, head_at(h)]) + bias[...]
            weights = jnp.exp(scores - log_totals[h][:1])
            weight_grad = across(value, grads[:, head_at(h)])
            delta = jnp.sum(weights * weight_grad, axis=0, keepdims=True)
            score_grads[:, columns] = (weights * (weight_grad - delta)).astype(low)
            weights_low[:, columns] = weights.astype(low)
            return carry

        lax.fori_loop(0, groups, one_head, 0)
        heads = [pl.ds((k * groups + g) * HD, HD) for g in range(groups)]
        query_stack = jnp.concatenate([query_low[:, at] for at in heads], axis=0)
        grad_stack = jnp.concatenate([grads[:, at] for at in heads], axis=0)
        key_grad = forward_product(score_grads[...], query_stack).astype(low)
        value_grad = forward_product(weights_low[...], grad_stack).astype(low)
        kv_grads[:, :, pl.ds(k * HD, HD)] = key_grad.reshape(ctx_count, rows, HD)
        kv_grads[:, :, pl.ds((KV_HEADS + k) * HD, HD)] = value_grad.reshape(ctx_count, rows, HD)
        query_grad = over_rows(key, score_grads[...])
        for g, at in enumerate(heads):
            query_grads[:, at] = query_grad[:, g * rows : (g + 1) * rows].T

    kv_sum.start_first()
    for b in range(pairs):
        kv_sum.end_first(b)
    kv_sum.start(0)
    for i in range(KV_HEADS, many):
        open_extra(i)
    cosine, sine_part = cosine_ref[...], sine_ref[...]

    def one_query(h, gain_grad):
        grad = turned(query_grads[:, head_at(h)], cosine, -sine_part)
        pulled, more = unit_rows_pull(raw[:, head_at(h)], grad, query_gain[...])
        back[:, head_at(h)] = pulled.astype(low)
        return gain_grad + more

    gain_grads[0:1] = lax.fori_loop(0, HEADS, one_query, jnp.zeros((1, HD), jnp.float32))
    for stage in range(1, bits - 1):
        kv_sum.end(stage - 1)
        kv_sum.start(stage)
    kv_sum.end(bits - 2)
    summed = kv_sum.mine_now()
    key_gain_grad = jnp.zeros((1, HD), jnp.float32)
    for k in range(KV_HEADS):
        grad = summed[:, pl.ds(k * HD, HD)].astype(jnp.float32)
        grad = turned(grad, cosine, -sine_part)
        at = pl.ds((HEADS + k) * HD, HD)
        pulled, more = unit_rows_pull(raw[:, at], grad, key_gain[...])
        back[:, at] = pulled.astype(low)
        key_gain_grad = key_gain_grad + more
        grad = summed[:, pl.ds((KV_HEADS + k) * HD, HD)].astype(jnp.float32)
        at = pl.ds((HEADS + KV_HEADS + k) * HD, HD)
        pulled, _ = unit_rows_pull(raw[:, at], grad, 1.0)
        back[:, at] = pulled.astype(low)
    gain_grads[1:2] = key_gain_grad
    for stage in range(1, bits - 1):
        for one in sums:
            one.end(stage - 1)
            one.start(stage)
    for i in range(many):
        sums[i].end(bits - 2)
        extra_out[i][...] = sums[i].mine_now()[...]


def attention_backward(
    grads, query_low, kv, log_totals, raw, cosine, sine_part, query_gain, key_gain, row_ids, key_ids, extra
):
    ctx_count = lax.axis_size("ctx")
    rows = raw.shape[0]
    length = ctx_count * rows
    pairs = ctx_count // 2
    groups = HEADS // KV_HEADS
    low = jnp.bfloat16
    vmem = pl.BlockSpec(memory_space=pltpu.VMEM)
    shapes = [(a.shape[0] // ctx_count, a.shape[1]) for a in extra]
    scratch = [
        pltpu.VMEM((length, rows), jnp.float32),
        pltpu.VMEM((length, groups * rows), low),
        pltpu.VMEM((length, groups * rows), low),
        pltpu.VMEM((rows, HEADS * HD), jnp.float32),
        pltpu.VMEM((ctx_count, rows, 2 * KV_HEADS * HD), low),
    ]
    scratch += halving_scratch(ctx_count, rows, 2 * KV_HEADS * HD)
    for shape in shapes:
        parts = halving_scratch(ctx_count, *shape)
        scratch += [pltpu.VMEM((pairs,) + shape, low)] + parts[:2]
        scratch += [pltpu.SemaphoreType.DMA((pairs,))] + parts[2:]
    outs = pl.pallas_call(
        functools.partial(attention_backward_kernel, ctx_count, shapes),
        out_shape=[
            jax.ShapeDtypeStruct(raw.shape, low),
            jax.ShapeDtypeStruct((8, HD), jnp.float32),
        ]
        + [jax.ShapeDtypeStruct(s, low) for s in shapes],
        in_specs=[vmem] * 11 + [pl.BlockSpec(memory_space=pl.ANY)] * len(extra),
        out_specs=[vmem] * (2 + len(extra)),
        scratch_shapes=scratch,
        compiler_params=pltpu.CompilerParams(
            collective_id=3, has_side_effects=True, vmem_limit_bytes=60 << 20
        ),
        cost_estimate=pl.CostEstimate(
            flops=10 * HEADS * HD * rows * length,
            bytes_accessed=64 << 20,
            transcendentals=HEADS * rows * length,
        ),
        name="attention_backward",
    )(
        grads,
        query_low,
        kv,
        log_totals,
        raw,
        cosine,
        sine_part,
        query_gain[None],
        key_gain[None],
        row_ids[None],
        key_ids[:, None],
        *extra,
    )
    return outs[0], outs[1][0], outs[1][1], outs[2:]


def owner_sum_kernel(ctx_count, fsdp_count, shapes, shared, *refs):
    many = len(shapes)
    whole = many - shared
    ins, outs = refs[:many], refs[many : 2 * many]
    rest = refs[2 * many :]
    parts = [rest[8 * i : 8 * i + 8] for i in range(many)]
    shares = rest[8 * many : 8 * many + shared]
    send_z, recv_z = rest[8 * many + shared :]
    position = ctx_position(ctx_count)
    bits, place, along, mine, partners, _ = position
    pairs = ctx_count // 2
    across_line = [(place, lax.rem(along + d, fsdp_count)) for d in range(1, fsdp_count)]
    partner_barrier(partners + across_line)
    sums, own_copies = [], []
    for i, (block, _) in enumerate(shapes):
        held, first_in, later_in, own_sem = parts[i][:4]

        def give(b, i=i, block=block):
            at = pl.multiple_of((2 * b + 1 - mine[0]) * block, 16)
            return ins[i].at[pl.ds(at, block)]

        sums.append(
            Halving(
                position,
                block,
                give,
                lambda b, held=held: held.at[b],
                first_in,
                later_in,
                parts[i][4:8],
            )
        )
        sums[i].start_first()
        copies = []
        for b in range(pairs):
            at = pl.multiple_of((2 * b + mine[0]) * block, 16)
            copies.append(
                pltpu.make_async_copy(ins[i].at[pl.ds(at, block)], held.at[b], own_sem.at[b])
            )
            copies[-1].start()
        own_copies.append(copies)
    order = list(range(whole, many)) + list(range(whole))
    for i in order:
        for b in range(pairs):
            own_copies[i][b].wait()
            sums[i].end_first(b)
        sums[i].start(0)
    for stage in range(1, bits - 1):
        for i in order:
            sums[i].end(stage - 1)
            sums[i].start(stage)

    def share_copies(i):
        size = shapes[i][0] // fsdp_count
        return [
            pltpu.make_async_remote_copy(
                src_ref=sums[i].mine_now().at[pl.ds(pl.multiple_of(peer[1] * size, 16), size)],
                dst_ref=shares[i - whole].at[d],
                send_sem=send_z.at[i - whole, d],
                recv_sem=recv_z.at[i - whole, d],
                device_id=peer,
                device_id_type=MESH,
            )
            for d, peer in enumerate(across_line)
        ]

    for i in range(whole, many):
        sums[i].end(bits - 2)
        for copy in share_copies(i):
            copy.start()
    for i in range(whole):
        sums[i].end(bits - 2)
        outs[i][...] = sums[i].mine_now()[...]
    for i in range(whole, many):
        for copy in share_copies(i):
            copy.wait()
        size = shapes[i][0] // fsdp_count
        own = sums[i].mine_now()[pl.ds(pl.multiple_of(along * size, 16), size)]
        total = own.astype(jnp.float32)
        for d in range(fsdp_count - 1):
            total = total + shares[i - whole][d].astype(jnp.float32)
        outs[i][...] = total.astype(outs[i].dtype)


def owner_sums(arrays, shared):
    ctx_count = lax.axis_size("ctx")
    fsdp_count = lax.axis_size("fsdp")
    pairs = ctx_count // 2
    many = len(arrays)
    whole = many - shared
    low = jnp.bfloat16
    shapes = [(a.shape[0] // ctx_count, a.shape[1]) for a in arrays]
    share_shapes = [(s[0] // fsdp_count, s[1]) for s in shapes[whole:]]
    scratch = []
    for shape in shapes:
        parts = halving_scratch(ctx_count, *shape)
        scratch += [pltpu.VMEM((pairs,) + shape, low)] + parts[:2]
        scratch += [pltpu.SemaphoreType.DMA((pairs,))] + parts[2:]
    scratch += [pltpu.VMEM((fsdp_count - 1,) + s, low) for s in share_shapes]
    scratch += [pltpu.SemaphoreType.DMA((shared, fsdp_count - 1))] * 2
    total = sum(a.size for a in arrays)
    return pl.pallas_call(
        functools.partial(owner_sum_kernel, ctx_count, fsdp_count, shapes, shared),
        out_shape=[jax.ShapeDtypeStruct(s, low) for s in shapes[:whole] + share_shapes],
        in_specs=[pl.BlockSpec(memory_space=pl.ANY)] * many,
        out_specs=[pl.BlockSpec(memory_space=pltpu.VMEM)] * many,
        scratch_shapes=scratch,
        compiler_params=pltpu.CompilerParams(
            collective_id=0, has_side_effects=True, vmem_limit_bytes=48 << 20
        ),
        cost_estimate=pl.CostEstimate(flops=total, bytes_accessed=4 * total, transcendentals=0),
        name="owner_sums",
    )(*arrays)


def body(
    tokens,
    per_layer,
    out_grad,
    segment_ids,
    query_weight,
    key_weight,
    value_weight,
    out_weight,
    left_weight,
    right_weight,
    gate_weight,
    up_weight,
    down_weight,
    side_gate,
    side_out,
    input_gain,
    laurel_gain,
    attn_gain,
    pre_gain,
    post_gain,
    side_gain,
    query_gain,
    key_gain,
):
    low = jnp.bfloat16
    inputs = tokens[0].astype(jnp.float32)
    extra_rows = per_layer[0].astype(jnp.float32)
    cotangent = out_grad[0].astype(jnp.float32)
    sequence_ids = segment_ids[0]
    rows_here, width = inputs.shape
    ctx_count = lax.axis_size("ctx")
    fsdp_count = lax.axis_size("fsdp")
    count = ctx_count * fsdp_count
    ctx_place = lax.axis_index("ctx")
    rank = left_weight.shape[1]
    side = side_gate.shape[1]
    query_width = HEADS * HD
    kv_width = KV_HEADS * HD
    query_pos = ctx_place * rows_here + jnp.arange(rows_here, dtype=jnp.int32)

    piece = width // count

    qkv_width = query_width + 2 * kv_width
    full_qkv, full_second, full_left, full_right, full_side_out = weight_gather(
        [[query_weight, key_weight, value_weight], [out_weight, side_gate]],
        [left_weight, right_weight, side_out],
    )
    full_out = full_second[:, :width]
    full_side_gate = full_second[:, width:]
    full_left = full_left.reshape(width, rank)
    full_right = full_right.transpose(1, 0, 2).reshape(rank, width)
    full_side_out = full_side_out.reshape(side, width)

    normed, input_pull = jax.vjp(rms_norm, inputs, input_gain)
    normed_low = normed.astype(low)
    qkv_raw = forward_product(normed_low, full_qkv)
    left_low = forward_product(normed_low, full_left).astype(low)
    right_out = forward_product(left_low, full_right)

    frequency = jnp.exp(
        jnp.arange(HD // 2).astype(jnp.float32) * (-2.0 * math.log(rope_theta) / HD)
    )
    angles = query_pos.astype(jnp.float32)[:, None] * frequency[None, :]
    cosine, sine_part = jnp.cos(angles), jnp.sin(angles)
    query_ids = lax.dynamic_slice_in_dim(sequence_ids, ctx_place * rows_here, rows_here)
    kv_all, query_low, attended_low, log_totals = attention_forward(
        qkv_raw, cosine, sine_part, query_gain, key_gain, query_ids, sequence_ids
    )
    attn_raw = forward_product(attended_low, full_out)

    def mix_piece(x, normed_in, attn_in, right_in, gain_one, gain_two, gain_three):
        mixed = (
            x + rms_norm(attn_in, gain_one) + normed_in + rms_norm(right_in, gain_two)
        ) * inverse_root
        return (mixed, rms_norm(mixed, gain_three))

    (mixed, ffn_in), mix_pull = jax.vjp(
        mix_piece, inputs, normed, attn_raw, right_out, attn_gain, laurel_gain, pre_gain
    )

    ffn_all = gather(ffn_in.astype(low), "fsdp")
    gate_raw = forward_product(ffn_all, gate_weight)
    up_raw = forward_product(ffn_all, up_weight)
    hidden, hidden_pull = jax.vjp(hidden_piece, gate_raw, up_raw)
    hidden_low = hidden.astype(low)
    ffn_out = scatter_sum(forward_product(hidden_low, down_weight).astype(low), "fsdp")
    ffn_out = ffn_out.astype(jnp.float32)
    middle, middle_pull = jax.vjp(middle_piece, mixed, ffn_out, post_gain)
    middle_low = middle.astype(low)
    layer_gate = forward_product(middle_low, full_side_gate)
    layer_act, extra_pull = jax.vjp(hidden_piece, layer_gate, extra_rows)
    layer_low = layer_act.astype(low)
    layer_out = forward_product(layer_low, full_side_out)
    result, out_pull = jax.vjp(middle_piece, middle, layer_out, side_gain)

    middle_grad_one, layer_out_grad, side_gain_grad = out_pull(cotangent)
    layer_grad_low = layer_out_grad.astype(low)
    side_out_grad = over_rows(layer_low, layer_grad_low)
    layer_gate_grad, extra_grad = extra_pull(across(layer_grad_low, full_side_out))
    gate_grad_low = layer_gate_grad.astype(low)
    side_gate_grad = over_rows(gate_grad_low, middle_low)
    mixed_grad_one, ffn_out_grad, post_gain_grad = middle_pull(
        middle_grad_one + across(gate_grad_low, full_side_gate)
    )
    ffn_grad_all = gather(ffn_out_grad.astype(low), "fsdp")
    down_weight_grad = over_rows(ffn_grad_all, hidden_low)
    gate_raw_grad, up_raw_grad = hidden_pull(across(ffn_grad_all, down_weight))
    gate_back_low = gate_raw_grad.astype(low)
    up_back_low = up_raw_grad.astype(low)
    ffn_in_grad = scatter_sum(
        (across(gate_back_low, gate_weight) + across(up_back_low, up_weight)).astype(low), "fsdp"
    )
    gate_weight_grad = over_rows(ffn_all, gate_back_low)
    up_weight_grad = over_rows(ffn_all, up_back_low)
    ffn_in_grad, ffn_weight_grads, late_low = lax.optimization_barrier(
        (
            ffn_in_grad,
            [g.astype(low) for g in (down_weight_grad, gate_weight_grad, up_weight_grad)],
            (attended_low, normed_low),
        )
    )
    down_weight_grad, gate_weight_grad, up_weight_grad = ffn_weight_grads
    attended_all, normed_all = (gather(part, "fsdp") for part in late_low)
    (
        inputs_grad_one,
        normed_grad_one,
        attn_raw_grad,
        right_out_grad,
        attn_gain_grad,
        laurel_gain_grad,
        pre_gain_grad,
    ) = mix_pull((mixed_grad_one, ffn_in_grad.astype(jnp.float32)))
    attn_grad_low = attn_raw_grad.astype(low)
    attended_grad_low = across(attn_grad_low, full_out).astype(low)
    right_grad_low = right_out_grad.astype(low)
    right_weight_grad = over_rows(right_grad_low, left_low)
    left_grad_low = across(right_grad_low, full_right).astype(low)
    left_weight_grad = over_rows(normed_low, left_grad_low)
    qkv_back_low, query_gain_grad, key_gain_grad, ffn_sums = attention_backward(
        attended_grad_low,
        query_low,
        kv_all,
        log_totals,
        qkv_raw,
        cosine,
        sine_part,
        query_gain,
        key_gain,
        query_ids,
        sequence_ids,
        [g.astype(low) for g in (gate_weight_grad, up_weight_grad)],
    )
    down_low, qkv_back_low = lax.optimization_barrier((down_weight_grad.astype(low), qkv_back_low))
    down_weight_grad = scatter_sum(down_low, "ctx")
    normed_grad_two = across(qkv_back_low, full_qkv) + across(left_grad_low, full_left)
    inputs_grad_two, input_gain_grad = input_pull(normed_grad_one + normed_grad_two)
    block_out = result.astype(low)[None]
    tokens_grad = (inputs_grad_one + inputs_grad_two).astype(low)[None]
    per_layer_grad = extra_grad.astype(low)[None]

    def columns_to_owner(x):
        parts = x.reshape(rows_here, fsdp_count, -1).transpose(1, 0, 2)
        return lax.all_to_all(parts, "fsdp", 0, 0, tiled=True).reshape(fsdp_count * rows_here, -1)

    out_columns = columns_to_owner(attn_grad_low)
    out_weight_grad = over_rows(attended_all, out_columns)
    qkv_parts = jnp.concatenate(
        [
            part.reshape(rows_here, fsdp_count, -1)
            for part in (
                qkv_back_low[:, :query_width],
                qkv_back_low[:, query_width : query_width + kv_width],
                qkv_back_low[:, query_width + kv_width :],
            )
        ],
        axis=2,
    )
    qkv_columns = columns_to_owner(qkv_parts.reshape(rows_here, -1))
    qkv_weight_grad = over_rows(normed_all, qkv_columns)

    small_gains = [
        jnp.pad(g.reshape(count, -1), ((0, 0), (0, piece - g.shape[0] // count))).reshape(-1)
        for g in (query_gain_grad, key_gain_grad)
    ]
    gains = jnp.stack(
        [
            input_gain_grad,
            laurel_gain_grad,
            attn_gain_grad,
            pre_gain_grad,
            post_gain_grad,
            side_gain_grad,
            *small_gains,
        ]
    )
    gate_blocks = side_gate_grad.astype(low).reshape(side, ctx_count, -1).transpose(1, 0, 2)
    gate_columns = width // ctx_count
    tall = jnp.concatenate(
        [
            left_weight_grad.astype(low),
            right_weight_grad.astype(low),
            jnp.pad(gains.astype(low).T, ((0, 0), (0, 128 - gains.shape[0]))),
        ],
        axis=1,
    )
    out_blocks = side_out_grad.astype(low).reshape(
        ctx_count, side // ctx_count, fsdp_count, width // fsdp_count
    )
    out_blocks = out_blocks.transpose(0, 2, 1, 3).reshape(-1, width // fsdp_count)
    out_weight_grad, qkv_weight_grad, tall, gate_blocks, side_out_grad = owner_sums(
        [
            out_weight_grad.astype(low),
            qkv_weight_grad.astype(low),
            tall,
            gate_blocks.reshape(-1, gate_columns),
            out_blocks,
        ],
        3,
    )
    gate_weight_grad, up_weight_grad = ffn_sums
    down_weight_grad = down_weight_grad.T
    query_part = query_width // fsdp_count
    kv_part = kv_width // fsdp_count
    query_weight_grad = qkv_weight_grad[:, :query_part]
    key_weight_grad = qkv_weight_grad[:, query_part : query_part + kv_part]
    value_weight_grad = qkv_weight_grad[:, query_part + kv_part :]
    wide = jnp.float32
    tall = tall.astype(wide)
    left_weight_grad = tall[:, :rank]
    right_weight_grad = tall[:, rank : 2 * rank].T
    gains = tall[:, 2 * rank : 2 * rank + 8].T
    small_part = query_gain.shape[0] // count
    side_gate_grad = gate_blocks.astype(wide).T
    side_out_grad = side_out_grad.astype(wide)
    return (
        block_out,
        tokens_grad,
        per_layer_grad,
        query_weight_grad.astype(wide),
        key_weight_grad.astype(wide),
        value_weight_grad.astype(wide),
        out_weight_grad.astype(wide),
        left_weight_grad,
        right_weight_grad,
        gate_weight_grad.astype(wide),
        up_weight_grad.astype(wide),
        down_weight_grad.astype(wide),
        side_gate_grad,
        side_out_grad,
        *(gains[n] for n in range(6)),
        gains[6, :small_part],
        gains[7, :small_part],
    )


def solution(mesh):
    placed = (
        P("fsdp", "ctx", None),
        P("fsdp", "ctx", None),
        P("fsdp", "ctx", None),
        P("fsdp", None),
        P("fsdp", None),
        P("fsdp", None),
        P("fsdp", None),
        P("fsdp", None),
        P("fsdp", None),
        P(None, "fsdp"),
        P(None, "fsdp"),
        P(None, "fsdp"),
        P("fsdp", None),
        P("fsdp", None),
        P("fsdp", None),
        P(),
        P(),
        P(),
        P(),
        P(),
        P(),
        P(),
        P(),
    )
    return jax.shard_map(
        body,
        mesh=mesh,
        in_specs=placed,
        out_specs=(
            P("fsdp", "ctx", None),
            P("fsdp", "ctx", None),
            P("fsdp", "ctx", None),
            P("ctx", "fsdp"),
            P("ctx", "fsdp"),
            P("ctx", "fsdp"),
            P("ctx", "fsdp"),
            P(("ctx", "fsdp"), None),
            P(None, ("ctx", "fsdp")),
            P("ctx", "fsdp"),
            P("ctx", "fsdp"),
            P("fsdp", "ctx"),
            P("ctx", "fsdp"),
            P("ctx", "fsdp"),
            P(("ctx", "fsdp")),
            P(("ctx", "fsdp")),
            P(("ctx", "fsdp")),
            P(("ctx", "fsdp")),
            P(("ctx", "fsdp")),
            P(("ctx", "fsdp")),
            P(("ctx", "fsdp")),
            P(("ctx", "fsdp")),
        ),
        check_vma=False,
    )
```

```python
import functools
import math

import jax
import jax.numpy as jnp
from jax import lax
from jax.experimental import pallas as pl
from jax.experimental.pallas import tpu as pltpu
from jax.sharding import PartitionSpec as P

HEADS = 8
KV_HEADS = 2
HD = 256
MESH = pl.DeviceIdType.MESH
FF_TILE = 512
BACK_TILE = 512
GRAD_TILE = 256


epsilon = 1e-06
rope_theta = 1000000.0
masked_score = -1e30
inverse_root = 1.0 / math.sqrt(2.0)


def rms_norm(v, factor):
    return v * lax.rsqrt(jnp.mean(v * v, axis=-1, keepdims=True) + epsilon) * factor


def forward_product(a, b):
    return jnp.dot(a, b, preferred_element_type=jnp.float32)


def across(a, b):
    return lax.dot_general(a, b, (((1,), (1,)), ((), ())), preferred_element_type=jnp.float32)


def over_rows(a, b):
    return lax.dot_general(a, b, (((0,), (0,)), ((), ())), preferred_element_type=jnp.float32)


def hidden_piece(gate_in, up_in):
    return jax.nn.gelu(gate_in, approximate=True) * up_in


def middle_piece(mixed_in, ffn_in_rows, factor):
    return mixed_in + rms_norm(ffn_in_rows, factor)


def gather(x, axis):
    return lax.all_gather(x, axis, axis=0, tiled=True)


def scatter_sum(x, axis):
    return lax.psum_scatter(x, axis, scatter_dimension=0, tiled=True)


def partner_barrier(partners):
    barrier = pltpu.get_barrier_semaphore()
    for partner in partners:
        pl.semaphore_signal(barrier, inc=1, device_id=partner, device_id_type=MESH)
    pl.semaphore_wait(barrier, len(partners))


def add_rows(target, source, first, rows):
    tile = 16

    def one(step, carry):
        at = pl.ds(pl.multiple_of(first + step * tile, tile), tile)
        from_at = pl.ds(pl.multiple_of(step * tile, tile), tile)
        total = target[at].astype(jnp.float32) + source[from_at].astype(jnp.float32)
        target[at] = total.astype(target.dtype)
        return carry

    lax.fori_loop(0, rows // tile, one, 0)


def held_index(mine, done, bits):
    return tuple(slice(None) if t in done else mine[t] for t in reversed(range(bits)))


def ctx_position(ctx_count):
    bits = ctx_count.bit_length() - 1
    place = lax.axis_index("ctx")
    along = lax.axis_index("fsdp")
    mine = [lax.rem(place // (1 << t), 2) for t in range(bits)]
    partners = [(place + (1 - 2 * mine[t]) * (1 << t), along) for t in range(bits)]
    orders = [list(range(1, bits)), list(range(bits - 1, 0, -1))]
    return bits, place, along, mine, partners, orders


def spread_copy(out, lead, half, stage, position, send_sem, recv_sem):
    bits, _, _, mine, partners, orders = position
    order = orders[half]
    rows = out.shape[-2] // 2
    at = lead + held_index(mine, order[:stage], bits) + (pl.ds(half * rows, rows),)
    return pltpu.make_async_remote_copy(
        src_ref=out.at[at],
        dst_ref=out.at[at],
        send_sem=send_sem.at[half, stage],
        recv_sem=recv_sem.at[half, stage],
        device_id=partners[order[stage]],
        device_id_type=MESH,
    )


def sibling_copy(out, lead, position, send_sem, recv_sem):
    bits, _, _, mine, partners, orders = position
    at = lead + held_index(mine, orders[0], bits)
    return pltpu.make_async_remote_copy(
        src_ref=out.at[at],
        dst_ref=out.at[at],
        send_sem=send_sem,
        recv_sem=recv_sem,
        device_id=partners[0],
        device_id_type=MESH,
    )


def weight_gather_kernel(ctx_count, fsdp_count, members, lines, *refs):
    sets = len(members)
    own_count = sum(members)
    own, line_own = refs[:own_count], refs[own_count : own_count + lines]
    rest = refs[own_count + lines :]
    outs, line_outs = rest[:sets], rest[sets : sets + lines]
    rest = rest[sets + lines :]
    passing, pieces = rest[: own_count + lines], rest[own_count + lines : own_count + lines + sets]
    own_sem, line_send, line_recv, send_sem, recv_sem, core_send, core_recv = rest[
        own_count + lines + sets :
    ]
    position = ctx_position(ctx_count)
    bits, place, along, mine, partners, _ = position
    steps = fsdp_count - 1
    here = held_index(mine, (), bits)
    columns = []
    for i in range(sets):
        start = 0
        for _ in range(members[i]):
            wide = own[len(columns)].shape[-1]
            columns.append((i, pl.ds(start, wide)))
            start += wide
    piece_loads = [
        pltpu.make_async_copy(own[n].at[here], pieces[i].at[:, at], own_sem.at[0, n])
        for n, (i, at) in enumerate(columns)
    ]
    for load in piece_loads:
        load.start()
    loads = [
        pltpu.make_async_copy(source, passing[n], own_sem.at[1, n])
        for n, source in enumerate(own + line_own)
    ]
    for load in loads:
        load.start()
    partner_barrier(
        partners
        + [(place, lax.rem(along + 1, fsdp_count)), (place, lax.rem(along + steps, fsdp_count))]
    )

    def line_copy(i, way, step, origin):
        toward = along + 1 if way == 0 else along - 1
        if i < sets:
            first, target = pieces[i], outs[i].at[(origin,) + here]
        else:
            first, target = line_own[i - sets], line_outs[i - sets].at[origin]
        return pltpu.make_async_remote_copy(
            src_ref=first if step == 1 else target,
            dst_ref=target,
            send_sem=line_send.at[i, way, step - 1],
            recv_sem=line_recv.at[i, way, step - 1],
            device_id=(place, toward),
            device_id_type=MESH,
        )

    def comes(way, step):
        return along >= step if way == 0 else along + step < fsdp_count

    def goes(way, step):
        if way == 0:
            return (along + 1 < fsdp_count) & (along >= step - 1)
        return (along >= 1) & (along + step - 1 < fsdp_count)

    def origin_of(way, step):
        return along - step if way == 0 else along + step

    def each(flag, action):
        pl.when(flag)(action)

    def forward(i, step):
        for way in range(2):
            each(goes(way, step), lambda: line_copy(i, way, step, origin_of(way, step - 1)).start())

    for load in piece_loads:
        load.wait()
    for i in range(sets):
        forward(i, 1)
    stores = []
    for n, load in enumerate(loads):
        load.wait()
        if n < own_count:
            i, at = columns[n]
            target = outs[i].at[(along,) + (slice(None),) * (bits + 1) + (at,)]
        else:
            target = line_outs[n - own_count].at[along]
        stores.append(pltpu.make_async_copy(passing[n], target, own_sem.at[2, n]))
        stores[-1].start()

    def stage_copies(i, way, step, stage):
        lead = (origin_of(way, step),)
        at = (i, way, step - 1)
        return [
            spread_copy(outs[i], lead, half, stage, position, send_sem.at[at], recv_sem.at[at])
            for half in range(2)
        ]

    def core_copy(i, way, step):
        at = (i, way, step - 1)
        return sibling_copy(
            outs[i], (origin_of(way, step),), position, core_send.at[at], core_recv.at[at]
        )

    def arrive(i, step):
        for way in range(2):

            def landed():
                line_copy(i, way, step, origin_of(way, step)).wait_recv()

            each(comes(way, step), landed)
        if step < steps:
            forward(i, step + 1)
        if i >= sets:
            return
        for way in range(2):

            def begin():
                for copy in stage_copies(i, way, step, 0):
                    copy.start()

            each(comes(way, step), begin)

    def advance(i, step, stage):
        if i >= sets:
            return
        for way in range(2):

            def proceed():
                for copy in stage_copies(i, way, step, stage):
                    copy.wait_recv()
                if stage < bits - 2:
                    for copy in stage_copies(i, way, step, stage + 1):
                        copy.start()
                else:
                    core_copy(i, way, step).start()

            each(comes(way, step), proceed)

    order = [(i, step) for i in range(sets + lines) for step in range(1, steps + 1)]
    for tick in range(len(order) + bits - 1):
        if tick < len(order):
            if order[tick] == (sets - 1, 1):
                for i in range(sets, sets + lines):
                    forward(i, 1)
            arrive(*order[tick])
        for stage in range(bits - 1):
            at = tick - 1 - stage
            if 0 <= at < len(order):
                advance(*order[at], stage)
    for copy in stores:
        copy.wait()
    for i, step in order:
        for way in range(2):

            def leave():
                line_copy(i, way, step, origin_of(way, step - 1)).wait_send()

            def finish():
                for stage in range(bits - 1):
                    for copy in stage_copies(i, way, step, stage):
                        copy.wait_send()
                core_copy(i, way, step).wait()

            each(goes(way, step), leave)
            if i < sets:
                each(comes(way, step), finish)


def weight_gather(own, lines):
    ctx_count = lax.axis_size("ctx")
    fsdp_count = lax.axis_size("fsdp")
    bits = ctx_count.bit_length() - 1
    steps = fsdp_count - 1
    sets = len(own)
    cut = (2,) * bits
    low = jnp.bfloat16
    flat = [w.reshape(cut + (w.shape[0] // ctx_count, w.shape[1])) for group in own for w in group]
    pieces = [(g[0].shape[0] // ctx_count, sum(w.shape[1] for w in g)) for g in own]
    out_shapes = [(fsdp_count,) + cut + p for p in pieces]
    out_shapes += [(fsdp_count,) + w.shape for w in lines]
    total = sum(rows * columns for rows, columns in pieces) * ctx_count * fsdp_count
    outs = pl.pallas_call(
        functools.partial(
            weight_gather_kernel, ctx_count, fsdp_count, [len(g) for g in own], len(lines)
        ),
        out_shape=[jax.ShapeDtypeStruct(s, low) for s in out_shapes],
        in_specs=[pl.BlockSpec(memory_space=pltpu.HBM)] * (len(flat) + len(lines)),
        out_specs=[pl.BlockSpec(memory_space=pltpu.HBM)] * len(out_shapes),
        scratch_shapes=[pltpu.VMEM(w.shape, low) for w in flat + list(lines)]
        + [pltpu.VMEM(p, low) for p in pieces]
        + [
            pltpu.SemaphoreType.DMA((3, len(flat) + len(lines))),
            pltpu.SemaphoreType.DMA((sets + len(lines), 2, steps)),
            pltpu.SemaphoreType.DMA((sets + len(lines), 2, steps)),
            pltpu.SemaphoreType.DMA((sets, 2, steps, 2, bits - 1)),
            pltpu.SemaphoreType.DMA((sets, 2, steps, 2, bits - 1)),
            pltpu.SemaphoreType.DMA((sets, 2, steps)),
            pltpu.SemaphoreType.DMA((sets, 2, steps)),
        ],
        compiler_params=pltpu.CompilerParams(
            collective_id=1, has_side_effects=True, vmem_limit_bytes=60 << 20
        ),
        cost_estimate=pl.CostEstimate(flops=0, bytes_accessed=4 * total, transcendentals=0),
        name="weight_gather",
    )(*flat, *lines)
    return [o.reshape(-1, o.shape[-1]) for o in outs[:sets]] + list(outs[sets:])


class Halving:
    def __init__(self, position, rows, give, held, first_in, later_in, sems):
        self.bits, self.place, self.along, self.mine, self.partners, self.orders = position
        self.rows, self.give, self.held = rows, give, held
        self.first_in, self.later_in = first_in, later_in
        self.send_zero, self.recv_zero, self.send_sem, self.recv_sem = sems
        self.pairs = 1 << (self.bits - 1)

    def first_copy(self, b):
        return pltpu.make_async_remote_copy(
            src_ref=self.give(b),
            dst_ref=self.first_in.at[b],
            send_sem=self.send_zero.at[b],
            recv_sem=self.recv_zero.at[b],
            device_id=self.partners[0],
            device_id_type=MESH,
        )

    def start_first(self):
        for b in range(self.pairs):
            self.first_copy(b).start()

    def end_first(self, b):
        self.first_copy(b).wait()
        add_rows(self.held(b), self.first_in.at[b], 0, self.rows)

    def slot_of(self, stage):
        return sum(1 << (self.bits - 2 - s) for s in range(stage))

    def block_sets(self, half, stage):
        order = self.orders[half]
        bit = order[stage]
        free = order[stage + 1 :]
        fixed = sum(self.mine[t] * (1 << (t - 1)) for t in order[:stage])
        sent, kept = [], []
        for combo in range(1 << len(free)):
            value = sum(((combo >> n) & 1) << (t - 1) for n, t in enumerate(free))
            sent.append(fixed + (1 - self.mine[bit]) * (1 << (bit - 1)) + value)
            kept.append(fixed + self.mine[bit] * (1 << (bit - 1)) + value)
        return bit, sent, kept

    def stage_copies(self, stage):
        rows = self.rows // 2
        copies = []
        for half in range(2):
            bit, sent, _ = self.block_sets(half, stage)
            for n, block in enumerate(sent):
                at = (half, self.slot_of(stage) + n)
                copies.append(
                    pltpu.make_async_remote_copy(
                        src_ref=self.held(block).at[pl.ds(half * rows, rows)],
                        dst_ref=self.later_in.at[at],
                        send_sem=self.send_sem.at[at],
                        recv_sem=self.recv_sem.at[at],
                        device_id=self.partners[bit],
                        device_id_type=MESH,
                    )
                )
        return copies

    def start(self, stage):
        for copy in self.stage_copies(stage):
            copy.start()

    def end(self, stage):
        for copy in self.stage_copies(stage):
            copy.wait()
        rows = self.rows // 2
        for half in range(2):
            _, _, kept = self.block_sets(half, stage)
            for n, block in enumerate(kept):
                at = (half, self.slot_of(stage) + n)
                add_rows(self.held(block), self.later_in.at[at], half * rows, rows)

    def mine_now(self):
        return self.held(self.place // 2)


def halving_scratch(ctx_count, rows, columns):
    pairs = ctx_count // 2
    return [
        pltpu.VMEM((pairs, rows, columns), jnp.bfloat16),
        pltpu.VMEM((2, pairs - 1, rows // 2, columns), jnp.bfloat16),
        pltpu.SemaphoreType.DMA((pairs,)),
        pltpu.SemaphoreType.DMA((pairs,)),
        pltpu.SemaphoreType.DMA((2, pairs - 1)),
        pltpu.SemaphoreType.DMA((2, pairs - 1)),
    ]


def unit_rows(v):
    scale = lax.rsqrt(jnp.mean(v * v, axis=-1, keepdims=True) + epsilon)
    return v * scale, scale


def turned(v, cosine, sine_part):
    halfway = v.shape[-1] // 2
    leading, trailing = v[:, :halfway], v[:, halfway:]
    return jnp.concatenate(
        [leading * cosine - trailing * sine_part, trailing * cosine + leading * sine_part], axis=-1
    )


def unit_rows_pull(v, grad, gain):
    unit, scale = unit_rows(v)
    gain_grad = jnp.sum(grad * unit, axis=0, keepdims=True)
    scaled = grad * gain
    return scale * (scaled - unit * jnp.mean(unit * scaled, axis=-1, keepdims=True)), gain_grad


def head_at(h):
    return pl.ds(pl.multiple_of(h * HD, HD), HD)


def attention_forward_kernel(
    ctx_count,
    raw,
    cosine_ref,
    sine_ref,
    query_gain,
    key_gain,
    row_ids,
    key_ids,
    kv,
    query_low,
    attended_low,
    log_totals,
    bias,
    send_sem,
    recv_sem,
    core_send,
    core_recv,
):
    position = ctx_position(ctx_count)
    bits, place, _, mine, partners, _ = position
    rows = raw.shape[0]
    groups = HEADS // KV_HEADS
    length = ctx_count * rows
    here = held_index(mine, (), bits)
    cosine, sine_part = cosine_ref[...], sine_ref[...]
    for k in range(KV_HEADS):
        unit, _ = unit_rows(raw[:, pl.ds((HEADS + k) * HD, HD)])
        key = turned(unit * key_gain[...], cosine, sine_part)
        kv[here + (slice(None), pl.ds(k * HD, HD))] = key.astype(kv.dtype)
        value, _ = unit_rows(raw[:, pl.ds((HEADS + KV_HEADS + k) * HD, HD)])
        kv[here + (slice(None), pl.ds((KV_HEADS + k) * HD, HD))] = value.astype(kv.dtype)
    partner_barrier(partners)

    def copies_of(stage):
        return [spread_copy(kv, (), h, stage, position, send_sem, recv_sem) for h in range(2)]

    for copy in copies_of(0):
        copy.start()
    allowed = (row_ids[...] == key_ids[...]) & (
        lax.broadcasted_iota(jnp.int32, (rows, length), 1)
        <= lax.broadcasted_iota(jnp.int32, (rows, length), 0) + place * rows
    )
    bias[...] = jnp.where(allowed, 0.0, masked_score)

    def one_query(h, carry):
        unit, _ = unit_rows(raw[:, head_at(h)])
        query = turned(unit * query_gain[...], cosine, sine_part)
        query_low[:, head_at(h)] = query.astype(query_low.dtype)
        return carry

    lax.fori_loop(0, HEADS, one_query, 0)
    for stage in range(1, bits - 1):
        for copy in copies_of(stage - 1):
            copy.wait()
        for copy in copies_of(stage):
            copy.start()
    for copy in copies_of(bits - 2):
        copy.wait()
    last = sibling_copy(kv, (), position, core_send, core_recv)
    last.start()
    last.wait()
    everywhere = (slice(None),) * (bits + 1)
    for k in range(KV_HEADS):
        key = kv[everywhere + (pl.ds(k * HD, HD),)].reshape(length, HD)
        value = kv[everywhere + (pl.ds((KV_HEADS + k) * HD, HD),)].reshape(length, HD)

        def one_head(g, carry, k=k, key=key, value=value):
            h = k * groups + g
            scores = across(query_low[:, head_at(h)], key) + bias[...]
            row_max = jnp.max(scores, axis=-1, keepdims=True)
            weights = jnp.exp(scores - row_max)
            row_total = jnp.sum(weights, axis=-1, keepdims=True)
            weights = (weights * (1.0 / row_total)).astype(value.dtype)
            attended_low[:, head_at(h)] = forward_product(weights, value).astype(attended_low.dtype)
            log_total = jnp.broadcast_to(row_max + jnp.log(row_total), (rows, rows))
            log_totals[h] = log_total.T[:8]
            return carry

        lax.fori_loop(0, groups, one_head, 0)


def attention_forward(raw, cosine, sine_part, query_gain, key_gain, row_ids, key_ids):
    ctx_count = lax.axis_size("ctx")
    bits = ctx_count.bit_length() - 1
    rows = raw.shape[0]
    length = ctx_count * rows
    low = jnp.bfloat16
    vmem = pl.BlockSpec(memory_space=pltpu.VMEM)
    return pl.pallas_call(
        functools.partial(attention_forward_kernel, ctx_count),
        out_shape=[
            jax.ShapeDtypeStruct((2,) * bits + (rows, 2 * KV_HEADS * HD), low),
            jax.ShapeDtypeStruct((rows, HEADS * HD), low),
            jax.ShapeDtypeStruct((rows, HEADS * HD), low),
            jax.ShapeDtypeStruct((HEADS, 8, rows), jnp.float32),
        ],
        in_specs=[vmem] * 7,
        out_specs=[vmem] * 4,
        scratch_shapes=[
            pltpu.VMEM((rows, length), jnp.float32),
            pltpu.SemaphoreType.DMA((2, bits - 1)),
            pltpu.SemaphoreType.DMA((2, bits - 1)),
            pltpu.SemaphoreType.DMA,
            pltpu.SemaphoreType.DMA,
        ],
        compiler_params=pltpu.CompilerParams(
            collective_id=2, has_side_effects=True, vmem_limit_bytes=40 << 20
        ),
        cost_estimate=pl.CostEstimate(
            flops=4 * HEADS * HD * rows * length,
            bytes_accessed=8 << 20,
            transcendentals=HEADS * rows * length,
        ),
        name="attention_forward",
    )(raw, cosine, sine_part, query_gain[None], key_gain[None], row_ids[:, None], key_ids[None])


def attention_backward_kernel(ctx_count, extra, *refs):
    (
        grads,
        query_low,
        kv,
        log_totals,
        raw,
        cosine_ref,
        sine_ref,
        query_gain,
        key_gain,
        row_ids,
        key_ids,
    ) = refs[:11]
    many = len(extra)
    extra_in = refs[11 : 11 + many]
    back, gain_grads = refs[11 + many : 13 + many]
    extra_out = refs[13 + many : 13 + 2 * many]
    rest = refs[13 + 2 * many :]
    bias, score_grads, weights_low, query_grads, kv_grads = rest[:5]
    kv_parts = rest[5:11]
    extra_parts = [rest[11 + 8 * i : 19 + 8 * i] for i in range(many)]
    position = ctx_position(ctx_count)
    bits, place, _, mine, partners, _ = position
    pairs = ctx_count // 2
    rows = raw.shape[0]
    groups = HEADS // KV_HEADS
    length = ctx_count * rows
    low = jnp.bfloat16

    kv_sum = Halving(
        position,
        rows,
        lambda b: kv_grads.at[2 * b + 1 - mine[0]],
        lambda b: kv_grads.at[2 * b + mine[0]],
        kv_parts[0],
        kv_parts[1],
        kv_parts[2:6],
    )
    sums, own_copies = [], []
    for i, (block, _) in enumerate(extra):
        held, first_in, later_in, own_sem = extra_parts[i][:4]

        def give(b, i=i, block=block):
            at = pl.multiple_of((2 * b + 1 - mine[0]) * block, 16)
            return extra_in[i].at[pl.ds(at, block)]

        sums.append(
            Halving(
                position,
                block,
                give,
                lambda b, held=held: held.at[b],
                first_in,
                later_in,
                extra_parts[i][4:8],
            )
        )
        copies = []
        for b in range(pairs):
            at = pl.multiple_of((2 * b + mine[0]) * block, 16)
            copies.append(
                pltpu.make_async_copy(
                    extra_in[i].at[pl.ds(at, block)], held.at[b], own_sem.at[b]
                )
            )
            copies[-1].start()
        own_copies.append(copies)

    partner_barrier(partners)
    for one in sums:
        one.start_first()

    def open_extra(i):
        for b in range(pairs):
            own_copies[i][b].wait()
            sums[i].end_first(b)
        sums[i].start(0)

    allowed = (key_ids[...] == row_ids[...]) & (
        lax.broadcasted_iota(jnp.int32, (length, rows), 0)
        <= lax.broadcasted_iota(jnp.int32, (length, rows), 1) + place * rows
    )
    bias[...] = jnp.where(allowed, 0.0, masked_score)
    everywhere = (slice(None),) * (bits + 1)
    for k in range(KV_HEADS):
        if k < many:
            open_extra(k)
        key = kv[everywhere + (pl.ds(k * HD, HD),)].reshape(length, HD)
        value = kv[everywhere + (pl.ds((KV_HEADS + k) * HD, HD),)].reshape(length, HD)

        def one_head(g, carry, k=k, key=key, value=value):
            h = k * groups + g
            columns = pl.ds(pl.multiple_of(g * rows, rows), rows)
            scores = across(key, query_low[:, head_at(h)]) + bias[...]
            weights = jnp.exp(scores - log_totals[h][:1])
            weight_grad = across(value, grads[:, head_at(h)])
            delta = jnp.sum(weights * weight_grad, axis=0, keepdims=True)
            score_grads[:, columns] = (weights * (weight_grad - delta)).astype(low)
            weights_low[:, columns] = weights.astype(low)
            return carry

        lax.fori_loop(0, groups, one_head, 0)
        heads = [pl.ds((k * groups + g) * HD, HD) for g in range(groups)]
        query_stack = jnp.concatenate([query_low[:, at] for at in heads], axis=0)
        grad_stack = jnp.concatenate([grads[:, at] for at in heads], axis=0)
        key_grad = forward_product(score_grads[...], query_stack).astype(low)
        value_grad = forward_product(weights_low[...], grad_stack).astype(low)
        kv_grads[:, :, pl.ds(k * HD, HD)] = key_grad.reshape(ctx_count, rows, HD)
        kv_grads[:, :, pl.ds((KV_HEADS + k) * HD, HD)] = value_grad.reshape(ctx_count, rows, HD)
        query_grad = over_rows(key, score_grads[...])
        for g, at in enumerate(heads):
            query_grads[:, at] = query_grad[:, g * rows : (g + 1) * rows].T

    kv_sum.start_first()
    for b in range(pairs):
        kv_sum.end_first(b)
    kv_sum.start(0)
    for i in range(KV_HEADS, many):
        open_extra(i)
    cosine, sine_part = cosine_ref[...], sine_ref[...]

    def one_query(h, gain_grad):
        grad = turned(query_grads[:, head_at(h)], cosine, -sine_part)
        pulled, more = unit_rows_pull(raw[:, head_at(h)], grad, query_gain[...])
        back[:, head_at(h)] = pulled.astype(low)
        return gain_grad + more

    gain_grads[0:1] = lax.fori_loop(0, HEADS, one_query, jnp.zeros((1, HD), jnp.float32))
    for stage in range(1, bits - 1):
        kv_sum.end(stage - 1)
        kv_sum.start(stage)
    kv_sum.end(bits - 2)
    summed = kv_sum.mine_now()
    key_gain_grad = jnp.zeros((1, HD), jnp.float32)
    for k in range(KV_HEADS):
        grad = summed[:, pl.ds(k * HD, HD)].astype(jnp.float32)
        grad = turned(grad, cosine, -sine_part)
        at = pl.ds((HEADS + k) * HD, HD)
        pulled, more = unit_rows_pull(raw[:, at], grad, key_gain[...])
        back[:, at] = pulled.astype(low)
        key_gain_grad = key_gain_grad + more
        grad = summed[:, pl.ds((KV_HEADS + k) * HD, HD)].astype(jnp.float32)
        at = pl.ds((HEADS + KV_HEADS + k) * HD, HD)
        pulled, _ = unit_rows_pull(raw[:, at], grad, 1.0)
        back[:, at] = pulled.astype(low)
    gain_grads[1:2] = key_gain_grad
    for stage in range(1, bits - 1):
        for one in sums:
            one.end(stage - 1)
            one.start(stage)
    for i in range(many):
        sums[i].end(bits - 2)
        extra_out[i][...] = sums[i].mine_now()[...]


def attention_backward(
    grads, query_low, kv, log_totals, raw, cosine, sine_part, query_gain, key_gain, row_ids, key_ids, extra
):
    ctx_count = lax.axis_size("ctx")
    rows = raw.shape[0]
    length = ctx_count * rows
    pairs = ctx_count // 2
    groups = HEADS // KV_HEADS
    low = jnp.bfloat16
    vmem = pl.BlockSpec(memory_space=pltpu.VMEM)
    shapes = [(a.shape[0] // ctx_count, a.shape[1]) for a in extra]
    scratch = [
        pltpu.VMEM((length, rows), jnp.float32),
        pltpu.VMEM((length, groups * rows), low),
        pltpu.VMEM((length, groups * rows), low),
        pltpu.VMEM((rows, HEADS * HD), jnp.float32),
        pltpu.VMEM((ctx_count, rows, 2 * KV_HEADS * HD), low),
    ]
    scratch += halving_scratch(ctx_count, rows, 2 * KV_HEADS * HD)
    for shape in shapes:
        parts = halving_scratch(ctx_count, *shape)
        scratch += [pltpu.VMEM((pairs,) + shape, low)] + parts[:2]
        scratch += [pltpu.SemaphoreType.DMA((pairs,))] + parts[2:]
    outs = pl.pallas_call(
        functools.partial(attention_backward_kernel, ctx_count, shapes),
        out_shape=[
            jax.ShapeDtypeStruct(raw.shape, low),
            jax.ShapeDtypeStruct((8, HD), jnp.float32),
        ]
        + [jax.ShapeDtypeStruct(s, low) for s in shapes],
        in_specs=[vmem] * 11 + [pl.BlockSpec(memory_space=pl.ANY)] * len(extra),
        out_specs=[vmem] * (2 + len(extra)),
        scratch_shapes=scratch,
        compiler_params=pltpu.CompilerParams(
            collective_id=3, has_side_effects=True, vmem_limit_bytes=60 << 20
        ),
        cost_estimate=pl.CostEstimate(
            flops=10 * HEADS * HD * rows * length,
            bytes_accessed=64 << 20,
            transcendentals=HEADS * rows * length,
        ),
        name="attention_backward",
    )(
        grads,
        query_low,
        kv,
        log_totals,
        raw,
        cosine,
        sine_part,
        query_gain[None],
        key_gain[None],
        row_ids[None],
        key_ids[:, None],
        *extra,
    )
    return outs[0], outs[1][0], outs[1][1], outs[2:]


def owner_sum_kernel(ctx_count, fsdp_count, shapes, shared, *refs):
    many = len(shapes)
    whole = many - shared
    ins, outs = refs[:many], refs[many : 2 * many]
    rest = refs[2 * many :]
    parts = [rest[8 * i : 8 * i + 8] for i in range(many)]
    shares = rest[8 * many : 8 * many + shared]
    send_z, recv_z = rest[8 * many + shared :]
    position = ctx_position(ctx_count)
    bits, place, along, mine, partners, _ = position
    pairs = ctx_count // 2
    across_line = [(place, lax.rem(along + d, fsdp_count)) for d in range(1, fsdp_count)]
    partner_barrier(partners + across_line)
    sums, own_copies = [], []
    for i, (block, _) in enumerate(shapes):
        held, first_in, later_in, own_sem = parts[i][:4]

        def give(b, i=i, block=block):
            at = pl.multiple_of((2 * b + 1 - mine[0]) * block, 16)
            return ins[i].at[pl.ds(at, block)]

        sums.append(
            Halving(
                position,
                block,
                give,
                lambda b, held=held: held.at[b],
                first_in,
                later_in,
                parts[i][4:8],
            )
        )
        sums[i].start_first()
        copies = []
        for b in range(pairs):
            at = pl.multiple_of((2 * b + mine[0]) * block, 16)
            copies.append(
                pltpu.make_async_copy(ins[i].at[pl.ds(at, block)], held.at[b], own_sem.at[b])
            )
            copies[-1].start()
        own_copies.append(copies)
    order = list(range(whole, many)) + list(range(whole))
    for i in order:
        for b in range(pairs):
            own_copies[i][b].wait()
            sums[i].end_first(b)
        sums[i].start(0)
    for stage in range(1, bits - 1):
        for i in order:
            sums[i].end(stage - 1)
            sums[i].start(stage)

    def share_copies(i):
        size = shapes[i][0] // fsdp_count
        return [
            pltpu.make_async_remote_copy(
                src_ref=sums[i].mine_now().at[pl.ds(pl.multiple_of(peer[1] * size, 16), size)],
                dst_ref=shares[i - whole].at[d],
                send_sem=send_z.at[i - whole, d],
                recv_sem=recv_z.at[i - whole, d],
                device_id=peer,
                device_id_type=MESH,
            )
            for d, peer in enumerate(across_line)
        ]

    for i in range(whole, many):
        sums[i].end(bits - 2)
        for copy in share_copies(i):
            copy.start()
    for i in range(whole):
        sums[i].end(bits - 2)
        outs[i][...] = sums[i].mine_now()[...]
    for i in range(whole, many):
        for copy in share_copies(i):
            copy.wait()
        size = shapes[i][0] // fsdp_count
        own = sums[i].mine_now()[pl.ds(pl.multiple_of(along * size, 16), size)]
        total = own.astype(jnp.float32)
        for d in range(fsdp_count - 1):
            total = total + shares[i - whole][d].astype(jnp.float32)
        outs[i][...] = total.astype(outs[i].dtype)


def owner_sums(arrays, shared):
    ctx_count = lax.axis_size("ctx")
    fsdp_count = lax.axis_size("fsdp")
    pairs = ctx_count // 2
    many = len(arrays)
    whole = many - shared
    low = jnp.bfloat16
    shapes = [(a.shape[0] // ctx_count, a.shape[1]) for a in arrays]
    share_shapes = [(s[0] // fsdp_count, s[1]) for s in shapes[whole:]]
    scratch = []
    for shape in shapes:
        parts = halving_scratch(ctx_count, *shape)
        scratch += [pltpu.VMEM((pairs,) + shape, low)] + parts[:2]
        scratch += [pltpu.SemaphoreType.DMA((pairs,))] + parts[2:]
    scratch += [pltpu.VMEM((fsdp_count - 1,) + s, low) for s in share_shapes]
    scratch += [pltpu.SemaphoreType.DMA((shared, fsdp_count - 1))] * 2
    total = sum(a.size for a in arrays)
    return pl.pallas_call(
        functools.partial(owner_sum_kernel, ctx_count, fsdp_count, shapes, shared),
        out_shape=[jax.ShapeDtypeStruct(s, low) for s in shapes[:whole] + share_shapes],
        in_specs=[pl.BlockSpec(memory_space=pl.ANY)] * many,
        out_specs=[pl.BlockSpec(memory_space=pltpu.VMEM)] * many,
        scratch_shapes=scratch,
        compiler_params=pltpu.CompilerParams(
            collective_id=0, has_side_effects=True, vmem_limit_bytes=48 << 20
        ),
        cost_estimate=pl.CostEstimate(flops=total, bytes_accessed=4 * total, transcendentals=0),
        name="owner_sums",
    )(*arrays)


def line_comes(along, count, way, step):
    return along >= step if way == 0 else along + step < count


def line_goes(along, count, way, step):
    if way == 0:
        return (along + 1 < count) & (along >= step - 1)
    return (along >= 1) & (along + step - 1 < count)


def line_origin(along, way, step):
    return along - step if way == 0 else along + step


class LineExchange:
    def __init__(self, count, own, gathered, outgoing, incoming, sems):
        self.count, self.steps = count, count - 1
        self.own, self.gathered = own, gathered
        self.outgoing, self.incoming = outgoing, incoming
        self.line_send, self.line_recv, self.back_send, self.back_recv = sems
        self.place = lax.axis_index("ctx")
        self.along = lax.axis_index("fsdp")
        self.width = outgoing.shape[-1]
        self.chunks = self.width // BACK_TILE

    def barrier(self):
        partner_barrier(
            [
                (self.place, lax.rem(self.along + d, self.count))
                for d in sorted({1, self.count - 1})
            ]
        )

    def line_copy(self, way, step, origin):
        toward = self.along + 1 if way == 0 else self.along - 1
        return pltpu.make_async_remote_copy(
            src_ref=self.own if step == 1 else self.gathered.at[origin],
            dst_ref=self.gathered.at[origin],
            send_sem=self.line_send.at[way, step - 1],
            recv_sem=self.line_recv.at[way, step - 1],
            device_id=(self.place, toward),
            device_id_type=MESH,
        )

    def forward(self, step):
        for way in range(2):
            origin = line_origin(self.along, way, step - 1)
            pl.when(line_goes(self.along, self.count, way, step))(
                lambda way=way, origin=origin: self.line_copy(way, step, origin).start()
            )

    def arrive(self, step):
        for way in range(2):
            origin = line_origin(self.along, way, step)
            pl.when(line_comes(self.along, self.count, way, step))(
                lambda way=way, origin=origin: self.line_copy(way, step, origin).wait_recv()
            )
        if step < self.steps:
            self.forward(step + 1)

    def back_copy(self, way, owner, chunk):
        toward = self.along + 1 if way == 0 else self.along - 1
        columns = pl.ds(chunk * BACK_TILE, BACK_TILE)
        landing = owner if way == 0 else jnp.where(owner == toward, self.count, owner)
        return pltpu.make_async_remote_copy(
            src_ref=self.outgoing.at[owner, :, columns],
            dst_ref=self.incoming.at[landing, :, columns],
            send_sem=self.back_send.at[way, owner, chunk],
            recv_sem=self.back_recv.at[way, owner, chunk],
            device_id=(self.place, toward),
            device_id_type=MESH,
        )

    def landed(self, way, owner, chunk, landing):
        columns = pl.ds(chunk * BACK_TILE, BACK_TILE)
        pltpu.make_async_remote_copy(
            src_ref=self.outgoing.at[owner, :, columns],
            dst_ref=self.incoming.at[landing, :, columns],
            send_sem=self.back_send.at[way, owner, chunk],
            recv_sem=self.back_recv.at[way, owner, chunk],
            device_id=(self.place, self.along),
            device_id_type=MESH,
        ).wait_recv()
        return self.incoming[landing, :, columns].astype(jnp.float32)

    def relays(self, way):
        return self.along >= 1 if way == 0 else self.along + 1 < self.count

    def run(self, compute, before_last):

        def one(way, step):
            back = 1 - way
            origin = line_origin(self.along, way, step)

            def work():
                def write(columns, tile):
                    self.outgoing[origin, :, columns] = tile.astype(self.outgoing.dtype)

                compute(origin, write)

                def begin():
                    for chunk in range(self.chunks):
                        self.back_copy(back, origin, chunk).start()

                pl.when(jnp.logical_not(self.relays(back)))(begin)

            pl.when(line_comes(self.along, self.count, way, step))(work)

        def relay(way, step):
            owner = step if way == 0 else self.steps - step
            passes = owner > self.along if way == 0 else owner < self.along

            def work():
                for chunk in range(self.chunks):
                    more = self.landed(way, owner, chunk, owner)
                    columns = pl.ds(chunk * BACK_TILE, BACK_TILE)
                    mine = self.outgoing[owner, :, columns].astype(jnp.float32)
                    self.outgoing[owner, :, columns] = (mine + more).astype(self.outgoing.dtype)
                    self.back_copy(way, owner, chunk).start()

            pl.when(self.relays(way) & passes)(work)

        for step in range(1, self.steps + 1):
            self.arrive(step)
            for way in range(2):
                one(way, step)
            if step == self.steps:
                before_last()
            for way in range(2):
                relay(way, step)

    def finish(self, total):
        for way in range(2):

            def receive(way=way):
                landing = self.along if way == 0 else self.count
                for chunk in range(self.chunks):
                    columns = pl.ds(chunk * BACK_TILE, BACK_TILE)
                    more = self.landed(way, self.along, chunk, landing)
                    total[:, columns] = total[:, columns] + more

            pl.when(self.relays(way))(receive)
        for step in range(1, self.steps + 1):
            for way in range(2):
                origin = line_origin(self.along, way, step - 1)

                def left(way=way, step=step, origin=origin):
                    self.line_copy(way, step, origin).wait_send()

                def returned(way=way, step=step):
                    for chunk in range(self.chunks):
                        self.back_copy(1 - way, line_origin(self.along, way, step), chunk).wait_send()

                pl.when(line_goes(self.along, self.count, way, step))(left)
                pl.when(line_comes(self.along, self.count, way, step))(returned)


def line_scratch(count, rows, columns):
    steps = count - 1
    chunks = columns // BACK_TILE
    return [
        pltpu.VMEM((count, rows, columns), jnp.bfloat16),
        pltpu.VMEM((count + 1, rows, columns), jnp.bfloat16),
        pltpu.SemaphoreType.DMA((2, steps)),
        pltpu.SemaphoreType.DMA((2, steps)),
        pltpu.SemaphoreType.DMA((2, count, chunks)),
        pltpu.SemaphoreType.DMA((2, count, chunks)),
    ]


def tile_at(t, size):
    return pl.ds(pl.multiple_of(t * size, size), size)


def feed_forward_kernel(
    count,
    rows_in,
    gate_hbm,
    up_hbm,
    down_hbm,
    total,
    gathered,
    gate_keep,
    up_keep,
    hidden_keep,
    gate_w,
    up_w,
    down_w,
    weight_sem,
    *parts,
):
    rows, width = rows_in.shape
    units = gate_w.shape[1]
    tile = FF_TILE
    line = LineExchange(count, rows_in, gathered, parts[0], parts[1], parts[2:])
    loads = []
    for n, (source, target) in enumerate(((gate_hbm, gate_w), (up_hbm, up_w), (down_hbm, down_w))):
        group = []
        for t in range(target.shape[1] // tile):
            at = (slice(None), pl.ds(t * tile, tile))
            group.append(pltpu.make_async_copy(source.at[at], target.at[at], weight_sem.at[n, t]))
        loads.append(group)
    for t in range(units // tile):
        loads[0][t].start()
        loads[1][t].start()
    for load in loads[2]:
        load.start()
    line.barrier()
    line.forward(1)
    gathered[line.along] = rows_in[...]

    def hidden_tile(origin, columns):
        at = pl.ds(pl.multiple_of(origin * rows, rows), rows)
        gate = forward_product(gathered[origin], gate_w[:, columns])
        up = forward_product(gathered[origin], up_w[:, columns])
        gate_keep[at, columns] = gate.astype(gate_keep.dtype)
        up_keep[at, columns] = up.astype(up_keep.dtype)
        hidden_keep[at, columns] = hidden_piece(gate, up).astype(hidden_keep.dtype)

    def out_tile(origin, columns):
        at = pl.ds(pl.multiple_of(origin * rows, rows), rows)
        return forward_product(hidden_keep[at], down_w[:, columns])

    for t in range(units // tile):
        loads[0][t].wait()
        loads[1][t].wait()
        hidden_tile(line.along, pl.ds(t * tile, tile))
    for t in range(width // tile):
        loads[2][t].wait()
        columns = pl.ds(t * tile, tile)
        total[:, columns] = out_tile(line.along, columns)

    def compute(origin, write):
        def hidden_step(t, carry):
            hidden_tile(origin, tile_at(t, tile))
            return carry

        def out_step(t, carry):
            columns = tile_at(t, tile)
            write(columns, out_tile(origin, columns))
            return carry

        lax.fori_loop(0, units // tile, hidden_step, 0)
        lax.fori_loop(0, width // tile, out_step, 0)

    line.run(compute, lambda: None)
    line.finish(total)


def feed_forward(rows_in, gate_weight, up_weight, down_weight):
    count = lax.axis_size("fsdp")
    rows, width = rows_in.shape
    units = gate_weight.shape[1]
    low = jnp.bfloat16
    vmem = pl.BlockSpec(memory_space=pltpu.VMEM)
    hbm = pl.BlockSpec(memory_space=pltpu.HBM)
    kept = jax.ShapeDtypeStruct((count * rows, units), low)
    out, gathered, gate, up, hidden = pl.pallas_call(
        functools.partial(feed_forward_kernel, count),
        out_shape=[
            jax.ShapeDtypeStruct((rows, width), jnp.float32),
            jax.ShapeDtypeStruct((count, rows, width), low),
            kept,
            kept,
            kept,
        ],
        in_specs=[vmem, hbm, hbm, hbm],
        out_specs=[vmem] * 5,
        scratch_shapes=[
            pltpu.VMEM((width, units), low),
            pltpu.VMEM((width, units), low),
            pltpu.VMEM((units, width), low),
            pltpu.SemaphoreType.DMA((3, max(width, units) // FF_TILE)),
        ]
        + line_scratch(count, rows, width),
        compiler_params=pltpu.CompilerParams(
            collective_id=4, has_side_effects=True, vmem_limit_bytes=56 << 20
        ),
        cost_estimate=pl.CostEstimate(
            flops=6 * count * rows * width * units,
            bytes_accessed=6 * width * units,
            transcendentals=count * rows * units,
        ),
        name="feed_forward",
    )(rows_in, gate_weight, up_weight, down_weight)
    return out, gathered.reshape(count * rows, width), gate, up, hidden


def hidden_pull_tile(grad, gate, up):
    slope = math.sqrt(2.0 / math.pi)
    square = gate * gate
    curve = jnp.tanh(slope * gate * (1.0 + 0.044715 * square))
    bend = 0.5 * (1.0 + curve)
    steep = bend + 0.5 * gate * (1.0 - curve * curve) * slope * (1.0 + 3.0 * 0.044715 * square)
    return grad * up * steep, grad * gate * bend


def feed_forward_backward_kernel(
    count,
    grads_in,
    gate_keep,
    up_keep,
    hidden_keep,
    tokens,
    gate_hbm,
    up_hbm,
    down_hbm,
    total,
    down_grad,
    gate_grad,
    up_grad,
    gathered,
    gate_back,
    up_back,
    gate_w,
    up_w,
    down_w,
    weight_sem,
    staged,
    staged_sem,
    *parts,
):
    rows, width = grads_in.shape
    units = gate_w.shape[1]
    tile = FF_TILE
    line = LineExchange(count, grads_in, gathered, parts[0], parts[1], parts[2:])
    loads = []
    for n, (source, target) in enumerate(((gate_hbm, gate_w), (up_hbm, up_w), (down_hbm, down_w))):
        group = []
        for t in range(target.shape[0] // tile):
            at = pl.ds(t * tile, tile)
            group.append(pltpu.make_async_copy(source.at[at], target.at[at], weight_sem.at[n, t]))
        loads.append(group)
    for load in loads[2]:
        load.start()
    for t in range(width // tile):
        loads[0][t].start()
        loads[1][t].start()
    line.barrier()
    line.forward(1)
    gathered[line.along] = grads_in[...]

    def hidden_tile(origin, columns):
        at = pl.ds(pl.multiple_of(origin * rows, rows), rows)
        grad = across(gathered[origin], down_w[columns])
        gate = gate_keep[at, columns].astype(jnp.float32)
        up = up_keep[at, columns].astype(jnp.float32)
        gate_pull, up_pull = hidden_pull_tile(grad, gate, up)
        gate_back[at, columns] = gate_pull.astype(gate_back.dtype)
        up_back[at, columns] = up_pull.astype(up_back.dtype)

    def out_tile(origin, columns):
        at = pl.ds(pl.multiple_of(origin * rows, rows), rows)
        return across(gate_back[at], gate_w[columns]) + across(up_back[at], up_w[columns])

    for t in range(units // tile):
        loads[2][t].wait()
        hidden_tile(line.along, pl.ds(t * tile, tile))
    for t in range(width // tile):
        loads[0][t].wait()
        loads[1][t].wait()
        columns = pl.ds(t * tile, tile)
        total[:, columns] = out_tile(line.along, columns)

    def compute(origin, write):
        def hidden_step(t, carry):
            hidden_tile(origin, tile_at(t, tile))
            return carry

        def out_step(t, carry):
            columns = tile_at(t, tile)
            write(columns, out_tile(origin, columns))
            return carry

        lax.fori_loop(0, units // tile, hidden_step, 0)
        lax.fori_loop(0, width // tile, out_step, 0)

    band = GRAD_TILE
    bands = width // band

    def stage(slot, which, t, target):
        return pltpu.make_async_copy(
            staged.at[slot, which], target.at[tile_at(t, band)], staged_sem.at[slot, which]
        )

    def grad_bands(jobs):
        def step(t, carry):
            slot = lax.rem(t, 2)
            for left, right, target, which in jobs:

                @pl.when(t >= 2)
                def _(target=target, which=which):
                    stage(slot, which, t, target).wait()

                product = over_rows(left(tile_at(t, band)), right[...])
                staged[slot, which] = product.astype(staged.dtype)
                stage(slot, which, t, target).start()
            return carry

        lax.fori_loop(0, bands, step, 0)
        for back in range(2):
            t = bands - 2 + back
            for _, _, target, which in jobs:
                stage(t % 2, which, t, target).wait()

    def grads_at(columns):
        return gathered[:, :, columns].reshape(count * rows, band)

    line.run(
        compute, lambda: grad_bands([(grads_at, hidden_keep, down_grad, 0)])
    )
    grad_bands(
        [
            (lambda columns: tokens[:, columns], gate_back, gate_grad, 0),
            (lambda columns: tokens[:, columns], up_back, up_grad, 1),
        ]
    )
    line.finish(total)


def feed_forward_backward(
    grads_in, gate_keep, up_keep, hidden_keep, tokens, gate_weight, up_weight, down_weight
):
    count = lax.axis_size("fsdp")
    rows, width = grads_in.shape
    units = gate_weight.shape[1]
    low = jnp.bfloat16
    vmem = pl.BlockSpec(memory_space=pltpu.VMEM)
    hbm = pl.BlockSpec(memory_space=pltpu.HBM)
    grad_shape = jax.ShapeDtypeStruct((width, units), low)
    return pl.pallas_call(
        functools.partial(feed_forward_backward_kernel, count),
        out_shape=[jax.ShapeDtypeStruct((rows, width), jnp.float32)] + [grad_shape] * 3,
        in_specs=[vmem] * 5 + [hbm] * 3,
        out_specs=[vmem] + [hbm] * 3,
        scratch_shapes=[
            pltpu.VMEM((count, rows, width), low),
            pltpu.VMEM((count * rows, units), low),
            pltpu.VMEM((count * rows, units), low),
            pltpu.VMEM((width, units), low),
            pltpu.VMEM((width, units), low),
            pltpu.VMEM((units, width), low),
            pltpu.SemaphoreType.DMA((3, max(width, units) // FF_TILE)),
            pltpu.VMEM((2, 2, GRAD_TILE, units), low),
            pltpu.SemaphoreType.DMA((2, 2)),
        ]
        + line_scratch(count, rows, width),
        compiler_params=pltpu.CompilerParams(
            collective_id=5, has_side_effects=True, vmem_limit_bytes=60 << 20
        ),
        cost_estimate=pl.CostEstimate(
            flops=12 * count * rows * width * units,
            bytes_accessed=12 * width * units,
            transcendentals=count * rows * units,
        ),
        name="feed_forward_backward",
    )(grads_in, gate_keep, up_keep, hidden_keep, tokens, gate_weight, up_weight, down_weight)


def body(
    tokens,
    per_layer,
    out_grad,
    segment_ids,
    query_weight,
    key_weight,
    value_weight,
    out_weight,
    left_weight,
    right_weight,
    gate_weight,
    up_weight,
    down_weight,
    side_gate,
    side_out,
    input_gain,
    laurel_gain,
    attn_gain,
    pre_gain,
    post_gain,
    side_gain,
    query_gain,
    key_gain,
):
    low = jnp.bfloat16
    inputs = tokens[0].astype(jnp.float32)
    extra_rows = per_layer[0].astype(jnp.float32)
    cotangent = out_grad[0].astype(jnp.float32)
    sequence_ids = segment_ids[0]
    rows_here, width = inputs.shape
    ctx_count = lax.axis_size("ctx")
    fsdp_count = lax.axis_size("fsdp")
    count = ctx_count * fsdp_count
    ctx_place = lax.axis_index("ctx")
    rank = left_weight.shape[1]
    side = side_gate.shape[1]
    query_width = HEADS * HD
    kv_width = KV_HEADS * HD
    query_pos = ctx_place * rows_here + jnp.arange(rows_here, dtype=jnp.int32)

    piece = width // count

    qkv_width = query_width + 2 * kv_width
    full_qkv, full_second, full_left, full_right, full_side_out = weight_gather(
        [[query_weight, key_weight, value_weight], [out_weight, side_gate]],
        [left_weight, right_weight, side_out],
    )
    full_out = full_second[:, :width]
    full_side_gate = full_second[:, width:]
    full_left = full_left.reshape(width, rank)
    full_right = full_right.transpose(1, 0, 2).reshape(rank, width)
    full_side_out = full_side_out.reshape(side, width)

    normed, input_pull = jax.vjp(rms_norm, inputs, input_gain)
    normed_low = normed.astype(low)
    qkv_raw = forward_product(normed_low, full_qkv)
    left_low = forward_product(normed_low, full_left).astype(low)
    right_out = forward_product(left_low, full_right)

    frequency = jnp.exp(
        jnp.arange(HD // 2).astype(jnp.float32) * (-2.0 * math.log(rope_theta) / HD)
    )
    angles = query_pos.astype(jnp.float32)[:, None] * frequency[None, :]
    cosine, sine_part = jnp.cos(angles), jnp.sin(angles)
    query_ids = lax.dynamic_slice_in_dim(sequence_ids, ctx_place * rows_here, rows_here)
    kv_all, query_low, attended_low, log_totals = attention_forward(
        qkv_raw, cosine, sine_part, query_gain, key_gain, query_ids, sequence_ids
    )
    attn_raw = forward_product(attended_low, full_out)

    def mix_piece(x, normed_in, attn_in, right_in, gain_one, gain_two, gain_three):
        mixed = (
            x + rms_norm(attn_in, gain_one) + normed_in + rms_norm(right_in, gain_two)
        ) * inverse_root
        return (mixed, rms_norm(mixed, gain_three))

    (mixed, ffn_in), mix_pull = jax.vjp(
        mix_piece, inputs, normed, attn_raw, right_out, attn_gain, laurel_gain, pre_gain
    )

    ffn_out, ffn_all, gate_raw, up_raw, hidden_low = feed_forward(
        ffn_in.astype(low), gate_weight, up_weight, down_weight
    )
    middle, middle_pull = jax.vjp(middle_piece, mixed, ffn_out, post_gain)
    middle_low = middle.astype(low)
    layer_gate = forward_product(middle_low, full_side_gate)
    layer_act, extra_pull = jax.vjp(hidden_piece, layer_gate, extra_rows)
    layer_low = layer_act.astype(low)
    layer_out = forward_product(layer_low, full_side_out)
    result, out_pull = jax.vjp(middle_piece, middle, layer_out, side_gain)

    middle_grad_one, layer_out_grad, side_gain_grad = out_pull(cotangent)
    layer_grad_low = layer_out_grad.astype(low)
    side_out_grad = over_rows(layer_low, layer_grad_low)
    layer_gate_grad, extra_grad = extra_pull(across(layer_grad_low, full_side_out))
    gate_grad_low = layer_gate_grad.astype(low)
    side_gate_grad = over_rows(gate_grad_low, middle_low)
    mixed_grad_one, ffn_out_grad, post_gain_grad = middle_pull(
        middle_grad_one + across(gate_grad_low, full_side_gate)
    )
    ffn_in_grad, down_weight_grad, gate_weight_grad, up_weight_grad = feed_forward_backward(
        ffn_out_grad.astype(low),
        gate_raw,
        up_raw,
        hidden_low,
        ffn_all,
        gate_weight,
        up_weight,
        down_weight,
    )
    ffn_in_grad, late_low = lax.optimization_barrier((ffn_in_grad, (attended_low, normed_low)))
    attended_all, normed_all = (gather(part, "fsdp") for part in late_low)
    (
        inputs_grad_one,
        normed_grad_one,
        attn_raw_grad,
        right_out_grad,
        attn_gain_grad,
        laurel_gain_grad,
        pre_gain_grad,
    ) = mix_pull((mixed_grad_one, ffn_in_grad))
    attn_grad_low = attn_raw_grad.astype(low)
    attended_grad_low = across(attn_grad_low, full_out).astype(low)
    right_grad_low = right_out_grad.astype(low)
    right_weight_grad = over_rows(right_grad_low, left_low)
    left_grad_low = across(right_grad_low, full_right).astype(low)
    left_weight_grad = over_rows(normed_low, left_grad_low)
    qkv_back_low, query_gain_grad, key_gain_grad, ffn_sums = attention_backward(
        attended_grad_low,
        query_low,
        kv_all,
        log_totals,
        qkv_raw,
        cosine,
        sine_part,
        query_gain,
        key_gain,
        query_ids,
        sequence_ids,
        [gate_weight_grad, up_weight_grad],
    )
    down_low, qkv_back_low = lax.optimization_barrier((down_weight_grad, qkv_back_low))
    down_weight_grad = scatter_sum(down_low, "ctx")
    normed_grad_two = across(qkv_back_low, full_qkv) + across(left_grad_low, full_left)
    inputs_grad_two, input_gain_grad = input_pull(normed_grad_one + normed_grad_two)
    block_out = result.astype(low)[None]
    tokens_grad = (inputs_grad_one + inputs_grad_two).astype(low)[None]
    per_layer_grad = extra_grad.astype(low)[None]

    def columns_to_owner(x):
        parts = x.reshape(rows_here, fsdp_count, -1).transpose(1, 0, 2)
        return lax.all_to_all(parts, "fsdp", 0, 0, tiled=True).reshape(fsdp_count * rows_here, -1)

    out_columns = columns_to_owner(attn_grad_low)
    out_weight_grad = over_rows(attended_all, out_columns)
    qkv_parts = jnp.concatenate(
        [
            part.reshape(rows_here, fsdp_count, -1)
            for part in (
                qkv_back_low[:, :query_width],
                qkv_back_low[:, query_width : query_width + kv_width],
                qkv_back_low[:, query_width + kv_width :],
            )
        ],
        axis=2,
    )
    qkv_columns = columns_to_owner(qkv_parts.reshape(rows_here, -1))
    qkv_weight_grad = over_rows(normed_all, qkv_columns)

    small_gains = [
        jnp.pad(g.reshape(count, -1), ((0, 0), (0, piece - g.shape[0] // count))).reshape(-1)
        for g in (query_gain_grad, key_gain_grad)
    ]
    gains = jnp.stack(
        [
            input_gain_grad,
            laurel_gain_grad,
            attn_gain_grad,
            pre_gain_grad,
            post_gain_grad,
            side_gain_grad,
            *small_gains,
        ]
    )
    gate_blocks = side_gate_grad.astype(low).reshape(side, ctx_count, -1).transpose(1, 0, 2)
    gate_columns = width // ctx_count
    tall = jnp.concatenate(
        [
            left_weight_grad.astype(low),
            right_weight_grad.astype(low),
            jnp.pad(gains.astype(low).T, ((0, 0), (0, 128 - gains.shape[0]))),
        ],
        axis=1,
    )
    out_blocks = side_out_grad.astype(low).reshape(
        ctx_count, side // ctx_count, fsdp_count, width // fsdp_count
    )
    out_blocks = out_blocks.transpose(0, 2, 1, 3).reshape(-1, width // fsdp_count)
    out_weight_grad, qkv_weight_grad, tall, gate_blocks, side_out_grad = owner_sums(
        [
            out_weight_grad.astype(low),
            qkv_weight_grad.astype(low),
            tall,
            gate_blocks.reshape(-1, gate_columns),
            out_blocks,
        ],
        3,
    )
    gate_weight_grad, up_weight_grad = ffn_sums
    down_weight_grad = down_weight_grad.T
    query_part = query_width // fsdp_count
    kv_part = kv_width // fsdp_count
    query_weight_grad = qkv_weight_grad[:, :query_part]
    key_weight_grad = qkv_weight_grad[:, query_part : query_part + kv_part]
    value_weight_grad = qkv_weight_grad[:, query_part + kv_part :]
    wide = jnp.float32
    tall = tall.astype(wide)
    left_weight_grad = tall[:, :rank]
    right_weight_grad = tall[:, rank : 2 * rank].T
    gains = tall[:, 2 * rank : 2 * rank + 8].T
    small_part = query_gain.shape[0] // count
    side_gate_grad = gate_blocks.astype(wide).T
    side_out_grad = side_out_grad.astype(wide)
    return (
        block_out,
        tokens_grad,
        per_layer_grad,
        query_weight_grad.astype(wide),
        key_weight_grad.astype(wide),
        value_weight_grad.astype(wide),
        out_weight_grad.astype(wide),
        left_weight_grad,
        right_weight_grad,
        gate_weight_grad.astype(wide),
        up_weight_grad.astype(wide),
        down_weight_grad.astype(wide),
        side_gate_grad,
        side_out_grad,
        *(gains[n] for n in range(6)),
        gains[6, :small_part],
        gains[7, :small_part],
    )


def solution(mesh):
    placed = (
        P("fsdp", "ctx", None),
        P("fsdp", "ctx", None),
        P("fsdp", "ctx", None),
        P("fsdp", None),
        P("fsdp", None),
        P("fsdp", None),
        P("fsdp", None),
        P("fsdp", None),
        P("fsdp", None),
        P(None, "fsdp"),
        P(None, "fsdp"),
        P(None, "fsdp"),
        P("fsdp", None),
        P("fsdp", None),
        P("fsdp", None),
        P(),
        P(),
        P(),
        P(),
        P(),
        P(),
        P(),
        P(),
    )
    return jax.shard_map(
        body,
        mesh=mesh,
        in_specs=placed,
        out_specs=(
            P("fsdp", "ctx", None),
            P("fsdp", "ctx", None),
            P("fsdp", "ctx", None),
            P("ctx", "fsdp"),
            P("ctx", "fsdp"),
            P("ctx", "fsdp"),
            P("ctx", "fsdp"),
            P(("ctx", "fsdp"), None),
            P(None, ("ctx", "fsdp")),
            P("ctx", "fsdp"),
            P("ctx", "fsdp"),
            P("fsdp", "ctx"),
            P("ctx", "fsdp"),
            P("ctx", "fsdp"),
            P(("ctx", "fsdp")),
            P(("ctx", "fsdp")),
            P(("ctx", "fsdp")),
            P(("ctx", "fsdp")),
            P(("ctx", "fsdp")),
            P(("ctx", "fsdp")),
            P(("ctx", "fsdp")),
            P(("ctx", "fsdp")),
        ),
        check_vma=False,
    )
```

```python
import functools
import math

import jax
import jax.numpy as jnp
from jax import lax
from jax.experimental import pallas as pl
from jax.experimental.pallas import tpu as pltpu
from jax.sharding import PartitionSpec as P

HEADS = 8
KV_HEADS = 2
HD = 256
MESH = pl.DeviceIdType.MESH
FF_TILE = 512
BACK_TILE = 512
GRAD_TILE = 256


epsilon = 1e-06
rope_theta = 1000000.0
masked_score = -1e30
inverse_root = 1.0 / math.sqrt(2.0)


def rms_norm(v, factor):
    return v * lax.rsqrt(jnp.mean(v * v, axis=-1, keepdims=True) + epsilon) * factor


def forward_product(a, b):
    return jnp.dot(a, b, preferred_element_type=jnp.float32)


def across(a, b):
    return lax.dot_general(a, b, (((1,), (1,)), ((), ())), preferred_element_type=jnp.float32)


def over_rows(a, b):
    return lax.dot_general(a, b, (((0,), (0,)), ((), ())), preferred_element_type=jnp.float32)


def hidden_piece(gate_in, up_in):
    return jax.nn.gelu(gate_in, approximate=True) * up_in


def middle_piece(mixed_in, ffn_in_rows, factor):
    return mixed_in + rms_norm(ffn_in_rows, factor)


def gather(x, axis):
    return lax.all_gather(x, axis, axis=0, tiled=True)


def scatter_sum(x, axis):
    return lax.psum_scatter(x, axis, scatter_dimension=0, tiled=True)


def partner_barrier(partners):
    barrier = pltpu.get_barrier_semaphore()
    for partner in partners:
        pl.semaphore_signal(barrier, inc=1, device_id=partner, device_id_type=MESH)
    pl.semaphore_wait(barrier, len(partners))


def add_rows(target, source, first, rows):
    tile = 16

    def one(step, carry):
        at = pl.ds(pl.multiple_of(first + step * tile, tile), tile)
        from_at = pl.ds(pl.multiple_of(step * tile, tile), tile)
        total = target[at].astype(jnp.float32) + source[from_at].astype(jnp.float32)
        target[at] = total.astype(target.dtype)
        return carry

    lax.fori_loop(0, rows // tile, one, 0)


def held_index(mine, done, bits):
    return tuple(slice(None) if t in done else mine[t] for t in reversed(range(bits)))


def ctx_position(ctx_count):
    bits = ctx_count.bit_length() - 1
    place = lax.axis_index("ctx")
    along = lax.axis_index("fsdp")
    mine = [lax.rem(place // (1 << t), 2) for t in range(bits)]
    partners = [(place + (1 - 2 * mine[t]) * (1 << t), along) for t in range(bits)]
    orders = [list(range(1, bits)), list(range(bits - 1, 0, -1))]
    return bits, place, along, mine, partners, orders


def spread_copy(out, lead, half, stage, position, send_sem, recv_sem):
    bits, _, _, mine, partners, orders = position
    order = orders[half]
    rows = out.shape[-2] // 2
    at = lead + held_index(mine, order[:stage], bits) + (pl.ds(half * rows, rows),)
    return pltpu.make_async_remote_copy(
        src_ref=out.at[at],
        dst_ref=out.at[at],
        send_sem=send_sem.at[half, stage],
        recv_sem=recv_sem.at[half, stage],
        device_id=partners[order[stage]],
        device_id_type=MESH,
    )


def sibling_copy(out, lead, position, send_sem, recv_sem):
    bits, _, _, mine, partners, orders = position
    at = lead + held_index(mine, orders[0], bits)
    return pltpu.make_async_remote_copy(
        src_ref=out.at[at],
        dst_ref=out.at[at],
        send_sem=send_sem,
        recv_sem=recv_sem,
        device_id=partners[0],
        device_id_type=MESH,
    )


def weight_gather_kernel(ctx_count, fsdp_count, members, spread, *refs):
    sets = len(members)
    own_count = sum(members)
    own, outs = refs[:own_count], refs[own_count : own_count + sets]
    rest = refs[own_count + sets :]
    passing, pieces = rest[:own_count], rest[own_count : own_count + sets]
    own_sem, line_send, line_recv, send_sem, recv_sem, core_send, core_recv = rest[
        own_count + sets :
    ]
    position = ctx_position(ctx_count)
    bits, place, along, mine, partners, _ = position
    steps = fsdp_count - 1
    here = held_index(mine, (), bits)
    columns = []
    for i in range(sets):
        start = 0
        for _ in range(members[i]):
            wide = own[len(columns)].shape[-1]
            columns.append((i, pl.ds(start, wide)))
            start += wide
    piece_loads = [
        pltpu.make_async_copy(own[n].at[here], pieces[i].at[:, at], own_sem.at[0, n])
        for n, (i, at) in enumerate(columns)
    ]
    for load in piece_loads:
        load.start()
    loads = [
        pltpu.make_async_copy(source, passing[n], own_sem.at[1, n])
        for n, source in enumerate(own)
    ]
    for load in loads:
        load.start()
    partner_barrier(
        partners
        + [(place, lax.rem(along + 1, fsdp_count)), (place, lax.rem(along + steps, fsdp_count))]
    )

    def line_copy(i, way, step, origin):
        toward = along + 1 if way == 0 else along - 1
        first, target = pieces[i], outs[i].at[(origin,) + here]
        return pltpu.make_async_remote_copy(
            src_ref=first if step == 1 else target,
            dst_ref=target,
            send_sem=line_send.at[i, way, step - 1],
            recv_sem=line_recv.at[i, way, step - 1],
            device_id=(place, toward),
            device_id_type=MESH,
        )

    def comes(way, step):
        return along >= step if way == 0 else along + step < fsdp_count

    def goes(way, step):
        if way == 0:
            return (along + 1 < fsdp_count) & (along >= step - 1)
        return (along >= 1) & (along + step - 1 < fsdp_count)

    def origin_of(way, step):
        return along - step if way == 0 else along + step

    def each(flag, action):
        pl.when(flag)(action)

    def forward(i, step):
        for way in range(2):
            each(goes(way, step), lambda: line_copy(i, way, step, origin_of(way, step - 1)).start())

    for load in piece_loads:
        load.wait()
    for i in range(sets):
        forward(i, 1)
    stores = []
    for n, load in enumerate(loads):
        load.wait()
        i, at = columns[n]
        target = outs[i].at[(along,) + (slice(None),) * (bits + 1) + (at,)]
        stores.append(pltpu.make_async_copy(passing[n], target, own_sem.at[2, n]))
        stores[-1].start()

    def stage_copies(i, way, step, stage):
        lead = (origin_of(way, step),)
        at = (i, way, step - 1)
        return [
            spread_copy(outs[i], lead, half, stage, position, send_sem.at[at], recv_sem.at[at])
            for half in range(2)
        ]

    def core_copy(i, way, step):
        at = (i, way, step - 1)
        return sibling_copy(
            outs[i], (origin_of(way, step),), position, core_send.at[at], core_recv.at[at]
        )

    def arrive(i, step):
        for way in range(2):

            def landed():
                line_copy(i, way, step, origin_of(way, step)).wait_recv()

            each(comes(way, step), landed)
        if step < steps:
            forward(i, step + 1)
        if i >= spread:
            return
        for way in range(2):

            def begin():
                for copy in stage_copies(i, way, step, 0):
                    copy.start()

            each(comes(way, step), begin)

    def advance(i, step, stage):
        if i >= spread:
            return
        for way in range(2):

            def proceed():
                for copy in stage_copies(i, way, step, stage):
                    copy.wait_recv()
                if stage < bits - 2:
                    for copy in stage_copies(i, way, step, stage + 1):
                        copy.start()
                else:
                    core_copy(i, way, step).start()

            each(comes(way, step), proceed)

    order = [(i, step) for i in range(sets) for step in range(1, steps + 1)]
    for tick in range(len(order) + bits - 1):
        if tick < len(order):
            arrive(*order[tick])
        for stage in range(bits - 1):
            at = tick - 1 - stage
            if 0 <= at < len(order):
                advance(*order[at], stage)
    for copy in stores:
        copy.wait()
    for i, step in order:
        for way in range(2):

            def leave():
                line_copy(i, way, step, origin_of(way, step - 1)).wait_send()

            def finish():
                for stage in range(bits - 1):
                    for copy in stage_copies(i, way, step, stage):
                        copy.wait_send()
                core_copy(i, way, step).wait()

            each(goes(way, step), leave)
            if i < spread:
                each(comes(way, step), finish)


def weight_gather(own, spread):
    ctx_count = lax.axis_size("ctx")
    fsdp_count = lax.axis_size("fsdp")
    bits = ctx_count.bit_length() - 1
    steps = fsdp_count - 1
    sets = len(own)
    cut = (2,) * bits
    low = jnp.bfloat16
    flat = [w.reshape(cut + (w.shape[0] // ctx_count, w.shape[1])) for group in own for w in group]
    pieces = [(g[0].shape[0] // ctx_count, sum(w.shape[1] for w in g)) for g in own]
    out_shapes = [(fsdp_count,) + cut + p for p in pieces]
    total = sum(rows * columns for rows, columns in pieces) * ctx_count * fsdp_count
    outs = pl.pallas_call(
        functools.partial(
            weight_gather_kernel, ctx_count, fsdp_count, [len(g) for g in own], spread
        ),
        out_shape=[jax.ShapeDtypeStruct(s, low) for s in out_shapes],
        in_specs=[pl.BlockSpec(memory_space=pltpu.HBM)] * len(flat),
        out_specs=[pl.BlockSpec(memory_space=pltpu.HBM)] * len(out_shapes),
        scratch_shapes=[pltpu.VMEM(w.shape, low) for w in flat]
        + [pltpu.VMEM(p, low) for p in pieces]
        + [
            pltpu.SemaphoreType.DMA((3, len(flat))),
            pltpu.SemaphoreType.DMA((sets, 2, steps)),
            pltpu.SemaphoreType.DMA((sets, 2, steps)),
            pltpu.SemaphoreType.DMA((spread, 2, steps, 2, bits - 1)),
            pltpu.SemaphoreType.DMA((spread, 2, steps, 2, bits - 1)),
            pltpu.SemaphoreType.DMA((spread, 2, steps)),
            pltpu.SemaphoreType.DMA((spread, 2, steps)),
        ],
        compiler_params=pltpu.CompilerParams(
            collective_id=1, has_side_effects=True, vmem_limit_bytes=60 << 20
        ),
        cost_estimate=pl.CostEstimate(flops=0, bytes_accessed=4 * total, transcendentals=0),
        name="weight_gather",
    )(*flat)
    return [o.reshape(-1, o.shape[-1]) for o in outs[:spread]] + list(outs[spread:])


def line_comes(along, count, way, step):
    return along >= step if way == 0 else along + step < count


def line_goes(along, count, way, step):
    if way == 0:
        return (along + 1 < count) & (along >= step - 1)
    return (along >= 1) & (along + step - 1 < count)


def line_origin(along, way, step):
    return along - step if way == 0 else along + step


class LineGather:
    def __init__(self, count, owns, outs, passing, own_sems, send_sems, recv_sems):
        self.count, self.steps = count, count - 1
        self.owns, self.outs, self.passing = owns, outs, passing
        self.own_sems, self.send_sems, self.recv_sems = own_sems, send_sems, recv_sems
        self.place = lax.axis_index("ctx")
        self.along = lax.axis_index("fsdp")
        self.done = 0

    def partners(self):
        return [(self.place, lax.rem(self.along + d, self.count)) for d in sorted({1, self.steps})]

    def own_copies(self, n):
        return (
            pltpu.make_async_copy(self.owns[n], self.passing[n], self.own_sems.at[0, n]),
            pltpu.make_async_copy(self.passing[n], self.outs[n].at[self.along], self.own_sems.at[1, n]),
        )

    def copies(self, way, step, origin):
        toward = self.along + 1 if way == 0 else self.along - 1
        return [
            pltpu.make_async_remote_copy(
                src_ref=self.owns[n] if step == 1 else self.outs[n].at[origin],
                dst_ref=self.outs[n].at[origin],
                send_sem=self.send_sems.at[n, way, step - 1],
                recv_sem=self.recv_sems.at[n, way, step - 1],
                device_id=(self.place, toward),
                device_id_type=MESH,
            )
            for n in range(len(self.owns))
        ]

    def forward(self, step):
        for way in range(2):

            def go(way=way):
                for copy in self.copies(way, step, line_origin(self.along, way, step - 1)):
                    copy.start()

            pl.when(line_goes(self.along, self.count, way, step))(go)

    def load(self):
        for n in range(len(self.owns)):
            self.own_copies(n)[0].start()

    def store(self):
        for n in range(len(self.owns)):
            self.own_copies(n)[0].wait()
            self.own_copies(n)[1].start()

    def arrive(self):
        if self.done == self.steps:
            return
        self.done += 1
        step = self.done
        for way in range(2):

            def land(way=way):
                for copy in self.copies(way, step, line_origin(self.along, way, step)):
                    copy.wait_recv()

            pl.when(line_comes(self.along, self.count, way, step))(land)
        if step < self.steps:
            self.forward(step + 1)

    def finish(self):
        while self.done < self.steps:
            self.arrive()
        for n in range(len(self.owns)):
            self.own_copies(n)[1].wait()
        for step in range(1, self.steps + 1):
            for way in range(2):

                def leave(way=way, step=step):
                    for copy in self.copies(way, step, line_origin(self.along, way, step - 1)):
                        copy.wait_send()

                pl.when(line_goes(self.along, self.count, way, step))(leave)


class Halving:
    def __init__(self, position, rows, give, held, first_in, later_in, sems):
        self.bits, self.place, self.along, self.mine, self.partners, self.orders = position
        self.rows, self.give, self.held = rows, give, held
        self.first_in, self.later_in = first_in, later_in
        self.send_zero, self.recv_zero, self.send_sem, self.recv_sem = sems
        self.pairs = 1 << (self.bits - 1)

    def first_copy(self, b):
        return pltpu.make_async_remote_copy(
            src_ref=self.give(b),
            dst_ref=self.first_in.at[b],
            send_sem=self.send_zero.at[b],
            recv_sem=self.recv_zero.at[b],
            device_id=self.partners[0],
            device_id_type=MESH,
        )

    def start_first(self):
        for b in range(self.pairs):
            self.first_copy(b).start()

    def end_first(self, b):
        self.first_copy(b).wait()
        add_rows(self.held(b), self.first_in.at[b], 0, self.rows)

    def slot_of(self, stage):
        return sum(1 << (self.bits - 2 - s) for s in range(stage))

    def block_sets(self, half, stage):
        order = self.orders[half]
        bit = order[stage]
        free = order[stage + 1 :]
        fixed = sum(self.mine[t] * (1 << (t - 1)) for t in order[:stage])
        sent, kept = [], []
        for combo in range(1 << len(free)):
            value = sum(((combo >> n) & 1) << (t - 1) for n, t in enumerate(free))
            sent.append(fixed + (1 - self.mine[bit]) * (1 << (bit - 1)) + value)
            kept.append(fixed + self.mine[bit] * (1 << (bit - 1)) + value)
        return bit, sent, kept

    def stage_copies(self, stage):
        rows = self.rows // 2
        copies = []
        for half in range(2):
            bit, sent, _ = self.block_sets(half, stage)
            for n, block in enumerate(sent):
                at = (half, self.slot_of(stage) + n)
                copies.append(
                    pltpu.make_async_remote_copy(
                        src_ref=self.held(block).at[pl.ds(half * rows, rows)],
                        dst_ref=self.later_in.at[at],
                        send_sem=self.send_sem.at[at],
                        recv_sem=self.recv_sem.at[at],
                        device_id=self.partners[bit],
                        device_id_type=MESH,
                    )
                )
        return copies

    def start(self, stage):
        for copy in self.stage_copies(stage):
            copy.start()

    def end(self, stage):
        for copy in self.stage_copies(stage):
            copy.wait()
        rows = self.rows // 2
        for half in range(2):
            _, _, kept = self.block_sets(half, stage)
            for n, block in enumerate(kept):
                at = (half, self.slot_of(stage) + n)
                add_rows(self.held(block), self.later_in.at[at], half * rows, rows)

    def mine_now(self):
        return self.held(self.place // 2)


def halving_scratch(ctx_count, rows, columns):
    pairs = ctx_count // 2
    return [
        pltpu.VMEM((pairs, rows, columns), jnp.bfloat16),
        pltpu.VMEM((2, pairs - 1, rows // 2, columns), jnp.bfloat16),
        pltpu.SemaphoreType.DMA((pairs,)),
        pltpu.SemaphoreType.DMA((pairs,)),
        pltpu.SemaphoreType.DMA((2, pairs - 1)),
        pltpu.SemaphoreType.DMA((2, pairs - 1)),
    ]


def unit_rows(v):
    scale = lax.rsqrt(jnp.mean(v * v, axis=-1, keepdims=True) + epsilon)
    return v * scale, scale


def turned(v, cosine, sine_part):
    halfway = v.shape[-1] // 2
    leading, trailing = v[:, :halfway], v[:, halfway:]
    return jnp.concatenate(
        [leading * cosine - trailing * sine_part, trailing * cosine + leading * sine_part], axis=-1
    )


def unit_rows_pull(v, grad, gain):
    unit, scale = unit_rows(v)
    gain_grad = jnp.sum(grad * unit, axis=0, keepdims=True)
    scaled = grad * gain
    return scale * (scaled - unit * jnp.mean(unit * scaled, axis=-1, keepdims=True)), gain_grad


def head_at(h):
    return pl.ds(pl.multiple_of(h * HD, HD), HD)


def attention_forward_kernel(
    ctx_count,
    lines,
    raw,
    cosine_ref,
    sine_ref,
    query_gain,
    key_gain,
    row_ids,
    key_ids,
    _,
    *refs,
):
    line_owns, refs = refs[:lines], refs[lines:]
    kv, query_low, attended_low, log_totals, weights_out = refs[:5]
    line_outs, refs = refs[5 : 5 + lines], refs[5 + lines :]
    bias, send_sem, recv_sem, core_send, core_recv, weight_sems, weight_core_sems = refs[:7]
    line = LineGather(
        weights_out.shape[0], line_owns, line_outs, refs[7 : 7 + lines], *refs[7 + lines :]
    )
    line.load()
    position = ctx_position(ctx_count)
    bits, place, along, mine, partners, _ = position
    count = weights_out.shape[0]
    units = [(way, step) for step in range(1, count) for way in range(2)]

    def weight_copies(way, step, stage):
        lead = (line_origin(along, way, step),)
        at = (way, step - 1)
        return [
            spread_copy(
                weights_out,
                lead,
                half,
                stage,
                position,
                weight_sems.at[(0,) + at],
                weight_sems.at[(1,) + at],
            )
            for half in range(2)
        ]

    def weight_core_copy(way, step):
        at = (way, step - 1)
        return sibling_copy(
            weights_out,
            (line_origin(along, way, step),),
            position,
            weight_core_sems.at[(0,) + at],
            weight_core_sems.at[(1,) + at],
        )

    def each_unit(action):
        for way, step in units:
            pl.when(line_comes(along, count, way, step))(functools.partial(action, way, step))

    def start_weights(stage):
        def action(way, step):
            for copy in weight_copies(way, step, stage):
                copy.start()

        each_unit(action)

    def land_weights(stage):
        def action(way, step):
            for copy in weight_copies(way, step, stage):
                copy.wait_recv()

        each_unit(action)

    rows = raw.shape[0]
    groups = HEADS // KV_HEADS
    length = ctx_count * rows
    here = held_index(mine, (), bits)
    cosine, sine_part = cosine_ref[...], sine_ref[...]
    partner_barrier(partners + line.partners())
    start_weights(0)
    line.forward(1)
    for k in range(KV_HEADS):
        unit, _ = unit_rows(raw[:, pl.ds((HEADS + k) * HD, HD)])
        key = turned(unit * key_gain[...], cosine, sine_part)
        kv[here + (slice(None), pl.ds(k * HD, HD))] = key.astype(kv.dtype)
        value, _ = unit_rows(raw[:, pl.ds((HEADS + KV_HEADS + k) * HD, HD)])
        kv[here + (slice(None), pl.ds((KV_HEADS + k) * HD, HD))] = value.astype(kv.dtype)

    def copies_of(stage):
        return [spread_copy(kv, (), h, stage, position, send_sem, recv_sem) for h in range(2)]

    for copy in copies_of(0):
        copy.start()
    line.store()
    allowed = (row_ids[...] == key_ids[...]) & (
        lax.broadcasted_iota(jnp.int32, (rows, length), 1)
        <= lax.broadcasted_iota(jnp.int32, (rows, length), 0) + place * rows
    )
    bias[...] = jnp.where(allowed, 0.0, masked_score)

    def one_query(h, carry):
        unit, _ = unit_rows(raw[:, head_at(h)])
        query = turned(unit * query_gain[...], cosine, sine_part)
        query_low[:, head_at(h)] = query.astype(query_low.dtype)
        return carry

    lax.fori_loop(0, HEADS, one_query, 0)
    for stage in range(1, bits - 1):
        for copy in copies_of(stage - 1):
            copy.wait()
        for copy in copies_of(stage):
            copy.start()
        land_weights(stage - 1)
        start_weights(stage)
        line.arrive()
    for copy in copies_of(bits - 2):
        copy.wait()
    last = sibling_copy(kv, (), position, core_send, core_recv)
    last.start()
    last.wait()
    everywhere = (slice(None),) * (bits + 1)
    for k in range(KV_HEADS):
        key = kv[everywhere + (pl.ds(k * HD, HD),)].reshape(length, HD)
        value = kv[everywhere + (pl.ds((KV_HEADS + k) * HD, HD),)].reshape(length, HD)

        def one_head(g, carry, k=k, key=key, value=value):
            h = k * groups + g
            scores = across(query_low[:, head_at(h)], key) + bias[...]
            row_max = jnp.max(scores, axis=-1, keepdims=True)
            weights = jnp.exp(scores - row_max)
            row_total = jnp.sum(weights, axis=-1, keepdims=True)
            weights = (weights * (1.0 / row_total)).astype(value.dtype)
            attended_low[:, head_at(h)] = forward_product(weights, value).astype(attended_low.dtype)
            log_total = jnp.broadcast_to(row_max + jnp.log(row_total), (rows, rows))
            log_totals[h] = log_total.T[:8]
            return carry

        lax.fori_loop(0, groups, one_head, 0)
        line.arrive()
        if k == KV_HEADS - 2:
            land_weights(bits - 2)
            each_unit(lambda way, step: weight_core_copy(way, step).start())

    def finish(way, step):
        for stage in range(bits - 1):
            for copy in weight_copies(way, step, stage):
                copy.wait_send()
        weight_core_copy(way, step).wait()

    each_unit(finish)
    line.finish()


def attention_forward(raw, cosine, sine_part, query_gain, key_gain, row_ids, key_ids, weights, lines):
    ctx_count = lax.axis_size("ctx")
    steps = lax.axis_size("fsdp") - 1
    hbm = pl.BlockSpec(memory_space=pltpu.HBM)
    bits = ctx_count.bit_length() - 1
    rows = raw.shape[0]
    length = ctx_count * rows
    low = jnp.bfloat16
    vmem = pl.BlockSpec(memory_space=pltpu.VMEM)
    return pl.pallas_call(
        functools.partial(attention_forward_kernel, ctx_count, len(lines)),
        out_shape=[
            jax.ShapeDtypeStruct((2,) * bits + (rows, 2 * KV_HEADS * HD), low),
            jax.ShapeDtypeStruct((rows, HEADS * HD), low),
            jax.ShapeDtypeStruct((rows, HEADS * HD), low),
            jax.ShapeDtypeStruct((HEADS, 8, rows), jnp.float32),
            jax.ShapeDtypeStruct(weights.shape, low),
        ]
        + [jax.ShapeDtypeStruct((steps + 1,) + w.shape, low) for w in lines],
        in_specs=[vmem] * 7 + [hbm] * (1 + len(lines)),
        out_specs=[vmem] * 4 + [hbm] * (1 + len(lines)),
        input_output_aliases={7: 4},
        scratch_shapes=[
            pltpu.VMEM((rows, length), jnp.float32),
            pltpu.SemaphoreType.DMA((2, bits - 1)),
            pltpu.SemaphoreType.DMA((2, bits - 1)),
            pltpu.SemaphoreType.DMA,
            pltpu.SemaphoreType.DMA,
            pltpu.SemaphoreType.DMA((2, 2, steps, 2, bits - 1)),
            pltpu.SemaphoreType.DMA((2, 2, steps)),
        ]
        + [pltpu.VMEM(w.shape, low) for w in lines]
        + [
            pltpu.SemaphoreType.DMA((2, len(lines))),
            pltpu.SemaphoreType.DMA((len(lines), 2, steps)),
            pltpu.SemaphoreType.DMA((len(lines), 2, steps)),
        ],
        compiler_params=pltpu.CompilerParams(
            collective_id=2, has_side_effects=True, vmem_limit_bytes=56 << 20
        ),
        cost_estimate=pl.CostEstimate(
            flops=4 * HEADS * HD * rows * length,
            bytes_accessed=8 << 20,
            transcendentals=HEADS * rows * length,
        ),
        name="attention_forward",
    )(
        raw,
        cosine,
        sine_part,
        query_gain[None],
        key_gain[None],
        row_ids[:, None],
        key_ids[None],
        weights,
        *lines,
    )


def attention_backward_kernel(ctx_count, fsdp_count, extra, *refs):
    (
        query_low,
        kv,
        log_totals,
        raw,
        cosine_ref,
        sine_ref,
        query_gain,
        key_gain,
        row_ids,
        key_ids,
        row_grads,
        out_weight,
        qkv_weight,
    ) = refs[:13]
    many = len(extra)
    extra_in = refs[13 : 13 + many]
    back, gain_grads, column_grads, normed_grads = refs[13 + many : 17 + many]
    extra_out = refs[17 + many : 17 + 2 * many]
    rest = refs[17 + 2 * many :]
    bias, score_grads, weights_low, query_grads, kv_grads = rest[:5]
    kv_parts = rest[5:11]
    extra_parts = [rest[11 + 8 * i : 19 + 8 * i] for i in range(many)]
    position = ctx_position(ctx_count)
    bits, place, along, mine, partners, _ = position
    pairs = ctx_count // 2
    rows = raw.shape[0]
    column_send, column_recv, grads, streamed, stream_sem = rest[11 + 8 * many :]
    tile = streamed.shape[1]

    def stream(weight, columns, use):
        tiles = weight.shape[0] // tile

        def copy(t):
            return pltpu.make_async_copy(
                weight.at[pl.ds(t * tile, tile), pl.ds(0, columns)],
                streamed.at[t % 2, :, pl.ds(0, columns)],
                stream_sem.at[t % 2],
            )

        copy(0).start()
        for t in range(tiles):
            if t + 1 < tiles:
                copy(t + 1).start()
            copy(t).wait()
            use(pl.ds(t * tile, tile), streamed[t % 2, :, :columns])

    peers = [lax.rem(along + d, fsdp_count) for d in range(1, fsdp_count)]
    wide = column_grads.shape[-1]
    column_copies = [
        pltpu.make_async_remote_copy(
            src_ref=row_grads.at[:, pl.ds(pl.multiple_of(peer * wide, wide), wide)],
            dst_ref=column_grads.at[along],
            send_sem=column_send.at[d],
            recv_sem=column_recv.at[d],
            device_id=(place, peer),
            device_id_type=MESH,
        )
        for d, peer in enumerate(peers)
    ]
    groups = HEADS // KV_HEADS
    length = ctx_count * rows
    low = jnp.bfloat16

    kv_sum = Halving(
        position,
        rows,
        lambda b: kv_grads.at[2 * b + 1 - mine[0]],
        lambda b: kv_grads.at[2 * b + mine[0]],
        kv_parts[0],
        kv_parts[1],
        kv_parts[2:6],
    )
    sums, own_copies = [], []
    for i, (block, _) in enumerate(extra):
        held, first_in, later_in, own_sem = extra_parts[i][:4]

        def give(b, i=i, block=block):
            at = pl.multiple_of((2 * b + 1 - mine[0]) * block, 16)
            return extra_in[i].at[pl.ds(at, block)]

        sums.append(
            Halving(
                position,
                block,
                give,
                lambda b, held=held: held.at[b],
                first_in,
                later_in,
                extra_parts[i][4:8],
            )
        )
        copies = []
        for b in range(pairs):
            at = pl.multiple_of((2 * b + mine[0]) * block, 16)
            copies.append(
                pltpu.make_async_copy(
                    extra_in[i].at[pl.ds(at, block)], held.at[b], own_sem.at[b]
                )
            )
            copies[-1].start()
        own_copies.append(copies)

    partner_barrier(partners + [(place, peer) for peer in peers])
    for one in sums:
        one.start_first()
    for copy in column_copies:
        copy.start()
    column_grads[along] = row_grads[:, pl.ds(pl.multiple_of(along * wide, wide), wide)]

    def attended_tile(columns, weight):
        grads[:, columns] = across(row_grads[...], weight).astype(low)

    stream(out_weight, row_grads.shape[1], attended_tile)

    def open_extra(i):
        for b in range(pairs):
            own_copies[i][b].wait()
            sums[i].end_first(b)
        sums[i].start(0)

    allowed = (key_ids[...] == row_ids[...]) & (
        lax.broadcasted_iota(jnp.int32, (length, rows), 0)
        <= lax.broadcasted_iota(jnp.int32, (length, rows), 1) + place * rows
    )
    bias[...] = jnp.where(allowed, 0.0, masked_score)
    everywhere = (slice(None),) * (bits + 1)
    for k in range(KV_HEADS):
        if k < many:
            open_extra(k)
        key = kv[everywhere + (pl.ds(k * HD, HD),)].reshape(length, HD)
        value = kv[everywhere + (pl.ds((KV_HEADS + k) * HD, HD),)].reshape(length, HD)

        def one_head(g, carry, k=k, key=key, value=value):
            h = k * groups + g
            columns = pl.ds(pl.multiple_of(g * rows, rows), rows)
            scores = across(key, query_low[:, head_at(h)]) + bias[...]
            weights = jnp.exp(scores - log_totals[h][:1])
            weight_grad = across(value, grads[:, head_at(h)])
            delta = jnp.sum(weights * weight_grad, axis=0, keepdims=True)
            score_grads[:, columns] = (weights * (weight_grad - delta)).astype(low)
            weights_low[:, columns] = weights.astype(low)
            return carry

        lax.fori_loop(0, groups, one_head, 0)
        heads = [pl.ds((k * groups + g) * HD, HD) for g in range(groups)]
        query_stack = jnp.concatenate([query_low[:, at] for at in heads], axis=0)
        grad_stack = jnp.concatenate([grads[:, at] for at in heads], axis=0)
        key_grad = forward_product(score_grads[...], query_stack).astype(low)
        value_grad = forward_product(weights_low[...], grad_stack).astype(low)
        kv_grads[:, :, pl.ds(k * HD, HD)] = key_grad.reshape(ctx_count, rows, HD)
        kv_grads[:, :, pl.ds((KV_HEADS + k) * HD, HD)] = value_grad.reshape(ctx_count, rows, HD)
        query_grad = over_rows(key, score_grads[...])
        for g, at in enumerate(heads):
            query_grads[:, at] = query_grad[:, g * rows : (g + 1) * rows].T

    kv_sum.start_first()
    for b in range(pairs):
        kv_sum.end_first(b)
    kv_sum.start(0)
    for i in range(KV_HEADS, many):
        open_extra(i)

    def step_extra(i, stage):
        sums[i].end(stage - 1)
        sums[i].start(stage)

    cosine, sine_part = cosine_ref[...], sine_ref[...]

    def one_query(h, gain_grad):
        grad = turned(query_grads[:, head_at(h)], cosine, -sine_part)
        pulled, more = unit_rows_pull(raw[:, head_at(h)], grad, query_gain[...])
        back[:, head_at(h)] = pulled.astype(low)
        return gain_grad + more

    gain_grads[0:1] = lax.fori_loop(0, HEADS, one_query, jnp.zeros((1, HD), jnp.float32))
    for stage in range(1, bits - 1):
        kv_sum.end(stage - 1)
        kv_sum.start(stage)
    kv_sum.end(bits - 2)
    for i in range(many):
        step_extra(i, 1)
    summed = kv_sum.mine_now()
    key_gain_grad = jnp.zeros((1, HD), jnp.float32)
    for k in range(KV_HEADS):
        grad = summed[:, pl.ds(k * HD, HD)].astype(jnp.float32)
        grad = turned(grad, cosine, -sine_part)
        at = pl.ds((HEADS + k) * HD, HD)
        pulled, more = unit_rows_pull(raw[:, at], grad, key_gain[...])
        back[:, at] = pulled.astype(low)
        key_gain_grad = key_gain_grad + more
        grad = summed[:, pl.ds((KV_HEADS + k) * HD, HD)].astype(jnp.float32)
        at = pl.ds((HEADS + KV_HEADS + k) * HD, HD)
        pulled, _ = unit_rows_pull(raw[:, at], grad, 1.0)
        back[:, at] = pulled.astype(low)
    gain_grads[1:2] = key_gain_grad

    def normed_tile(columns, weight):
        normed_grads[:, columns] = across(back[...], weight)

    stream(qkv_weight, back.shape[1], normed_tile)
    for stage in range(2, bits - 1):
        for i in range(many):
            step_extra(i, stage)
    for copy in column_copies:
        copy.wait()
    for i in range(many):
        sums[i].end(bits - 2)
        extra_out[i][...] = sums[i].mine_now()[...]


def attention_backward(
    query_low,
    kv,
    log_totals,
    raw,
    cosine,
    sine_part,
    query_gain,
    key_gain,
    row_ids,
    key_ids,
    row_grads,
    out_weight,
    qkv_weight,
    extra,
):
    fsdp_count = lax.axis_size("fsdp")
    hbm = pl.BlockSpec(memory_space=pltpu.HBM)
    ctx_count = lax.axis_size("ctx")
    rows = raw.shape[0]
    length = ctx_count * rows
    pairs = ctx_count // 2
    groups = HEADS // KV_HEADS
    low = jnp.bfloat16
    vmem = pl.BlockSpec(memory_space=pltpu.VMEM)
    shapes = [(a.shape[0] // ctx_count, a.shape[1]) for a in extra]
    scratch = [
        pltpu.VMEM((length, rows), jnp.float32),
        pltpu.VMEM((length, groups * rows), low),
        pltpu.VMEM((length, groups * rows), low),
        pltpu.VMEM((rows, HEADS * HD), jnp.float32),
        pltpu.VMEM((ctx_count, rows, 2 * KV_HEADS * HD), low),
    ]
    scratch += halving_scratch(ctx_count, rows, 2 * KV_HEADS * HD)
    for shape in shapes:
        parts = halving_scratch(ctx_count, *shape)
        scratch += [pltpu.VMEM((pairs,) + shape, low)] + parts[:2]
        scratch += [pltpu.SemaphoreType.DMA((pairs,))] + parts[2:]
    scratch += [pltpu.SemaphoreType.DMA((fsdp_count - 1,))] * 2
    scratch += [
        pltpu.VMEM((rows, HEADS * HD), low),
        pltpu.VMEM((2, FF_TILE, qkv_weight.shape[1]), low),
        pltpu.SemaphoreType.DMA((2,)),
    ]
    columns_shape = (fsdp_count, rows, row_grads.shape[1] // fsdp_count)
    outs = pl.pallas_call(
        functools.partial(attention_backward_kernel, ctx_count, fsdp_count, shapes),
        out_shape=[
            jax.ShapeDtypeStruct(raw.shape, low),
            jax.ShapeDtypeStruct((8, HD), jnp.float32),
            jax.ShapeDtypeStruct(columns_shape, low),
            jax.ShapeDtypeStruct((rows, qkv_weight.shape[0]), jnp.float32),
        ]
        + [jax.ShapeDtypeStruct(s, low) for s in shapes],
        in_specs=[vmem] * 11 + [hbm] * (2 + len(extra)),
        out_specs=[vmem] * (4 + len(extra)),
        scratch_shapes=scratch,
        compiler_params=pltpu.CompilerParams(
            collective_id=3, has_side_effects=True, vmem_limit_bytes=60 << 20
        ),
        cost_estimate=pl.CostEstimate(
            flops=10 * HEADS * HD * rows * length,
            bytes_accessed=64 << 20,
            transcendentals=HEADS * rows * length,
        ),
        name="attention_backward",
    )(
        query_low,
        kv,
        log_totals,
        raw,
        cosine,
        sine_part,
        query_gain[None],
        key_gain[None],
        row_ids[None],
        key_ids[:, None],
        row_grads,
        out_weight,
        qkv_weight,
        *extra,
    )
    columns = outs[2].reshape(-1, outs[2].shape[-1])
    return outs[0], outs[1][0], outs[1][1], columns, outs[3], outs[4:]


def owner_sum_kernel(ctx_count, fsdp_count, shapes, shared, *refs):
    many = len(shapes)
    whole = many - shared
    ins, outs = refs[:many], refs[many : 2 * many]
    rest = refs[2 * many :]
    parts = [rest[8 * i : 8 * i + 8] for i in range(many)]
    shares = rest[8 * many : 8 * many + shared]
    send_z, recv_z = rest[8 * many + shared :]
    position = ctx_position(ctx_count)
    bits, place, along, mine, partners, _ = position
    pairs = ctx_count // 2
    across_line = [(place, lax.rem(along + d, fsdp_count)) for d in range(1, fsdp_count)]
    partner_barrier(partners + across_line)
    sums, own_copies = [], []
    for i, (block, _) in enumerate(shapes):
        held, first_in, later_in, own_sem = parts[i][:4]

        def give(b, i=i, block=block):
            at = pl.multiple_of((2 * b + 1 - mine[0]) * block, 16)
            return ins[i].at[pl.ds(at, block)]

        sums.append(
            Halving(
                position,
                block,
                give,
                lambda b, held=held: held.at[b],
                first_in,
                later_in,
                parts[i][4:8],
            )
        )
        sums[i].start_first()
        copies = []
        for b in range(pairs):
            at = pl.multiple_of((2 * b + mine[0]) * block, 16)
            copies.append(
                pltpu.make_async_copy(ins[i].at[pl.ds(at, block)], held.at[b], own_sem.at[b])
            )
            copies[-1].start()
        own_copies.append(copies)
    order = list(range(whole, many)) + list(range(whole))
    for i in order:
        for b in range(pairs):
            own_copies[i][b].wait()
            sums[i].end_first(b)
        sums[i].start(0)
    for stage in range(1, bits - 1):
        for i in order:
            sums[i].end(stage - 1)
            sums[i].start(stage)

    def share_copies(i):
        size = shapes[i][0] // fsdp_count
        return [
            pltpu.make_async_remote_copy(
                src_ref=sums[i].mine_now().at[pl.ds(pl.multiple_of(peer[1] * size, 16), size)],
                dst_ref=shares[i - whole].at[d],
                send_sem=send_z.at[i - whole, d],
                recv_sem=recv_z.at[i - whole, d],
                device_id=peer,
                device_id_type=MESH,
            )
            for d, peer in enumerate(across_line)
        ]

    for i in range(whole, many):
        sums[i].end(bits - 2)
        for copy in share_copies(i):
            copy.start()
    for i in range(whole):
        sums[i].end(bits - 2)
        outs[i][...] = sums[i].mine_now()[...]
    for i in range(whole, many):
        for copy in share_copies(i):
            copy.wait()
        size = shapes[i][0] // fsdp_count
        own = sums[i].mine_now()[pl.ds(pl.multiple_of(along * size, 16), size)]
        total = own.astype(jnp.float32)
        for d in range(fsdp_count - 1):
            total = total + shares[i - whole][d].astype(jnp.float32)
        outs[i][...] = total.astype(outs[i].dtype)


def owner_sums(arrays, shared):
    ctx_count = lax.axis_size("ctx")
    fsdp_count = lax.axis_size("fsdp")
    pairs = ctx_count // 2
    many = len(arrays)
    whole = many - shared
    low = jnp.bfloat16
    shapes = [(a.shape[0] // ctx_count, a.shape[1]) for a in arrays]
    share_shapes = [(s[0] // fsdp_count, s[1]) for s in shapes[whole:]]
    scratch = []
    for shape in shapes:
        parts = halving_scratch(ctx_count, *shape)
        scratch += [pltpu.VMEM((pairs,) + shape, low)] + parts[:2]
        scratch += [pltpu.SemaphoreType.DMA((pairs,))] + parts[2:]
    scratch += [pltpu.VMEM((fsdp_count - 1,) + s, low) for s in share_shapes]
    scratch += [pltpu.SemaphoreType.DMA((shared, fsdp_count - 1))] * 2
    total = sum(a.size for a in arrays)
    return pl.pallas_call(
        functools.partial(owner_sum_kernel, ctx_count, fsdp_count, shapes, shared),
        out_shape=[jax.ShapeDtypeStruct(s, low) for s in shapes[:whole] + share_shapes],
        in_specs=[pl.BlockSpec(memory_space=pl.ANY)] * many,
        out_specs=[pl.BlockSpec(memory_space=pltpu.VMEM)] * many,
        scratch_shapes=scratch,
        compiler_params=pltpu.CompilerParams(
            collective_id=0, has_side_effects=True, vmem_limit_bytes=48 << 20
        ),
        cost_estimate=pl.CostEstimate(flops=total, bytes_accessed=4 * total, transcendentals=0),
        name="owner_sums",
    )(*arrays)


class LineExchange:
    def __init__(self, count, own, gathered, outgoing, incoming, sems):
        self.count, self.steps = count, count - 1
        self.own, self.gathered = own, gathered
        self.outgoing, self.incoming = outgoing, incoming
        self.line_send, self.line_recv, self.back_send, self.back_recv = sems
        self.place = lax.axis_index("ctx")
        self.along = lax.axis_index("fsdp")
        self.width = outgoing.shape[-1]
        self.chunks = self.width // BACK_TILE

    def barrier(self):
        partner_barrier(
            [
                (self.place, lax.rem(self.along + d, self.count))
                for d in sorted({1, self.count - 1})
            ]
        )

    def line_copy(self, way, step, origin):
        toward = self.along + 1 if way == 0 else self.along - 1
        return pltpu.make_async_remote_copy(
            src_ref=self.own if step == 1 else self.gathered.at[origin],
            dst_ref=self.gathered.at[origin],
            send_sem=self.line_send.at[way, step - 1],
            recv_sem=self.line_recv.at[way, step - 1],
            device_id=(self.place, toward),
            device_id_type=MESH,
        )

    def forward(self, step):
        for way in range(2):
            origin = line_origin(self.along, way, step - 1)
            pl.when(line_goes(self.along, self.count, way, step))(
                lambda way=way, origin=origin: self.line_copy(way, step, origin).start()
            )

    def arrive(self, step):
        for way in range(2):
            origin = line_origin(self.along, way, step)
            pl.when(line_comes(self.along, self.count, way, step))(
                lambda way=way, origin=origin: self.line_copy(way, step, origin).wait_recv()
            )
        if step < self.steps:
            self.forward(step + 1)

    def back_copy(self, way, owner, chunk):
        toward = self.along + 1 if way == 0 else self.along - 1
        columns = pl.ds(chunk * BACK_TILE, BACK_TILE)
        landing = owner if way == 0 else jnp.where(owner == toward, self.count, owner)
        return pltpu.make_async_remote_copy(
            src_ref=self.outgoing.at[owner, :, columns],
            dst_ref=self.incoming.at[landing, :, columns],
            send_sem=self.back_send.at[way, owner, chunk],
            recv_sem=self.back_recv.at[way, owner, chunk],
            device_id=(self.place, toward),
            device_id_type=MESH,
        )

    def landed(self, way, owner, chunk, landing):
        columns = pl.ds(chunk * BACK_TILE, BACK_TILE)
        pltpu.make_async_remote_copy(
            src_ref=self.outgoing.at[owner, :, columns],
            dst_ref=self.incoming.at[landing, :, columns],
            send_sem=self.back_send.at[way, owner, chunk],
            recv_sem=self.back_recv.at[way, owner, chunk],
            device_id=(self.place, self.along),
            device_id_type=MESH,
        ).wait_recv()
        return self.incoming[landing, :, columns].astype(jnp.float32)

    def relays(self, way):
        return self.along >= 1 if way == 0 else self.along + 1 < self.count

    def run(self, compute, before_last):

        def one(way, step):
            back = 1 - way
            origin = line_origin(self.along, way, step)

            def work():
                def write(columns, tile):
                    self.outgoing[origin, :, columns] = tile.astype(self.outgoing.dtype)

                compute(origin, write)

                def begin():
                    for chunk in range(self.chunks):
                        self.back_copy(back, origin, chunk).start()

                pl.when(jnp.logical_not(self.relays(back)))(begin)

            pl.when(line_comes(self.along, self.count, way, step))(work)

        def relay(way, step):
            owner = step if way == 0 else self.steps - step
            passes = owner > self.along if way == 0 else owner < self.along

            def work():
                for chunk in range(self.chunks):
                    more = self.landed(way, owner, chunk, owner)
                    columns = pl.ds(chunk * BACK_TILE, BACK_TILE)
                    mine = self.outgoing[owner, :, columns].astype(jnp.float32)
                    self.outgoing[owner, :, columns] = (mine + more).astype(self.outgoing.dtype)
                    self.back_copy(way, owner, chunk).start()

            pl.when(self.relays(way) & passes)(work)

        for step in range(1, self.steps + 1):
            self.arrive(step)
            for way in range(2):
                one(way, step)
            if step == self.steps:
                before_last()
            for way in range(2):
                relay(way, step)

    def finish(self, total):
        for way in range(2):

            def receive(way=way):
                landing = self.along if way == 0 else self.count
                for chunk in range(self.chunks):
                    columns = pl.ds(chunk * BACK_TILE, BACK_TILE)
                    more = self.landed(way, self.along, chunk, landing)
                    total[:, columns] = total[:, columns] + more

            pl.when(self.relays(way))(receive)
        for step in range(1, self.steps + 1):
            for way in range(2):
                origin = line_origin(self.along, way, step - 1)

                def left(way=way, step=step, origin=origin):
                    self.line_copy(way, step, origin).wait_send()

                def returned(way=way, step=step):
                    for chunk in range(self.chunks):
                        self.back_copy(1 - way, line_origin(self.along, way, step), chunk).wait_send()

                pl.when(line_goes(self.along, self.count, way, step))(left)
                pl.when(line_comes(self.along, self.count, way, step))(returned)


def line_scratch(count, rows, columns):
    steps = count - 1
    chunks = columns // BACK_TILE
    return [
        pltpu.VMEM((count, rows, columns), jnp.bfloat16),
        pltpu.VMEM((count + 1, rows, columns), jnp.bfloat16),
        pltpu.SemaphoreType.DMA((2, steps)),
        pltpu.SemaphoreType.DMA((2, steps)),
        pltpu.SemaphoreType.DMA((2, count, chunks)),
        pltpu.SemaphoreType.DMA((2, count, chunks)),
    ]


def tile_at(t, size):
    return pl.ds(pl.multiple_of(t * size, size), size)


def feed_forward_kernel(
    count,
    rows_in,
    gate_hbm,
    up_hbm,
    down_hbm,
    total,
    gathered,
    gate_keep,
    up_keep,
    hidden_keep,
    gate_w,
    up_w,
    down_w,
    weight_sem,
    *parts,
):
    rows, width = rows_in.shape
    units = gate_w.shape[1]
    tile = FF_TILE
    line = LineExchange(count, rows_in, gathered, parts[0], parts[1], parts[2:])
    loads = []
    for n, (source, target) in enumerate(((gate_hbm, gate_w), (up_hbm, up_w), (down_hbm, down_w))):
        group = []
        for t in range(target.shape[1] // tile):
            at = (slice(None), pl.ds(t * tile, tile))
            group.append(pltpu.make_async_copy(source.at[at], target.at[at], weight_sem.at[n, t]))
        loads.append(group)
    for t in range(units // tile):
        loads[0][t].start()
        loads[1][t].start()
    for load in loads[2]:
        load.start()
    line.barrier()
    line.forward(1)
    gathered[line.along] = rows_in[...]

    def hidden_tile(origin, columns):
        at = pl.ds(pl.multiple_of(origin * rows, rows), rows)
        gate = forward_product(gathered[origin], gate_w[:, columns])
        up = forward_product(gathered[origin], up_w[:, columns])
        gate_keep[at, columns] = gate.astype(gate_keep.dtype)
        up_keep[at, columns] = up.astype(up_keep.dtype)
        hidden_keep[at, columns] = hidden_piece(gate, up).astype(hidden_keep.dtype)

    def out_tile(origin, columns):
        at = pl.ds(pl.multiple_of(origin * rows, rows), rows)
        return forward_product(hidden_keep[at], down_w[:, columns])

    for t in range(units // tile):
        loads[0][t].wait()
        loads[1][t].wait()
        hidden_tile(line.along, pl.ds(t * tile, tile))
    for t in range(width // tile):
        loads[2][t].wait()
        columns = pl.ds(t * tile, tile)
        total[:, columns] = out_tile(line.along, columns)

    def compute(origin, write):
        def hidden_step(t, carry):
            hidden_tile(origin, tile_at(t, tile))
            return carry

        def out_step(t, carry):
            columns = tile_at(t, tile)
            write(columns, out_tile(origin, columns))
            return carry

        lax.fori_loop(0, units // tile, hidden_step, 0)
        lax.fori_loop(0, width // tile, out_step, 0)

    line.run(compute, lambda: None)
    line.finish(total)


def feed_forward(rows_in, gate_weight, up_weight, down_weight):
    count = lax.axis_size("fsdp")
    rows, width = rows_in.shape
    units = gate_weight.shape[1]
    low = jnp.bfloat16
    vmem = pl.BlockSpec(memory_space=pltpu.VMEM)
    hbm = pl.BlockSpec(memory_space=pltpu.HBM)
    kept = jax.ShapeDtypeStruct((count * rows, units), low)
    out, gathered, gate, up, hidden = pl.pallas_call(
        functools.partial(feed_forward_kernel, count),
        out_shape=[
            jax.ShapeDtypeStruct((rows, width), jnp.float32),
            jax.ShapeDtypeStruct((count, rows, width), low),
            kept,
            kept,
            kept,
        ],
        in_specs=[vmem, hbm, hbm, hbm],
        out_specs=[vmem] * 5,
        scratch_shapes=[
            pltpu.VMEM((width, units), low),
            pltpu.VMEM((width, units), low),
            pltpu.VMEM((units, width), low),
            pltpu.SemaphoreType.DMA((3, max(width, units) // FF_TILE)),
        ]
        + line_scratch(count, rows, width),
        compiler_params=pltpu.CompilerParams(
            collective_id=4, has_side_effects=True, vmem_limit_bytes=56 << 20
        ),
        cost_estimate=pl.CostEstimate(
            flops=6 * count * rows * width * units,
            bytes_accessed=6 * width * units,
            transcendentals=count * rows * units,
        ),
        name="feed_forward",
    )(rows_in, gate_weight, up_weight, down_weight)
    return out, gathered.reshape(count * rows, width), gate, up, hidden


def hidden_pull_tile(grad, gate, up):
    slope = math.sqrt(2.0 / math.pi)
    square = gate * gate
    curve = jnp.tanh(slope * gate * (1.0 + 0.044715 * square))
    bend = 0.5 * (1.0 + curve)
    steep = bend + 0.5 * gate * (1.0 - curve * curve) * slope * (1.0 + 3.0 * 0.044715 * square)
    return grad * up * steep, grad * gate * bend


def feed_forward_backward_kernel(
    count,
    grads_in,
    gate_keep,
    up_keep,
    hidden_keep,
    tokens,
    gate_hbm,
    up_hbm,
    down_hbm,
    total,
    down_grad,
    gate_grad,
    up_grad,
    gathered,
    gate_back,
    up_back,
    gate_w,
    up_w,
    down_w,
    weight_sem,
    staged,
    staged_sem,
    *parts,
):
    rows, width = grads_in.shape
    units = gate_w.shape[1]
    tile = FF_TILE
    line = LineExchange(count, grads_in, gathered, parts[0], parts[1], parts[2:])
    loads = []
    for n, (source, target) in enumerate(((gate_hbm, gate_w), (up_hbm, up_w), (down_hbm, down_w))):
        group = []
        for t in range(target.shape[0] // tile):
            at = pl.ds(t * tile, tile)
            group.append(pltpu.make_async_copy(source.at[at], target.at[at], weight_sem.at[n, t]))
        loads.append(group)
    for load in loads[2]:
        load.start()
    for t in range(width // tile):
        loads[0][t].start()
        loads[1][t].start()
    line.barrier()
    line.forward(1)
    gathered[line.along] = grads_in[...]

    def hidden_tile(origin, columns):
        at = pl.ds(pl.multiple_of(origin * rows, rows), rows)
        grad = across(gathered[origin], down_w[columns])
        gate = gate_keep[at, columns].astype(jnp.float32)
        up = up_keep[at, columns].astype(jnp.float32)
        gate_pull, up_pull = hidden_pull_tile(grad, gate, up)
        gate_back[at, columns] = gate_pull.astype(gate_back.dtype)
        up_back[at, columns] = up_pull.astype(up_back.dtype)

    def out_tile(origin, columns):
        at = pl.ds(pl.multiple_of(origin * rows, rows), rows)
        return across(gate_back[at], gate_w[columns]) + across(up_back[at], up_w[columns])

    for t in range(units // tile):
        loads[2][t].wait()
        hidden_tile(line.along, pl.ds(t * tile, tile))
    for t in range(width // tile):
        loads[0][t].wait()
        loads[1][t].wait()
        columns = pl.ds(t * tile, tile)
        total[:, columns] = out_tile(line.along, columns)

    def compute(origin, write):
        def hidden_step(t, carry):
            hidden_tile(origin, tile_at(t, tile))
            return carry

        def out_step(t, carry):
            columns = tile_at(t, tile)
            write(columns, out_tile(origin, columns))
            return carry

        lax.fori_loop(0, units // tile, hidden_step, 0)
        lax.fori_loop(0, width // tile, out_step, 0)

    band = GRAD_TILE
    bands = width // band

    def stage(slot, which, t, target):
        return pltpu.make_async_copy(
            staged.at[slot, which], target.at[tile_at(t, band)], staged_sem.at[slot, which]
        )

    def grad_bands(jobs):
        def step(t, carry):
            slot = lax.rem(t, 2)
            for left, right, target, which in jobs:

                @pl.when(t >= 2)
                def _(target=target, which=which):
                    stage(slot, which, t, target).wait()

                product = over_rows(left(tile_at(t, band)), right[...])
                staged[slot, which] = product.astype(staged.dtype)
                stage(slot, which, t, target).start()
            return carry

        lax.fori_loop(0, bands, step, 0)
        for back in range(2):
            t = bands - 2 + back
            for _, _, target, which in jobs:
                stage(t % 2, which, t, target).wait()

    def grads_at(columns):
        return gathered[:, :, columns].reshape(count * rows, band)

    line.run(
        compute, lambda: grad_bands([(grads_at, hidden_keep, down_grad, 0)])
    )
    grad_bands(
        [
            (lambda columns: tokens[:, columns], gate_back, gate_grad, 0),
            (lambda columns: tokens[:, columns], up_back, up_grad, 1),
        ]
    )
    line.finish(total)


def feed_forward_backward(
    grads_in, gate_keep, up_keep, hidden_keep, tokens, gate_weight, up_weight, down_weight
):
    count = lax.axis_size("fsdp")
    rows, width = grads_in.shape
    units = gate_weight.shape[1]
    low = jnp.bfloat16
    vmem = pl.BlockSpec(memory_space=pltpu.VMEM)
    hbm = pl.BlockSpec(memory_space=pltpu.HBM)
    grad_shape = jax.ShapeDtypeStruct((width, units), low)
    return pl.pallas_call(
        functools.partial(feed_forward_backward_kernel, count),
        out_shape=[jax.ShapeDtypeStruct((rows, width), jnp.float32)] + [grad_shape] * 3,
        in_specs=[vmem] * 5 + [hbm] * 3,
        out_specs=[vmem] + [hbm] * 3,
        scratch_shapes=[
            pltpu.VMEM((count, rows, width), low),
            pltpu.VMEM((count * rows, units), low),
            pltpu.VMEM((count * rows, units), low),
            pltpu.VMEM((width, units), low),
            pltpu.VMEM((width, units), low),
            pltpu.VMEM((units, width), low),
            pltpu.SemaphoreType.DMA((3, max(width, units) // FF_TILE)),
            pltpu.VMEM((2, 2, GRAD_TILE, units), low),
            pltpu.SemaphoreType.DMA((2, 2)),
        ]
        + line_scratch(count, rows, width),
        compiler_params=pltpu.CompilerParams(
            collective_id=5, has_side_effects=True, vmem_limit_bytes=60 << 20
        ),
        cost_estimate=pl.CostEstimate(
            flops=12 * count * rows * width * units,
            bytes_accessed=12 * width * units,
            transcendentals=count * rows * units,
        ),
        name="feed_forward_backward",
    )(grads_in, gate_keep, up_keep, hidden_keep, tokens, gate_weight, up_weight, down_weight)


def body(
    tokens,
    per_layer,
    out_grad,
    segment_ids,
    query_weight,
    key_weight,
    value_weight,
    out_weight,
    left_weight,
    right_weight,
    gate_weight,
    up_weight,
    down_weight,
    side_gate,
    side_out,
    input_gain,
    laurel_gain,
    attn_gain,
    pre_gain,
    post_gain,
    side_gain,
    query_gain,
    key_gain,
):
    low = jnp.bfloat16
    inputs = tokens[0].astype(jnp.float32)
    extra_rows = per_layer[0].astype(jnp.float32)
    cotangent = out_grad[0].astype(jnp.float32)
    sequence_ids = segment_ids[0]
    rows_here, width = inputs.shape
    ctx_count = lax.axis_size("ctx")
    fsdp_count = lax.axis_size("fsdp")
    count = ctx_count * fsdp_count
    ctx_place = lax.axis_index("ctx")
    rank = left_weight.shape[1]
    side = side_gate.shape[1]
    query_width = HEADS * HD
    kv_width = KV_HEADS * HD
    query_pos = ctx_place * rows_here + jnp.arange(rows_here, dtype=jnp.int32)

    piece = width // count

    qkv_width = query_width + 2 * kv_width
    full_qkv, second_line = weight_gather(
        [[query_weight, key_weight, value_weight], [out_weight, side_gate]], 1
    )

    normed, input_pull = jax.vjp(rms_norm, inputs, input_gain)
    normed_low = normed.astype(low)
    qkv_raw = forward_product(normed_low, full_qkv)
    frequency = jnp.exp(
        jnp.arange(HD // 2).astype(jnp.float32) * (-2.0 * math.log(rope_theta) / HD)
    )
    angles = query_pos.astype(jnp.float32)[:, None] * frequency[None, :]
    cosine, sine_part = jnp.cos(angles), jnp.sin(angles)
    query_ids = lax.dynamic_slice_in_dim(sequence_ids, ctx_place * rows_here, rows_here)
    kv_all, query_low, attended_low, log_totals, full_second, *full_small = attention_forward(
        qkv_raw,
        cosine,
        sine_part,
        query_gain,
        key_gain,
        query_ids,
        sequence_ids,
        second_line,
        [left_weight, right_weight, side_out],
    )
    full_left, full_right, full_side_out = full_small
    full_left = full_left.reshape(width, rank)
    full_right = full_right.transpose(1, 0, 2).reshape(rank, width)
    full_side_out = full_side_out.reshape(side, width)
    full_second = full_second.reshape(width, -1)
    full_out = full_second[:, :width]
    full_side_gate = full_second[:, width:]
    left_low = forward_product(normed_low, full_left).astype(low)
    right_out = forward_product(left_low, full_right)
    attn_raw = forward_product(attended_low, full_out)

    def mix_piece(x, normed_in, attn_in, right_in, gain_one, gain_two, gain_three):
        mixed = (
            x + rms_norm(attn_in, gain_one) + normed_in + rms_norm(right_in, gain_two)
        ) * inverse_root
        return (mixed, rms_norm(mixed, gain_three))

    (mixed, ffn_in), mix_pull = jax.vjp(
        mix_piece, inputs, normed, attn_raw, right_out, attn_gain, laurel_gain, pre_gain
    )

    ffn_out, ffn_all, gate_raw, up_raw, hidden_low = feed_forward(
        ffn_in.astype(low), gate_weight, up_weight, down_weight
    )
    middle, middle_pull = jax.vjp(middle_piece, mixed, ffn_out, post_gain)
    middle_low = middle.astype(low)
    layer_gate = forward_product(middle_low, full_side_gate)
    layer_act, extra_pull = jax.vjp(hidden_piece, layer_gate, extra_rows)
    layer_low = layer_act.astype(low)
    layer_out = forward_product(layer_low, full_side_out)
    result, out_pull = jax.vjp(middle_piece, middle, layer_out, side_gain)

    middle_grad_one, layer_out_grad, side_gain_grad = out_pull(cotangent)
    layer_grad_low = layer_out_grad.astype(low)
    side_out_grad = over_rows(layer_low, layer_grad_low)
    layer_gate_grad, extra_grad = extra_pull(across(layer_grad_low, full_side_out))
    gate_grad_low = layer_gate_grad.astype(low)
    side_gate_grad = over_rows(gate_grad_low, middle_low)
    mixed_grad_one, ffn_out_grad, post_gain_grad = middle_pull(
        middle_grad_one + across(gate_grad_low, full_side_gate)
    )
    ffn_in_grad, down_weight_grad, gate_weight_grad, up_weight_grad = feed_forward_backward(
        ffn_out_grad.astype(low),
        gate_raw,
        up_raw,
        hidden_low,
        ffn_all,
        gate_weight,
        up_weight,
        down_weight,
    )
    ffn_in_grad, late_low = lax.optimization_barrier((ffn_in_grad, (attended_low, normed_low)))
    attended_all, normed_all = (gather(part, "fsdp") for part in late_low)
    (
        inputs_grad_one,
        normed_grad_one,
        attn_raw_grad,
        right_out_grad,
        attn_gain_grad,
        laurel_gain_grad,
        pre_gain_grad,
    ) = mix_pull((mixed_grad_one, ffn_in_grad))
    attn_grad_low = attn_raw_grad.astype(low)
    right_grad_low = right_out_grad.astype(low)
    right_weight_grad = over_rows(right_grad_low, left_low)
    left_grad_low = across(right_grad_low, full_right).astype(low)
    left_weight_grad = over_rows(normed_low, left_grad_low)
    (
        qkv_back_low,
        query_gain_grad,
        key_gain_grad,
        out_columns,
        normed_grad_two,
        ffn_sums,
    ) = attention_backward(
        query_low,
        kv_all,
        log_totals,
        qkv_raw,
        cosine,
        sine_part,
        query_gain,
        key_gain,
        query_ids,
        sequence_ids,
        attn_grad_low,
        full_second,
        full_qkv,
        [gate_weight_grad, up_weight_grad],
    )
    down_low, qkv_back_low = lax.optimization_barrier((down_weight_grad, qkv_back_low))
    down_weight_grad = scatter_sum(down_low, "ctx")
    normed_grad_two = normed_grad_two + across(left_grad_low, full_left)
    inputs_grad_two, input_gain_grad = input_pull(normed_grad_one + normed_grad_two)
    block_out = result.astype(low)[None]
    tokens_grad = (inputs_grad_one + inputs_grad_two).astype(low)[None]
    per_layer_grad = extra_grad.astype(low)[None]

    def columns_to_owner(x):
        parts = x.reshape(rows_here, fsdp_count, -1).transpose(1, 0, 2)
        return lax.all_to_all(parts, "fsdp", 0, 0, tiled=True).reshape(fsdp_count * rows_here, -1)

    out_weight_grad = over_rows(attended_all, out_columns)
    qkv_parts = jnp.concatenate(
        [
            part.reshape(rows_here, fsdp_count, -1)
            for part in (
                qkv_back_low[:, :query_width],
                qkv_back_low[:, query_width : query_width + kv_width],
                qkv_back_low[:, query_width + kv_width :],
            )
        ],
        axis=2,
    )
    qkv_columns = columns_to_owner(qkv_parts.reshape(rows_here, -1))
    qkv_weight_grad = over_rows(normed_all, qkv_columns)

    small_gains = [
        jnp.pad(g.reshape(count, -1), ((0, 0), (0, piece - g.shape[0] // count))).reshape(-1)
        for g in (query_gain_grad, key_gain_grad)
    ]
    gains = jnp.stack(
        [
            input_gain_grad,
            laurel_gain_grad,
            attn_gain_grad,
            pre_gain_grad,
            post_gain_grad,
            side_gain_grad,
            *small_gains,
        ]
    )
    gate_blocks = side_gate_grad.astype(low).reshape(side, ctx_count, -1).transpose(1, 0, 2)
    gate_columns = width // ctx_count
    tall = jnp.concatenate(
        [
            left_weight_grad.astype(low),
            right_weight_grad.astype(low),
            jnp.pad(gains.astype(low).T, ((0, 0), (0, 128 - gains.shape[0]))),
        ],
        axis=1,
    )
    out_blocks = side_out_grad.astype(low).reshape(
        ctx_count, side // ctx_count, fsdp_count, width // fsdp_count
    )
    out_blocks = out_blocks.transpose(0, 2, 1, 3).reshape(-1, width // fsdp_count)
    out_weight_grad, qkv_weight_grad, tall, gate_blocks, side_out_grad = owner_sums(
        [
            out_weight_grad.astype(low),
            qkv_weight_grad.astype(low),
            tall,
            gate_blocks.reshape(-1, gate_columns),
            out_blocks,
        ],
        3,
    )
    gate_weight_grad, up_weight_grad = ffn_sums
    down_weight_grad = down_weight_grad.T
    query_part = query_width // fsdp_count
    kv_part = kv_width // fsdp_count
    query_weight_grad = qkv_weight_grad[:, :query_part]
    key_weight_grad = qkv_weight_grad[:, query_part : query_part + kv_part]
    value_weight_grad = qkv_weight_grad[:, query_part + kv_part :]
    wide = jnp.float32
    tall = tall.astype(wide)
    left_weight_grad = tall[:, :rank]
    right_weight_grad = tall[:, rank : 2 * rank].T
    gains = tall[:, 2 * rank : 2 * rank + 8].T
    small_part = query_gain.shape[0] // count
    side_gate_grad = gate_blocks.astype(wide).T
    side_out_grad = side_out_grad.astype(wide)
    return (
        block_out,
        tokens_grad,
        per_layer_grad,
        query_weight_grad.astype(wide),
        key_weight_grad.astype(wide),
        value_weight_grad.astype(wide),
        out_weight_grad.astype(wide),
        left_weight_grad,
        right_weight_grad,
        gate_weight_grad.astype(wide),
        up_weight_grad.astype(wide),
        down_weight_grad.astype(wide),
        side_gate_grad,
        side_out_grad,
        *(gains[n] for n in range(6)),
        gains[6, :small_part],
        gains[7, :small_part],
    )


def solution(mesh):
    placed = (
        P("fsdp", "ctx", None),
        P("fsdp", "ctx", None),
        P("fsdp", "ctx", None),
        P("fsdp", None),
        P("fsdp", None),
        P("fsdp", None),
        P("fsdp", None),
        P("fsdp", None),
        P("fsdp", None),
        P(None, "fsdp"),
        P(None, "fsdp"),
        P(None, "fsdp"),
        P("fsdp", None),
        P("fsdp", None),
        P("fsdp", None),
        P(),
        P(),
        P(),
        P(),
        P(),
        P(),
        P(),
        P(),
    )
    return jax.shard_map(
        body,
        mesh=mesh,
        in_specs=placed,
        out_specs=(
            P("fsdp", "ctx", None),
            P("fsdp", "ctx", None),
            P("fsdp", "ctx", None),
            P("ctx", "fsdp"),
            P("ctx", "fsdp"),
            P("ctx", "fsdp"),
            P("ctx", "fsdp"),
            P(("ctx", "fsdp"), None),
            P(None, ("ctx", "fsdp")),
            P("ctx", "fsdp"),
            P("ctx", "fsdp"),
            P("fsdp", "ctx"),
            P("ctx", "fsdp"),
            P("ctx", "fsdp"),
            P(("ctx", "fsdp")),
            P(("ctx", "fsdp")),
            P(("ctx", "fsdp")),
            P(("ctx", "fsdp")),
            P(("ctx", "fsdp")),
            P(("ctx", "fsdp")),
            P(("ctx", "fsdp")),
            P(("ctx", "fsdp")),
        ),
        check_vma=False,
    )
```

```python
import functools
import math

import jax
import jax.numpy as jnp
from jax import lax
from jax.experimental import pallas as pl
from jax.experimental.pallas import tpu as pltpu
from jax.sharding import PartitionSpec as P

HEADS = 8
KV_HEADS = 2
HD = 256
MESH = pl.DeviceIdType.MESH
FF_TILE = 512
BACK_TILE = FF_TILE
GRAD_TILE = 256


epsilon = 1e-06
rope_theta = 1000000.0
masked_score = -1e30
inverse_root = 1.0 / math.sqrt(2.0)


def rms_norm(v, factor):
    return v * lax.rsqrt(jnp.mean(v * v, axis=-1, keepdims=True) + epsilon) * factor


def forward_product(a, b):
    return jnp.dot(a, b, preferred_element_type=jnp.float32)


def across(a, b):
    return lax.dot_general(a, b, (((1,), (1,)), ((), ())), preferred_element_type=jnp.float32)


def over_rows(a, b):
    return lax.dot_general(a, b, (((0,), (0,)), ((), ())), preferred_element_type=jnp.float32)


def hidden_piece(gate_in, up_in):
    return jax.nn.gelu(gate_in, approximate=True) * up_in


def middle_piece(mixed_in, ffn_in_rows, factor):
    return mixed_in + rms_norm(ffn_in_rows, factor)


def gather(x, axis):
    return lax.all_gather(x, axis, axis=0, tiled=True)


def scatter_sum(x, axis):
    return lax.psum_scatter(x, axis, scatter_dimension=0, tiled=True)


def partner_barrier(partners):
    barrier = pltpu.get_barrier_semaphore()
    for partner in partners:
        pl.semaphore_signal(barrier, inc=1, device_id=partner, device_id_type=MESH)
    pl.semaphore_wait(barrier, len(partners))


def add_rows(target, source, first, rows):
    tile = 16

    def one(step, carry):
        at = pl.ds(pl.multiple_of(first + step * tile, tile), tile)
        from_at = pl.ds(pl.multiple_of(step * tile, tile), tile)
        total = target[at].astype(jnp.float32) + source[from_at].astype(jnp.float32)
        target[at] = total.astype(target.dtype)
        return carry

    lax.fori_loop(0, rows // tile, one, 0)


def held_index(mine, done, bits):
    return tuple(slice(None) if t in done else mine[t] for t in reversed(range(bits)))


def ctx_position(ctx_count):
    bits = ctx_count.bit_length() - 1
    place = lax.axis_index("ctx")
    along = lax.axis_index("fsdp")
    mine = [lax.rem(place // (1 << t), 2) for t in range(bits)]
    partners = [(place + (1 - 2 * mine[t]) * (1 << t), along) for t in range(bits)]
    orders = [list(range(1, bits)), list(range(bits - 1, 0, -1))]
    return bits, place, along, mine, partners, orders


def spread_copy(out, lead, half, stage, position, send_sem, recv_sem):
    bits, _, _, mine, partners, orders = position
    order = orders[half]
    rows = out.shape[-2] // 2
    at = lead + held_index(mine, order[:stage], bits) + (pl.ds(half * rows, rows),)
    return pltpu.make_async_remote_copy(
        src_ref=out.at[at],
        dst_ref=out.at[at],
        send_sem=send_sem.at[half, stage],
        recv_sem=recv_sem.at[half, stage],
        device_id=partners[order[stage]],
        device_id_type=MESH,
    )


def sibling_copy(out, lead, position, send_sem, recv_sem):
    bits, _, _, mine, partners, orders = position
    at = lead + held_index(mine, orders[0], bits)
    return pltpu.make_async_remote_copy(
        src_ref=out.at[at],
        dst_ref=out.at[at],
        send_sem=send_sem,
        recv_sem=recv_sem,
        device_id=partners[0],
        device_id_type=MESH,
    )


def weight_gather_kernel(ctx_count, fsdp_count, members, spread, *refs):
    sets = len(members)
    own_count = sum(members)
    own, outs = refs[:own_count], refs[own_count : own_count + sets]
    rest = refs[own_count + sets :]
    passing, pieces = rest[:own_count], rest[own_count : own_count + sets]
    own_sem, line_send, line_recv, send_sem, recv_sem, core_send, core_recv = rest[
        own_count + sets :
    ]
    position = ctx_position(ctx_count)
    bits, place, along, mine, partners, _ = position
    steps = fsdp_count - 1
    here = held_index(mine, (), bits)
    columns = []
    for i in range(sets):
        start = 0
        for _ in range(members[i]):
            wide = own[len(columns)].shape[-1]
            columns.append((i, pl.ds(start, wide)))
            start += wide
    piece_loads = [
        pltpu.make_async_copy(own[n].at[here], pieces[i].at[:, at], own_sem.at[0, n])
        for n, (i, at) in enumerate(columns)
    ]
    for load in piece_loads:
        load.start()
    loads = [
        pltpu.make_async_copy(source, passing[n], own_sem.at[1, n])
        for n, source in enumerate(own)
    ]
    for load in loads:
        load.start()
    partner_barrier(
        partners
        + [(place, lax.rem(along + 1, fsdp_count)), (place, lax.rem(along + steps, fsdp_count))]
    )

    def line_copy(i, way, step, origin):
        toward = along + 1 if way == 0 else along - 1
        first, target = pieces[i], outs[i].at[(origin,) + here]
        return pltpu.make_async_remote_copy(
            src_ref=first if step == 1 else target,
            dst_ref=target,
            send_sem=line_send.at[i, way, step - 1],
            recv_sem=line_recv.at[i, way, step - 1],
            device_id=(place, toward),
            device_id_type=MESH,
        )

    def comes(way, step):
        return along >= step if way == 0 else along + step < fsdp_count

    def goes(way, step):
        if way == 0:
            return (along + 1 < fsdp_count) & (along >= step - 1)
        return (along >= 1) & (along + step - 1 < fsdp_count)

    def origin_of(way, step):
        return along - step if way == 0 else along + step

    def each(flag, action):
        pl.when(flag)(action)

    def forward(i, step):
        for way in range(2):
            each(goes(way, step), lambda: line_copy(i, way, step, origin_of(way, step - 1)).start())

    for load in piece_loads:
        load.wait()
    for i in range(sets):
        forward(i, 1)
    stores = []
    for n, load in enumerate(loads):
        load.wait()
        i, at = columns[n]
        target = outs[i].at[(along,) + (slice(None),) * (bits + 1) + (at,)]
        stores.append(pltpu.make_async_copy(passing[n], target, own_sem.at[2, n]))
        stores[-1].start()

    def stage_copies(i, way, step, stage):
        lead = (origin_of(way, step),)
        at = (i, way, step - 1)
        return [
            spread_copy(outs[i], lead, half, stage, position, send_sem.at[at], recv_sem.at[at])
            for half in range(2)
        ]

    def core_copy(i, way, step):
        at = (i, way, step - 1)
        return sibling_copy(
            outs[i], (origin_of(way, step),), position, core_send.at[at], core_recv.at[at]
        )

    def arrive(i, step):
        for way in range(2):

            def landed():
                line_copy(i, way, step, origin_of(way, step)).wait_recv()

            each(comes(way, step), landed)
        if step < steps:
            forward(i, step + 1)
        if i >= spread:
            return
        for way in range(2):

            def begin():
                for copy in stage_copies(i, way, step, 0):
                    copy.start()

            each(comes(way, step), begin)

    def advance(i, step, stage):
        if i >= spread:
            return
        for way in range(2):

            def proceed():
                for copy in stage_copies(i, way, step, stage):
                    copy.wait_recv()
                if stage < bits - 2:
                    for copy in stage_copies(i, way, step, stage + 1):
                        copy.start()
                else:
                    core_copy(i, way, step).start()

            each(comes(way, step), proceed)

    order = [(i, step) for i in range(sets) for step in range(1, steps + 1)]
    for tick in range(len(order) + bits - 1):
        if tick < len(order):
            arrive(*order[tick])
        for stage in range(bits - 1):
            at = tick - 1 - stage
            if 0 <= at < len(order):
                advance(*order[at], stage)
    for copy in stores:
        copy.wait()
    for i, step in order:
        for way in range(2):

            def leave():
                line_copy(i, way, step, origin_of(way, step - 1)).wait_send()

            def finish():
                for stage in range(bits - 1):
                    for copy in stage_copies(i, way, step, stage):
                        copy.wait_send()
                core_copy(i, way, step).wait()

            each(goes(way, step), leave)
            if i < spread:
                each(comes(way, step), finish)


def weight_gather(own, spread):
    ctx_count = lax.axis_size("ctx")
    fsdp_count = lax.axis_size("fsdp")
    bits = ctx_count.bit_length() - 1
    steps = fsdp_count - 1
    sets = len(own)
    cut = (2,) * bits
    low = jnp.bfloat16
    flat = [w.reshape(cut + (w.shape[0] // ctx_count, w.shape[1])) for group in own for w in group]
    pieces = [(g[0].shape[0] // ctx_count, sum(w.shape[1] for w in g)) for g in own]
    out_shapes = [(fsdp_count,) + cut + p for p in pieces]
    total = sum(rows * columns for rows, columns in pieces) * ctx_count * fsdp_count
    outs = pl.pallas_call(
        functools.partial(
            weight_gather_kernel, ctx_count, fsdp_count, [len(g) for g in own], spread
        ),
        out_shape=[jax.ShapeDtypeStruct(s, low) for s in out_shapes],
        in_specs=[pl.BlockSpec(memory_space=pltpu.HBM)] * len(flat),
        out_specs=[pl.BlockSpec(memory_space=pltpu.HBM)] * len(out_shapes),
        scratch_shapes=[pltpu.VMEM(w.shape, low) for w in flat]
        + [pltpu.VMEM(p, low) for p in pieces]
        + [
            pltpu.SemaphoreType.DMA((3, len(flat))),
            pltpu.SemaphoreType.DMA((sets, 2, steps)),
            pltpu.SemaphoreType.DMA((sets, 2, steps)),
            pltpu.SemaphoreType.DMA((spread, 2, steps, 2, bits - 1)),
            pltpu.SemaphoreType.DMA((spread, 2, steps, 2, bits - 1)),
            pltpu.SemaphoreType.DMA((spread, 2, steps)),
            pltpu.SemaphoreType.DMA((spread, 2, steps)),
        ],
        compiler_params=pltpu.CompilerParams(
            collective_id=1, has_side_effects=True, vmem_limit_bytes=60 << 20
        ),
        cost_estimate=pl.CostEstimate(flops=0, bytes_accessed=4 * total, transcendentals=0),
        name="weight_gather",
    )(*flat)
    return [o.reshape(-1, o.shape[-1]) for o in outs[:spread]] + list(outs[spread:])


def line_comes(along, count, way, step):
    return along >= step if way == 0 else along + step < count


def line_goes(along, count, way, step):
    if way == 0:
        return (along + 1 < count) & (along >= step - 1)
    return (along >= 1) & (along + step - 1 < count)


def line_origin(along, way, step):
    return along - step if way == 0 else along + step


class LineGather:
    def __init__(self, count, owns, outs, passing, own_sems, send_sems, recv_sems):
        self.count, self.steps = count, count - 1
        self.owns, self.outs, self.passing = owns, outs, passing
        self.own_sems, self.send_sems, self.recv_sems = own_sems, send_sems, recv_sems
        self.place = lax.axis_index("ctx")
        self.along = lax.axis_index("fsdp")
        self.done = 0

    def partners(self):
        return [(self.place, lax.rem(self.along + d, self.count)) for d in sorted({1, self.steps})]

    def own_copies(self, n):
        return (
            pltpu.make_async_copy(self.owns[n], self.passing[n], self.own_sems.at[0, n]),
            pltpu.make_async_copy(self.passing[n], self.outs[n].at[self.along], self.own_sems.at[1, n]),
        )

    def copies(self, way, step, origin):
        toward = self.along + 1 if way == 0 else self.along - 1
        return [
            pltpu.make_async_remote_copy(
                src_ref=self.owns[n] if step == 1 else self.outs[n].at[origin],
                dst_ref=self.outs[n].at[origin],
                send_sem=self.send_sems.at[n, way, step - 1],
                recv_sem=self.recv_sems.at[n, way, step - 1],
                device_id=(self.place, toward),
                device_id_type=MESH,
            )
            for n in range(len(self.owns))
        ]

    def forward(self, step):
        for way in range(2):

            def go(way=way):
                for copy in self.copies(way, step, line_origin(self.along, way, step - 1)):
                    copy.start()

            pl.when(line_goes(self.along, self.count, way, step))(go)

    def load(self):
        for n in range(len(self.owns)):
            self.own_copies(n)[0].start()

    def store(self):
        for n in range(len(self.owns)):
            self.own_copies(n)[0].wait()
            self.own_copies(n)[1].start()

    def arrive(self):
        if self.done == self.steps:
            return
        self.done += 1
        step = self.done
        for way in range(2):

            def land(way=way):
                for copy in self.copies(way, step, line_origin(self.along, way, step)):
                    copy.wait_recv()

            pl.when(line_comes(self.along, self.count, way, step))(land)
        if step < self.steps:
            self.forward(step + 1)

    def finish(self):
        while self.done < self.steps:
            self.arrive()
        for n in range(len(self.owns)):
            self.own_copies(n)[1].wait()
        for step in range(1, self.steps + 1):
            for way in range(2):

                def leave(way=way, step=step):
                    for copy in self.copies(way, step, line_origin(self.along, way, step - 1)):
                        copy.wait_send()

                pl.when(line_goes(self.along, self.count, way, step))(leave)


class Halving:
    def __init__(self, position, rows, give, held, first_in, later_in, sems):
        self.bits, self.place, self.along, self.mine, self.partners, self.orders = position
        self.rows, self.give, self.held = rows, give, held
        self.first_in, self.later_in = first_in, later_in
        self.send_zero, self.recv_zero, self.send_sem, self.recv_sem = sems
        self.pairs = 1 << (self.bits - 1)

    def first_copy(self, b):
        return pltpu.make_async_remote_copy(
            src_ref=self.give(b),
            dst_ref=self.first_in.at[b],
            send_sem=self.send_zero.at[b],
            recv_sem=self.recv_zero.at[b],
            device_id=self.partners[0],
            device_id_type=MESH,
        )

    def start_first(self):
        for b in range(self.pairs):
            self.first_copy(b).start()

    def end_first(self, b):
        self.first_copy(b).wait()
        add_rows(self.held(b), self.first_in.at[b], 0, self.rows)

    def slot_of(self, stage):
        return sum(1 << (self.bits - 2 - s) for s in range(stage))

    def block_sets(self, half, stage):
        order = self.orders[half]
        bit = order[stage]
        free = order[stage + 1 :]
        fixed = sum(self.mine[t] * (1 << (t - 1)) for t in order[:stage])
        sent, kept = [], []
        for combo in range(1 << len(free)):
            value = sum(((combo >> n) & 1) << (t - 1) for n, t in enumerate(free))
            sent.append(fixed + (1 - self.mine[bit]) * (1 << (bit - 1)) + value)
            kept.append(fixed + self.mine[bit] * (1 << (bit - 1)) + value)
        return bit, sent, kept

    def stage_copies(self, stage):
        rows = self.rows // 2
        copies = []
        for half in range(2):
            bit, sent, _ = self.block_sets(half, stage)
            for n, block in enumerate(sent):
                at = (half, self.slot_of(stage) + n)
                copies.append(
                    pltpu.make_async_remote_copy(
                        src_ref=self.held(block).at[pl.ds(half * rows, rows)],
                        dst_ref=self.later_in.at[at],
                        send_sem=self.send_sem.at[at],
                        recv_sem=self.recv_sem.at[at],
                        device_id=self.partners[bit],
                        device_id_type=MESH,
                    )
                )
        return copies

    def start(self, stage):
        for copy in self.stage_copies(stage):
            copy.start()

    def end(self, stage):
        for copy in self.stage_copies(stage):
            copy.wait()
        rows = self.rows // 2
        for half in range(2):
            _, _, kept = self.block_sets(half, stage)
            for n, block in enumerate(kept):
                at = (half, self.slot_of(stage) + n)
                add_rows(self.held(block), self.later_in.at[at], half * rows, rows)

    def mine_now(self):
        return self.held(self.place // 2)


def halving_scratch(ctx_count, rows, columns):
    pairs = ctx_count // 2
    return [
        pltpu.VMEM((pairs, rows, columns), jnp.bfloat16),
        pltpu.VMEM((2, pairs - 1, rows // 2, columns), jnp.bfloat16),
        pltpu.SemaphoreType.DMA((pairs,)),
        pltpu.SemaphoreType.DMA((pairs,)),
        pltpu.SemaphoreType.DMA((2, pairs - 1)),
        pltpu.SemaphoreType.DMA((2, pairs - 1)),
    ]


def unit_rows(v):
    scale = lax.rsqrt(jnp.mean(v * v, axis=-1, keepdims=True) + epsilon)
    return v * scale, scale


def turned(v, cosine, sine_part):
    halfway = v.shape[-1] // 2
    leading, trailing = v[:, :halfway], v[:, halfway:]
    return jnp.concatenate(
        [leading * cosine - trailing * sine_part, trailing * cosine + leading * sine_part], axis=-1
    )


def unit_rows_pull(v, grad, gain):
    unit, scale = unit_rows(v)
    gain_grad = jnp.sum(grad * unit, axis=0, keepdims=True)
    scaled = grad * gain
    return scale * (scaled - unit * jnp.mean(unit * scaled, axis=-1, keepdims=True)), gain_grad


def head_at(h):
    return pl.ds(pl.multiple_of(h * HD, HD), HD)


def attention_forward_kernel(
    ctx_count,
    lines,
    raw,
    cosine_ref,
    sine_ref,
    query_gain,
    key_gain,
    row_ids,
    key_ids,
    _,
    *refs,
):
    line_owns, refs = refs[:lines], refs[lines:]
    kv, query_low, attended_low, log_totals, weights_out = refs[:5]
    line_outs, refs = refs[5 : 5 + lines], refs[5 + lines :]
    bias, send_sem, recv_sem, core_send, core_recv, weight_sems, weight_core_sems = refs[:7]
    line = LineGather(
        weights_out.shape[0], line_owns, line_outs, refs[7 : 7 + lines], *refs[7 + lines :]
    )
    line.load()
    position = ctx_position(ctx_count)
    bits, place, along, mine, partners, _ = position
    count = weights_out.shape[0]
    units = [(way, step) for step in range(1, count) for way in range(2)]

    def weight_copies(way, step, stage):
        lead = (line_origin(along, way, step),)
        at = (way, step - 1)
        return [
            spread_copy(
                weights_out,
                lead,
                half,
                stage,
                position,
                weight_sems.at[(0,) + at],
                weight_sems.at[(1,) + at],
            )
            for half in range(2)
        ]

    def weight_core_copy(way, step):
        at = (way, step - 1)
        return sibling_copy(
            weights_out,
            (line_origin(along, way, step),),
            position,
            weight_core_sems.at[(0,) + at],
            weight_core_sems.at[(1,) + at],
        )

    def each_unit(action):
        for way, step in units:
            pl.when(line_comes(along, count, way, step))(functools.partial(action, way, step))

    def start_weights(stage):
        def action(way, step):
            for copy in weight_copies(way, step, stage):
                copy.start()

        each_unit(action)

    def land_weights(stage):
        def action(way, step):
            for copy in weight_copies(way, step, stage):
                copy.wait_recv()

        each_unit(action)

    rows = raw.shape[0]
    groups = HEADS // KV_HEADS
    length = ctx_count * rows
    here = held_index(mine, (), bits)
    cosine, sine_part = cosine_ref[...], sine_ref[...]
    partner_barrier(partners + line.partners())
    start_weights(0)
    line.forward(1)
    for k in range(KV_HEADS):
        unit, _ = unit_rows(raw[:, pl.ds((HEADS + k) * HD, HD)])
        key = turned(unit * key_gain[...], cosine, sine_part)
        kv[here + (slice(None), pl.ds(k * HD, HD))] = key.astype(kv.dtype)
        value, _ = unit_rows(raw[:, pl.ds((HEADS + KV_HEADS + k) * HD, HD)])
        kv[here + (slice(None), pl.ds((KV_HEADS + k) * HD, HD))] = value.astype(kv.dtype)

    def copies_of(stage):
        return [spread_copy(kv, (), h, stage, position, send_sem, recv_sem) for h in range(2)]

    for copy in copies_of(0):
        copy.start()
    line.store()
    allowed = (row_ids[...] == key_ids[...]) & (
        lax.broadcasted_iota(jnp.int32, (rows, length), 1)
        <= lax.broadcasted_iota(jnp.int32, (rows, length), 0) + place * rows
    )
    bias[...] = jnp.where(allowed, 0.0, masked_score)

    def one_query(h, carry):
        unit, _ = unit_rows(raw[:, head_at(h)])
        query = turned(unit * query_gain[...], cosine, sine_part)
        query_low[:, head_at(h)] = query.astype(query_low.dtype)
        return carry

    lax.fori_loop(0, HEADS, one_query, 0)
    for stage in range(1, bits - 1):
        for copy in copies_of(stage - 1):
            copy.wait()
        for copy in copies_of(stage):
            copy.start()
        land_weights(stage - 1)
        start_weights(stage)
        line.arrive()
    for copy in copies_of(bits - 2):
        copy.wait()
    last = sibling_copy(kv, (), position, core_send, core_recv)
    last.start()
    last.wait()
    everywhere = (slice(None),) * (bits + 1)
    for k in range(KV_HEADS):
        key = kv[everywhere + (pl.ds(k * HD, HD),)].reshape(length, HD)
        value = kv[everywhere + (pl.ds((KV_HEADS + k) * HD, HD),)].reshape(length, HD)

        def one_head(g, carry, k=k, key=key, value=value):
            h = k * groups + g
            scores = across(query_low[:, head_at(h)], key) + bias[...]
            row_max = jnp.max(scores, axis=-1, keepdims=True)
            weights = jnp.exp(scores - row_max)
            row_total = jnp.sum(weights, axis=-1, keepdims=True)
            weights = (weights * (1.0 / row_total)).astype(value.dtype)
            attended_low[:, head_at(h)] = forward_product(weights, value).astype(attended_low.dtype)
            log_total = jnp.broadcast_to(row_max + jnp.log(row_total), (rows, rows))
            log_totals[h] = log_total.T[:8]
            return carry

        lax.fori_loop(0, groups, one_head, 0)
        line.arrive()
        if k == KV_HEADS - 2:
            land_weights(bits - 2)
            each_unit(lambda way, step: weight_core_copy(way, step).start())

    def finish(way, step):
        for stage in range(bits - 1):
            for copy in weight_copies(way, step, stage):
                copy.wait_send()
        weight_core_copy(way, step).wait()

    each_unit(finish)
    line.finish()


def attention_forward(raw, cosine, sine_part, query_gain, key_gain, row_ids, key_ids, weights, lines):
    ctx_count = lax.axis_size("ctx")
    steps = lax.axis_size("fsdp") - 1
    hbm = pl.BlockSpec(memory_space=pltpu.HBM)
    bits = ctx_count.bit_length() - 1
    rows = raw.shape[0]
    length = ctx_count * rows
    low = jnp.bfloat16
    vmem = pl.BlockSpec(memory_space=pltpu.VMEM)
    return pl.pallas_call(
        functools.partial(attention_forward_kernel, ctx_count, len(lines)),
        out_shape=[
            jax.ShapeDtypeStruct((2,) * bits + (rows, 2 * KV_HEADS * HD), low),
            jax.ShapeDtypeStruct((rows, HEADS * HD), low),
            jax.ShapeDtypeStruct((rows, HEADS * HD), low),
            jax.ShapeDtypeStruct((HEADS, 8, rows), jnp.float32),
            jax.ShapeDtypeStruct(weights.shape, low),
        ]
        + [jax.ShapeDtypeStruct((steps + 1,) + w.shape, low) for w in lines],
        in_specs=[vmem] * 7 + [hbm] * (1 + len(lines)),
        out_specs=[vmem] * 4 + [hbm] * (1 + len(lines)),
        input_output_aliases={7: 4},
        scratch_shapes=[
            pltpu.VMEM((rows, length), jnp.float32),
            pltpu.SemaphoreType.DMA((2, bits - 1)),
            pltpu.SemaphoreType.DMA((2, bits - 1)),
            pltpu.SemaphoreType.DMA,
            pltpu.SemaphoreType.DMA,
            pltpu.SemaphoreType.DMA((2, 2, steps, 2, bits - 1)),
            pltpu.SemaphoreType.DMA((2, 2, steps)),
        ]
        + [pltpu.VMEM(w.shape, low) for w in lines]
        + [
            pltpu.SemaphoreType.DMA((2, len(lines))),
            pltpu.SemaphoreType.DMA((len(lines), 2, steps)),
            pltpu.SemaphoreType.DMA((len(lines), 2, steps)),
        ],
        compiler_params=pltpu.CompilerParams(
            collective_id=2, has_side_effects=True, vmem_limit_bytes=56 << 20
        ),
        cost_estimate=pl.CostEstimate(
            flops=4 * HEADS * HD * rows * length,
            bytes_accessed=8 << 20,
            transcendentals=HEADS * rows * length,
        ),
        name="attention_forward",
    )(
        raw,
        cosine,
        sine_part,
        query_gain[None],
        key_gain[None],
        row_ids[:, None],
        key_ids[None],
        weights,
        *lines,
    )


def attention_backward_kernel(ctx_count, fsdp_count, extra, exchange, *refs):
    (
        query_low,
        kv,
        log_totals,
        raw,
        cosine_ref,
        sine_ref,
        query_gain,
        key_gain,
        row_ids,
        key_ids,
        row_grads,
        out_weight,
        qkv_weight,
    ) = refs[:13]
    many = len(extra)
    extra_in = refs[13 : 13 + many]
    back, gain_grads, column_grads, normed_grads = refs[13 + many : 17 + many]
    extra_out = refs[17 + many : 17 + 2 * many]
    rest = refs[17 + 2 * many :]
    if exchange:
        back_columns, rest = rest[0], rest[1:]
        *rest, back_send, back_recv = rest
    bias, score_grads, weights_low, query_grads, kv_grads = rest[:5]
    kv_parts = rest[5:11]
    extra_parts = [rest[11 + 8 * i : 19 + 8 * i] for i in range(many)]
    position = ctx_position(ctx_count)
    bits, place, along, mine, partners, _ = position
    pairs = ctx_count // 2
    rows = raw.shape[0]
    column_send, column_recv, grads, streamed, stream_sem = rest[11 + 8 * many :]
    tile = streamed.shape[1]

    head_parts = [(0, HEADS), (HEADS, KV_HEADS), (HEADS + KV_HEADS, KV_HEADS)]

    def back_span(part, owner):
        first, heads = head_parts[part]
        size = heads * HD // fsdp_count
        start = pl.multiple_of(first * HD + owner * size, size)
        return pl.ds(start, size), pl.ds(first * HD // fsdp_count, size)

    def back_copies(part):
        copies = []
        for d, peer in enumerate(peers):
            source, target = back_span(part, peer)
            copies.append(
                pltpu.make_async_remote_copy(
                    src_ref=back.at[:, source],
                    dst_ref=back_columns.at[along, :, target],
                    send_sem=back_send.at[part, d],
                    recv_sem=back_recv.at[part, d],
                    device_id=(place, peer),
                    device_id_type=MESH,
                )
            )
        return copies

    def start_back(part):
        if exchange:
            for copy in back_copies(part):
                copy.start()
            source, target = back_span(part, along)
            back_columns[along, :, target] = back[:, source]

    def stream(weight, columns, use):
        tiles = weight.shape[0] // tile

        def copy(t):
            return pltpu.make_async_copy(
                weight.at[pl.ds(t * tile, tile), pl.ds(0, columns)],
                streamed.at[t % 2, :, pl.ds(0, columns)],
                stream_sem.at[t % 2],
            )

        copy(0).start()
        for t in range(tiles):
            if t + 1 < tiles:
                copy(t + 1).start()
            copy(t).wait()
            use(pl.ds(t * tile, tile), streamed[t % 2, :, :columns])

    peers = [lax.rem(along + d, fsdp_count) for d in range(1, fsdp_count)]
    wide = column_grads.shape[-1]
    column_copies = [
        pltpu.make_async_remote_copy(
            src_ref=row_grads.at[:, pl.ds(pl.multiple_of(peer * wide, wide), wide)],
            dst_ref=column_grads.at[along],
            send_sem=column_send.at[d],
            recv_sem=column_recv.at[d],
            device_id=(place, peer),
            device_id_type=MESH,
        )
        for d, peer in enumerate(peers)
    ]
    groups = HEADS // KV_HEADS
    length = ctx_count * rows
    low = jnp.bfloat16

    kv_sum = Halving(
        position,
        rows,
        lambda b: kv_grads.at[2 * b + 1 - mine[0]],
        lambda b: kv_grads.at[2 * b + mine[0]],
        kv_parts[0],
        kv_parts[1],
        kv_parts[2:6],
    )
    sums, own_copies = [], []
    for i, (block, _) in enumerate(extra):
        held, first_in, later_in, own_sem = extra_parts[i][:4]

        def give(b, i=i, block=block):
            at = pl.multiple_of((2 * b + 1 - mine[0]) * block, 16)
            return extra_in[i].at[pl.ds(at, block)]

        sums.append(
            Halving(
                position,
                block,
                give,
                lambda b, held=held: held.at[b],
                first_in,
                later_in,
                extra_parts[i][4:8],
            )
        )
        copies = []
        for b in range(pairs):
            at = pl.multiple_of((2 * b + mine[0]) * block, 16)
            copies.append(
                pltpu.make_async_copy(
                    extra_in[i].at[pl.ds(at, block)], held.at[b], own_sem.at[b]
                )
            )
            copies[-1].start()
        own_copies.append(copies)

    partner_barrier(partners + [(place, peer) for peer in peers])
    for one in sums:
        one.start_first()
    for copy in column_copies:
        copy.start()
    column_grads[along] = row_grads[:, pl.ds(pl.multiple_of(along * wide, wide), wide)]

    def attended_tile(columns, weight):
        grads[:, columns] = across(row_grads[...], weight).astype(low)

    stream(out_weight, row_grads.shape[1], attended_tile)

    def open_extra(i):
        for b in range(pairs):
            own_copies[i][b].wait()
            sums[i].end_first(b)
        sums[i].start(0)

    allowed = (key_ids[...] == row_ids[...]) & (
        lax.broadcasted_iota(jnp.int32, (length, rows), 0)
        <= lax.broadcasted_iota(jnp.int32, (length, rows), 1) + place * rows
    )
    bias[...] = jnp.where(allowed, 0.0, masked_score)
    everywhere = (slice(None),) * (bits + 1)
    for k in range(KV_HEADS):
        if k < many:
            open_extra(k)
        key = kv[everywhere + (pl.ds(k * HD, HD),)].reshape(length, HD)
        value = kv[everywhere + (pl.ds((KV_HEADS + k) * HD, HD),)].reshape(length, HD)

        def one_head(g, carry, k=k, key=key, value=value):
            h = k * groups + g
            columns = pl.ds(pl.multiple_of(g * rows, rows), rows)
            scores = across(key, query_low[:, head_at(h)]) + bias[...]
            weights = jnp.exp(scores - log_totals[h][:1])
            weight_grad = across(value, grads[:, head_at(h)])
            delta = jnp.sum(weights * weight_grad, axis=0, keepdims=True)
            score_grads[:, columns] = (weights * (weight_grad - delta)).astype(low)
            weights_low[:, columns] = weights.astype(low)
            return carry

        lax.fori_loop(0, groups, one_head, 0)
        heads = [pl.ds((k * groups + g) * HD, HD) for g in range(groups)]
        query_stack = jnp.concatenate([query_low[:, at] for at in heads], axis=0)
        grad_stack = jnp.concatenate([grads[:, at] for at in heads], axis=0)
        key_grad = forward_product(score_grads[...], query_stack).astype(low)
        value_grad = forward_product(weights_low[...], grad_stack).astype(low)
        kv_grads[:, :, pl.ds(k * HD, HD)] = key_grad.reshape(ctx_count, rows, HD)
        kv_grads[:, :, pl.ds((KV_HEADS + k) * HD, HD)] = value_grad.reshape(ctx_count, rows, HD)
        query_grad = over_rows(key, score_grads[...])
        for g, at in enumerate(heads):
            query_grads[:, at] = query_grad[:, g * rows : (g + 1) * rows].T

    kv_sum.start_first()
    for b in range(pairs):
        kv_sum.end_first(b)
    kv_sum.start(0)
    for i in range(KV_HEADS, many):
        open_extra(i)

    def step_extra(i, stage):
        sums[i].end(stage - 1)
        sums[i].start(stage)

    cosine, sine_part = cosine_ref[...], sine_ref[...]

    def one_query(h, gain_grad):
        grad = turned(query_grads[:, head_at(h)], cosine, -sine_part)
        pulled, more = unit_rows_pull(raw[:, head_at(h)], grad, query_gain[...])
        back[:, head_at(h)] = pulled.astype(low)
        return gain_grad + more

    gain_grads[0:1] = lax.fori_loop(0, HEADS, one_query, jnp.zeros((1, HD), jnp.float32))
    start_back(0)
    for stage in range(1, bits - 1):
        kv_sum.end(stage - 1)
        kv_sum.start(stage)
    kv_sum.end(bits - 2)
    for i in range(many):
        step_extra(i, 1)
    summed = kv_sum.mine_now()
    key_gain_grad = jnp.zeros((1, HD), jnp.float32)
    for k in range(KV_HEADS):
        grad = summed[:, pl.ds(k * HD, HD)].astype(jnp.float32)
        grad = turned(grad, cosine, -sine_part)
        at = pl.ds((HEADS + k) * HD, HD)
        pulled, more = unit_rows_pull(raw[:, at], grad, key_gain[...])
        back[:, at] = pulled.astype(low)
        key_gain_grad = key_gain_grad + more
        grad = summed[:, pl.ds((KV_HEADS + k) * HD, HD)].astype(jnp.float32)
        at = pl.ds((HEADS + KV_HEADS + k) * HD, HD)
        pulled, _ = unit_rows_pull(raw[:, at], grad, 1.0)
        back[:, at] = pulled.astype(low)
    gain_grads[1:2] = key_gain_grad
    start_back(1)
    start_back(2)

    def normed_tile(columns, weight):
        normed_grads[:, columns] = across(back[...], weight)

    stream(qkv_weight, back.shape[1], normed_tile)
    for stage in range(2, bits - 1):
        for i in range(many):
            step_extra(i, stage)
    for copy in column_copies:
        copy.wait()
    if exchange:
        for part in range(3):
            for copy in back_copies(part):
                copy.wait()
    for i in range(many):
        sums[i].end(bits - 2)
        extra_out[i][...] = sums[i].mine_now()[...]


def attention_backward(
    query_low,
    kv,
    log_totals,
    raw,
    cosine,
    sine_part,
    query_gain,
    key_gain,
    row_ids,
    key_ids,
    row_grads,
    out_weight,
    qkv_weight,
    extra,
):
    fsdp_count = lax.axis_size("fsdp")
    hbm = pl.BlockSpec(memory_space=pltpu.HBM)
    ctx_count = lax.axis_size("ctx")
    rows = raw.shape[0]
    length = ctx_count * rows
    pairs = ctx_count // 2
    groups = HEADS // KV_HEADS
    low = jnp.bfloat16
    vmem = pl.BlockSpec(memory_space=pltpu.VMEM)
    shapes = [(a.shape[0] // ctx_count, a.shape[1]) for a in extra]
    scratch = [
        pltpu.VMEM((length, rows), jnp.float32),
        pltpu.VMEM((length, groups * rows), low),
        pltpu.VMEM((length, groups * rows), low),
        pltpu.VMEM((rows, HEADS * HD), jnp.float32),
        pltpu.VMEM((ctx_count, rows, 2 * KV_HEADS * HD), low),
    ]
    scratch += halving_scratch(ctx_count, rows, 2 * KV_HEADS * HD)
    for shape in shapes:
        parts = halving_scratch(ctx_count, *shape)
        scratch += [pltpu.VMEM((pairs,) + shape, low)] + parts[:2]
        scratch += [pltpu.SemaphoreType.DMA((pairs,))] + parts[2:]
    scratch += [pltpu.SemaphoreType.DMA((fsdp_count - 1,))] * 2
    scratch += [
        pltpu.VMEM((rows, HEADS * HD), low),
        pltpu.VMEM((2, FF_TILE, qkv_weight.shape[1]), low),
        pltpu.SemaphoreType.DMA((2,)),
    ]
    exchange = KV_HEADS * HD // fsdp_count % 128 == 0
    back_out = []
    if exchange:
        scratch += [pltpu.SemaphoreType.DMA((3, fsdp_count - 1))] * 2
        back_out = [jax.ShapeDtypeStruct((fsdp_count, rows, raw.shape[1] // fsdp_count), low)]
    columns_shape = (fsdp_count, rows, row_grads.shape[1] // fsdp_count)
    outs = pl.pallas_call(
        functools.partial(attention_backward_kernel, ctx_count, fsdp_count, shapes, exchange),
        out_shape=[
            jax.ShapeDtypeStruct(raw.shape, low),
            jax.ShapeDtypeStruct((8, HD), jnp.float32),
            jax.ShapeDtypeStruct(columns_shape, low),
            jax.ShapeDtypeStruct((rows, qkv_weight.shape[0]), jnp.float32),
        ]
        + [jax.ShapeDtypeStruct(s, low) for s in shapes]
        + back_out,
        in_specs=[vmem] * 11 + [hbm] * (2 + len(extra)),
        out_specs=[vmem] * (4 + len(extra) + len(back_out)),
        scratch_shapes=scratch,
        compiler_params=pltpu.CompilerParams(
            collective_id=3, has_side_effects=True, vmem_limit_bytes=60 << 20
        ),
        cost_estimate=pl.CostEstimate(
            flops=10 * HEADS * HD * rows * length,
            bytes_accessed=64 << 20,
            transcendentals=HEADS * rows * length,
        ),
        name="attention_backward",
    )(
        query_low,
        kv,
        log_totals,
        raw,
        cosine,
        sine_part,
        query_gain[None],
        key_gain[None],
        row_ids[None],
        key_ids[:, None],
        row_grads,
        out_weight,
        qkv_weight,
        *extra,
    )
    columns = outs[2].reshape(-1, outs[2].shape[-1])
    back_columns = None
    if exchange:
        back_columns = outs[-1].reshape(-1, outs[-1].shape[-1])
    sums = outs[4 : 4 + len(extra)]
    return outs[0], outs[1][0], outs[1][1], columns, outs[3], sums, back_columns


def owner_sum_kernel(ctx_count, fsdp_count, shapes, shared, *refs):
    many = len(shapes)
    whole = many - shared
    ins, outs = refs[:many], refs[many : 2 * many]
    rest = refs[2 * many :]
    parts = [rest[8 * i : 8 * i + 8] for i in range(many)]
    shares = rest[8 * many : 8 * many + shared]
    send_z, recv_z = rest[8 * many + shared :]
    position = ctx_position(ctx_count)
    bits, place, along, mine, partners, _ = position
    pairs = ctx_count // 2
    across_line = [(place, lax.rem(along + d, fsdp_count)) for d in range(1, fsdp_count)]
    partner_barrier(partners + across_line)
    sums, own_copies = [], []
    for i, (block, _) in enumerate(shapes):
        held, first_in, later_in, own_sem = parts[i][:4]

        def give(b, i=i, block=block):
            at = pl.multiple_of((2 * b + 1 - mine[0]) * block, 16)
            return ins[i].at[pl.ds(at, block)]

        sums.append(
            Halving(
                position,
                block,
                give,
                lambda b, held=held: held.at[b],
                first_in,
                later_in,
                parts[i][4:8],
            )
        )
        sums[i].start_first()
        copies = []
        for b in range(pairs):
            at = pl.multiple_of((2 * b + mine[0]) * block, 16)
            copies.append(
                pltpu.make_async_copy(ins[i].at[pl.ds(at, block)], held.at[b], own_sem.at[b])
            )
            copies[-1].start()
        own_copies.append(copies)
    order = list(range(whole, many)) + list(range(whole))
    for i in order:
        for b in range(pairs):
            own_copies[i][b].wait()
            sums[i].end_first(b)
        sums[i].start(0)
    for stage in range(1, bits - 1):
        for i in order:
            sums[i].end(stage - 1)
            sums[i].start(stage)

    def share_copies(i):
        size = shapes[i][0] // fsdp_count
        return [
            pltpu.make_async_remote_copy(
                src_ref=sums[i].mine_now().at[pl.ds(pl.multiple_of(peer[1] * size, 16), size)],
                dst_ref=shares[i - whole].at[d],
                send_sem=send_z.at[i - whole, d],
                recv_sem=recv_z.at[i - whole, d],
                device_id=peer,
                device_id_type=MESH,
            )
            for d, peer in enumerate(across_line)
        ]

    for i in range(whole, many):
        sums[i].end(bits - 2)
        for copy in share_copies(i):
            copy.start()
    for i in range(whole):
        sums[i].end(bits - 2)
        outs[i][...] = sums[i].mine_now()[...]
    for i in range(whole, many):
        for copy in share_copies(i):
            copy.wait()
        size = shapes[i][0] // fsdp_count
        own = sums[i].mine_now()[pl.ds(pl.multiple_of(along * size, 16), size)]
        total = own.astype(jnp.float32)
        for d in range(fsdp_count - 1):
            total = total + shares[i - whole][d].astype(jnp.float32)
        outs[i][...] = total.astype(outs[i].dtype)


def owner_sums(arrays, shared):
    ctx_count = lax.axis_size("ctx")
    fsdp_count = lax.axis_size("fsdp")
    pairs = ctx_count // 2
    many = len(arrays)
    whole = many - shared
    low = jnp.bfloat16
    shapes = [(a.shape[0] // ctx_count, a.shape[1]) for a in arrays]
    share_shapes = [(s[0] // fsdp_count, s[1]) for s in shapes[whole:]]
    scratch = []
    for shape in shapes:
        parts = halving_scratch(ctx_count, *shape)
        scratch += [pltpu.VMEM((pairs,) + shape, low)] + parts[:2]
        scratch += [pltpu.SemaphoreType.DMA((pairs,))] + parts[2:]
    scratch += [pltpu.VMEM((fsdp_count - 1,) + s, low) for s in share_shapes]
    scratch += [pltpu.SemaphoreType.DMA((shared, fsdp_count - 1))] * 2
    total = sum(a.size for a in arrays)
    return pl.pallas_call(
        functools.partial(owner_sum_kernel, ctx_count, fsdp_count, shapes, shared),
        out_shape=[jax.ShapeDtypeStruct(s, low) for s in shapes[:whole] + share_shapes],
        in_specs=[pl.BlockSpec(memory_space=pl.ANY)] * many,
        out_specs=[pl.BlockSpec(memory_space=pltpu.VMEM)] * many,
        scratch_shapes=scratch,
        compiler_params=pltpu.CompilerParams(
            collective_id=0, has_side_effects=True, vmem_limit_bytes=48 << 20
        ),
        cost_estimate=pl.CostEstimate(flops=total, bytes_accessed=4 * total, transcendentals=0),
        name="owner_sums",
    )(*arrays)


class LineExchange:
    def __init__(self, count, own, gathered, outgoing, incoming, sems):
        self.count, self.steps = count, count - 1
        self.own, self.gathered = own, gathered
        self.outgoing, self.incoming = outgoing, incoming
        self.line_send, self.line_recv, self.back_send, self.back_recv = sems
        self.place = lax.axis_index("ctx")
        self.along = lax.axis_index("fsdp")
        self.width = outgoing.shape[-1]
        self.chunks = self.width // BACK_TILE

    def barrier(self):
        partner_barrier(
            [
                (self.place, lax.rem(self.along + d, self.count))
                for d in sorted({1, self.count - 1})
            ]
        )

    def line_copy(self, way, step, origin):
        toward = self.along + 1 if way == 0 else self.along - 1
        return pltpu.make_async_remote_copy(
            src_ref=self.own if step == 1 else self.gathered.at[origin],
            dst_ref=self.gathered.at[origin],
            send_sem=self.line_send.at[way, step - 1],
            recv_sem=self.line_recv.at[way, step - 1],
            device_id=(self.place, toward),
            device_id_type=MESH,
        )

    def forward(self, step):
        for way in range(2):
            origin = line_origin(self.along, way, step - 1)
            pl.when(line_goes(self.along, self.count, way, step))(
                lambda way=way, origin=origin: self.line_copy(way, step, origin).start()
            )

    def arrive(self, step):
        for way in range(2):
            origin = line_origin(self.along, way, step)
            pl.when(line_comes(self.along, self.count, way, step))(
                lambda way=way, origin=origin: self.line_copy(way, step, origin).wait_recv()
            )
        if step < self.steps:
            self.forward(step + 1)

    def back_copy(self, way, owner, chunk):
        toward = self.along + 1 if way == 0 else self.along - 1
        columns = tile_at(chunk, BACK_TILE)
        landing = owner if way == 0 else jnp.where(owner == toward, self.count, owner)
        return pltpu.make_async_remote_copy(
            src_ref=self.outgoing.at[owner, :, columns],
            dst_ref=self.incoming.at[landing, :, columns],
            send_sem=self.back_send.at[way, owner, chunk],
            recv_sem=self.back_recv.at[way, owner, chunk],
            device_id=(self.place, toward),
            device_id_type=MESH,
        )

    def landed(self, way, owner, chunk, landing):
        columns = pl.ds(chunk * BACK_TILE, BACK_TILE)
        pltpu.make_async_remote_copy(
            src_ref=self.outgoing.at[owner, :, columns],
            dst_ref=self.incoming.at[landing, :, columns],
            send_sem=self.back_send.at[way, owner, chunk],
            recv_sem=self.back_recv.at[way, owner, chunk],
            device_id=(self.place, self.along),
            device_id_type=MESH,
        ).wait_recv()
        return self.incoming[landing, :, columns].astype(jnp.float32)

    def relays(self, way):
        return self.along >= 1 if way == 0 else self.along + 1 < self.count

    def run(self, compute, before_last):

        def one(way, step):
            back = 1 - way
            origin = line_origin(self.along, way, step)

            def work():
                def write(chunk, tile):
                    columns = tile_at(chunk, BACK_TILE)
                    self.outgoing[origin, :, columns] = tile.astype(self.outgoing.dtype)
                    pl.when(jnp.logical_not(self.relays(back)))(
                        lambda: self.back_copy(back, origin, chunk).start()
                    )

                compute(origin, write)

            pl.when(line_comes(self.along, self.count, way, step))(work)

        near_start = 2 * self.along < self.steps

        def relay(way, step, turn):
            owner = step if way == 0 else self.steps - step
            passes = owner > self.along if way == 0 else owner < self.along

            def work():
                for chunk in range(self.chunks):
                    more = self.landed(way, owner, chunk, owner)
                    columns = pl.ds(chunk * BACK_TILE, BACK_TILE)
                    mine = self.outgoing[owner, :, columns].astype(jnp.float32)
                    self.outgoing[owner, :, columns] = (mine + more).astype(self.outgoing.dtype)
                    self.back_copy(way, owner, chunk).start()

            pl.when(self.relays(way) & passes & turn)(work)

        for step in range(1, self.steps + 1):
            self.arrive(step)
            for way in range(2):
                one(way, step)
            if step == self.steps:
                before_last()
            relay(0, step, near_start)
            relay(1, step, True)
            relay(0, step, jnp.logical_not(near_start))

    def finish(self, total):
        for way in range(2):

            def receive(way=way):
                landing = self.along if way == 0 else self.count
                for chunk in range(self.chunks):
                    columns = pl.ds(chunk * BACK_TILE, BACK_TILE)
                    more = self.landed(way, self.along, chunk, landing)
                    total[:, columns] = total[:, columns] + more

            pl.when(self.relays(way))(receive)
        for step in range(1, self.steps + 1):
            for way in range(2):
                origin = line_origin(self.along, way, step - 1)

                def left(way=way, step=step, origin=origin):
                    self.line_copy(way, step, origin).wait_send()

                def returned(way=way, step=step):
                    for chunk in range(self.chunks):
                        self.back_copy(1 - way, line_origin(self.along, way, step), chunk).wait_send()

                pl.when(line_goes(self.along, self.count, way, step))(left)
                pl.when(line_comes(self.along, self.count, way, step))(returned)


def line_scratch(count, rows, columns):
    steps = count - 1
    chunks = columns // BACK_TILE
    return [
        pltpu.VMEM((count, rows, columns), jnp.bfloat16),
        pltpu.VMEM((count + 1, rows, columns), jnp.bfloat16),
        pltpu.SemaphoreType.DMA((2, steps)),
        pltpu.SemaphoreType.DMA((2, steps)),
        pltpu.SemaphoreType.DMA((2, count, chunks)),
        pltpu.SemaphoreType.DMA((2, count, chunks)),
    ]


def tile_at(t, size):
    return pl.ds(pl.multiple_of(t * size, size), size)


def feed_forward_kernel(
    count,
    rows_in,
    gate_hbm,
    up_hbm,
    down_hbm,
    total,
    gathered,
    gate_keep,
    up_keep,
    hidden_keep,
    gate_w,
    up_w,
    down_w,
    weight_sem,
    *parts,
):
    rows, width = rows_in.shape
    units = gate_w.shape[1]
    tile = FF_TILE
    line = LineExchange(count, rows_in, gathered, parts[0], parts[1], parts[2:])
    loads = []
    for n, (source, target) in enumerate(((gate_hbm, gate_w), (up_hbm, up_w), (down_hbm, down_w))):
        group = []
        for t in range(target.shape[1] // tile):
            at = (slice(None), pl.ds(t * tile, tile))
            group.append(pltpu.make_async_copy(source.at[at], target.at[at], weight_sem.at[n, t]))
        loads.append(group)
    for t in range(units // tile):
        loads[0][t].start()
        loads[1][t].start()
    for load in loads[2]:
        load.start()
    line.barrier()
    line.forward(1)
    gathered[line.along] = rows_in[...]

    def hidden_tile(origin, columns):
        at = pl.ds(pl.multiple_of(origin * rows, rows), rows)
        gate = forward_product(gathered[origin], gate_w[:, columns])
        up = forward_product(gathered[origin], up_w[:, columns])
        gate_keep[at, columns] = gate.astype(gate_keep.dtype)
        up_keep[at, columns] = up.astype(up_keep.dtype)
        hidden_keep[at, columns] = hidden_piece(gate, up).astype(hidden_keep.dtype)

    def out_tile(origin, columns):
        at = pl.ds(pl.multiple_of(origin * rows, rows), rows)
        return forward_product(hidden_keep[at], down_w[:, columns])

    for t in range(units // tile):
        loads[0][t].wait()
        loads[1][t].wait()
        hidden_tile(line.along, pl.ds(t * tile, tile))
    for t in range(width // tile):
        loads[2][t].wait()
        columns = pl.ds(t * tile, tile)
        total[:, columns] = out_tile(line.along, columns)

    def compute(origin, write):
        def hidden_step(t, carry):
            hidden_tile(origin, tile_at(t, tile))
            return carry

        def out_step(t, carry):
            write(t, out_tile(origin, tile_at(t, tile)))
            return carry

        lax.fori_loop(0, units // tile, hidden_step, 0)
        lax.fori_loop(0, width // tile, out_step, 0)

    line.run(compute, lambda: None)
    line.finish(total)


def feed_forward(rows_in, gate_weight, up_weight, down_weight):
    count = lax.axis_size("fsdp")
    rows, width = rows_in.shape
    units = gate_weight.shape[1]
    low = jnp.bfloat16
    vmem = pl.BlockSpec(memory_space=pltpu.VMEM)
    hbm = pl.BlockSpec(memory_space=pltpu.HBM)
    kept = jax.ShapeDtypeStruct((count * rows, units), low)
    out, gathered, gate, up, hidden = pl.pallas_call(
        functools.partial(feed_forward_kernel, count),
        out_shape=[
            jax.ShapeDtypeStruct((rows, width), jnp.float32),
            jax.ShapeDtypeStruct((count, rows, width), low),
            kept,
            kept,
            kept,
        ],
        in_specs=[vmem, hbm, hbm, hbm],
        out_specs=[vmem] * 5,
        scratch_shapes=[
            pltpu.VMEM((width, units), low),
            pltpu.VMEM((width, units), low),
            pltpu.VMEM((units, width), low),
            pltpu.SemaphoreType.DMA((3, max(width, units) // FF_TILE)),
        ]
        + line_scratch(count, rows, width),
        compiler_params=pltpu.CompilerParams(
            collective_id=4, has_side_effects=True, vmem_limit_bytes=56 << 20
        ),
        cost_estimate=pl.CostEstimate(
            flops=6 * count * rows * width * units,
            bytes_accessed=6 * width * units,
            transcendentals=count * rows * units,
        ),
        name="feed_forward",
    )(rows_in, gate_weight, up_weight, down_weight)
    return out, gathered.reshape(count * rows, width), gate, up, hidden


def hidden_pull_tile(grad, gate, up):
    slope = math.sqrt(2.0 / math.pi)
    square = gate * gate
    curve = jnp.tanh(slope * gate * (1.0 + 0.044715 * square))
    bend = 0.5 * (1.0 + curve)
    steep = bend + 0.5 * gate * (1.0 - curve * curve) * slope * (1.0 + 3.0 * 0.044715 * square)
    return grad * up * steep, grad * gate * bend


def feed_forward_backward_kernel(
    count,
    grads_in,
    gate_keep,
    up_keep,
    hidden_keep,
    tokens,
    gate_hbm,
    up_hbm,
    down_hbm,
    total,
    down_grad,
    gate_grad,
    up_grad,
    gathered,
    gate_back,
    up_back,
    gate_w,
    up_w,
    down_w,
    weight_sem,
    staged,
    staged_sem,
    *parts,
):
    rows, width = grads_in.shape
    units = gate_w.shape[1]
    tile = FF_TILE
    line = LineExchange(count, grads_in, gathered, parts[0], parts[1], parts[2:])
    loads = []
    for n, (source, target) in enumerate(((gate_hbm, gate_w), (up_hbm, up_w), (down_hbm, down_w))):
        group = []
        for t in range(target.shape[0] // tile):
            at = pl.ds(t * tile, tile)
            group.append(pltpu.make_async_copy(source.at[at], target.at[at], weight_sem.at[n, t]))
        loads.append(group)
    for load in loads[2]:
        load.start()
    for t in range(width // tile):
        loads[0][t].start()
        loads[1][t].start()
    line.barrier()
    line.forward(1)
    gathered[line.along] = grads_in[...]

    def hidden_tile(origin, columns):
        at = pl.ds(pl.multiple_of(origin * rows, rows), rows)
        grad = across(gathered[origin], down_w[columns])
        gate = gate_keep[at, columns].astype(jnp.float32)
        up = up_keep[at, columns].astype(jnp.float32)
        gate_pull, up_pull = hidden_pull_tile(grad, gate, up)
        gate_back[at, columns] = gate_pull.astype(gate_back.dtype)
        up_back[at, columns] = up_pull.astype(up_back.dtype)

    def out_tile(origin, columns):
        at = pl.ds(pl.multiple_of(origin * rows, rows), rows)
        return across(gate_back[at], gate_w[columns]) + across(up_back[at], up_w[columns])

    for t in range(units // tile):
        loads[2][t].wait()
        hidden_tile(line.along, pl.ds(t * tile, tile))
    for t in range(width // tile):
        loads[0][t].wait()
        loads[1][t].wait()
        columns = pl.ds(t * tile, tile)
        total[:, columns] = out_tile(line.along, columns)

    def compute(origin, write):
        def hidden_step(t, carry):
            hidden_tile(origin, tile_at(t, tile))
            return carry

        def out_step(t, carry):
            write(t, out_tile(origin, tile_at(t, tile)))
            return carry

        lax.fori_loop(0, units // tile, hidden_step, 0)
        lax.fori_loop(0, width // tile, out_step, 0)

    band = GRAD_TILE
    bands = width // band

    def stage(slot, which, t, target):
        return pltpu.make_async_copy(
            staged.at[slot, which], target.at[tile_at(t, band)], staged_sem.at[slot, which]
        )

    def grad_bands(jobs):
        def step(t, carry):
            slot = lax.rem(t, 2)
            for left, right, target, which in jobs:

                @pl.when(t >= 2)
                def _(target=target, which=which):
                    stage(slot, which, t, target).wait()

                product = over_rows(left(tile_at(t, band)), right[...])
                staged[slot, which] = product.astype(staged.dtype)
                stage(slot, which, t, target).start()
            return carry

        lax.fori_loop(0, bands, step, 0)
        for back in range(2):
            t = bands - 2 + back
            for _, _, target, which in jobs:
                stage(t % 2, which, t, target).wait()

    def grads_at(columns):
        return gathered[:, :, columns].reshape(count * rows, band)

    line.run(
        compute, lambda: grad_bands([(grads_at, hidden_keep, down_grad, 0)])
    )
    grad_bands(
        [
            (lambda columns: tokens[:, columns], gate_back, gate_grad, 0),
            (lambda columns: tokens[:, columns], up_back, up_grad, 1),
        ]
    )
    line.finish(total)


def feed_forward_backward(
    grads_in, gate_keep, up_keep, hidden_keep, tokens, gate_weight, up_weight, down_weight
):
    count = lax.axis_size("fsdp")
    rows, width = grads_in.shape
    units = gate_weight.shape[1]
    low = jnp.bfloat16
    vmem = pl.BlockSpec(memory_space=pltpu.VMEM)
    hbm = pl.BlockSpec(memory_space=pltpu.HBM)
    grad_shape = jax.ShapeDtypeStruct((width, units), low)
    return pl.pallas_call(
        functools.partial(feed_forward_backward_kernel, count),
        out_shape=[jax.ShapeDtypeStruct((rows, width), jnp.float32)] + [grad_shape] * 3,
        in_specs=[vmem] * 5 + [hbm] * 3,
        out_specs=[vmem] + [hbm] * 3,
        scratch_shapes=[
            pltpu.VMEM((count, rows, width), low),
            pltpu.VMEM((count * rows, units), low),
            pltpu.VMEM((count * rows, units), low),
            pltpu.VMEM((width, units), low),
            pltpu.VMEM((width, units), low),
            pltpu.VMEM((units, width), low),
            pltpu.SemaphoreType.DMA((3, max(width, units) // FF_TILE)),
            pltpu.VMEM((2, 2, GRAD_TILE, units), low),
            pltpu.SemaphoreType.DMA((2, 2)),
        ]
        + line_scratch(count, rows, width),
        compiler_params=pltpu.CompilerParams(
            collective_id=5, has_side_effects=True, vmem_limit_bytes=60 << 20
        ),
        cost_estimate=pl.CostEstimate(
            flops=12 * count * rows * width * units,
            bytes_accessed=12 * width * units,
            transcendentals=count * rows * units,
        ),
        name="feed_forward_backward",
    )(grads_in, gate_keep, up_keep, hidden_keep, tokens, gate_weight, up_weight, down_weight)


def body(
    tokens,
    per_layer,
    out_grad,
    segment_ids,
    query_weight,
    key_weight,
    value_weight,
    out_weight,
    left_weight,
    right_weight,
    gate_weight,
    up_weight,
    down_weight,
    side_gate,
    side_out,
    input_gain,
    laurel_gain,
    attn_gain,
    pre_gain,
    post_gain,
    side_gain,
    query_gain,
    key_gain,
):
    low = jnp.bfloat16
    inputs = tokens[0].astype(jnp.float32)
    extra_rows = per_layer[0].astype(jnp.float32)
    cotangent = out_grad[0].astype(jnp.float32)
    sequence_ids = segment_ids[0]
    rows_here, width = inputs.shape
    ctx_count = lax.axis_size("ctx")
    fsdp_count = lax.axis_size("fsdp")
    count = ctx_count * fsdp_count
    ctx_place = lax.axis_index("ctx")
    rank = left_weight.shape[1]
    side = side_gate.shape[1]
    query_width = HEADS * HD
    kv_width = KV_HEADS * HD
    query_pos = ctx_place * rows_here + jnp.arange(rows_here, dtype=jnp.int32)

    piece = width // count

    qkv_width = query_width + 2 * kv_width
    full_qkv, second_line = weight_gather(
        [[query_weight, key_weight, value_weight], [out_weight, side_gate]], 1
    )

    normed, input_pull = jax.vjp(rms_norm, inputs, input_gain)
    normed_low = normed.astype(low)
    qkv_raw = forward_product(normed_low, full_qkv)
    frequency = jnp.exp(
        jnp.arange(HD // 2).astype(jnp.float32) * (-2.0 * math.log(rope_theta) / HD)
    )
    angles = query_pos.astype(jnp.float32)[:, None] * frequency[None, :]
    cosine, sine_part = jnp.cos(angles), jnp.sin(angles)
    query_ids = lax.dynamic_slice_in_dim(sequence_ids, ctx_place * rows_here, rows_here)
    kv_all, query_low, attended_low, log_totals, full_second, *full_small = attention_forward(
        qkv_raw,
        cosine,
        sine_part,
        query_gain,
        key_gain,
        query_ids,
        sequence_ids,
        second_line,
        [left_weight, right_weight, side_out],
    )
    full_left, full_right, full_side_out = full_small
    full_left = full_left.reshape(width, rank)
    full_right = full_right.transpose(1, 0, 2).reshape(rank, width)
    full_side_out = full_side_out.reshape(side, width)
    full_second = full_second.reshape(width, -1)
    full_out = full_second[:, :width]
    full_side_gate = full_second[:, width:]
    left_low = forward_product(normed_low, full_left).astype(low)
    right_out = forward_product(left_low, full_right)
    attn_raw = forward_product(attended_low, full_out)

    def mix_piece(x, normed_in, attn_in, right_in, gain_one, gain_two, gain_three):
        mixed = (
            x + rms_norm(attn_in, gain_one) + normed_in + rms_norm(right_in, gain_two)
        ) * inverse_root
        return (mixed, rms_norm(mixed, gain_three))

    (mixed, ffn_in), mix_pull = jax.vjp(
        mix_piece, inputs, normed, attn_raw, right_out, attn_gain, laurel_gain, pre_gain
    )

    ffn_out, ffn_all, gate_raw, up_raw, hidden_low = feed_forward(
        ffn_in.astype(low), gate_weight, up_weight, down_weight
    )
    middle, middle_pull = jax.vjp(middle_piece, mixed, ffn_out, post_gain)
    middle_low = middle.astype(low)
    layer_gate = forward_product(middle_low, full_side_gate)
    layer_act, extra_pull = jax.vjp(hidden_piece, layer_gate, extra_rows)
    layer_low = layer_act.astype(low)
    layer_out = forward_product(layer_low, full_side_out)
    result, out_pull = jax.vjp(middle_piece, middle, layer_out, side_gain)

    middle_grad_one, layer_out_grad, side_gain_grad = out_pull(cotangent)
    layer_grad_low = layer_out_grad.astype(low)
    side_out_grad = over_rows(layer_low, layer_grad_low)
    layer_gate_grad, extra_grad = extra_pull(across(layer_grad_low, full_side_out))
    gate_grad_low = layer_gate_grad.astype(low)
    side_gate_grad = over_rows(gate_grad_low, middle_low)
    mixed_grad_one, ffn_out_grad, post_gain_grad = middle_pull(
        middle_grad_one + across(gate_grad_low, full_side_gate)
    )
    ffn_in_grad, down_weight_grad, gate_weight_grad, up_weight_grad = feed_forward_backward(
        ffn_out_grad.astype(low),
        gate_raw,
        up_raw,
        hidden_low,
        ffn_all,
        gate_weight,
        up_weight,
        down_weight,
    )
    ffn_in_grad, late_low = lax.optimization_barrier((ffn_in_grad, (attended_low, normed_low)))
    attended_all, normed_all = (gather(part, "fsdp") for part in late_low)
    (
        inputs_grad_one,
        normed_grad_one,
        attn_raw_grad,
        right_out_grad,
        attn_gain_grad,
        laurel_gain_grad,
        pre_gain_grad,
    ) = mix_pull((mixed_grad_one, ffn_in_grad))
    attn_grad_low = attn_raw_grad.astype(low)
    right_grad_low = right_out_grad.astype(low)
    right_weight_grad = over_rows(right_grad_low, left_low)
    left_grad_low = across(right_grad_low, full_right).astype(low)
    left_weight_grad = over_rows(normed_low, left_grad_low)
    (
        qkv_back_low,
        query_gain_grad,
        key_gain_grad,
        out_columns,
        normed_grad_two,
        ffn_sums,
        qkv_columns,
    ) = attention_backward(
        query_low,
        kv_all,
        log_totals,
        qkv_raw,
        cosine,
        sine_part,
        query_gain,
        key_gain,
        query_ids,
        sequence_ids,
        attn_grad_low,
        full_second,
        full_qkv,
        [gate_weight_grad, up_weight_grad],
    )
    down_low, normed_grad_two = lax.optimization_barrier((down_weight_grad, normed_grad_two))
    down_weight_grad = scatter_sum(down_low, "ctx")
    normed_grad_two = normed_grad_two + across(left_grad_low, full_left)
    inputs_grad_two, input_gain_grad = input_pull(normed_grad_one + normed_grad_two)
    block_out = result.astype(low)[None]
    tokens_grad = (inputs_grad_one + inputs_grad_two).astype(low)[None]
    per_layer_grad = extra_grad.astype(low)[None]

    def columns_to_owner(x):
        parts = x.reshape(rows_here, fsdp_count, -1).transpose(1, 0, 2)
        return lax.all_to_all(parts, "fsdp", 0, 0, tiled=True).reshape(fsdp_count * rows_here, -1)

    out_weight_grad = over_rows(attended_all, out_columns)
    if qkv_columns is None:
        qkv_parts = jnp.concatenate(
            [
                part.reshape(rows_here, fsdp_count, -1)
                for part in (
                    qkv_back_low[:, :query_width],
                    qkv_back_low[:, query_width : query_width + kv_width],
                    qkv_back_low[:, query_width + kv_width :],
                )
            ],
            axis=2,
        )
        qkv_columns = columns_to_owner(qkv_parts.reshape(rows_here, -1))
    qkv_weight_grad = over_rows(normed_all, qkv_columns)

    small_gains = [
        jnp.pad(g.reshape(count, -1), ((0, 0), (0, piece - g.shape[0] // count))).reshape(-1)
        for g in (query_gain_grad, key_gain_grad)
    ]
    gains = jnp.stack(
        [
            input_gain_grad,
            laurel_gain_grad,
            attn_gain_grad,
            pre_gain_grad,
            post_gain_grad,
            side_gain_grad,
            *small_gains,
        ]
    )
    gate_blocks = side_gate_grad.astype(low).reshape(side, ctx_count, -1).transpose(1, 0, 2)
    gate_columns = width // ctx_count
    tall = jnp.concatenate(
        [
            left_weight_grad.astype(low),
            right_weight_grad.astype(low),
            jnp.pad(gains.astype(low).T, ((0, 0), (0, 128 - gains.shape[0]))),
        ],
        axis=1,
    )
    out_blocks = side_out_grad.astype(low).reshape(
        ctx_count, side // ctx_count, fsdp_count, width // fsdp_count
    )
    out_blocks = out_blocks.transpose(0, 2, 1, 3).reshape(-1, width // fsdp_count)
    out_weight_grad, qkv_weight_grad, tall, gate_blocks, side_out_grad = owner_sums(
        [
            out_weight_grad.astype(low),
            qkv_weight_grad.astype(low),
            tall,
            gate_blocks.reshape(-1, gate_columns),
            out_blocks,
        ],
        3,
    )
    gate_weight_grad, up_weight_grad = ffn_sums
    down_weight_grad = down_weight_grad.T
    query_part = query_width // fsdp_count
    kv_part = kv_width // fsdp_count
    query_weight_grad = qkv_weight_grad[:, :query_part]
    key_weight_grad = qkv_weight_grad[:, query_part : query_part + kv_part]
    value_weight_grad = qkv_weight_grad[:, query_part + kv_part :]
    wide = jnp.float32
    tall = tall.astype(wide)
    left_weight_grad = tall[:, :rank]
    right_weight_grad = tall[:, rank : 2 * rank].T
    gains = tall[:, 2 * rank : 2 * rank + 8].T
    small_part = query_gain.shape[0] // count
    side_gate_grad = gate_blocks.astype(wide).T
    side_out_grad = side_out_grad.astype(wide)
    return (
        block_out,
        tokens_grad,
        per_layer_grad,
        query_weight_grad.astype(wide),
        key_weight_grad.astype(wide),
        value_weight_grad.astype(wide),
        out_weight_grad.astype(wide),
        left_weight_grad,
        right_weight_grad,
        gate_weight_grad.astype(wide),
        up_weight_grad.astype(wide),
        down_weight_grad.astype(wide),
        side_gate_grad,
        side_out_grad,
        *(gains[n] for n in range(6)),
        gains[6, :small_part],
        gains[7, :small_part],
    )


def solution(mesh):
    placed = (
        P("fsdp", "ctx", None),
        P("fsdp", "ctx", None),
        P("fsdp", "ctx", None),
        P("fsdp", None),
        P("fsdp", None),
        P("fsdp", None),
        P("fsdp", None),
        P("fsdp", None),
        P("fsdp", None),
        P(None, "fsdp"),
        P(None, "fsdp"),
        P(None, "fsdp"),
        P("fsdp", None),
        P("fsdp", None),
        P("fsdp", None),
        P(),
        P(),
        P(),
        P(),
        P(),
        P(),
        P(),
        P(),
    )
    return jax.shard_map(
        body,
        mesh=mesh,
        in_specs=placed,
        out_specs=(
            P("fsdp", "ctx", None),
            P("fsdp", "ctx", None),
            P("fsdp", "ctx", None),
            P("ctx", "fsdp"),
            P("ctx", "fsdp"),
            P("ctx", "fsdp"),
            P("ctx", "fsdp"),
            P(("ctx", "fsdp"), None),
            P(None, ("ctx", "fsdp")),
            P("ctx", "fsdp"),
            P("ctx", "fsdp"),
            P("fsdp", "ctx"),
            P("ctx", "fsdp"),
            P("ctx", "fsdp"),
            P(("ctx", "fsdp")),
            P(("ctx", "fsdp")),
            P(("ctx", "fsdp")),
            P(("ctx", "fsdp")),
            P(("ctx", "fsdp")),
            P(("ctx", "fsdp")),
            P(("ctx", "fsdp")),
            P(("ctx", "fsdp")),
        ),
        check_vma=False,
    )
```

```python
import functools
import math

import jax
import jax.numpy as jnp
from jax import lax
from jax.experimental import pallas as pl
from jax.experimental.pallas import tpu as pltpu
from jax.sharding import PartitionSpec as P

HEADS = 8
KV_HEADS = 2
HD = 256
MESH = pl.DeviceIdType.MESH
FF_TILE = 512
BACK_TILE = FF_TILE


epsilon = 1e-06
rope_theta = 1000000.0
masked_score = -1e30
inverse_root = 1.0 / math.sqrt(2.0)


def rms_norm(v, factor):
    return v * lax.rsqrt(jnp.mean(v * v, axis=-1, keepdims=True) + epsilon) * factor


def forward_product(a, b):
    return jnp.dot(a, b, preferred_element_type=jnp.float32)


def across(a, b):
    return lax.dot_general(a, b, (((1,), (1,)), ((), ())), preferred_element_type=jnp.float32)


def over_rows(a, b):
    return lax.dot_general(a, b, (((0,), (0,)), ((), ())), preferred_element_type=jnp.float32)


def hidden_piece(gate_in, up_in):
    return jax.nn.gelu(gate_in, approximate=True) * up_in


def middle_piece(mixed_in, ffn_in_rows, factor):
    return mixed_in + rms_norm(ffn_in_rows, factor)


def gather(x, axis):
    return lax.all_gather(x, axis, axis=0, tiled=True)


def scatter_sum(x, axis):
    return lax.psum_scatter(x, axis, scatter_dimension=0, tiled=True)


def partner_barrier(partners):
    barrier = pltpu.get_barrier_semaphore()
    for partner in partners:
        pl.semaphore_signal(barrier, inc=1, device_id=partner, device_id_type=MESH)
    pl.semaphore_wait(barrier, len(partners))


def add_rows(target, source, first, rows):
    tile = 16

    def one(step, carry):
        at = pl.ds(pl.multiple_of(first + step * tile, tile), tile)
        from_at = pl.ds(pl.multiple_of(step * tile, tile), tile)
        total = target[at].astype(jnp.float32) + source[from_at].astype(jnp.float32)
        target[at] = total.astype(target.dtype)
        return carry

    lax.fori_loop(0, rows // tile, one, 0)


def held_index(mine, done, bits):
    return tuple(slice(None) if t in done else mine[t] for t in reversed(range(bits)))


def ctx_position(ctx_count):
    bits = ctx_count.bit_length() - 1
    place = lax.axis_index("ctx")
    along = lax.axis_index("fsdp")
    mine = [lax.rem(place // (1 << t), 2) for t in range(bits)]
    partners = [(place + (1 - 2 * mine[t]) * (1 << t), along) for t in range(bits)]
    orders = [list(range(1, bits)), list(range(bits - 1, 0, -1))]
    return bits, place, along, mine, partners, orders


def spread_copy(out, lead, half, stage, position, send_sem, recv_sem):
    bits, _, _, mine, partners, orders = position
    order = orders[half]
    rows = out.shape[-2] // 2
    at = lead + held_index(mine, order[:stage], bits) + (pl.ds(half * rows, rows),)
    return pltpu.make_async_remote_copy(
        src_ref=out.at[at],
        dst_ref=out.at[at],
        send_sem=send_sem.at[half, stage],
        recv_sem=recv_sem.at[half, stage],
        device_id=partners[order[stage]],
        device_id_type=MESH,
    )


def sibling_copy(out, lead, position, send_sem, recv_sem):
    bits, _, _, mine, partners, orders = position
    at = lead + held_index(mine, orders[0], bits)
    return pltpu.make_async_remote_copy(
        src_ref=out.at[at],
        dst_ref=out.at[at],
        send_sem=send_sem,
        recv_sem=recv_sem,
        device_id=partners[0],
        device_id_type=MESH,
    )


def weight_gather_kernel(ctx_count, fsdp_count, members, spread, *refs):
    sets = len(members)
    own_count = sum(members)
    own, outs = refs[:own_count], refs[own_count : own_count + sets]
    rest = refs[own_count + sets :]
    passing, pieces = rest[:own_count], rest[own_count : own_count + sets]
    own_sem, line_send, line_recv, send_sem, recv_sem, core_send, core_recv = rest[
        own_count + sets :
    ]
    position = ctx_position(ctx_count)
    bits, place, along, mine, partners, _ = position
    steps = fsdp_count - 1
    here = held_index(mine, (), bits)
    columns = []
    for i in range(sets):
        start = 0
        for _ in range(members[i]):
            wide = own[len(columns)].shape[-1]
            columns.append((i, pl.ds(start, wide)))
            start += wide
    piece_loads = [
        pltpu.make_async_copy(own[n].at[here], pieces[i].at[:, at], own_sem.at[0, n])
        for n, (i, at) in enumerate(columns)
    ]
    for load in piece_loads:
        load.start()
    loads = [
        pltpu.make_async_copy(source, passing[n], own_sem.at[1, n])
        for n, source in enumerate(own)
    ]
    for load in loads:
        load.start()
    partner_barrier(
        partners
        + [(place, lax.rem(along + 1, fsdp_count)), (place, lax.rem(along + steps, fsdp_count))]
    )

    def line_copy(i, way, step, origin):
        toward = along + 1 if way == 0 else along - 1
        first, target = pieces[i], outs[i].at[(origin,) + here]
        return pltpu.make_async_remote_copy(
            src_ref=first if step == 1 else target,
            dst_ref=target,
            send_sem=line_send.at[i, way, step - 1],
            recv_sem=line_recv.at[i, way, step - 1],
            device_id=(place, toward),
            device_id_type=MESH,
        )

    def comes(way, step):
        return along >= step if way == 0 else along + step < fsdp_count

    def goes(way, step):
        if way == 0:
            return (along + 1 < fsdp_count) & (along >= step - 1)
        return (along >= 1) & (along + step - 1 < fsdp_count)

    def origin_of(way, step):
        return along - step if way == 0 else along + step

    def each(flag, action):
        pl.when(flag)(action)

    def forward(i, step):
        for way in range(2):
            each(goes(way, step), lambda: line_copy(i, way, step, origin_of(way, step - 1)).start())

    for load in piece_loads:
        load.wait()
    for i in range(sets):
        forward(i, 1)
    stores = []
    for n, load in enumerate(loads):
        load.wait()
        i, at = columns[n]
        target = outs[i].at[(along,) + (slice(None),) * (bits + 1) + (at,)]
        stores.append(pltpu.make_async_copy(passing[n], target, own_sem.at[2, n]))
        stores[-1].start()

    def stage_copies(i, way, step, stage):
        lead = (origin_of(way, step),)
        at = (i, way, step - 1)
        return [
            spread_copy(outs[i], lead, half, stage, position, send_sem.at[at], recv_sem.at[at])
            for half in range(2)
        ]

    def core_copy(i, way, step):
        at = (i, way, step - 1)
        return sibling_copy(
            outs[i], (origin_of(way, step),), position, core_send.at[at], core_recv.at[at]
        )

    def arrive(i, step):
        for way in range(2):

            def landed():
                line_copy(i, way, step, origin_of(way, step)).wait_recv()

            each(comes(way, step), landed)
        if step < steps:
            forward(i, step + 1)
        if i >= spread:
            return
        for way in range(2):

            def begin():
                for copy in stage_copies(i, way, step, 0):
                    copy.start()

            each(comes(way, step), begin)

    def advance(i, step, stage):
        if i >= spread:
            return
        for way in range(2):

            def proceed():
                for copy in stage_copies(i, way, step, stage):
                    copy.wait_recv()
                if stage < bits - 2:
                    for copy in stage_copies(i, way, step, stage + 1):
                        copy.start()
                else:
                    core_copy(i, way, step).start()

            each(comes(way, step), proceed)

    order = [(i, step) for i in range(sets) for step in range(1, steps + 1)]
    for tick in range(len(order) + bits - 1):
        if tick < len(order):
            arrive(*order[tick])
        for stage in range(bits - 1):
            at = tick - 1 - stage
            if 0 <= at < len(order):
                advance(*order[at], stage)
    for copy in stores:
        copy.wait()
    for i, step in order:
        for way in range(2):

            def leave():
                line_copy(i, way, step, origin_of(way, step - 1)).wait_send()

            def finish():
                for stage in range(bits - 1):
                    for copy in stage_copies(i, way, step, stage):
                        copy.wait_send()
                core_copy(i, way, step).wait()

            each(goes(way, step), leave)
            if i < spread:
                each(comes(way, step), finish)


def weight_gather(own, spread):
    ctx_count = lax.axis_size("ctx")
    fsdp_count = lax.axis_size("fsdp")
    bits = ctx_count.bit_length() - 1
    steps = fsdp_count - 1
    sets = len(own)
    cut = (2,) * bits
    low = jnp.bfloat16
    flat = [w.reshape(cut + (w.shape[0] // ctx_count, w.shape[1])) for group in own for w in group]
    pieces = [(g[0].shape[0] // ctx_count, sum(w.shape[1] for w in g)) for g in own]
    out_shapes = [(fsdp_count,) + cut + p for p in pieces]
    total = sum(rows * columns for rows, columns in pieces) * ctx_count * fsdp_count
    outs = pl.pallas_call(
        functools.partial(
            weight_gather_kernel, ctx_count, fsdp_count, [len(g) for g in own], spread
        ),
        out_shape=[jax.ShapeDtypeStruct(s, low) for s in out_shapes],
        in_specs=[pl.BlockSpec(memory_space=pltpu.HBM)] * len(flat),
        out_specs=[pl.BlockSpec(memory_space=pltpu.HBM)] * len(out_shapes),
        scratch_shapes=[pltpu.VMEM(w.shape, low) for w in flat]
        + [pltpu.VMEM(p, low) for p in pieces]
        + [
            pltpu.SemaphoreType.DMA((3, len(flat))),
            pltpu.SemaphoreType.DMA((sets, 2, steps)),
            pltpu.SemaphoreType.DMA((sets, 2, steps)),
            pltpu.SemaphoreType.DMA((spread, 2, steps, 2, bits - 1)),
            pltpu.SemaphoreType.DMA((spread, 2, steps, 2, bits - 1)),
            pltpu.SemaphoreType.DMA((spread, 2, steps)),
            pltpu.SemaphoreType.DMA((spread, 2, steps)),
        ],
        compiler_params=pltpu.CompilerParams(
            collective_id=1, has_side_effects=True, vmem_limit_bytes=60 << 20
        ),
        cost_estimate=pl.CostEstimate(flops=0, bytes_accessed=4 * total, transcendentals=0),
        name="weight_gather",
    )(*flat)
    return [o.reshape(-1, o.shape[-1]) for o in outs[:spread]] + list(outs[spread:])


def line_comes(along, count, way, step):
    return along >= step if way == 0 else along + step < count


def line_goes(along, count, way, step):
    if way == 0:
        return (along + 1 < count) & (along >= step - 1)
    return (along >= 1) & (along + step - 1 < count)


def line_origin(along, way, step):
    return along - step if way == 0 else along + step


class LineGather:
    def __init__(self, count, owns, outs, passing, own_sems, send_sems, recv_sems):
        self.count, self.steps = count, count - 1
        self.owns, self.outs, self.passing = owns, outs, passing
        self.own_sems, self.send_sems, self.recv_sems = own_sems, send_sems, recv_sems
        self.place = lax.axis_index("ctx")
        self.along = lax.axis_index("fsdp")
        self.done = 0

    def partners(self):
        return [(self.place, lax.rem(self.along + d, self.count)) for d in sorted({1, self.steps})]

    def own_copies(self, n):
        return (
            pltpu.make_async_copy(self.owns[n], self.passing[n], self.own_sems.at[0, n]),
            pltpu.make_async_copy(self.passing[n], self.outs[n].at[self.along], self.own_sems.at[1, n]),
        )

    def copies(self, way, step, origin):
        toward = self.along + 1 if way == 0 else self.along - 1
        return [
            pltpu.make_async_remote_copy(
                src_ref=self.owns[n] if step == 1 else self.outs[n].at[origin],
                dst_ref=self.outs[n].at[origin],
                send_sem=self.send_sems.at[n, way, step - 1],
                recv_sem=self.recv_sems.at[n, way, step - 1],
                device_id=(self.place, toward),
                device_id_type=MESH,
            )
            for n in range(len(self.owns))
        ]

    def forward(self, step):
        for way in range(2):

            def go(way=way):
                for copy in self.copies(way, step, line_origin(self.along, way, step - 1)):
                    copy.start()

            pl.when(line_goes(self.along, self.count, way, step))(go)

    def load(self):
        for n in range(len(self.owns)):
            self.own_copies(n)[0].start()

    def store(self):
        for n in range(len(self.owns)):
            self.own_copies(n)[0].wait()
            self.own_copies(n)[1].start()

    def arrive(self):
        if self.done == self.steps:
            return
        self.done += 1
        step = self.done
        for way in range(2):

            def land(way=way):
                for copy in self.copies(way, step, line_origin(self.along, way, step)):
                    copy.wait_recv()

            pl.when(line_comes(self.along, self.count, way, step))(land)
        if step < self.steps:
            self.forward(step + 1)

    def finish(self):
        while self.done < self.steps:
            self.arrive()
        for n in range(len(self.owns)):
            self.own_copies(n)[1].wait()
        for step in range(1, self.steps + 1):
            for way in range(2):

                def leave(way=way, step=step):
                    for copy in self.copies(way, step, line_origin(self.along, way, step - 1)):
                        copy.wait_send()

                pl.when(line_goes(self.along, self.count, way, step))(leave)


class Halving:
    def __init__(self, position, rows, give, held, first_in, later_in, sems):
        self.bits, self.place, self.along, self.mine, self.partners, self.orders = position
        self.rows, self.give, self.held = rows, give, held
        self.first_in, self.later_in = first_in, later_in
        self.send_zero, self.recv_zero, self.send_sem, self.recv_sem = sems
        self.pairs = 1 << (self.bits - 1)

    def first_copy(self, b):
        return pltpu.make_async_remote_copy(
            src_ref=self.give(b),
            dst_ref=self.first_in.at[b],
            send_sem=self.send_zero.at[b],
            recv_sem=self.recv_zero.at[b],
            device_id=self.partners[0],
            device_id_type=MESH,
        )

    def start_first(self):
        for b in range(self.pairs):
            self.first_copy(b).start()

    def end_first(self, b):
        self.first_copy(b).wait()
        add_rows(self.held(b), self.first_in.at[b], 0, self.rows)

    def slot_of(self, stage):
        return sum(1 << (self.bits - 2 - s) for s in range(stage))

    def block_sets(self, half, stage):
        order = self.orders[half]
        bit = order[stage]
        free = order[stage + 1 :]
        fixed = sum(self.mine[t] * (1 << (t - 1)) for t in order[:stage])
        sent, kept = [], []
        for combo in range(1 << len(free)):
            value = sum(((combo >> n) & 1) << (t - 1) for n, t in enumerate(free))
            sent.append(fixed + (1 - self.mine[bit]) * (1 << (bit - 1)) + value)
            kept.append(fixed + self.mine[bit] * (1 << (bit - 1)) + value)
        return bit, sent, kept

    def stage_copies(self, stage):
        rows = self.rows // 2
        copies = []
        for half in range(2):
            bit, sent, _ = self.block_sets(half, stage)
            for n, block in enumerate(sent):
                at = (half, self.slot_of(stage) + n)
                copies.append(
                    pltpu.make_async_remote_copy(
                        src_ref=self.held(block).at[pl.ds(half * rows, rows)],
                        dst_ref=self.later_in.at[at],
                        send_sem=self.send_sem.at[at],
                        recv_sem=self.recv_sem.at[at],
                        device_id=self.partners[bit],
                        device_id_type=MESH,
                    )
                )
        return copies

    def start(self, stage):
        for copy in self.stage_copies(stage):
            copy.start()

    def end(self, stage):
        for copy in self.stage_copies(stage):
            copy.wait()
        rows = self.rows // 2
        for half in range(2):
            _, _, kept = self.block_sets(half, stage)
            for n, block in enumerate(kept):
                at = (half, self.slot_of(stage) + n)
                add_rows(self.held(block), self.later_in.at[at], half * rows, rows)

    def mine_now(self):
        return self.held(self.place // 2)


def halving_scratch(ctx_count, rows, columns):
    pairs = ctx_count // 2
    return [
        pltpu.VMEM((pairs, rows, columns), jnp.bfloat16),
        pltpu.VMEM((2, pairs - 1, rows // 2, columns), jnp.bfloat16),
        pltpu.SemaphoreType.DMA((pairs,)),
        pltpu.SemaphoreType.DMA((pairs,)),
        pltpu.SemaphoreType.DMA((2, pairs - 1)),
        pltpu.SemaphoreType.DMA((2, pairs - 1)),
    ]


def unit_rows(v):
    scale = lax.rsqrt(jnp.mean(v * v, axis=-1, keepdims=True) + epsilon)
    return v * scale, scale


def turned(v, cosine, sine_part):
    halfway = v.shape[-1] // 2
    leading, trailing = v[:, :halfway], v[:, halfway:]
    return jnp.concatenate(
        [leading * cosine - trailing * sine_part, trailing * cosine + leading * sine_part], axis=-1
    )


def unit_rows_pull(v, grad, gain):
    unit, scale = unit_rows(v)
    gain_grad = jnp.sum(grad * unit, axis=0, keepdims=True)
    scaled = grad * gain
    return scale * (scaled - unit * jnp.mean(unit * scaled, axis=-1, keepdims=True)), gain_grad


def head_at(h):
    return pl.ds(pl.multiple_of(h * HD, HD), HD)


def attention_forward_kernel(
    ctx_count,
    lines,
    raw,
    cosine_ref,
    sine_ref,
    query_gain,
    key_gain,
    row_ids,
    key_ids,
    _,
    *refs,
):
    line_owns, refs = refs[:lines], refs[lines:]
    kv, query_low, attended_low, log_totals, weights_out = refs[:5]
    line_outs, refs = refs[5 : 5 + lines], refs[5 + lines :]
    bias, send_sem, recv_sem, core_send, core_recv, weight_sems, weight_core_sems = refs[:7]
    line = LineGather(
        weights_out.shape[0], line_owns, line_outs, refs[7 : 7 + lines], *refs[7 + lines :]
    )
    line.load()
    position = ctx_position(ctx_count)
    bits, place, along, mine, partners, _ = position
    count = weights_out.shape[0]
    units = [(way, step) for step in range(1, count) for way in range(2)]

    def weight_copies(way, step, stage):
        lead = (line_origin(along, way, step),)
        at = (way, step - 1)
        return [
            spread_copy(
                weights_out,
                lead,
                half,
                stage,
                position,
                weight_sems.at[(0,) + at],
                weight_sems.at[(1,) + at],
            )
            for half in range(2)
        ]

    def weight_core_copy(way, step):
        at = (way, step - 1)
        return sibling_copy(
            weights_out,
            (line_origin(along, way, step),),
            position,
            weight_core_sems.at[(0,) + at],
            weight_core_sems.at[(1,) + at],
        )

    def each_unit(action):
        for way, step in units:
            pl.when(line_comes(along, count, way, step))(functools.partial(action, way, step))

    def start_weights(stage):
        def action(way, step):
            for copy in weight_copies(way, step, stage):
                copy.start()

        each_unit(action)

    def land_weights(stage):
        def action(way, step):
            for copy in weight_copies(way, step, stage):
                copy.wait_recv()

        each_unit(action)

    rows = raw.shape[0]
    groups = HEADS // KV_HEADS
    length = ctx_count * rows
    here = held_index(mine, (), bits)
    cosine, sine_part = cosine_ref[...], sine_ref[...]
    partner_barrier(partners + line.partners())
    start_weights(0)
    line.forward(1)
    for k in range(KV_HEADS):
        unit, _ = unit_rows(raw[:, pl.ds((HEADS + k) * HD, HD)])
        key = turned(unit * key_gain[...], cosine, sine_part)
        kv[here + (slice(None), pl.ds(k * HD, HD))] = key.astype(kv.dtype)
        value, _ = unit_rows(raw[:, pl.ds((HEADS + KV_HEADS + k) * HD, HD)])
        kv[here + (slice(None), pl.ds((KV_HEADS + k) * HD, HD))] = value.astype(kv.dtype)

    def copies_of(stage):
        return [spread_copy(kv, (), h, stage, position, send_sem, recv_sem) for h in range(2)]

    for copy in copies_of(0):
        copy.start()
    line.store()
    allowed = (row_ids[...] == key_ids[...]) & (
        lax.broadcasted_iota(jnp.int32, (rows, length), 1)
        <= lax.broadcasted_iota(jnp.int32, (rows, length), 0) + place * rows
    )
    bias[...] = jnp.where(allowed, 0.0, masked_score)

    def one_query(h, carry):
        unit, _ = unit_rows(raw[:, head_at(h)])
        query = turned(unit * query_gain[...], cosine, sine_part)
        query_low[:, head_at(h)] = query.astype(query_low.dtype)
        return carry

    lax.fori_loop(0, HEADS, one_query, 0)
    for stage in range(1, bits - 1):
        for copy in copies_of(stage - 1):
            copy.wait()
        for copy in copies_of(stage):
            copy.start()
        land_weights(stage - 1)
        start_weights(stage)
        line.arrive()
    for copy in copies_of(bits - 2):
        copy.wait()
    last = sibling_copy(kv, (), position, core_send, core_recv)
    last.start()
    last.wait()
    everywhere = (slice(None),) * (bits + 1)
    for k in range(KV_HEADS):
        key = kv[everywhere + (pl.ds(k * HD, HD),)].reshape(length, HD)
        value = kv[everywhere + (pl.ds((KV_HEADS + k) * HD, HD),)].reshape(length, HD)

        def one_head(g, carry, k=k, key=key, value=value):
            h = k * groups + g
            scores = across(query_low[:, head_at(h)], key) + bias[...]
            row_max = jnp.max(scores, axis=-1, keepdims=True)
            weights = jnp.exp(scores - row_max)
            row_total = jnp.sum(weights, axis=-1, keepdims=True)
            weights = (weights * (1.0 / row_total)).astype(value.dtype)
            attended_low[:, head_at(h)] = forward_product(weights, value).astype(attended_low.dtype)
            log_total = jnp.broadcast_to(row_max + jnp.log(row_total), (rows, rows))
            log_totals[h] = log_total.T[:8]
            return carry

        lax.fori_loop(0, groups, one_head, 0)
        line.arrive()
        if k == KV_HEADS - 2:
            land_weights(bits - 2)
            each_unit(lambda way, step: weight_core_copy(way, step).start())

    def finish(way, step):
        for stage in range(bits - 1):
            for copy in weight_copies(way, step, stage):
                copy.wait_send()
        weight_core_copy(way, step).wait()

    each_unit(finish)
    line.finish()


def attention_forward(raw, cosine, sine_part, query_gain, key_gain, row_ids, key_ids, weights, lines):
    ctx_count = lax.axis_size("ctx")
    steps = lax.axis_size("fsdp") - 1
    hbm = pl.BlockSpec(memory_space=pltpu.HBM)
    bits = ctx_count.bit_length() - 1
    rows = raw.shape[0]
    length = ctx_count * rows
    low = jnp.bfloat16
    vmem = pl.BlockSpec(memory_space=pltpu.VMEM)
    return pl.pallas_call(
        functools.partial(attention_forward_kernel, ctx_count, len(lines)),
        out_shape=[
            jax.ShapeDtypeStruct((2,) * bits + (rows, 2 * KV_HEADS * HD), low),
            jax.ShapeDtypeStruct((rows, HEADS * HD), low),
            jax.ShapeDtypeStruct((rows, HEADS * HD), low),
            jax.ShapeDtypeStruct((HEADS, 8, rows), jnp.float32),
            jax.ShapeDtypeStruct(weights.shape, low),
        ]
        + [jax.ShapeDtypeStruct((steps + 1,) + w.shape, low) for w in lines],
        in_specs=[vmem] * 7 + [hbm] * (1 + len(lines)),
        out_specs=[vmem] * 4 + [hbm] * (1 + len(lines)),
        input_output_aliases={7: 4},
        scratch_shapes=[
            pltpu.VMEM((rows, length), jnp.float32),
            pltpu.SemaphoreType.DMA((2, bits - 1)),
            pltpu.SemaphoreType.DMA((2, bits - 1)),
            pltpu.SemaphoreType.DMA,
            pltpu.SemaphoreType.DMA,
            pltpu.SemaphoreType.DMA((2, 2, steps, 2, bits - 1)),
            pltpu.SemaphoreType.DMA((2, 2, steps)),
        ]
        + [pltpu.VMEM(w.shape, low) for w in lines]
        + [
            pltpu.SemaphoreType.DMA((2, len(lines))),
            pltpu.SemaphoreType.DMA((len(lines), 2, steps)),
            pltpu.SemaphoreType.DMA((len(lines), 2, steps)),
        ],
        compiler_params=pltpu.CompilerParams(
            collective_id=2, has_side_effects=True, vmem_limit_bytes=56 << 20
        ),
        cost_estimate=pl.CostEstimate(
            flops=4 * HEADS * HD * rows * length,
            bytes_accessed=8 << 20,
            transcendentals=HEADS * rows * length,
        ),
        name="attention_forward",
    )(
        raw,
        cosine,
        sine_part,
        query_gain[None],
        key_gain[None],
        row_ids[:, None],
        key_ids[None],
        weights,
        *lines,
    )


def attention_backward_kernel(ctx_count, fsdp_count, extra, exchange, *refs):
    (
        query_low,
        kv,
        log_totals,
        raw,
        cosine_ref,
        sine_ref,
        query_gain,
        key_gain,
        row_ids,
        key_ids,
        row_grads,
        out_weight,
        qkv_weight,
    ) = refs[:13]
    many = len(extra)
    extra_in = refs[13 : 13 + many]
    back, gain_grads, column_grads, normed_grads = refs[13 + many : 17 + many]
    extra_out = refs[17 + many : 17 + 2 * many]
    rest = refs[17 + 2 * many :]
    if exchange:
        back_columns, rest = rest[0], rest[1:]
        *rest, back_send, back_recv = rest
    bias, score_grads, weights_low, query_grads, kv_grads = rest[:5]
    kv_parts = rest[5:11]
    extra_parts = [rest[11 + 8 * i : 19 + 8 * i] for i in range(many)]
    position = ctx_position(ctx_count)
    bits, place, along, mine, partners, _ = position
    pairs = ctx_count // 2
    rows = raw.shape[0]
    column_send, column_recv, grads, streamed, stream_sem = rest[11 + 8 * many :]
    tile = streamed.shape[1]

    head_parts = [(0, HEADS), (HEADS, KV_HEADS), (HEADS + KV_HEADS, KV_HEADS)]

    def back_span(part, owner):
        first, heads = head_parts[part]
        size = heads * HD // fsdp_count
        start = pl.multiple_of(first * HD + owner * size, size)
        return pl.ds(start, size), pl.ds(first * HD // fsdp_count, size)

    def back_copies(part):
        copies = []
        for d, peer in enumerate(peers):
            source, target = back_span(part, peer)
            copies.append(
                pltpu.make_async_remote_copy(
                    src_ref=back.at[:, source],
                    dst_ref=back_columns.at[along, :, target],
                    send_sem=back_send.at[part, d],
                    recv_sem=back_recv.at[part, d],
                    device_id=(place, peer),
                    device_id_type=MESH,
                )
            )
        return copies

    def start_back(part):
        if exchange:
            for copy in back_copies(part):
                copy.start()
            source, target = back_span(part, along)
            back_columns[along, :, target] = back[:, source]

    def stream(weight, columns, use):
        tiles = weight.shape[0] // tile

        def copy(t):
            return pltpu.make_async_copy(
                weight.at[pl.ds(t * tile, tile), pl.ds(0, columns)],
                streamed.at[t % 2, :, pl.ds(0, columns)],
                stream_sem.at[t % 2],
            )

        copy(0).start()
        for t in range(tiles):
            if t + 1 < tiles:
                copy(t + 1).start()
            copy(t).wait()
            use(pl.ds(t * tile, tile), streamed[t % 2, :, :columns])

    peers = [lax.rem(along + d, fsdp_count) for d in range(1, fsdp_count)]
    wide = column_grads.shape[-1]
    column_copies = [
        pltpu.make_async_remote_copy(
            src_ref=row_grads.at[:, pl.ds(pl.multiple_of(peer * wide, wide), wide)],
            dst_ref=column_grads.at[along],
            send_sem=column_send.at[d],
            recv_sem=column_recv.at[d],
            device_id=(place, peer),
            device_id_type=MESH,
        )
        for d, peer in enumerate(peers)
    ]
    groups = HEADS // KV_HEADS
    length = ctx_count * rows
    low = jnp.bfloat16

    kv_sum = Halving(
        position,
        rows,
        lambda b: kv_grads.at[2 * b + 1 - mine[0]],
        lambda b: kv_grads.at[2 * b + mine[0]],
        kv_parts[0],
        kv_parts[1],
        kv_parts[2:6],
    )
    sums, own_copies = [], []
    for i, (block, _) in enumerate(extra):
        held, first_in, later_in, own_sem = extra_parts[i][:4]

        def give(b, i=i, block=block):
            at = pl.multiple_of((2 * b + 1 - mine[0]) * block, 16)
            return extra_in[i].at[pl.ds(at, block)]

        sums.append(
            Halving(
                position,
                block,
                give,
                lambda b, held=held: held.at[b],
                first_in,
                later_in,
                extra_parts[i][4:8],
            )
        )
        copies = []
        for b in range(pairs):
            at = pl.multiple_of((2 * b + mine[0]) * block, 16)
            copies.append(
                pltpu.make_async_copy(
                    extra_in[i].at[pl.ds(at, block)], held.at[b], own_sem.at[b]
                )
            )
            copies[-1].start()
        own_copies.append(copies)

    partner_barrier(partners + [(place, peer) for peer in peers])
    for one in sums:
        one.start_first()
    for copy in column_copies:
        copy.start()
    column_grads[along] = row_grads[:, pl.ds(pl.multiple_of(along * wide, wide), wide)]

    def attended_tile(columns, weight):
        grads[:, columns] = across(row_grads[...], weight).astype(low)

    stream(out_weight, row_grads.shape[1], attended_tile)

    def open_extra(i):
        for b in range(pairs):
            own_copies[i][b].wait()
            sums[i].end_first(b)
        sums[i].start(0)

    allowed = (key_ids[...] == row_ids[...]) & (
        lax.broadcasted_iota(jnp.int32, (length, rows), 0)
        <= lax.broadcasted_iota(jnp.int32, (length, rows), 1) + place * rows
    )
    bias[...] = jnp.where(allowed, 0.0, masked_score)
    everywhere = (slice(None),) * (bits + 1)
    for k in range(KV_HEADS):
        if k < many:
            open_extra(k)
        key = kv[everywhere + (pl.ds(k * HD, HD),)].reshape(length, HD)
        value = kv[everywhere + (pl.ds((KV_HEADS + k) * HD, HD),)].reshape(length, HD)

        def one_head(g, carry, k=k, key=key, value=value):
            h = k * groups + g
            columns = pl.ds(pl.multiple_of(g * rows, rows), rows)
            scores = across(key, query_low[:, head_at(h)]) + bias[...]
            weights = jnp.exp(scores - log_totals[h][:1])
            weight_grad = across(value, grads[:, head_at(h)])
            delta = jnp.sum(weights * weight_grad, axis=0, keepdims=True)
            score_grads[:, columns] = (weights * (weight_grad - delta)).astype(low)
            weights_low[:, columns] = weights.astype(low)
            return carry

        lax.fori_loop(0, groups, one_head, 0)
        heads = [pl.ds((k * groups + g) * HD, HD) for g in range(groups)]
        query_stack = jnp.concatenate([query_low[:, at] for at in heads], axis=0)
        grad_stack = jnp.concatenate([grads[:, at] for at in heads], axis=0)
        key_grad = forward_product(score_grads[...], query_stack).astype(low)
        value_grad = forward_product(weights_low[...], grad_stack).astype(low)
        kv_grads[:, :, pl.ds(k * HD, HD)] = key_grad.reshape(ctx_count, rows, HD)
        kv_grads[:, :, pl.ds((KV_HEADS + k) * HD, HD)] = value_grad.reshape(ctx_count, rows, HD)
        query_grad = over_rows(key, score_grads[...])
        for g, at in enumerate(heads):
            query_grads[:, at] = query_grad[:, g * rows : (g + 1) * rows].T

    kv_sum.start_first()
    for b in range(pairs):
        kv_sum.end_first(b)
    kv_sum.start(0)
    for i in range(KV_HEADS, many):
        open_extra(i)

    def step_extra(i, stage):
        sums[i].end(stage - 1)
        sums[i].start(stage)

    cosine, sine_part = cosine_ref[...], sine_ref[...]

    def one_query(h, gain_grad):
        grad = turned(query_grads[:, head_at(h)], cosine, -sine_part)
        pulled, more = unit_rows_pull(raw[:, head_at(h)], grad, query_gain[...])
        back[:, head_at(h)] = pulled.astype(low)
        return gain_grad + more

    gain_grads[0:1] = lax.fori_loop(0, HEADS, one_query, jnp.zeros((1, HD), jnp.float32))
    start_back(0)
    for stage in range(1, bits - 1):
        kv_sum.end(stage - 1)
        kv_sum.start(stage)
    kv_sum.end(bits - 2)
    for i in range(many):
        step_extra(i, 1)
    summed = kv_sum.mine_now()
    key_gain_grad = jnp.zeros((1, HD), jnp.float32)
    for k in range(KV_HEADS):
        grad = summed[:, pl.ds(k * HD, HD)].astype(jnp.float32)
        grad = turned(grad, cosine, -sine_part)
        at = pl.ds((HEADS + k) * HD, HD)
        pulled, more = unit_rows_pull(raw[:, at], grad, key_gain[...])
        back[:, at] = pulled.astype(low)
        key_gain_grad = key_gain_grad + more
        grad = summed[:, pl.ds((KV_HEADS + k) * HD, HD)].astype(jnp.float32)
        at = pl.ds((HEADS + KV_HEADS + k) * HD, HD)
        pulled, _ = unit_rows_pull(raw[:, at], grad, 1.0)
        back[:, at] = pulled.astype(low)
    gain_grads[1:2] = key_gain_grad
    start_back(1)
    start_back(2)

    def normed_tile(columns, weight):
        normed_grads[:, columns] = across(back[...], weight)

    stream(qkv_weight, back.shape[1], normed_tile)
    for stage in range(2, bits - 1):
        for i in range(many):
            step_extra(i, stage)
    for copy in column_copies:
        copy.wait()
    if exchange:
        for part in range(3):
            for copy in back_copies(part):
                copy.wait()
    for i in range(many):
        sums[i].end(bits - 2)
        extra_out[i][...] = sums[i].mine_now()[...]


def attention_backward(
    query_low,
    kv,
    log_totals,
    raw,
    cosine,
    sine_part,
    query_gain,
    key_gain,
    row_ids,
    key_ids,
    row_grads,
    out_weight,
    qkv_weight,
    extra,
):
    fsdp_count = lax.axis_size("fsdp")
    hbm = pl.BlockSpec(memory_space=pltpu.HBM)
    ctx_count = lax.axis_size("ctx")
    rows = raw.shape[0]
    length = ctx_count * rows
    pairs = ctx_count // 2
    groups = HEADS // KV_HEADS
    low = jnp.bfloat16
    vmem = pl.BlockSpec(memory_space=pltpu.VMEM)
    shapes = [(a.shape[0] // ctx_count, a.shape[1]) for a in extra]
    scratch = [
        pltpu.VMEM((length, rows), jnp.float32),
        pltpu.VMEM((length, groups * rows), low),
        pltpu.VMEM((length, groups * rows), low),
        pltpu.VMEM((rows, HEADS * HD), jnp.float32),
        pltpu.VMEM((ctx_count, rows, 2 * KV_HEADS * HD), low),
    ]
    scratch += halving_scratch(ctx_count, rows, 2 * KV_HEADS * HD)
    for shape in shapes:
        parts = halving_scratch(ctx_count, *shape)
        scratch += [pltpu.VMEM((pairs,) + shape, low)] + parts[:2]
        scratch += [pltpu.SemaphoreType.DMA((pairs,))] + parts[2:]
    scratch += [pltpu.SemaphoreType.DMA((fsdp_count - 1,))] * 2
    scratch += [
        pltpu.VMEM((rows, HEADS * HD), low),
        pltpu.VMEM((2, FF_TILE, qkv_weight.shape[1]), low),
        pltpu.SemaphoreType.DMA((2,)),
    ]
    exchange = KV_HEADS * HD // fsdp_count % 128 == 0
    back_out = []
    if exchange:
        scratch += [pltpu.SemaphoreType.DMA((3, fsdp_count - 1))] * 2
        back_out = [jax.ShapeDtypeStruct((fsdp_count, rows, raw.shape[1] // fsdp_count), low)]
    columns_shape = (fsdp_count, rows, row_grads.shape[1] // fsdp_count)
    outs = pl.pallas_call(
        functools.partial(attention_backward_kernel, ctx_count, fsdp_count, shapes, exchange),
        out_shape=[
            jax.ShapeDtypeStruct(raw.shape, low),
            jax.ShapeDtypeStruct((8, HD), jnp.float32),
            jax.ShapeDtypeStruct(columns_shape, low),
            jax.ShapeDtypeStruct((rows, qkv_weight.shape[0]), jnp.float32),
        ]
        + [jax.ShapeDtypeStruct(s, low) for s in shapes]
        + back_out,
        in_specs=[vmem] * 11 + [hbm] * (2 + len(extra)),
        out_specs=[vmem] * (4 + len(extra) + len(back_out)),
        scratch_shapes=scratch,
        compiler_params=pltpu.CompilerParams(
            collective_id=3, has_side_effects=True, vmem_limit_bytes=60 << 20
        ),
        cost_estimate=pl.CostEstimate(
            flops=10 * HEADS * HD * rows * length,
            bytes_accessed=64 << 20,
            transcendentals=HEADS * rows * length,
        ),
        name="attention_backward",
    )(
        query_low,
        kv,
        log_totals,
        raw,
        cosine,
        sine_part,
        query_gain[None],
        key_gain[None],
        row_ids[None],
        key_ids[:, None],
        row_grads,
        out_weight,
        qkv_weight,
        *extra,
    )
    columns = outs[2].reshape(-1, outs[2].shape[-1])
    back_columns = None
    if exchange:
        back_columns = outs[-1].reshape(-1, outs[-1].shape[-1])
    sums = outs[4 : 4 + len(extra)]
    return outs[0], outs[1][0], outs[1][1], columns, outs[3], sums, back_columns


def owner_sum_kernel(ctx_count, fsdp_count, shapes, shared, *refs):
    many = len(shapes)
    whole = many - shared
    ins, outs = refs[:many], refs[many : 2 * many]
    rest = refs[2 * many :]
    parts = [rest[8 * i : 8 * i + 8] for i in range(many)]
    shares = rest[8 * many : 8 * many + shared]
    send_z, recv_z = rest[8 * many + shared :]
    position = ctx_position(ctx_count)
    bits, place, along, mine, partners, _ = position
    pairs = ctx_count // 2
    across_line = [(place, lax.rem(along + d, fsdp_count)) for d in range(1, fsdp_count)]
    partner_barrier(partners + across_line)
    sums, own_copies = [], []
    for i, (block, _) in enumerate(shapes):
        held, first_in, later_in, own_sem = parts[i][:4]

        def give(b, i=i, block=block):
            at = pl.multiple_of((2 * b + 1 - mine[0]) * block, 16)
            return ins[i].at[pl.ds(at, block)]

        sums.append(
            Halving(
                position,
                block,
                give,
                lambda b, held=held: held.at[b],
                first_in,
                later_in,
                parts[i][4:8],
            )
        )
        sums[i].start_first()
        copies = []
        for b in range(pairs):
            at = pl.multiple_of((2 * b + mine[0]) * block, 16)
            copies.append(
                pltpu.make_async_copy(ins[i].at[pl.ds(at, block)], held.at[b], own_sem.at[b])
            )
            copies[-1].start()
        own_copies.append(copies)
    order = list(range(whole, many)) + list(range(whole))
    for i in order:
        for b in range(pairs):
            own_copies[i][b].wait()
            sums[i].end_first(b)
        sums[i].start(0)
    for stage in range(1, bits - 1):
        for i in order:
            sums[i].end(stage - 1)
            sums[i].start(stage)

    def share_copies(i):
        size = shapes[i][0] // fsdp_count
        return [
            pltpu.make_async_remote_copy(
                src_ref=sums[i].mine_now().at[pl.ds(pl.multiple_of(peer[1] * size, 16), size)],
                dst_ref=shares[i - whole].at[d],
                send_sem=send_z.at[i - whole, d],
                recv_sem=recv_z.at[i - whole, d],
                device_id=peer,
                device_id_type=MESH,
            )
            for d, peer in enumerate(across_line)
        ]

    for i in range(whole, many):
        sums[i].end(bits - 2)
        for copy in share_copies(i):
            copy.start()
    for i in range(whole):
        sums[i].end(bits - 2)
        outs[i][...] = sums[i].mine_now()[...]
    for i in range(whole, many):
        for copy in share_copies(i):
            copy.wait()
        size = shapes[i][0] // fsdp_count
        own = sums[i].mine_now()[pl.ds(pl.multiple_of(along * size, 16), size)]
        total = own.astype(jnp.float32)
        for d in range(fsdp_count - 1):
            total = total + shares[i - whole][d].astype(jnp.float32)
        outs[i][...] = total.astype(outs[i].dtype)


def owner_sums(arrays, shared):
    ctx_count = lax.axis_size("ctx")
    fsdp_count = lax.axis_size("fsdp")
    pairs = ctx_count // 2
    many = len(arrays)
    whole = many - shared
    low = jnp.bfloat16
    shapes = [(a.shape[0] // ctx_count, a.shape[1]) for a in arrays]
    share_shapes = [(s[0] // fsdp_count, s[1]) for s in shapes[whole:]]
    scratch = []
    for shape in shapes:
        parts = halving_scratch(ctx_count, *shape)
        scratch += [pltpu.VMEM((pairs,) + shape, low)] + parts[:2]
        scratch += [pltpu.SemaphoreType.DMA((pairs,))] + parts[2:]
    scratch += [pltpu.VMEM((fsdp_count - 1,) + s, low) for s in share_shapes]
    scratch += [pltpu.SemaphoreType.DMA((shared, fsdp_count - 1))] * 2
    total = sum(a.size for a in arrays)
    return pl.pallas_call(
        functools.partial(owner_sum_kernel, ctx_count, fsdp_count, shapes, shared),
        out_shape=[jax.ShapeDtypeStruct(s, low) for s in shapes[:whole] + share_shapes],
        in_specs=[pl.BlockSpec(memory_space=pl.ANY)] * many,
        out_specs=[pl.BlockSpec(memory_space=pltpu.VMEM)] * many,
        scratch_shapes=scratch,
        compiler_params=pltpu.CompilerParams(
            collective_id=0, has_side_effects=True, vmem_limit_bytes=48 << 20
        ),
        cost_estimate=pl.CostEstimate(flops=total, bytes_accessed=4 * total, transcendentals=0),
        name="owner_sums",
    )(*arrays)


class LineExchange:
    def __init__(self, count, own, gathered, outgoing, incoming, sems):
        self.count, self.steps = count, count - 1
        self.own, self.gathered = own, gathered
        self.outgoing, self.incoming = outgoing, incoming
        self.line_send, self.line_recv, self.back_send, self.back_recv = sems
        self.place = lax.axis_index("ctx")
        self.along = lax.axis_index("fsdp")
        self.width = outgoing.shape[-1]
        self.chunks = self.width // BACK_TILE

    def partners(self):
        return [
            (self.place, lax.rem(self.along + d, self.count)) for d in sorted({1, self.count - 1})
        ]

    def line_copy(self, way, step, origin):
        toward = self.along + 1 if way == 0 else self.along - 1
        return pltpu.make_async_remote_copy(
            src_ref=self.own if step == 1 else self.gathered.at[origin],
            dst_ref=self.gathered.at[origin],
            send_sem=self.line_send.at[way, step - 1],
            recv_sem=self.line_recv.at[way, step - 1],
            device_id=(self.place, toward),
            device_id_type=MESH,
        )

    def forward(self, step):
        for way in range(2):
            origin = line_origin(self.along, way, step - 1)
            pl.when(line_goes(self.along, self.count, way, step))(
                lambda way=way, origin=origin: self.line_copy(way, step, origin).start()
            )

    def arrive(self, step):
        for way in range(2):
            origin = line_origin(self.along, way, step)
            pl.when(line_comes(self.along, self.count, way, step))(
                lambda way=way, origin=origin: self.line_copy(way, step, origin).wait_recv()
            )
        if step < self.steps:
            self.forward(step + 1)

    def back_copy(self, way, owner, chunk):
        toward = self.along + 1 if way == 0 else self.along - 1
        columns = tile_at(chunk, BACK_TILE)
        landing = owner if way == 0 else jnp.where(owner == toward, self.count, owner)
        return pltpu.make_async_remote_copy(
            src_ref=self.outgoing.at[owner, :, columns],
            dst_ref=self.incoming.at[landing, :, columns],
            send_sem=self.back_send.at[way, owner, chunk],
            recv_sem=self.back_recv.at[way, owner, chunk],
            device_id=(self.place, toward),
            device_id_type=MESH,
        )

    def landed(self, way, owner, chunk, landing):
        columns = pl.ds(chunk * BACK_TILE, BACK_TILE)
        pltpu.make_async_remote_copy(
            src_ref=self.outgoing.at[owner, :, columns],
            dst_ref=self.incoming.at[landing, :, columns],
            send_sem=self.back_send.at[way, owner, chunk],
            recv_sem=self.back_recv.at[way, owner, chunk],
            device_id=(self.place, self.along),
            device_id_type=MESH,
        ).wait_recv()
        return self.incoming[landing, :, columns].astype(jnp.float32)

    def relays(self, way):
        return self.along >= 1 if way == 0 else self.along + 1 < self.count

    def run(self, compute, before_last):

        def one(way, step):
            back = 1 - way
            origin = line_origin(self.along, way, step)

            def work():
                def write(chunk, tile):
                    columns = tile_at(chunk, BACK_TILE)
                    self.outgoing[origin, :, columns] = tile.astype(self.outgoing.dtype)
                    pl.when(jnp.logical_not(self.relays(back)))(
                        lambda: self.back_copy(back, origin, chunk).start()
                    )

                compute(origin, write)

            pl.when(line_comes(self.along, self.count, way, step))(work)

        near_start = 2 * self.along < self.steps

        def relay(way, step, turn):
            owner = step if way == 0 else self.steps - step
            passes = owner > self.along if way == 0 else owner < self.along

            def work():
                for chunk in range(self.chunks):
                    more = self.landed(way, owner, chunk, owner)
                    columns = pl.ds(chunk * BACK_TILE, BACK_TILE)
                    mine = self.outgoing[owner, :, columns].astype(jnp.float32)
                    self.outgoing[owner, :, columns] = (mine + more).astype(self.outgoing.dtype)
                    self.back_copy(way, owner, chunk).start()

            pl.when(self.relays(way) & passes & turn)(work)

        for step in range(1, self.steps + 1):
            self.arrive(step)
            for way in range(2):
                one(way, step)
            if step == self.steps:
                before_last()
            relay(0, step, near_start)
            relay(1, step, True)
            relay(0, step, jnp.logical_not(near_start))

    def finish(self, total):
        for way in range(2):

            def receive(way=way):
                landing = self.along if way == 0 else self.count
                for chunk in range(self.chunks):
                    columns = pl.ds(chunk * BACK_TILE, BACK_TILE)
                    more = self.landed(way, self.along, chunk, landing)
                    total[:, columns] = total[:, columns] + more

            pl.when(self.relays(way))(receive)
        for step in range(1, self.steps + 1):
            for way in range(2):
                origin = line_origin(self.along, way, step - 1)

                def left(way=way, step=step, origin=origin):
                    self.line_copy(way, step, origin).wait_send()

                def returned(way=way, step=step):
                    for chunk in range(self.chunks):
                        self.back_copy(1 - way, line_origin(self.along, way, step), chunk).wait_send()

                pl.when(line_goes(self.along, self.count, way, step))(left)
                pl.when(line_comes(self.along, self.count, way, step))(returned)


def line_scratch(count, rows, columns):
    steps = count - 1
    chunks = columns // BACK_TILE
    return [
        pltpu.VMEM((count, rows, columns), jnp.bfloat16),
        pltpu.VMEM((count + 1, rows, columns), jnp.bfloat16),
        pltpu.SemaphoreType.DMA((2, steps)),
        pltpu.SemaphoreType.DMA((2, steps)),
        pltpu.SemaphoreType.DMA((2, count, chunks)),
        pltpu.SemaphoreType.DMA((2, count, chunks)),
    ]


def tile_at(t, size):
    return pl.ds(pl.multiple_of(t * size, size), size)


def feed_forward_kernel(
    count,
    rows_in,
    gate_hbm,
    up_hbm,
    down_hbm,
    total,
    gathered,
    gate_keep,
    up_keep,
    hidden_keep,
    gate_w,
    up_w,
    down_w,
    weight_sem,
    *parts,
):
    rows, width = rows_in.shape
    units = gate_w.shape[1]
    tile = FF_TILE
    line = LineExchange(count, rows_in, gathered, parts[0], parts[1], parts[2:])
    loads = []
    for n, (source, target) in enumerate(((gate_hbm, gate_w), (up_hbm, up_w), (down_hbm, down_w))):
        group = []
        for t in range(target.shape[1] // tile):
            at = (slice(None), pl.ds(t * tile, tile))
            group.append(pltpu.make_async_copy(source.at[at], target.at[at], weight_sem.at[n, t]))
        loads.append(group)
    for t in range(units // tile):
        loads[0][t].start()
        loads[1][t].start()
    for load in loads[2]:
        load.start()
    partner_barrier(line.partners())
    line.forward(1)
    gathered[line.along] = rows_in[...]

    def hidden_tile(origin, columns):
        at = pl.ds(pl.multiple_of(origin * rows, rows), rows)
        gate = forward_product(gathered[origin], gate_w[:, columns])
        up = forward_product(gathered[origin], up_w[:, columns])
        gate_keep[at, columns] = gate.astype(gate_keep.dtype)
        up_keep[at, columns] = up.astype(up_keep.dtype)
        hidden_keep[at, columns] = hidden_piece(gate, up).astype(hidden_keep.dtype)

    def out_tile(origin, columns):
        at = pl.ds(pl.multiple_of(origin * rows, rows), rows)
        return forward_product(hidden_keep[at], down_w[:, columns])

    for t in range(units // tile):
        loads[0][t].wait()
        loads[1][t].wait()
        hidden_tile(line.along, pl.ds(t * tile, tile))
    for t in range(width // tile):
        loads[2][t].wait()
        columns = pl.ds(t * tile, tile)
        total[:, columns] = out_tile(line.along, columns)

    def compute(origin, write):
        def hidden_step(t, carry):
            hidden_tile(origin, tile_at(t, tile))
            return carry

        def out_step(t, carry):
            write(t, out_tile(origin, tile_at(t, tile)))
            return carry

        lax.fori_loop(0, units // tile, hidden_step, 0)
        lax.fori_loop(0, width // tile, out_step, 0)

    line.run(compute, lambda: None)
    line.finish(total)


def feed_forward(rows_in, gate_weight, up_weight, down_weight):
    count = lax.axis_size("fsdp")
    rows, width = rows_in.shape
    units = gate_weight.shape[1]
    low = jnp.bfloat16
    vmem = pl.BlockSpec(memory_space=pltpu.VMEM)
    hbm = pl.BlockSpec(memory_space=pltpu.HBM)
    kept = jax.ShapeDtypeStruct((count * rows, units), low)
    out, gathered, gate, up, hidden = pl.pallas_call(
        functools.partial(feed_forward_kernel, count),
        out_shape=[
            jax.ShapeDtypeStruct((rows, width), jnp.float32),
            jax.ShapeDtypeStruct((count, rows, width), low),
            kept,
            kept,
            kept,
        ],
        in_specs=[vmem, hbm, hbm, hbm],
        out_specs=[vmem] * 5,
        scratch_shapes=[
            pltpu.VMEM((width, units), low),
            pltpu.VMEM((width, units), low),
            pltpu.VMEM((units, width), low),
            pltpu.SemaphoreType.DMA((3, max(width, units) // FF_TILE)),
        ]
        + line_scratch(count, rows, width),
        compiler_params=pltpu.CompilerParams(
            collective_id=4, has_side_effects=True, vmem_limit_bytes=56 << 20
        ),
        cost_estimate=pl.CostEstimate(
            flops=6 * count * rows * width * units,
            bytes_accessed=6 * width * units,
            transcendentals=count * rows * units,
        ),
        name="feed_forward",
    )(rows_in, gate_weight, up_weight, down_weight)
    return out, gathered.reshape(count * rows, width), gate, up, hidden


def hidden_pull_tile(grad, gate, up):
    slope = math.sqrt(2.0 / math.pi)
    square = gate * gate
    curve = jnp.tanh(slope * gate * (1.0 + 0.044715 * square))
    bend = 0.5 * (1.0 + curve)
    steep = bend + 0.5 * gate * (1.0 - curve * curve) * slope * (1.0 + 3.0 * 0.044715 * square)
    return grad * up * steep, grad * gate * bend


def feed_forward_backward_kernel(
    count,
    grads_in,
    gate_keep,
    up_keep,
    hidden_keep,
    tokens,
    gate_hbm,
    up_hbm,
    down_hbm,
    total,
    down_sum,
    down_rest,
    gate_grad,
    up_grad,
    gathered,
    gate_back,
    up_back,
    gate_w,
    up_w,
    down_w,
    weight_sem,
    staged,
    staged_sem,
    later_in,
    send_zero,
    recv_zero,
    send_sem,
    recv_sem,
    ready_sem,
    rest_sem,
    *parts,
):
    rows, width = grads_in.shape
    ctx_count, block, units = gate_w.shape
    pairs = ctx_count // 2
    position = ctx_position(ctx_count)
    bits, _, _, mine, partners, _ = position
    tile = FF_TILE
    blocks = tile // block
    line = LineExchange(count, grads_in, gathered, parts[0], parts[1], parts[2:])
    loads = []
    for n, (source, target) in enumerate(((gate_hbm, gate_w), (up_hbm, up_w), (down_hbm, down_w))):
        group = []
        size = tile if n else blocks
        for t in range(target.shape[0] // size):
            at = pl.ds(t * size, size)
            group.append(pltpu.make_async_copy(source.at[at], target.at[at], weight_sem.at[n, t]))
        loads.append(group)
    for load in loads[2]:
        load.start()
    for t in range(width // tile):
        loads[0][t].start()
        loads[1][t].start()
    partner_barrier(partners + line.partners())
    line.forward(1)
    gathered[line.along] = grads_in[...]

    def hidden_tile(origin, columns):
        at = pl.ds(pl.multiple_of(origin * rows, rows), rows)
        grad = across(gathered[origin], down_w[columns])
        gate = gate_keep[at, columns].astype(jnp.float32)
        up = up_keep[at, columns].astype(jnp.float32)
        gate_pull, up_pull = hidden_pull_tile(grad, gate, up)
        gate_back[at, columns] = gate_pull.astype(gate_back.dtype)
        up_back[at, columns] = up_pull.astype(up_back.dtype)

    def out_tile(origin, t):
        at = pl.ds(pl.multiple_of(origin * rows, rows), rows)
        gate_rows = gate_w[pl.ds(t * blocks, blocks)].reshape(tile, units)
        return across(gate_back[at], gate_rows) + across(up_back[at], up_w[tile_at(t, tile)])

    for t in range(units // tile):
        loads[2][t].wait()
        hidden_tile(line.along, pl.ds(t * tile, tile))
    for t in range(width // tile):
        loads[0][t].wait()
        loads[1][t].wait()
        total[:, pl.ds(t * tile, tile)] = out_tile(line.along, t)

    def compute(origin, write):
        def hidden_step(t, carry):
            hidden_tile(origin, tile_at(t, tile))
            return carry

        def out_step(t, carry):
            write(t, out_tile(origin, t))
            return carry

        lax.fori_loop(0, units // tile, hidden_step, 0)
        lax.fori_loop(0, width // tile, out_step, 0)

    half = down_sum.shape[1]
    here, there = pl.ds(0, half), pl.ds(half, units - half)
    down = Halving(
        position,
        block,
        lambda b: staged.at[b // 2 % 2, b % 2, :, here],
        lambda b: gate_w.at[b, :, here],
        gate_w.at[pl.ds(pairs, pairs), :, here],
        later_in,
        (send_zero, recv_zero, send_sem, recv_sem),
    )

    def down_block(c):
        left = gathered[:, :, tile_at(c, block)].reshape(count * rows, block)
        return over_rows(left, hidden_keep[...]).astype(gate_w.dtype)

    def rest_copy(source, c):
        return pltpu.make_async_copy(
            source.at[:, there], down_rest.at[tile_at(c, block)], rest_sem.at[c]
        )

    def given(b):
        return rest_copy(staged.at[b // 2 % 2, b % 2], 2 * b + 1 - mine[0])

    def kept(b):
        return rest_copy(gate_w.at[b], 2 * b + mine[0])

    def start_down():
        pl.semaphore_signal(ready_sem, inc=1, device_id=partners[0], device_id_type=MESH)
        pl.semaphore_wait(ready_sem, 1)
        for b in range(pairs):
            if b >= 4:
                down.first_copy(b - 4).wait_send()
                given(b - 4).wait()
            staged[b // 2 % 2, b % 2] = down_block(2 * b + 1 - mine[0])
            down.first_copy(b).start()
            given(b).start()
        for b in range(pairs):
            gate_w[b] = down_block(2 * b + mine[0])
            kept(b).start()
        for b in range(pairs):
            copy = down.first_copy(b)
            if b >= pairs - 4:
                copy.wait_send()
                given(b).wait()
            copy.wait_recv()
            add_rows(down.held(b), down.first_in.at[b], 0, block)
        down.start(0)

    def stage(slot, which, t, target):
        return pltpu.make_async_copy(
            staged.at[slot, which], target.at[tile_at(t, block)], staged_sem.at[slot, which]
        )

    def grad_bands(first, last):
        def step(t, carry):
            slot = lax.rem(t, 2)
            left = tokens[:, tile_at(t, block)]
            for which, (right, target) in enumerate(((gate_back, gate_grad), (up_back, up_grad))):

                @pl.when(t >= 2)
                def _(target=target, which=which):
                    stage(slot, which, t, target).wait()

                staged[slot, which] = over_rows(left, right[...]).astype(staged.dtype)
                stage(slot, which, t, target).start()
            return carry

        lax.fori_loop(first, last, step, 0)

    line.run(compute, start_down)
    grad_bands(0, ctx_count * 3 // 4)
    for step in range(1, bits - 1):
        down.end(step - 1)
        down.start(step)
    grad_bands(ctx_count * 3 // 4, ctx_count)
    line.finish(total)
    for t in (ctx_count - 2, ctx_count - 1):
        for which, target in enumerate((gate_grad, up_grad)):
            stage(t % 2, which, t, target).wait()
    for b in range(pairs):
        kept(b).wait()
    down.end(bits - 2)
    down_sum[...] = down.mine_now()[...]


def feed_forward_backward(
    grads_in, gate_keep, up_keep, hidden_keep, tokens, gate_weight, up_weight, down_weight
):
    count = lax.axis_size("fsdp")
    ctx_count = lax.axis_size("ctx")
    pairs = ctx_count // 2
    rows, width = grads_in.shape
    block = width // ctx_count
    half = gate_weight.shape[1] // 2
    units = gate_weight.shape[1]
    low = jnp.bfloat16
    vmem = pl.BlockSpec(memory_space=pltpu.VMEM)
    hbm = pl.BlockSpec(memory_space=pltpu.HBM)
    grad_shape = jax.ShapeDtypeStruct((width, units), low)
    return pl.pallas_call(
        functools.partial(feed_forward_backward_kernel, count),
        out_shape=[
            jax.ShapeDtypeStruct((rows, width), jnp.float32),
            jax.ShapeDtypeStruct((block, half), low),
            jax.ShapeDtypeStruct((width, units - half), low),
            grad_shape,
            grad_shape,
        ],
        in_specs=[vmem] * 5 + [hbm] * 3,
        out_specs=[vmem, vmem, hbm, hbm, hbm],
        scratch_shapes=[
            pltpu.VMEM((count, rows, width), low),
            pltpu.VMEM((count * rows, units), low),
            pltpu.VMEM((count * rows, units), low),
            pltpu.VMEM((ctx_count, block, units), low),
            pltpu.VMEM((width, units), low),
            pltpu.VMEM((units, width), low),
            pltpu.SemaphoreType.DMA((3, max(width, units) // FF_TILE)),
            pltpu.VMEM((2, 2, block, units), low),
            pltpu.SemaphoreType.DMA((2, 2)),
            *halving_scratch(ctx_count, block, half)[1:],
            pltpu.SemaphoreType.REGULAR,
            pltpu.SemaphoreType.DMA((ctx_count,)),
        ]
        + line_scratch(count, rows, width),
        compiler_params=pltpu.CompilerParams(
            collective_id=5, has_side_effects=True, vmem_limit_bytes=60 << 20
        ),
        cost_estimate=pl.CostEstimate(
            flops=12 * count * rows * width * units,
            bytes_accessed=12 * width * units,
            transcendentals=count * rows * units,
        ),
        name="feed_forward_backward",
    )(
        grads_in,
        gate_keep,
        up_keep,
        hidden_keep,
        tokens,
        gate_weight.reshape(ctx_count, block, units),
        up_weight,
        down_weight,
    )


def body(
    tokens,
    per_layer,
    out_grad,
    segment_ids,
    query_weight,
    key_weight,
    value_weight,
    out_weight,
    left_weight,
    right_weight,
    gate_weight,
    up_weight,
    down_weight,
    side_gate,
    side_out,
    input_gain,
    laurel_gain,
    attn_gain,
    pre_gain,
    post_gain,
    side_gain,
    query_gain,
    key_gain,
):
    low = jnp.bfloat16
    inputs = tokens[0].astype(jnp.float32)
    extra_rows = per_layer[0].astype(jnp.float32)
    cotangent = out_grad[0].astype(jnp.float32)
    sequence_ids = segment_ids[0]
    rows_here, width = inputs.shape
    ctx_count = lax.axis_size("ctx")
    fsdp_count = lax.axis_size("fsdp")
    count = ctx_count * fsdp_count
    ctx_place = lax.axis_index("ctx")
    rank = left_weight.shape[1]
    side = side_gate.shape[1]
    query_width = HEADS * HD
    kv_width = KV_HEADS * HD
    query_pos = ctx_place * rows_here + jnp.arange(rows_here, dtype=jnp.int32)

    piece = width // count

    qkv_width = query_width + 2 * kv_width
    full_qkv, second_line = weight_gather(
        [[query_weight, key_weight, value_weight], [out_weight, side_gate]], 1
    )

    normed, input_pull = jax.vjp(rms_norm, inputs, input_gain)
    normed_low = normed.astype(low)
    qkv_raw = forward_product(normed_low, full_qkv)
    frequency = jnp.exp(
        jnp.arange(HD // 2).astype(jnp.float32) * (-2.0 * math.log(rope_theta) / HD)
    )
    angles = query_pos.astype(jnp.float32)[:, None] * frequency[None, :]
    cosine, sine_part = jnp.cos(angles), jnp.sin(angles)
    query_ids = lax.dynamic_slice_in_dim(sequence_ids, ctx_place * rows_here, rows_here)
    kv_all, query_low, attended_low, log_totals, full_second, *full_small = attention_forward(
        qkv_raw,
        cosine,
        sine_part,
        query_gain,
        key_gain,
        query_ids,
        sequence_ids,
        second_line,
        [left_weight, right_weight, side_out],
    )
    full_left, full_right, full_side_out = full_small
    full_left = full_left.reshape(width, rank)
    full_right = full_right.transpose(1, 0, 2).reshape(rank, width)
    full_side_out = full_side_out.reshape(side, width)
    full_second = full_second.reshape(width, -1)
    full_out = full_second[:, :width]
    full_side_gate = full_second[:, width:]
    left_low = forward_product(normed_low, full_left).astype(low)
    right_out = forward_product(left_low, full_right)
    attn_raw = forward_product(attended_low, full_out)

    def mix_piece(x, normed_in, attn_in, right_in, gain_one, gain_two, gain_three):
        mixed = (
            x + rms_norm(attn_in, gain_one) + normed_in + rms_norm(right_in, gain_two)
        ) * inverse_root
        return (mixed, rms_norm(mixed, gain_three))

    (mixed, ffn_in), mix_pull = jax.vjp(
        mix_piece, inputs, normed, attn_raw, right_out, attn_gain, laurel_gain, pre_gain
    )

    ffn_out, ffn_all, gate_raw, up_raw, hidden_low = feed_forward(
        ffn_in.astype(low), gate_weight, up_weight, down_weight
    )
    middle, middle_pull = jax.vjp(middle_piece, mixed, ffn_out, post_gain)
    middle_low = middle.astype(low)
    layer_gate = forward_product(middle_low, full_side_gate)
    layer_act, extra_pull = jax.vjp(hidden_piece, layer_gate, extra_rows)
    layer_low = layer_act.astype(low)
    layer_out = forward_product(layer_low, full_side_out)
    result, out_pull = jax.vjp(middle_piece, middle, layer_out, side_gain)

    middle_grad_one, layer_out_grad, side_gain_grad = out_pull(cotangent)
    layer_grad_low = layer_out_grad.astype(low)
    side_out_grad = over_rows(layer_low, layer_grad_low)
    layer_gate_grad, extra_grad = extra_pull(across(layer_grad_low, full_side_out))
    gate_grad_low = layer_gate_grad.astype(low)
    side_gate_grad = over_rows(gate_grad_low, middle_low)
    mixed_grad_one, ffn_out_grad, post_gain_grad = middle_pull(
        middle_grad_one + across(gate_grad_low, full_side_gate)
    )
    ffn_in_grad, down_sum, down_rest, gate_weight_grad, up_weight_grad = feed_forward_backward(
        ffn_out_grad.astype(low),
        gate_raw,
        up_raw,
        hidden_low,
        ffn_all,
        gate_weight,
        up_weight,
        down_weight,
    )
    ffn_in_grad, late_low = lax.optimization_barrier((ffn_in_grad, (attended_low, normed_low)))
    attended_all, normed_all = (gather(part, "fsdp") for part in late_low)
    (
        inputs_grad_one,
        normed_grad_one,
        attn_raw_grad,
        right_out_grad,
        attn_gain_grad,
        laurel_gain_grad,
        pre_gain_grad,
    ) = mix_pull((mixed_grad_one, ffn_in_grad))
    attn_grad_low = attn_raw_grad.astype(low)
    right_grad_low = right_out_grad.astype(low)
    right_weight_grad = over_rows(right_grad_low, left_low)
    left_grad_low = across(right_grad_low, full_right).astype(low)
    left_weight_grad = over_rows(normed_low, left_grad_low)
    (
        qkv_back_low,
        query_gain_grad,
        key_gain_grad,
        out_columns,
        normed_grad_two,
        ffn_sums,
        qkv_columns,
    ) = attention_backward(
        query_low,
        kv_all,
        log_totals,
        qkv_raw,
        cosine,
        sine_part,
        query_gain,
        key_gain,
        query_ids,
        sequence_ids,
        attn_grad_low,
        full_second,
        full_qkv,
        [gate_weight_grad, up_weight_grad],
    )
    down_rest, normed_grad_two = lax.optimization_barrier((down_rest, normed_grad_two))
    down_rest = scatter_sum(down_rest, "ctx")
    normed_grad_two = normed_grad_two + across(left_grad_low, full_left)
    inputs_grad_two, input_gain_grad = input_pull(normed_grad_one + normed_grad_two)
    block_out = result.astype(low)[None]
    tokens_grad = (inputs_grad_one + inputs_grad_two).astype(low)[None]
    per_layer_grad = extra_grad.astype(low)[None]

    def columns_to_owner(x):
        parts = x.reshape(rows_here, fsdp_count, -1).transpose(1, 0, 2)
        return lax.all_to_all(parts, "fsdp", 0, 0, tiled=True).reshape(fsdp_count * rows_here, -1)

    out_weight_grad = over_rows(attended_all, out_columns)
    if qkv_columns is None:
        qkv_parts = jnp.concatenate(
            [
                part.reshape(rows_here, fsdp_count, -1)
                for part in (
                    qkv_back_low[:, :query_width],
                    qkv_back_low[:, query_width : query_width + kv_width],
                    qkv_back_low[:, query_width + kv_width :],
                )
            ],
            axis=2,
        )
        qkv_columns = columns_to_owner(qkv_parts.reshape(rows_here, -1))
    qkv_weight_grad = over_rows(normed_all, qkv_columns)

    small_gains = [
        jnp.pad(g.reshape(count, -1), ((0, 0), (0, piece - g.shape[0] // count))).reshape(-1)
        for g in (query_gain_grad, key_gain_grad)
    ]
    gains = jnp.stack(
        [
            input_gain_grad,
            laurel_gain_grad,
            attn_gain_grad,
            pre_gain_grad,
            post_gain_grad,
            side_gain_grad,
            *small_gains,
        ]
    )
    gate_blocks = side_gate_grad.astype(low).reshape(side, ctx_count, -1).transpose(1, 0, 2)
    gate_columns = width // ctx_count
    tall = jnp.concatenate(
        [
            left_weight_grad.astype(low),
            right_weight_grad.astype(low),
            jnp.pad(gains.astype(low).T, ((0, 0), (0, 128 - gains.shape[0]))),
        ],
        axis=1,
    )
    out_blocks = side_out_grad.astype(low).reshape(
        ctx_count, side // ctx_count, fsdp_count, width // fsdp_count
    )
    out_blocks = out_blocks.transpose(0, 2, 1, 3).reshape(-1, width // fsdp_count)
    out_weight_grad, qkv_weight_grad, tall, gate_blocks, side_out_grad = owner_sums(
        [
            out_weight_grad.astype(low),
            qkv_weight_grad.astype(low),
            tall,
            gate_blocks.reshape(-1, gate_columns),
            out_blocks,
        ],
        3,
    )
    gate_weight_grad, up_weight_grad = ffn_sums
    down_weight_grad = jnp.concatenate([down_sum.T, down_rest.T], axis=0)
    query_part = query_width // fsdp_count
    kv_part = kv_width // fsdp_count
    query_weight_grad = qkv_weight_grad[:, :query_part]
    key_weight_grad = qkv_weight_grad[:, query_part : query_part + kv_part]
    value_weight_grad = qkv_weight_grad[:, query_part + kv_part :]
    wide = jnp.float32
    tall = tall.astype(wide)
    left_weight_grad = tall[:, :rank]
    right_weight_grad = tall[:, rank : 2 * rank].T
    gains = tall[:, 2 * rank : 2 * rank + 8].T
    small_part = query_gain.shape[0] // count
    side_gate_grad = gate_blocks.astype(wide).T
    side_out_grad = side_out_grad.astype(wide)
    return (
        block_out,
        tokens_grad,
        per_layer_grad,
        query_weight_grad.astype(wide),
        key_weight_grad.astype(wide),
        value_weight_grad.astype(wide),
        out_weight_grad.astype(wide),
        left_weight_grad,
        right_weight_grad,
        gate_weight_grad.astype(wide),
        up_weight_grad.astype(wide),
        down_weight_grad.astype(wide),
        side_gate_grad,
        side_out_grad,
        *(gains[n] for n in range(6)),
        gains[6, :small_part],
        gains[7, :small_part],
    )


def solution(mesh):
    placed = (
        P("fsdp", "ctx", None),
        P("fsdp", "ctx", None),
        P("fsdp", "ctx", None),
        P("fsdp", None),
        P("fsdp", None),
        P("fsdp", None),
        P("fsdp", None),
        P("fsdp", None),
        P("fsdp", None),
        P(None, "fsdp"),
        P(None, "fsdp"),
        P(None, "fsdp"),
        P("fsdp", None),
        P("fsdp", None),
        P("fsdp", None),
        P(),
        P(),
        P(),
        P(),
        P(),
        P(),
        P(),
        P(),
    )
    return jax.shard_map(
        body,
        mesh=mesh,
        in_specs=placed,
        out_specs=(
            P("fsdp", "ctx", None),
            P("fsdp", "ctx", None),
            P("fsdp", "ctx", None),
            P("ctx", "fsdp"),
            P("ctx", "fsdp"),
            P("ctx", "fsdp"),
            P("ctx", "fsdp"),
            P(("ctx", "fsdp"), None),
            P(None, ("ctx", "fsdp")),
            P("ctx", "fsdp"),
            P("ctx", "fsdp"),
            P("fsdp", "ctx"),
            P("ctx", "fsdp"),
            P("ctx", "fsdp"),
            P(("ctx", "fsdp")),
            P(("ctx", "fsdp")),
            P(("ctx", "fsdp")),
            P(("ctx", "fsdp")),
            P(("ctx", "fsdp")),
            P(("ctx", "fsdp")),
            P(("ctx", "fsdp")),
            P(("ctx", "fsdp")),
        ),
        check_vma=False,
    )
```

```python
import functools
import math

import jax
import jax.numpy as jnp
from jax import lax
from jax.experimental import pallas as pl
from jax.experimental.pallas import tpu as pltpu
from jax.sharding import PartitionSpec as P

HEADS = 8
KV_HEADS = 2
HD = 256
MESH = pl.DeviceIdType.MESH
FF_TILE = 512
BACK_TILE = FF_TILE


epsilon = 1e-06
rope_theta = 1000000.0
masked_score = -1e30
inverse_root = 1.0 / math.sqrt(2.0)


def rms_norm(v, factor):
    return v * lax.rsqrt(jnp.mean(v * v, axis=-1, keepdims=True) + epsilon) * factor


def forward_product(a, b):
    return jnp.dot(a, b, preferred_element_type=jnp.float32)


def across(a, b):
    return lax.dot_general(a, b, (((1,), (1,)), ((), ())), preferred_element_type=jnp.float32)


def over_rows(a, b):
    return lax.dot_general(a, b, (((0,), (0,)), ((), ())), preferred_element_type=jnp.float32)


def hidden_piece(gate_in, up_in):
    return jax.nn.gelu(gate_in, approximate=True) * up_in


def middle_piece(mixed_in, ffn_in_rows, factor):
    return mixed_in + rms_norm(ffn_in_rows, factor)


def gather(x, axis):
    return lax.all_gather(x, axis, axis=0, tiled=True)


def scatter_sum(x, axis):
    return lax.psum_scatter(x, axis, scatter_dimension=0, tiled=True)


def partner_barrier(partners):
    barrier = pltpu.get_barrier_semaphore()
    for partner in partners:
        pl.semaphore_signal(barrier, inc=1, device_id=partner, device_id_type=MESH)
    pl.semaphore_wait(barrier, len(partners))


def add_rows(target, source, first, rows):
    tile = 16

    def one(step, carry):
        at = pl.ds(pl.multiple_of(first + step * tile, tile), tile)
        from_at = pl.ds(pl.multiple_of(step * tile, tile), tile)
        total = target[at].astype(jnp.float32) + source[from_at].astype(jnp.float32)
        target[at] = total.astype(target.dtype)
        return carry

    lax.fori_loop(0, rows // tile, one, 0)


def held_index(mine, done, bits):
    return tuple(slice(None) if t in done else mine[t] for t in reversed(range(bits)))


def ctx_position(ctx_count):
    bits = ctx_count.bit_length() - 1
    place = lax.axis_index("ctx")
    along = lax.axis_index("fsdp")
    mine = [lax.rem(place // (1 << t), 2) for t in range(bits)]
    partners = [(place + (1 - 2 * mine[t]) * (1 << t), along) for t in range(bits)]
    orders = [list(range(1, bits)), list(range(bits - 1, 0, -1))]
    return bits, place, along, mine, partners, orders


def spread_copy(out, lead, half, stage, position, send_sem, recv_sem):
    bits, _, _, mine, partners, orders = position
    order = orders[half]
    rows = out.shape[-2] // 2
    at = lead + held_index(mine, order[:stage], bits) + (pl.ds(half * rows, rows),)
    return pltpu.make_async_remote_copy(
        src_ref=out.at[at],
        dst_ref=out.at[at],
        send_sem=send_sem.at[half, stage],
        recv_sem=recv_sem.at[half, stage],
        device_id=partners[order[stage]],
        device_id_type=MESH,
    )


def sibling_copy(out, lead, position, send_sem, recv_sem):
    bits, _, _, mine, partners, orders = position
    at = lead + held_index(mine, orders[0], bits)
    return pltpu.make_async_remote_copy(
        src_ref=out.at[at],
        dst_ref=out.at[at],
        send_sem=send_sem,
        recv_sem=recv_sem,
        device_id=partners[0],
        device_id_type=MESH,
    )


def weight_gather_kernel(ctx_count, fsdp_count, members, spread, *refs):
    sets = len(members)
    own_count = sum(members)
    own, outs = refs[:own_count], refs[own_count : own_count + sets]
    rest = refs[own_count + sets :]
    passing, pieces = rest[:own_count], rest[own_count : own_count + sets]
    own_sem, line_send, line_recv, send_sem, recv_sem, core_send, core_recv = rest[
        own_count + sets :
    ]
    position = ctx_position(ctx_count)
    bits, place, along, mine, partners, _ = position
    steps = fsdp_count - 1
    here = held_index(mine, (), bits)
    columns = []
    for i in range(sets):
        start = 0
        for _ in range(members[i]):
            wide = own[len(columns)].shape[-1]
            columns.append((i, pl.ds(start, wide)))
            start += wide
    piece_loads = [
        pltpu.make_async_copy(own[n].at[here], pieces[i].at[:, at], own_sem.at[0, n])
        for n, (i, at) in enumerate(columns)
    ]
    for load in piece_loads:
        load.start()
    loads = [
        pltpu.make_async_copy(source, passing[n], own_sem.at[1, n])
        for n, source in enumerate(own)
    ]
    for load in loads:
        load.start()
    partner_barrier(
        partners
        + [(place, lax.rem(along + 1, fsdp_count)), (place, lax.rem(along + steps, fsdp_count))]
    )

    def line_copy(i, way, step, origin):
        toward = along + 1 if way == 0 else along - 1
        first, target = pieces[i], outs[i].at[(origin,) + here]
        return pltpu.make_async_remote_copy(
            src_ref=first if step == 1 else target,
            dst_ref=target,
            send_sem=line_send.at[i, way, step - 1],
            recv_sem=line_recv.at[i, way, step - 1],
            device_id=(place, toward),
            device_id_type=MESH,
        )

    def comes(way, step):
        return along >= step if way == 0 else along + step < fsdp_count

    def goes(way, step):
        if way == 0:
            return (along + 1 < fsdp_count) & (along >= step - 1)
        return (along >= 1) & (along + step - 1 < fsdp_count)

    def origin_of(way, step):
        return along - step if way == 0 else along + step

    def each(flag, action):
        pl.when(flag)(action)

    def forward(i, step):
        for way in range(2):
            each(goes(way, step), lambda: line_copy(i, way, step, origin_of(way, step - 1)).start())

    for load in piece_loads:
        load.wait()
    for i in range(sets):
        forward(i, 1)
    stores = []
    for n, load in enumerate(loads):
        load.wait()
        i, at = columns[n]
        target = outs[i].at[(along,) + (slice(None),) * (bits + 1) + (at,)]
        stores.append(pltpu.make_async_copy(passing[n], target, own_sem.at[2, n]))
        stores[-1].start()

    def stage_copies(i, way, step, stage):
        lead = (origin_of(way, step),)
        at = (i, way, step - 1)
        return [
            spread_copy(outs[i], lead, half, stage, position, send_sem.at[at], recv_sem.at[at])
            for half in range(2)
        ]

    def core_copy(i, way, step):
        at = (i, way, step - 1)
        return sibling_copy(
            outs[i], (origin_of(way, step),), position, core_send.at[at], core_recv.at[at]
        )

    def arrive(i, step):
        for way in range(2):

            def landed():
                line_copy(i, way, step, origin_of(way, step)).wait_recv()

            each(comes(way, step), landed)
        if step < steps:
            forward(i, step + 1)
        if i >= spread:
            return
        for way in range(2):

            def begin():
                for copy in stage_copies(i, way, step, 0):
                    copy.start()

            each(comes(way, step), begin)

    def advance(i, step, stage):
        if i >= spread:
            return
        for way in range(2):

            def proceed():
                for copy in stage_copies(i, way, step, stage):
                    copy.wait_recv()
                if stage < bits - 2:
                    for copy in stage_copies(i, way, step, stage + 1):
                        copy.start()
                else:
                    core_copy(i, way, step).start()

            each(comes(way, step), proceed)

    order = [(i, step) for i in range(sets) for step in range(1, steps + 1)]
    for tick in range(len(order) + bits - 1):
        if 1 <= tick <= len(order):
            advance(*order[tick - 1], 0)
        if tick < len(order):
            arrive(*order[tick])
        for stage in range(1, bits - 1):
            at = tick - 1 - stage
            if 0 <= at < len(order):
                advance(*order[at], stage)
    for copy in stores:
        copy.wait()
    for i, step in order:
        for way in range(2):

            def leave():
                line_copy(i, way, step, origin_of(way, step - 1)).wait_send()

            def finish():
                for stage in range(bits - 1):
                    for copy in stage_copies(i, way, step, stage):
                        copy.wait_send()
                core_copy(i, way, step).wait()

            each(goes(way, step), leave)
            if i < spread:
                each(comes(way, step), finish)


def weight_gather(own, spread):
    ctx_count = lax.axis_size("ctx")
    fsdp_count = lax.axis_size("fsdp")
    bits = ctx_count.bit_length() - 1
    steps = fsdp_count - 1
    sets = len(own)
    cut = (2,) * bits
    low = jnp.bfloat16
    flat = [w.reshape(cut + (w.shape[0] // ctx_count, w.shape[1])) for group in own for w in group]
    pieces = [(g[0].shape[0] // ctx_count, sum(w.shape[1] for w in g)) for g in own]
    out_shapes = [(fsdp_count,) + cut + p for p in pieces]
    total = sum(rows * columns for rows, columns in pieces) * ctx_count * fsdp_count
    outs = pl.pallas_call(
        functools.partial(
            weight_gather_kernel, ctx_count, fsdp_count, [len(g) for g in own], spread
        ),
        out_shape=[jax.ShapeDtypeStruct(s, low) for s in out_shapes],
        in_specs=[pl.BlockSpec(memory_space=pltpu.HBM)] * len(flat),
        out_specs=[pl.BlockSpec(memory_space=pltpu.HBM)] * len(out_shapes),
        scratch_shapes=[pltpu.VMEM(w.shape, low) for w in flat]
        + [pltpu.VMEM(p, low) for p in pieces]
        + [
            pltpu.SemaphoreType.DMA((3, len(flat))),
            pltpu.SemaphoreType.DMA((sets, 2, steps)),
            pltpu.SemaphoreType.DMA((sets, 2, steps)),
            pltpu.SemaphoreType.DMA((spread, 2, steps, 2, bits - 1)),
            pltpu.SemaphoreType.DMA((spread, 2, steps, 2, bits - 1)),
            pltpu.SemaphoreType.DMA((spread, 2, steps)),
            pltpu.SemaphoreType.DMA((spread, 2, steps)),
        ],
        compiler_params=pltpu.CompilerParams(
            collective_id=1, has_side_effects=True, vmem_limit_bytes=60 << 20
        ),
        cost_estimate=pl.CostEstimate(flops=0, bytes_accessed=4 * total, transcendentals=0),
        name="weight_gather",
    )(*flat)
    return [o.reshape(-1, o.shape[-1]) for o in outs[:spread]] + list(outs[spread:])


def line_comes(along, count, way, step):
    return along >= step if way == 0 else along + step < count


def line_goes(along, count, way, step):
    if way == 0:
        return (along + 1 < count) & (along >= step - 1)
    return (along >= 1) & (along + step - 1 < count)


def line_origin(along, way, step):
    return along - step if way == 0 else along + step


class LineGather:
    def __init__(self, count, owns, outs, passing, own_sems, send_sems, recv_sems):
        self.count, self.steps = count, count - 1
        self.owns, self.outs, self.passing = owns, outs, passing
        self.own_sems, self.send_sems, self.recv_sems = own_sems, send_sems, recv_sems
        self.place = lax.axis_index("ctx")
        self.along = lax.axis_index("fsdp")
        self.done = 0

    def partners(self):
        return [(self.place, lax.rem(self.along + d, self.count)) for d in sorted({1, self.steps})]

    def own_copies(self, n):
        return (
            pltpu.make_async_copy(self.owns[n], self.passing[n], self.own_sems.at[0, n]),
            pltpu.make_async_copy(self.passing[n], self.outs[n].at[self.along], self.own_sems.at[1, n]),
        )

    def copies(self, way, step, origin):
        toward = self.along + 1 if way == 0 else self.along - 1
        return [
            pltpu.make_async_remote_copy(
                src_ref=self.owns[n] if step == 1 else self.outs[n].at[origin],
                dst_ref=self.outs[n].at[origin],
                send_sem=self.send_sems.at[n, way, step - 1],
                recv_sem=self.recv_sems.at[n, way, step - 1],
                device_id=(self.place, toward),
                device_id_type=MESH,
            )
            for n in range(len(self.owns))
        ]

    def forward(self, step):
        for way in range(2):

            def go(way=way):
                for copy in self.copies(way, step, line_origin(self.along, way, step - 1)):
                    copy.start()

            pl.when(line_goes(self.along, self.count, way, step))(go)

    def load(self):
        for n in range(len(self.owns)):
            self.own_copies(n)[0].start()

    def store(self):
        for n in range(len(self.owns)):
            self.own_copies(n)[0].wait()
            self.own_copies(n)[1].start()

    def arrive(self):
        if self.done == self.steps:
            return
        self.done += 1
        step = self.done
        for way in range(2):

            def land(way=way):
                for copy in self.copies(way, step, line_origin(self.along, way, step)):
                    copy.wait_recv()

            pl.when(line_comes(self.along, self.count, way, step))(land)
        if step < self.steps:
            self.forward(step + 1)

    def finish(self):
        while self.done < self.steps:
            self.arrive()
        for n in range(len(self.owns)):
            self.own_copies(n)[1].wait()
        for step in range(1, self.steps + 1):
            for way in range(2):

                def leave(way=way, step=step):
                    for copy in self.copies(way, step, line_origin(self.along, way, step - 1)):
                        copy.wait_send()

                pl.when(line_goes(self.along, self.count, way, step))(leave)


class Halving:
    def __init__(self, position, rows, give, held, first_in, later_in, sems):
        self.bits, self.place, self.along, self.mine, self.partners, self.orders = position
        self.rows, self.give, self.held = rows, give, held
        self.first_in, self.later_in = first_in, later_in
        self.send_zero, self.recv_zero, self.send_sem, self.recv_sem = sems
        self.pairs = 1 << (self.bits - 1)

    def first_copy(self, b):
        return pltpu.make_async_remote_copy(
            src_ref=self.give(b),
            dst_ref=self.first_in.at[b],
            send_sem=self.send_zero.at[b],
            recv_sem=self.recv_zero.at[b],
            device_id=self.partners[0],
            device_id_type=MESH,
        )

    def start_first(self):
        for b in range(self.pairs):
            self.first_copy(b).start()

    def end_first(self, b):
        self.first_copy(b).wait()
        add_rows(self.held(b), self.first_in.at[b], 0, self.rows)

    def slot_of(self, stage):
        return sum(1 << (self.bits - 2 - s) for s in range(stage))

    def block_sets(self, half, stage):
        order = self.orders[half]
        bit = order[stage]
        free = order[stage + 1 :]
        fixed = sum(self.mine[t] * (1 << (t - 1)) for t in order[:stage])
        sent, kept = [], []
        for combo in range(1 << len(free)):
            value = sum(((combo >> n) & 1) << (t - 1) for n, t in enumerate(free))
            sent.append(fixed + (1 - self.mine[bit]) * (1 << (bit - 1)) + value)
            kept.append(fixed + self.mine[bit] * (1 << (bit - 1)) + value)
        return bit, sent, kept

    def stage_copies(self, stage):
        rows = self.rows // 2
        copies = []
        for half in range(2):
            bit, sent, _ = self.block_sets(half, stage)
            for n, block in enumerate(sent):
                at = (half, self.slot_of(stage) + n)
                copies.append(
                    pltpu.make_async_remote_copy(
                        src_ref=self.held(block).at[pl.ds(half * rows, rows)],
                        dst_ref=self.later_in.at[at],
                        send_sem=self.send_sem.at[at],
                        recv_sem=self.recv_sem.at[at],
                        device_id=self.partners[bit],
                        device_id_type=MESH,
                    )
                )
        return copies

    def start(self, stage):
        for copy in self.stage_copies(stage):
            copy.start()

    def end(self, stage):
        for copy in self.stage_copies(stage):
            copy.wait()
        rows = self.rows // 2
        for half in range(2):
            _, _, kept = self.block_sets(half, stage)
            for n, block in enumerate(kept):
                at = (half, self.slot_of(stage) + n)
                add_rows(self.held(block), self.later_in.at[at], half * rows, rows)

    def mine_now(self):
        return self.held(self.place // 2)


def halving_scratch(ctx_count, rows, columns):
    pairs = ctx_count // 2
    return [
        pltpu.VMEM((pairs, rows, columns), jnp.bfloat16),
        pltpu.VMEM((2, pairs - 1, rows // 2, columns), jnp.bfloat16),
        pltpu.SemaphoreType.DMA((pairs,)),
        pltpu.SemaphoreType.DMA((pairs,)),
        pltpu.SemaphoreType.DMA((2, pairs - 1)),
        pltpu.SemaphoreType.DMA((2, pairs - 1)),
    ]


def unit_rows(v):
    scale = lax.rsqrt(jnp.mean(v * v, axis=-1, keepdims=True) + epsilon)
    return v * scale, scale


def turned(v, cosine, sine_part):
    halfway = v.shape[-1] // 2
    leading, trailing = v[:, :halfway], v[:, halfway:]
    return jnp.concatenate(
        [leading * cosine - trailing * sine_part, trailing * cosine + leading * sine_part], axis=-1
    )


def unit_rows_pull(v, grad, gain):
    unit, scale = unit_rows(v)
    gain_grad = jnp.sum(grad * unit, axis=0, keepdims=True)
    scaled = grad * gain
    return scale * (scaled - unit * jnp.mean(unit * scaled, axis=-1, keepdims=True)), gain_grad


def head_at(h):
    return pl.ds(pl.multiple_of(h * HD, HD), HD)


def attention_forward_kernel(
    ctx_count,
    lines,
    raw,
    cosine_ref,
    sine_ref,
    query_gain,
    key_gain,
    row_ids,
    key_ids,
    _,
    *refs,
):
    line_owns, refs = refs[:lines], refs[lines:]
    kv, query_low, attended_low, log_totals, weights_out = refs[:5]
    line_outs, refs = refs[5 : 5 + lines], refs[5 + lines :]
    bias, send_sem, recv_sem, core_send, core_recv, weight_sems, weight_core_sems = refs[:7]
    line = LineGather(
        weights_out.shape[0], line_owns, line_outs, refs[7 : 7 + lines], *refs[7 + lines :]
    )
    line.load()
    position = ctx_position(ctx_count)
    bits, place, along, mine, partners, _ = position
    count = weights_out.shape[0]
    units = [(way, step) for step in range(1, count) for way in range(2)]

    def weight_copies(way, step, stage):
        lead = (line_origin(along, way, step),)
        at = (way, step - 1)
        return [
            spread_copy(
                weights_out,
                lead,
                half,
                stage,
                position,
                weight_sems.at[(0,) + at],
                weight_sems.at[(1,) + at],
            )
            for half in range(2)
        ]

    def weight_core_copy(way, step):
        at = (way, step - 1)
        return sibling_copy(
            weights_out,
            (line_origin(along, way, step),),
            position,
            weight_core_sems.at[(0,) + at],
            weight_core_sems.at[(1,) + at],
        )

    def each_unit(action):
        for way, step in units:
            pl.when(line_comes(along, count, way, step))(functools.partial(action, way, step))

    def start_weights(stage):
        def action(way, step):
            for copy in weight_copies(way, step, stage):
                copy.start()

        each_unit(action)

    def land_weights(stage):
        def action(way, step):
            for copy in weight_copies(way, step, stage):
                copy.wait_recv()

        each_unit(action)

    rows = raw.shape[0]
    groups = HEADS // KV_HEADS
    length = ctx_count * rows
    here = held_index(mine, (), bits)
    cosine, sine_part = cosine_ref[...], sine_ref[...]
    partner_barrier(partners + line.partners())
    start_weights(0)
    line.forward(1)
    for k in range(KV_HEADS):
        unit, _ = unit_rows(raw[:, pl.ds((HEADS + k) * HD, HD)])
        key = turned(unit * key_gain[...], cosine, sine_part)
        kv[here + (slice(None), pl.ds(k * HD, HD))] = key.astype(kv.dtype)
        value, _ = unit_rows(raw[:, pl.ds((HEADS + KV_HEADS + k) * HD, HD)])
        kv[here + (slice(None), pl.ds((KV_HEADS + k) * HD, HD))] = value.astype(kv.dtype)

    def copies_of(stage):
        return [spread_copy(kv, (), h, stage, position, send_sem, recv_sem) for h in range(2)]

    for copy in copies_of(0):
        copy.start()
    line.store()
    allowed = (row_ids[...] == key_ids[...]) & (
        lax.broadcasted_iota(jnp.int32, (rows, length), 1)
        <= lax.broadcasted_iota(jnp.int32, (rows, length), 0) + place * rows
    )
    bias[...] = jnp.where(allowed, 0.0, masked_score)

    def one_query(h, carry):
        unit, _ = unit_rows(raw[:, head_at(h)])
        query = turned(unit * query_gain[...], cosine, sine_part)
        query_low[:, head_at(h)] = query.astype(query_low.dtype)
        return carry

    lax.fori_loop(0, HEADS, one_query, 0)
    for stage in range(1, bits - 1):
        for copy in copies_of(stage - 1):
            copy.wait()
        for copy in copies_of(stage):
            copy.start()
        land_weights(stage - 1)
        start_weights(stage)
        line.arrive()
    for copy in copies_of(bits - 2):
        copy.wait()
    last = sibling_copy(kv, (), position, core_send, core_recv)
    last.start()
    last.wait()
    everywhere = (slice(None),) * (bits + 1)
    for k in range(KV_HEADS):
        key = kv[everywhere + (pl.ds(k * HD, HD),)].reshape(length, HD)
        value = kv[everywhere + (pl.ds((KV_HEADS + k) * HD, HD),)].reshape(length, HD)

        def one_head(g, carry, k=k, key=key, value=value):
            h = k * groups + g
            scores = across(query_low[:, head_at(h)], key) + bias[...]
            row_max = jnp.max(scores, axis=-1, keepdims=True)
            weights = jnp.exp(scores - row_max)
            row_total = jnp.sum(weights, axis=-1, keepdims=True)
            weights = (weights * (1.0 / row_total)).astype(value.dtype)
            attended_low[:, head_at(h)] = forward_product(weights, value).astype(attended_low.dtype)
            log_total = jnp.broadcast_to(row_max + jnp.log(row_total), (rows, rows))
            log_totals[h] = log_total.T[:8]
            return carry

        lax.fori_loop(0, groups, one_head, 0)
        line.arrive()
        if k == KV_HEADS - 2:
            land_weights(bits - 2)
            each_unit(lambda way, step: weight_core_copy(way, step).start())

    def finish(way, step):
        for stage in range(bits - 1):
            for copy in weight_copies(way, step, stage):
                copy.wait_send()
        weight_core_copy(way, step).wait()

    each_unit(finish)
    line.finish()


def attention_forward(raw, cosine, sine_part, query_gain, key_gain, row_ids, key_ids, weights, lines):
    ctx_count = lax.axis_size("ctx")
    steps = lax.axis_size("fsdp") - 1
    hbm = pl.BlockSpec(memory_space=pltpu.HBM)
    bits = ctx_count.bit_length() - 1
    rows = raw.shape[0]
    length = ctx_count * rows
    low = jnp.bfloat16
    vmem = pl.BlockSpec(memory_space=pltpu.VMEM)
    return pl.pallas_call(
        functools.partial(attention_forward_kernel, ctx_count, len(lines)),
        out_shape=[
            jax.ShapeDtypeStruct((2,) * bits + (rows, 2 * KV_HEADS * HD), low),
            jax.ShapeDtypeStruct((rows, HEADS * HD), low),
            jax.ShapeDtypeStruct((rows, HEADS * HD), low),
            jax.ShapeDtypeStruct((HEADS, 8, rows), jnp.float32),
            jax.ShapeDtypeStruct(weights.shape, low),
        ]
        + [jax.ShapeDtypeStruct((steps + 1,) + w.shape, low) for w in lines],
        in_specs=[vmem] * 7 + [hbm] * (1 + len(lines)),
        out_specs=[vmem] * 4 + [hbm] * (1 + len(lines)),
        input_output_aliases={7: 4},
        scratch_shapes=[
            pltpu.VMEM((rows, length), jnp.float32),
            pltpu.SemaphoreType.DMA((2, bits - 1)),
            pltpu.SemaphoreType.DMA((2, bits - 1)),
            pltpu.SemaphoreType.DMA,
            pltpu.SemaphoreType.DMA,
            pltpu.SemaphoreType.DMA((2, 2, steps, 2, bits - 1)),
            pltpu.SemaphoreType.DMA((2, 2, steps)),
        ]
        + [pltpu.VMEM(w.shape, low) for w in lines]
        + [
            pltpu.SemaphoreType.DMA((2, len(lines))),
            pltpu.SemaphoreType.DMA((len(lines), 2, steps)),
            pltpu.SemaphoreType.DMA((len(lines), 2, steps)),
        ],
        compiler_params=pltpu.CompilerParams(
            collective_id=2, has_side_effects=True, vmem_limit_bytes=56 << 20
        ),
        cost_estimate=pl.CostEstimate(
            flops=4 * HEADS * HD * rows * length,
            bytes_accessed=8 << 20,
            transcendentals=HEADS * rows * length,
        ),
        name="attention_forward",
    )(
        raw,
        cosine,
        sine_part,
        query_gain[None],
        key_gain[None],
        row_ids[:, None],
        key_ids[None],
        weights,
        *lines,
    )


def attention_backward_kernel(ctx_count, fsdp_count, extra, exchange, *refs):
    (
        query_low,
        kv,
        log_totals,
        raw,
        cosine_ref,
        sine_ref,
        query_gain,
        key_gain,
        row_ids,
        key_ids,
        row_grads,
        out_weight,
        qkv_weight,
    ) = refs[:13]
    many = len(extra)
    extra_in = refs[13 : 13 + many]
    back, gain_grads, column_grads, normed_grads = refs[13 + many : 17 + many]
    extra_out = refs[17 + many : 17 + 2 * many]
    rest = refs[17 + 2 * many :]
    if exchange:
        back_columns, rest = rest[0], rest[1:]
        *rest, back_send, back_recv = rest
    bias, score_grads, weights_low, query_grads, kv_grads = rest[:5]
    kv_parts = rest[5:11]
    extra_parts = [rest[11 + 8 * i : 19 + 8 * i] for i in range(many)]
    position = ctx_position(ctx_count)
    bits, place, along, mine, partners, _ = position
    pairs = ctx_count // 2
    rows = raw.shape[0]
    column_send, column_recv, grads, streamed, stream_sem = rest[11 + 8 * many :]
    tile = streamed.shape[1]

    head_parts = [(0, HEADS), (HEADS, KV_HEADS), (HEADS + KV_HEADS, KV_HEADS)]

    def back_span(part, owner):
        first, heads = head_parts[part]
        size = heads * HD // fsdp_count
        start = pl.multiple_of(first * HD + owner * size, size)
        return pl.ds(start, size), pl.ds(first * HD // fsdp_count, size)

    def back_copies(part):
        copies = []
        for d, peer in enumerate(peers):
            source, target = back_span(part, peer)
            copies.append(
                pltpu.make_async_remote_copy(
                    src_ref=back.at[:, source],
                    dst_ref=back_columns.at[along, :, target],
                    send_sem=back_send.at[part, d],
                    recv_sem=back_recv.at[part, d],
                    device_id=(place, peer),
                    device_id_type=MESH,
                )
            )
        return copies

    def start_back(part):
        if exchange:
            for copy in back_copies(part):
                copy.start()
            source, target = back_span(part, along)
            back_columns[along, :, target] = back[:, source]

    def stream(weight, columns, use):
        tiles = weight.shape[0] // tile

        def copy(t):
            return pltpu.make_async_copy(
                weight.at[pl.ds(t * tile, tile), pl.ds(0, columns)],
                streamed.at[t % 2, :, pl.ds(0, columns)],
                stream_sem.at[t % 2],
            )

        copy(0).start()
        for t in range(tiles):
            if t + 1 < tiles:
                copy(t + 1).start()
            copy(t).wait()
            use(pl.ds(t * tile, tile), streamed[t % 2, :, :columns])

    peers = [lax.rem(along + d, fsdp_count) for d in range(1, fsdp_count)]
    wide = column_grads.shape[-1]
    column_copies = [
        pltpu.make_async_remote_copy(
            src_ref=row_grads.at[:, pl.ds(pl.multiple_of(peer * wide, wide), wide)],
            dst_ref=column_grads.at[along],
            send_sem=column_send.at[d],
            recv_sem=column_recv.at[d],
            device_id=(place, peer),
            device_id_type=MESH,
        )
        for d, peer in enumerate(peers)
    ]
    groups = HEADS // KV_HEADS
    length = ctx_count * rows
    low = jnp.bfloat16

    kv_sum = Halving(
        position,
        rows,
        lambda b: kv_grads.at[2 * b + 1 - mine[0]],
        lambda b: kv_grads.at[2 * b + mine[0]],
        kv_parts[0],
        kv_parts[1],
        kv_parts[2:6],
    )
    sums, own_copies = [], []
    for i, (block, _) in enumerate(extra):
        held, first_in, later_in, own_sem = extra_parts[i][:4]

        def give(b, i=i, block=block):
            at = pl.multiple_of((2 * b + 1 - mine[0]) * block, 16)
            return extra_in[i].at[pl.ds(at, block)]

        sums.append(
            Halving(
                position,
                block,
                give,
                lambda b, held=held: held.at[b],
                first_in,
                later_in,
                extra_parts[i][4:8],
            )
        )
        copies = []
        for b in range(pairs):
            at = pl.multiple_of((2 * b + mine[0]) * block, 16)
            copies.append(
                pltpu.make_async_copy(
                    extra_in[i].at[pl.ds(at, block)], held.at[b], own_sem.at[b]
                )
            )
            copies[-1].start()
        own_copies.append(copies)

    partner_barrier(partners + [(place, peer) for peer in peers])
    for one in sums:
        one.start_first()
    for copy in column_copies:
        copy.start()
    column_grads[along] = row_grads[:, pl.ds(pl.multiple_of(along * wide, wide), wide)]

    def attended_tile(columns, weight):
        grads[:, columns] = across(row_grads[...], weight).astype(low)

    stream(out_weight, row_grads.shape[1], attended_tile)

    def open_extra(i):
        for b in range(pairs):
            own_copies[i][b].wait()
            sums[i].end_first(b)
        sums[i].start(0)

    allowed = (key_ids[...] == row_ids[...]) & (
        lax.broadcasted_iota(jnp.int32, (length, rows), 0)
        <= lax.broadcasted_iota(jnp.int32, (length, rows), 1) + place * rows
    )
    bias[...] = jnp.where(allowed, 0.0, masked_score)
    everywhere = (slice(None),) * (bits + 1)
    for k in range(KV_HEADS):
        if k < many:
            open_extra(k)
        key = kv[everywhere + (pl.ds(k * HD, HD),)].reshape(length, HD)
        value = kv[everywhere + (pl.ds((KV_HEADS + k) * HD, HD),)].reshape(length, HD)

        def one_head(g, carry, k=k, key=key, value=value):
            h = k * groups + g
            columns = pl.ds(pl.multiple_of(g * rows, rows), rows)
            scores = across(key, query_low[:, head_at(h)]) + bias[...]
            weights = jnp.exp(scores - log_totals[h][:1])
            weight_grad = across(value, grads[:, head_at(h)])
            delta = jnp.sum(weights * weight_grad, axis=0, keepdims=True)
            score_grads[:, columns] = (weights * (weight_grad - delta)).astype(low)
            weights_low[:, columns] = weights.astype(low)
            return carry

        lax.fori_loop(0, groups, one_head, 0)
        heads = [pl.ds((k * groups + g) * HD, HD) for g in range(groups)]
        query_stack = jnp.concatenate([query_low[:, at] for at in heads], axis=0)
        grad_stack = jnp.concatenate([grads[:, at] for at in heads], axis=0)
        key_grad = forward_product(score_grads[...], query_stack).astype(low)
        value_grad = forward_product(weights_low[...], grad_stack).astype(low)
        kv_grads[:, :, pl.ds(k * HD, HD)] = key_grad.reshape(ctx_count, rows, HD)
        kv_grads[:, :, pl.ds((KV_HEADS + k) * HD, HD)] = value_grad.reshape(ctx_count, rows, HD)
        query_grad = over_rows(key, score_grads[...])
        for g, at in enumerate(heads):
            query_grads[:, at] = query_grad[:, g * rows : (g + 1) * rows].T

    kv_sum.start_first()
    for b in range(pairs):
        kv_sum.end_first(b)
    kv_sum.start(0)
    for i in range(KV_HEADS, many):
        open_extra(i)

    def step_extra(i, stage):
        sums[i].end(stage - 1)
        sums[i].start(stage)

    cosine, sine_part = cosine_ref[...], sine_ref[...]

    def one_query(h, gain_grad):
        grad = turned(query_grads[:, head_at(h)], cosine, -sine_part)
        pulled, more = unit_rows_pull(raw[:, head_at(h)], grad, query_gain[...])
        back[:, head_at(h)] = pulled.astype(low)
        return gain_grad + more

    gain_grads[0:1] = lax.fori_loop(0, HEADS, one_query, jnp.zeros((1, HD), jnp.float32))
    start_back(0)
    for stage in range(1, bits - 1):
        kv_sum.end(stage - 1)
        kv_sum.start(stage)
    kv_sum.end(bits - 2)
    for i in range(many):
        step_extra(i, 1)
    summed = kv_sum.mine_now()
    key_gain_grad = jnp.zeros((1, HD), jnp.float32)
    for k in range(KV_HEADS):
        grad = summed[:, pl.ds(k * HD, HD)].astype(jnp.float32)
        grad = turned(grad, cosine, -sine_part)
        at = pl.ds((HEADS + k) * HD, HD)
        pulled, more = unit_rows_pull(raw[:, at], grad, key_gain[...])
        back[:, at] = pulled.astype(low)
        key_gain_grad = key_gain_grad + more
        grad = summed[:, pl.ds((KV_HEADS + k) * HD, HD)].astype(jnp.float32)
        at = pl.ds((HEADS + KV_HEADS + k) * HD, HD)
        pulled, _ = unit_rows_pull(raw[:, at], grad, 1.0)
        back[:, at] = pulled.astype(low)
    gain_grads[1:2] = key_gain_grad
    start_back(1)
    start_back(2)

    def normed_tile(columns, weight):
        normed_grads[:, columns] = across(back[...], weight)

    stream(qkv_weight, back.shape[1], normed_tile)
    for stage in range(2, bits - 1):
        for i in range(many):
            step_extra(i, stage)
    for copy in column_copies:
        copy.wait()
    if exchange:
        for part in range(3):
            for copy in back_copies(part):
                copy.wait()
    for i in range(many):
        sums[i].end(bits - 2)
        extra_out[i][...] = sums[i].mine_now()[...]


def attention_backward(
    query_low,
    kv,
    log_totals,
    raw,
    cosine,
    sine_part,
    query_gain,
    key_gain,
    row_ids,
    key_ids,
    row_grads,
    out_weight,
    qkv_weight,
    extra,
):
    fsdp_count = lax.axis_size("fsdp")
    hbm = pl.BlockSpec(memory_space=pltpu.HBM)
    ctx_count = lax.axis_size("ctx")
    rows = raw.shape[0]
    length = ctx_count * rows
    pairs = ctx_count // 2
    groups = HEADS // KV_HEADS
    low = jnp.bfloat16
    vmem = pl.BlockSpec(memory_space=pltpu.VMEM)
    shapes = [(a.shape[0] // ctx_count, a.shape[1]) for a in extra]
    scratch = [
        pltpu.VMEM((length, rows), jnp.float32),
        pltpu.VMEM((length, groups * rows), low),
        pltpu.VMEM((length, groups * rows), low),
        pltpu.VMEM((rows, HEADS * HD), jnp.float32),
        pltpu.VMEM((ctx_count, rows, 2 * KV_HEADS * HD), low),
    ]
    scratch += halving_scratch(ctx_count, rows, 2 * KV_HEADS * HD)
    for shape in shapes:
        parts = halving_scratch(ctx_count, *shape)
        scratch += [pltpu.VMEM((pairs,) + shape, low)] + parts[:2]
        scratch += [pltpu.SemaphoreType.DMA((pairs,))] + parts[2:]
    scratch += [pltpu.SemaphoreType.DMA((fsdp_count - 1,))] * 2
    scratch += [
        pltpu.VMEM((rows, HEADS * HD), low),
        pltpu.VMEM((2, FF_TILE, qkv_weight.shape[1]), low),
        pltpu.SemaphoreType.DMA((2,)),
    ]
    exchange = KV_HEADS * HD // fsdp_count % 128 == 0
    back_out = []
    if exchange:
        scratch += [pltpu.SemaphoreType.DMA((3, fsdp_count - 1))] * 2
        back_out = [jax.ShapeDtypeStruct((fsdp_count, rows, raw.shape[1] // fsdp_count), low)]
    columns_shape = (fsdp_count, rows, row_grads.shape[1] // fsdp_count)
    outs = pl.pallas_call(
        functools.partial(attention_backward_kernel, ctx_count, fsdp_count, shapes, exchange),
        out_shape=[
            jax.ShapeDtypeStruct(raw.shape, low),
            jax.ShapeDtypeStruct((8, HD), jnp.float32),
            jax.ShapeDtypeStruct(columns_shape, low),
            jax.ShapeDtypeStruct((rows, qkv_weight.shape[0]), jnp.float32),
        ]
        + [jax.ShapeDtypeStruct(s, low) for s in shapes]
        + back_out,
        in_specs=[vmem] * 11 + [hbm] * (2 + len(extra)),
        out_specs=[vmem] * (4 + len(extra) + len(back_out)),
        scratch_shapes=scratch,
        compiler_params=pltpu.CompilerParams(
            collective_id=3, has_side_effects=True, vmem_limit_bytes=60 << 20
        ),
        cost_estimate=pl.CostEstimate(
            flops=10 * HEADS * HD * rows * length,
            bytes_accessed=64 << 20,
            transcendentals=HEADS * rows * length,
        ),
        name="attention_backward",
    )(
        query_low,
        kv,
        log_totals,
        raw,
        cosine,
        sine_part,
        query_gain[None],
        key_gain[None],
        row_ids[None],
        key_ids[:, None],
        row_grads,
        out_weight,
        qkv_weight,
        *extra,
    )
    columns = outs[2].reshape(-1, outs[2].shape[-1])
    back_columns = None
    if exchange:
        back_columns = outs[-1].reshape(-1, outs[-1].shape[-1])
    sums = outs[4 : 4 + len(extra)]
    return outs[0], outs[1][0], outs[1][1], columns, outs[3], sums, back_columns


def owner_sum_kernel(ctx_count, fsdp_count, shapes, shared, *refs):
    many = len(shapes)
    whole = many - shared
    ins, outs = refs[:many], refs[many : 2 * many]
    rest = refs[2 * many :]
    parts = [rest[8 * i : 8 * i + 8] for i in range(many)]
    shares = rest[8 * many : 8 * many + shared]
    send_z, recv_z = rest[8 * many + shared :]
    position = ctx_position(ctx_count)
    bits, place, along, mine, partners, _ = position
    pairs = ctx_count // 2
    across_line = [(place, lax.rem(along + d, fsdp_count)) for d in range(1, fsdp_count)]
    partner_barrier(partners + across_line)
    sums, own_copies = [], []
    for i, (block, _) in enumerate(shapes):
        held, first_in, later_in, own_sem = parts[i][:4]

        def give(b, i=i, block=block):
            at = pl.multiple_of((2 * b + 1 - mine[0]) * block, 16)
            return ins[i].at[pl.ds(at, block)]

        sums.append(
            Halving(
                position,
                block,
                give,
                lambda b, held=held: held.at[b],
                first_in,
                later_in,
                parts[i][4:8],
            )
        )
        sums[i].start_first()
        copies = []
        for b in range(pairs):
            at = pl.multiple_of((2 * b + mine[0]) * block, 16)
            copies.append(
                pltpu.make_async_copy(ins[i].at[pl.ds(at, block)], held.at[b], own_sem.at[b])
            )
            copies[-1].start()
        own_copies.append(copies)
    order = list(range(whole, many)) + list(range(whole))
    for i in order:
        for b in range(pairs):
            own_copies[i][b].wait()
            sums[i].end_first(b)
        sums[i].start(0)
    for stage in range(1, bits - 1):
        for i in order:
            sums[i].end(stage - 1)
            sums[i].start(stage)

    def share_copies(i):
        size = shapes[i][0] // fsdp_count
        return [
            pltpu.make_async_remote_copy(
                src_ref=sums[i].mine_now().at[pl.ds(pl.multiple_of(peer[1] * size, 16), size)],
                dst_ref=shares[i - whole].at[d],
                send_sem=send_z.at[i - whole, d],
                recv_sem=recv_z.at[i - whole, d],
                device_id=peer,
                device_id_type=MESH,
            )
            for d, peer in enumerate(across_line)
        ]

    for i in range(whole, many):
        sums[i].end(bits - 2)
        for copy in share_copies(i):
            copy.start()
    for i in range(whole):
        sums[i].end(bits - 2)
        outs[i][...] = sums[i].mine_now()[...]
    for i in range(whole, many):
        for copy in share_copies(i):
            copy.wait()
        size = shapes[i][0] // fsdp_count
        own = sums[i].mine_now()[pl.ds(pl.multiple_of(along * size, 16), size)]
        total = own.astype(jnp.float32)
        for d in range(fsdp_count - 1):
            total = total + shares[i - whole][d].astype(jnp.float32)
        outs[i][...] = total.astype(outs[i].dtype)


def owner_sums(arrays, shared):
    ctx_count = lax.axis_size("ctx")
    fsdp_count = lax.axis_size("fsdp")
    pairs = ctx_count // 2
    many = len(arrays)
    whole = many - shared
    low = jnp.bfloat16
    shapes = [(a.shape[0] // ctx_count, a.shape[1]) for a in arrays]
    share_shapes = [(s[0] // fsdp_count, s[1]) for s in shapes[whole:]]
    scratch = []
    for shape in shapes:
        parts = halving_scratch(ctx_count, *shape)
        scratch += [pltpu.VMEM((pairs,) + shape, low)] + parts[:2]
        scratch += [pltpu.SemaphoreType.DMA((pairs,))] + parts[2:]
    scratch += [pltpu.VMEM((fsdp_count - 1,) + s, low) for s in share_shapes]
    scratch += [pltpu.SemaphoreType.DMA((shared, fsdp_count - 1))] * 2
    total = sum(a.size for a in arrays)
    return pl.pallas_call(
        functools.partial(owner_sum_kernel, ctx_count, fsdp_count, shapes, shared),
        out_shape=[jax.ShapeDtypeStruct(s, low) for s in shapes[:whole] + share_shapes],
        in_specs=[pl.BlockSpec(memory_space=pl.ANY)] * many,
        out_specs=[pl.BlockSpec(memory_space=pltpu.VMEM)] * many,
        scratch_shapes=scratch,
        compiler_params=pltpu.CompilerParams(
            collective_id=0, has_side_effects=True, vmem_limit_bytes=48 << 20
        ),
        cost_estimate=pl.CostEstimate(flops=total, bytes_accessed=4 * total, transcendentals=0),
        name="owner_sums",
    )(*arrays)


class LineExchange:
    def __init__(self, count, own, gathered, outgoing, incoming, sems):
        self.count, self.steps = count, count - 1
        self.own, self.gathered = own, gathered
        self.outgoing, self.incoming = outgoing, incoming
        self.line_send, self.line_recv, self.back_send, self.back_recv = sems
        self.place = lax.axis_index("ctx")
        self.along = lax.axis_index("fsdp")
        self.width = outgoing.shape[-1]
        self.chunks = self.width // BACK_TILE

    def partners(self):
        return [
            (self.place, lax.rem(self.along + d, self.count)) for d in sorted({1, self.count - 1})
        ]

    def line_copy(self, way, step, origin):
        toward = self.along + 1 if way == 0 else self.along - 1
        return pltpu.make_async_remote_copy(
            src_ref=self.own if step == 1 else self.gathered.at[origin],
            dst_ref=self.gathered.at[origin],
            send_sem=self.line_send.at[way, step - 1],
            recv_sem=self.line_recv.at[way, step - 1],
            device_id=(self.place, toward),
            device_id_type=MESH,
        )

    def forward(self, step):
        for way in range(2):
            origin = line_origin(self.along, way, step - 1)
            pl.when(line_goes(self.along, self.count, way, step))(
                lambda way=way, origin=origin: self.line_copy(way, step, origin).start()
            )

    def arrive(self, step):
        for way in range(2):
            origin = line_origin(self.along, way, step)
            pl.when(line_comes(self.along, self.count, way, step))(
                lambda way=way, origin=origin: self.line_copy(way, step, origin).wait_recv()
            )
        if step < self.steps:
            self.forward(step + 1)

    def back_copy(self, way, owner, chunk):
        toward = self.along + 1 if way == 0 else self.along - 1
        columns = tile_at(chunk, BACK_TILE)
        landing = owner if way == 0 else jnp.where(owner == toward, self.count, owner)
        return pltpu.make_async_remote_copy(
            src_ref=self.outgoing.at[owner, :, columns],
            dst_ref=self.incoming.at[landing, :, columns],
            send_sem=self.back_send.at[way, owner, chunk],
            recv_sem=self.back_recv.at[way, owner, chunk],
            device_id=(self.place, toward),
            device_id_type=MESH,
        )

    def landed(self, way, owner, chunk, landing):
        columns = pl.ds(chunk * BACK_TILE, BACK_TILE)
        pltpu.make_async_remote_copy(
            src_ref=self.outgoing.at[owner, :, columns],
            dst_ref=self.incoming.at[landing, :, columns],
            send_sem=self.back_send.at[way, owner, chunk],
            recv_sem=self.back_recv.at[way, owner, chunk],
            device_id=(self.place, self.along),
            device_id_type=MESH,
        ).wait_recv()
        return self.incoming[landing, :, columns].astype(jnp.float32)

    def relays(self, way):
        return self.along >= 1 if way == 0 else self.along + 1 < self.count

    def run(self, compute, before_last):

        def one(way, step):
            back = 1 - way
            origin = line_origin(self.along, way, step)

            def work():
                def write(chunk, tile):
                    columns = tile_at(chunk, BACK_TILE)
                    self.outgoing[origin, :, columns] = tile.astype(self.outgoing.dtype)
                    pl.when(jnp.logical_not(self.relays(back)))(
                        lambda: self.back_copy(back, origin, chunk).start()
                    )

                compute(origin, write)

            pl.when(line_comes(self.along, self.count, way, step))(work)

        near_start = 2 * self.along < self.steps

        def relay(way, step, turn):
            owner = step if way == 0 else self.steps - step
            passes = owner > self.along if way == 0 else owner < self.along

            def work():
                for chunk in range(self.chunks):
                    more = self.landed(way, owner, chunk, owner)
                    columns = pl.ds(chunk * BACK_TILE, BACK_TILE)
                    mine = self.outgoing[owner, :, columns].astype(jnp.float32)
                    self.outgoing[owner, :, columns] = (mine + more).astype(self.outgoing.dtype)
                    self.back_copy(way, owner, chunk).start()

            pl.when(self.relays(way) & passes & turn)(work)

        for step in range(1, self.steps + 1):
            self.arrive(step)
            for way in range(2):
                one(way, step)
            if step == self.steps:
                before_last()
            relay(0, step, near_start)
            relay(1, step, True)
            relay(0, step, jnp.logical_not(near_start))

    def finish(self, total):
        for way in range(2):

            def receive(way=way):
                landing = self.along if way == 0 else self.count
                for chunk in range(self.chunks):
                    columns = pl.ds(chunk * BACK_TILE, BACK_TILE)
                    more = self.landed(way, self.along, chunk, landing)
                    total[:, columns] = total[:, columns] + more

            pl.when(self.relays(way))(receive)
        for step in range(1, self.steps + 1):
            for way in range(2):
                origin = line_origin(self.along, way, step - 1)

                def left(way=way, step=step, origin=origin):
                    self.line_copy(way, step, origin).wait_send()

                def returned(way=way, step=step):
                    for chunk in range(self.chunks):
                        self.back_copy(1 - way, line_origin(self.along, way, step), chunk).wait_send()

                pl.when(line_goes(self.along, self.count, way, step))(left)
                pl.when(line_comes(self.along, self.count, way, step))(returned)


def line_scratch(count, rows, columns):
    steps = count - 1
    chunks = columns // BACK_TILE
    return [
        pltpu.VMEM((count, rows, columns), jnp.bfloat16),
        pltpu.VMEM((count + 1, rows, columns), jnp.bfloat16),
        pltpu.SemaphoreType.DMA((2, steps)),
        pltpu.SemaphoreType.DMA((2, steps)),
        pltpu.SemaphoreType.DMA((2, count, chunks)),
        pltpu.SemaphoreType.DMA((2, count, chunks)),
    ]


def tile_at(t, size):
    return pl.ds(pl.multiple_of(t * size, size), size)


def feed_forward_kernel(
    count,
    rows_in,
    gate_hbm,
    up_hbm,
    down_hbm,
    total,
    gathered,
    gate_keep,
    up_keep,
    hidden_keep,
    gate_w,
    up_w,
    down_w,
    weight_sem,
    *parts,
):
    rows, width = rows_in.shape
    units = gate_w.shape[1]
    tile = FF_TILE
    line = LineExchange(count, rows_in, gathered, parts[0], parts[1], parts[2:])
    loads = []
    for n, (source, target) in enumerate(((gate_hbm, gate_w), (up_hbm, up_w), (down_hbm, down_w))):
        group = []
        for t in range(target.shape[1] // tile):
            at = (slice(None), pl.ds(t * tile, tile))
            group.append(pltpu.make_async_copy(source.at[at], target.at[at], weight_sem.at[n, t]))
        loads.append(group)
    for t in range(units // tile):
        loads[0][t].start()
        loads[1][t].start()
    for load in loads[2]:
        load.start()
    partner_barrier(line.partners())
    line.forward(1)
    gathered[line.along] = rows_in[...]

    def hidden_tile(origin, columns):
        at = pl.ds(pl.multiple_of(origin * rows, rows), rows)
        gate = forward_product(gathered[origin], gate_w[:, columns])
        up = forward_product(gathered[origin], up_w[:, columns])
        gate_keep[at, columns] = gate.astype(gate_keep.dtype)
        up_keep[at, columns] = up.astype(up_keep.dtype)
        hidden_keep[at, columns] = hidden_piece(gate, up).astype(hidden_keep.dtype)

    def out_tile(origin, columns):
        at = pl.ds(pl.multiple_of(origin * rows, rows), rows)
        return forward_product(hidden_keep[at], down_w[:, columns])

    for t in range(units // tile):
        loads[0][t].wait()
        loads[1][t].wait()
        hidden_tile(line.along, pl.ds(t * tile, tile))
    for t in range(width // tile):
        loads[2][t].wait()
        columns = pl.ds(t * tile, tile)
        total[:, columns] = out_tile(line.along, columns)

    def compute(origin, write):
        def hidden_step(t, carry):
            hidden_tile(origin, tile_at(t, tile))
            return carry

        def out_step(t, carry):
            write(t, out_tile(origin, tile_at(t, tile)))
            return carry

        lax.fori_loop(0, units // tile, hidden_step, 0)
        lax.fori_loop(0, width // tile, out_step, 0)

    line.run(compute, lambda: None)
    line.finish(total)


def feed_forward(rows_in, gate_weight, up_weight, down_weight):
    count = lax.axis_size("fsdp")
    rows, width = rows_in.shape
    units = gate_weight.shape[1]
    low = jnp.bfloat16
    vmem = pl.BlockSpec(memory_space=pltpu.VMEM)
    hbm = pl.BlockSpec(memory_space=pltpu.HBM)
    kept = jax.ShapeDtypeStruct((count * rows, units), low)
    out, gathered, gate, up, hidden = pl.pallas_call(
        functools.partial(feed_forward_kernel, count),
        out_shape=[
            jax.ShapeDtypeStruct((rows, width), jnp.float32),
            jax.ShapeDtypeStruct((count, rows, width), low),
            kept,
            kept,
            kept,
        ],
        in_specs=[vmem, hbm, hbm, hbm],
        out_specs=[vmem] * 5,
        scratch_shapes=[
            pltpu.VMEM((width, units), low),
            pltpu.VMEM((width, units), low),
            pltpu.VMEM((units, width), low),
            pltpu.SemaphoreType.DMA((3, max(width, units) // FF_TILE)),
        ]
        + line_scratch(count, rows, width),
        compiler_params=pltpu.CompilerParams(
            collective_id=4, has_side_effects=True, vmem_limit_bytes=56 << 20
        ),
        cost_estimate=pl.CostEstimate(
            flops=6 * count * rows * width * units,
            bytes_accessed=6 * width * units,
            transcendentals=count * rows * units,
        ),
        name="feed_forward",
    )(rows_in, gate_weight, up_weight, down_weight)
    return out, gathered.reshape(count * rows, width), gate, up, hidden


def hidden_pull_tile(grad, gate, up):
    slope = math.sqrt(2.0 / math.pi)
    square = gate * gate
    curve = jnp.tanh(slope * gate * (1.0 + 0.044715 * square))
    bend = 0.5 * (1.0 + curve)
    steep = bend + 0.5 * gate * (1.0 - curve * curve) * slope * (1.0 + 3.0 * 0.044715 * square)
    return grad * up * steep, grad * gate * bend


def feed_forward_backward_kernel(
    count,
    grads_in,
    gate_keep,
    up_keep,
    hidden_keep,
    tokens,
    gate_hbm,
    up_hbm,
    down_hbm,
    total,
    down_sum,
    down_rest,
    gate_grad,
    up_grad,
    gathered,
    gate_back,
    up_back,
    gate_w,
    up_w,
    down_w,
    weight_sem,
    staged,
    staged_sem,
    later_in,
    send_zero,
    recv_zero,
    send_sem,
    recv_sem,
    ready_sem,
    rest_sem,
    *parts,
):
    rows, width = grads_in.shape
    ctx_count, block, units = gate_w.shape
    pairs = ctx_count // 2
    position = ctx_position(ctx_count)
    bits, _, _, mine, partners, _ = position
    tile = FF_TILE
    blocks = tile // block
    line = LineExchange(count, grads_in, gathered, parts[0], parts[1], parts[2:])
    loads = []
    for n, (source, target) in enumerate(((gate_hbm, gate_w), (up_hbm, up_w), (down_hbm, down_w))):
        group = []
        size = tile if n else blocks
        for t in range(target.shape[0] // size):
            at = pl.ds(t * size, size)
            group.append(pltpu.make_async_copy(source.at[at], target.at[at], weight_sem.at[n, t]))
        loads.append(group)
    for load in loads[2]:
        load.start()
    for t in range(width // tile):
        loads[0][t].start()
        loads[1][t].start()
    partner_barrier(partners + line.partners())
    line.forward(1)
    gathered[line.along] = grads_in[...]

    def hidden_tile(origin, columns):
        at = pl.ds(pl.multiple_of(origin * rows, rows), rows)
        grad = across(gathered[origin], down_w[columns])
        gate = gate_keep[at, columns].astype(jnp.float32)
        up = up_keep[at, columns].astype(jnp.float32)
        gate_pull, up_pull = hidden_pull_tile(grad, gate, up)
        gate_back[at, columns] = gate_pull.astype(gate_back.dtype)
        up_back[at, columns] = up_pull.astype(up_back.dtype)

    def out_tile(origin, t):
        at = pl.ds(pl.multiple_of(origin * rows, rows), rows)
        gate_rows = gate_w[pl.ds(t * blocks, blocks)].reshape(tile, units)
        return across(gate_back[at], gate_rows) + across(up_back[at], up_w[tile_at(t, tile)])

    for t in range(units // tile):
        loads[2][t].wait()
        hidden_tile(line.along, pl.ds(t * tile, tile))
    for t in range(width // tile):
        loads[0][t].wait()
        loads[1][t].wait()
        total[:, pl.ds(t * tile, tile)] = out_tile(line.along, t)

    def compute(origin, write):
        def hidden_step(t, carry):
            hidden_tile(origin, tile_at(t, tile))
            return carry

        def out_step(t, carry):
            write(t, out_tile(origin, t))
            return carry

        lax.fori_loop(0, units // tile, hidden_step, 0)
        lax.fori_loop(0, width // tile, out_step, 0)

    half = down_sum.shape[1]
    here, there = pl.ds(0, half), pl.ds(half, units - half)
    down = Halving(
        position,
        block,
        lambda b: staged.at[b // 2 % 2, b % 2, :, here],
        lambda b: gate_w.at[b, :, here],
        gate_w.at[pl.ds(pairs, pairs), :, here],
        later_in,
        (send_zero, recv_zero, send_sem, recv_sem),
    )

    def down_block(c):
        left = gathered[:, :, tile_at(c, block)].reshape(count * rows, block)
        return over_rows(left, hidden_keep[...]).astype(gate_w.dtype)

    def rest_copy(source, c):
        return pltpu.make_async_copy(
            source.at[:, there], down_rest.at[tile_at(c, block)], rest_sem.at[c]
        )

    def given(b):
        return rest_copy(staged.at[b // 2 % 2, b % 2], 2 * b + 1 - mine[0])

    def kept(b):
        return rest_copy(gate_w.at[b], 2 * b + mine[0])

    def start_down():
        pl.semaphore_signal(ready_sem, inc=1, device_id=partners[0], device_id_type=MESH)
        pl.semaphore_wait(ready_sem, 1)
        for b in range(pairs):
            if b >= 4:
                down.first_copy(b - 4).wait_send()
                given(b - 4).wait()
            staged[b // 2 % 2, b % 2] = down_block(2 * b + 1 - mine[0])
            down.first_copy(b).start()
            given(b).start()
        for b in range(pairs):
            gate_w[b] = down_block(2 * b + mine[0])
            kept(b).start()
        for b in range(pairs):
            copy = down.first_copy(b)
            if b >= pairs - 4:
                copy.wait_send()
                given(b).wait()
            copy.wait_recv()
            add_rows(down.held(b), down.first_in.at[b], 0, block)
        down.start(0)

    def stage(slot, which, t, target):
        return pltpu.make_async_copy(
            staged.at[slot, which], target.at[tile_at(t, block)], staged_sem.at[slot, which]
        )

    def grad_bands(first, last):
        def step(t, carry):
            slot = lax.rem(t, 2)
            left = tokens[:, tile_at(t, block)]
            for which, (right, target) in enumerate(((gate_back, gate_grad), (up_back, up_grad))):

                @pl.when(t >= 2)
                def _(target=target, which=which):
                    stage(slot, which, t, target).wait()

                staged[slot, which] = over_rows(left, right[...]).astype(staged.dtype)
                stage(slot, which, t, target).start()
            return carry

        lax.fori_loop(first, last, step, 0)

    line.run(compute, start_down)
    grad_bands(0, ctx_count * 3 // 4)
    for step in range(1, bits - 1):
        down.end(step - 1)
        down.start(step)
    grad_bands(ctx_count * 3 // 4, ctx_count)
    line.finish(total)
    for t in (ctx_count - 2, ctx_count - 1):
        for which, target in enumerate((gate_grad, up_grad)):
            stage(t % 2, which, t, target).wait()
    for b in range(pairs):
        kept(b).wait()
    down.end(bits - 2)
    down_sum[...] = down.mine_now()[...]


def feed_forward_backward(
    grads_in, gate_keep, up_keep, hidden_keep, tokens, gate_weight, up_weight, down_weight
):
    count = lax.axis_size("fsdp")
    ctx_count = lax.axis_size("ctx")
    pairs = ctx_count // 2
    rows, width = grads_in.shape
    block = width // ctx_count
    half = gate_weight.shape[1] // 2
    units = gate_weight.shape[1]
    low = jnp.bfloat16
    vmem = pl.BlockSpec(memory_space=pltpu.VMEM)
    hbm = pl.BlockSpec(memory_space=pltpu.HBM)
    grad_shape = jax.ShapeDtypeStruct((width, units), low)
    return pl.pallas_call(
        functools.partial(feed_forward_backward_kernel, count),
        out_shape=[
            jax.ShapeDtypeStruct((rows, width), jnp.float32),
            jax.ShapeDtypeStruct((block, half), low),
            jax.ShapeDtypeStruct((width, units - half), low),
            grad_shape,
            grad_shape,
        ],
        in_specs=[vmem] * 5 + [hbm] * 3,
        out_specs=[vmem, vmem, hbm, hbm, hbm],
        scratch_shapes=[
            pltpu.VMEM((count, rows, width), low),
            pltpu.VMEM((count * rows, units), low),
            pltpu.VMEM((count * rows, units), low),
            pltpu.VMEM((ctx_count, block, units), low),
            pltpu.VMEM((width, units), low),
            pltpu.VMEM((units, width), low),
            pltpu.SemaphoreType.DMA((3, max(width, units) // FF_TILE)),
            pltpu.VMEM((2, 2, block, units), low),
            pltpu.SemaphoreType.DMA((2, 2)),
            *halving_scratch(ctx_count, block, half)[1:],
            pltpu.SemaphoreType.REGULAR,
            pltpu.SemaphoreType.DMA((ctx_count,)),
        ]
        + line_scratch(count, rows, width),
        compiler_params=pltpu.CompilerParams(
            collective_id=5, has_side_effects=True, vmem_limit_bytes=60 << 20
        ),
        cost_estimate=pl.CostEstimate(
            flops=12 * count * rows * width * units,
            bytes_accessed=12 * width * units,
            transcendentals=count * rows * units,
        ),
        name="feed_forward_backward",
    )(
        grads_in,
        gate_keep,
        up_keep,
        hidden_keep,
        tokens,
        gate_weight.reshape(ctx_count, block, units),
        up_weight,
        down_weight,
    )


def body(
    tokens,
    per_layer,
    out_grad,
    segment_ids,
    query_weight,
    key_weight,
    value_weight,
    out_weight,
    left_weight,
    right_weight,
    gate_weight,
    up_weight,
    down_weight,
    side_gate,
    side_out,
    input_gain,
    laurel_gain,
    attn_gain,
    pre_gain,
    post_gain,
    side_gain,
    query_gain,
    key_gain,
):
    low = jnp.bfloat16
    inputs = tokens[0].astype(jnp.float32)
    extra_rows = per_layer[0].astype(jnp.float32)
    cotangent = out_grad[0].astype(jnp.float32)
    sequence_ids = segment_ids[0]
    rows_here, width = inputs.shape
    ctx_count = lax.axis_size("ctx")
    fsdp_count = lax.axis_size("fsdp")
    count = ctx_count * fsdp_count
    ctx_place = lax.axis_index("ctx")
    rank = left_weight.shape[1]
    side = side_gate.shape[1]
    query_width = HEADS * HD
    kv_width = KV_HEADS * HD
    query_pos = ctx_place * rows_here + jnp.arange(rows_here, dtype=jnp.int32)

    piece = width // count

    qkv_width = query_width + 2 * kv_width
    full_qkv, second_line = weight_gather(
        [[query_weight, key_weight, value_weight], [out_weight, side_gate]], 1
    )

    normed, input_pull = jax.vjp(rms_norm, inputs, input_gain)
    normed_low = normed.astype(low)
    qkv_raw = forward_product(normed_low, full_qkv)
    frequency = jnp.exp(
        jnp.arange(HD // 2).astype(jnp.float32) * (-2.0 * math.log(rope_theta) / HD)
    )
    angles = query_pos.astype(jnp.float32)[:, None] * frequency[None, :]
    cosine, sine_part = jnp.cos(angles), jnp.sin(angles)
    query_ids = lax.dynamic_slice_in_dim(sequence_ids, ctx_place * rows_here, rows_here)
    kv_all, query_low, attended_low, log_totals, full_second, *full_small = attention_forward(
        qkv_raw,
        cosine,
        sine_part,
        query_gain,
        key_gain,
        query_ids,
        sequence_ids,
        second_line,
        [left_weight, right_weight, side_out],
    )
    full_left, full_right, full_side_out = full_small
    full_left = full_left.reshape(width, rank)
    full_right = full_right.transpose(1, 0, 2).reshape(rank, width)
    full_side_out = full_side_out.reshape(side, width)
    full_second = full_second.reshape(width, -1)
    full_out = full_second[:, :width]
    full_side_gate = full_second[:, width:]
    left_low = forward_product(normed_low, full_left).astype(low)
    right_out = forward_product(left_low, full_right)
    attn_raw = forward_product(attended_low, full_out)

    def mix_piece(x, normed_in, attn_in, right_in, gain_one, gain_two, gain_three):
        mixed = (
            x + rms_norm(attn_in, gain_one) + normed_in + rms_norm(right_in, gain_two)
        ) * inverse_root
        return (mixed, rms_norm(mixed, gain_three))

    (mixed, ffn_in), mix_pull = jax.vjp(
        mix_piece, inputs, normed, attn_raw, right_out, attn_gain, laurel_gain, pre_gain
    )

    ffn_out, ffn_all, gate_raw, up_raw, hidden_low = feed_forward(
        ffn_in.astype(low), gate_weight, up_weight, down_weight
    )
    middle, middle_pull = jax.vjp(middle_piece, mixed, ffn_out, post_gain)
    middle_low = middle.astype(low)
    layer_gate = forward_product(middle_low, full_side_gate)
    layer_act, extra_pull = jax.vjp(hidden_piece, layer_gate, extra_rows)
    layer_low = layer_act.astype(low)
    layer_out = forward_product(layer_low, full_side_out)
    result, out_pull = jax.vjp(middle_piece, middle, layer_out, side_gain)

    middle_grad_one, layer_out_grad, side_gain_grad = out_pull(cotangent)
    layer_grad_low = layer_out_grad.astype(low)
    side_out_grad = over_rows(layer_low, layer_grad_low)
    layer_gate_grad, extra_grad = extra_pull(across(layer_grad_low, full_side_out))
    gate_grad_low = layer_gate_grad.astype(low)
    side_gate_grad = over_rows(gate_grad_low, middle_low)
    mixed_grad_one, ffn_out_grad, post_gain_grad = middle_pull(
        middle_grad_one + across(gate_grad_low, full_side_gate)
    )
    ffn_in_grad, down_sum, down_rest, gate_weight_grad, up_weight_grad = feed_forward_backward(
        ffn_out_grad.astype(low),
        gate_raw,
        up_raw,
        hidden_low,
        ffn_all,
        gate_weight,
        up_weight,
        down_weight,
    )
    ffn_in_grad, late_low = lax.optimization_barrier((ffn_in_grad, (attended_low, normed_low)))
    attended_all, normed_all = (gather(part, "fsdp") for part in late_low)
    (
        inputs_grad_one,
        normed_grad_one,
        attn_raw_grad,
        right_out_grad,
        attn_gain_grad,
        laurel_gain_grad,
        pre_gain_grad,
    ) = mix_pull((mixed_grad_one, ffn_in_grad))
    attn_grad_low = attn_raw_grad.astype(low)
    right_grad_low = right_out_grad.astype(low)
    right_weight_grad = over_rows(right_grad_low, left_low)
    left_grad_low = across(right_grad_low, full_right).astype(low)
    left_weight_grad = over_rows(normed_low, left_grad_low)
    (
        qkv_back_low,
        query_gain_grad,
        key_gain_grad,
        out_columns,
        normed_grad_two,
        ffn_sums,
        qkv_columns,
    ) = attention_backward(
        query_low,
        kv_all,
        log_totals,
        qkv_raw,
        cosine,
        sine_part,
        query_gain,
        key_gain,
        query_ids,
        sequence_ids,
        attn_grad_low,
        full_second,
        full_qkv,
        [gate_weight_grad, up_weight_grad],
    )
    down_rest, normed_grad_two = lax.optimization_barrier((down_rest, normed_grad_two))
    down_rest = scatter_sum(down_rest, "ctx")
    normed_grad_two = normed_grad_two + across(left_grad_low, full_left)
    inputs_grad_two, input_gain_grad = input_pull(normed_grad_one + normed_grad_two)
    block_out = result.astype(low)[None]
    tokens_grad = (inputs_grad_one + inputs_grad_two).astype(low)[None]
    per_layer_grad = extra_grad.astype(low)[None]

    def columns_to_owner(x):
        parts = x.reshape(rows_here, fsdp_count, -1).transpose(1, 0, 2)
        return lax.all_to_all(parts, "fsdp", 0, 0, tiled=True).reshape(fsdp_count * rows_here, -1)

    out_weight_grad = over_rows(attended_all, out_columns)
    if qkv_columns is None:
        qkv_parts = jnp.concatenate(
            [
                part.reshape(rows_here, fsdp_count, -1)
                for part in (
                    qkv_back_low[:, :query_width],
                    qkv_back_low[:, query_width : query_width + kv_width],
                    qkv_back_low[:, query_width + kv_width :],
                )
            ],
            axis=2,
        )
        qkv_columns = columns_to_owner(qkv_parts.reshape(rows_here, -1))
    qkv_weight_grad = over_rows(normed_all, qkv_columns)

    small_gains = [
        jnp.pad(g.reshape(count, -1), ((0, 0), (0, piece - g.shape[0] // count))).reshape(-1)
        for g in (query_gain_grad, key_gain_grad)
    ]
    gains = jnp.stack(
        [
            input_gain_grad,
            laurel_gain_grad,
            attn_gain_grad,
            pre_gain_grad,
            post_gain_grad,
            side_gain_grad,
            *small_gains,
        ]
    )
    gate_blocks = side_gate_grad.astype(low).reshape(side, ctx_count, -1).transpose(1, 0, 2)
    gate_columns = width // ctx_count
    tall = jnp.concatenate(
        [
            left_weight_grad.astype(low),
            right_weight_grad.astype(low),
            jnp.pad(gains.astype(low).T, ((0, 0), (0, 128 - gains.shape[0]))),
        ],
        axis=1,
    )
    out_blocks = side_out_grad.astype(low).reshape(
        ctx_count, side // ctx_count, fsdp_count, width // fsdp_count
    )
    out_blocks = out_blocks.transpose(0, 2, 1, 3).reshape(-1, width // fsdp_count)
    out_weight_grad, qkv_weight_grad, tall, gate_blocks, side_out_grad = owner_sums(
        [
            out_weight_grad.astype(low),
            qkv_weight_grad.astype(low),
            tall,
            gate_blocks.reshape(-1, gate_columns),
            out_blocks,
        ],
        3,
    )
    gate_weight_grad, up_weight_grad = ffn_sums
    down_weight_grad = jnp.concatenate([down_sum.T, down_rest.T], axis=0)
    query_part = query_width // fsdp_count
    kv_part = kv_width // fsdp_count
    query_weight_grad = qkv_weight_grad[:, :query_part]
    key_weight_grad = qkv_weight_grad[:, query_part : query_part + kv_part]
    value_weight_grad = qkv_weight_grad[:, query_part + kv_part :]
    wide = jnp.float32
    tall = tall.astype(wide)
    left_weight_grad = tall[:, :rank]
    right_weight_grad = tall[:, rank : 2 * rank].T
    gains = tall[:, 2 * rank : 2 * rank + 8].T
    small_part = query_gain.shape[0] // count
    side_gate_grad = gate_blocks.astype(wide).T
    side_out_grad = side_out_grad.astype(wide)
    return (
        block_out,
        tokens_grad,
        per_layer_grad,
        query_weight_grad.astype(wide),
        key_weight_grad.astype(wide),
        value_weight_grad.astype(wide),
        out_weight_grad.astype(wide),
        left_weight_grad,
        right_weight_grad,
        gate_weight_grad.astype(wide),
        up_weight_grad.astype(wide),
        down_weight_grad.astype(wide),
        side_gate_grad,
        side_out_grad,
        *(gains[n] for n in range(6)),
        gains[6, :small_part],
        gains[7, :small_part],
    )


def solution(mesh):
    placed = (
        P("fsdp", "ctx", None),
        P("fsdp", "ctx", None),
        P("fsdp", "ctx", None),
        P("fsdp", None),
        P("fsdp", None),
        P("fsdp", None),
        P("fsdp", None),
        P("fsdp", None),
        P("fsdp", None),
        P(None, "fsdp"),
        P(None, "fsdp"),
        P(None, "fsdp"),
        P("fsdp", None),
        P("fsdp", None),
        P("fsdp", None),
        P(),
        P(),
        P(),
        P(),
        P(),
        P(),
        P(),
        P(),
    )
    return jax.shard_map(
        body,
        mesh=mesh,
        in_specs=placed,
        out_specs=(
            P("fsdp", "ctx", None),
            P("fsdp", "ctx", None),
            P("fsdp", "ctx", None),
            P("ctx", "fsdp"),
            P("ctx", "fsdp"),
            P("ctx", "fsdp"),
            P("ctx", "fsdp"),
            P(("ctx", "fsdp"), None),
            P(None, ("ctx", "fsdp")),
            P("ctx", "fsdp"),
            P("ctx", "fsdp"),
            P("fsdp", "ctx"),
            P("ctx", "fsdp"),
            P("ctx", "fsdp"),
            P(("ctx", "fsdp")),
            P(("ctx", "fsdp")),
            P(("ctx", "fsdp")),
            P(("ctx", "fsdp")),
            P(("ctx", "fsdp")),
            P(("ctx", "fsdp")),
            P(("ctx", "fsdp")),
            P(("ctx", "fsdp")),
        ),
        check_vma=False,
    )
```
